32 devices in a mesh: slab: 8 (over z, x), pencil: 4 (over y, core).
Axes of the slice: x: 2, y: 2, z: 4, core: 2. Of those that a mesh axis runs over, the one named last changes fastest.
Arguments:
- atom_cell: int32 [3, 262144], P(None, ('slab', 'pencil')), may hold values from 0 to 511, as said below
- charge: float32 [262144], P(('slab', 'pencil')), may hold values from -4 to 4
Outputs:
- potential: float32 [64, 128, 512], P('slab', 'pencil')
- forces: float32 [3, 262144], P(None, ('slab', 'pencil'))
The draws below stay inside these ranges and needn't reach their ends.
Inputs may be any that keep to these rules, and one draw needn't show every extreme that they name: `atom_cell`: the atoms of rows b * 8192 to (b + 1) * 8192 - 1, with b = s * 4 + r, lie in z planes s * 8 to (s + 1) * 8 - 1 and y rows r * 32 to (r + 1) * 32 - 1. Row 0 is at cell (0, 0, 0) and the last row at cell (63, 127, 511).
All inputs are finite; a program needn't handle non-finite values.
Results may differ from the reference program's by a relative error of at most 0.0003.
Values sent between devices are 32-bit elements; how exact they have to be, the bound alone decides.
A program may use at most 128 MiB of HBM per device.

```python
import math
from functools import partial
import jax
import jax.numpy as jnp
from jax import lax

CZ = 8
CY = 32
NX = 512
A_DEV = 8192
LEVELS = 5
RADIUS = 2
F = 32
NZ = 64
NY = 128
TZ = 2
TY = 4
TX = 16
TOPS = 128
ATOMS = 262144


def draw_atom_cell(key, part):
    row_ids = jnp.arange(ATOMS, dtype=jnp.int32)
    block_ids = row_ids // A_DEV
    per_slab = NY // CY
    slab_ids = block_ids // per_slab
    pencil_ids = block_ids % per_slab
    key_z, key_y, key_x = jax.random.split(key, 3)
    cell_z = slab_ids * CZ + jax.random.randint(key_z, (ATOMS,), 0, CZ, dtype=jnp.int32)
    cell_y = pencil_ids * CY + jax.random.randint(key_y, (ATOMS,), 0, CY, dtype=jnp.int32)
    cell_x = jax.random.randint(key_x, (ATOMS,), 0, NX, dtype=jnp.int32)
    first_row = row_ids == 0
    final_row = row_ids == ATOMS - 1
    cell_z = jnp.where(first_row, 0, jnp.where(final_row, NZ - 1, cell_z))
    cell_y = jnp.where(first_row, 0, jnp.where(final_row, NY - 1, cell_y))
    cell_x = jnp.where(first_row, 0, jnp.where(final_row, NX - 1, cell_x))
    return jnp.stack([cell_z, cell_y, cell_x]).astype(jnp.int32)


def draw_charge(key, part):
    values = jnp.clip(jax.random.normal(key, (ATOMS,), jnp.float32), -4.0, 4.0)
    return values


def setup_inputs(seed: int = 0) -> dict:
    streams_of = jax.random.split(jax.random.key(seed), 3)
    return {
        "atom_cell": draw_atom_cell(jax.random.fold_in(streams_of[2], 71), 0),
        "charge": draw_charge(jax.random.fold_in(streams_of[2], 71), 0),
    }


def kernel_weight(step_z, step_y, step_x):
    squared = step_z * step_z + step_y * step_y + step_x * step_x
    return 1.0 / math.sqrt(squared + 0.25) - 1.0 / math.sqrt(squared + 4.0)

def level_weight(scale, step_z, step_y, step_x):
    squared = step_z * step_z + step_y * step_y + step_x * step_x
    return scale * (1.0 / math.sqrt(squared + 1.0) - 1.0 / math.sqrt(squared + 4.0))

def short_field(padded, plane_count, row_count, row_length, radius_cells, weight_of):
    accumulated = jnp.zeros((plane_count, row_count, row_length), jnp.float32)
    for step_z in range(-radius_cells, radius_cells + 1):
        for step_y in range(-radius_cells, radius_cells + 1):
            for step_x in range(-radius_cells, radius_cells + 1):
                corner_z = radius_cells + step_z
                corner_y = radius_cells + step_y
                corner_x = radius_cells + step_x
                accumulated = accumulated + weight_of(step_z, step_y, step_x) * padded[corner_z:corner_z + plane_count, corner_y:corner_y + row_count, corner_x:corner_x + row_length]
    return accumulated

def restrict(grid):
    planes, rows, length = grid.shape
    return grid.reshape(planes // 2, 2, rows // 2, 2, length // 2, 2).sum(axis=(1, 3, 5))

def level_field(grid, weight_of):
    planes, rows, length = grid.shape
    padded = jnp.pad(grid, RADIUS)
    span = 2 * RADIUS + 1

    def one_plane(plane_id):
        window = lax.dynamic_slice_in_dim(padded, plane_id, span, 0)
        return short_field(window, 1, rows, length, RADIUS, weight_of)[0]
    return lax.map(one_plane, jnp.arange(planes, dtype=jnp.int32))

def interp_axis(values, axis, fine_ids, level_count, factor, first_col):
    numerator = jnp.clip(2 * fine_ids + 1 - factor, 0, 2 * factor * (level_count - 1))
    lower_index = jnp.minimum(numerator // (2 * factor), level_count - 2)
    fraction = (numerator - lower_index * 2 * factor).astype(jnp.float32) / (2.0 * factor)
    local_index = (lower_index - first_col).astype(jnp.int32)
    low_values = jnp.take(values, local_index, axis=axis)
    high_values = jnp.take(values, local_index + 1, axis=axis)
    shape = [1, 1, 1]
    shape[axis] = fine_ids.shape[0]
    weight_high = fraction.reshape(shape)
    return (1.0 - weight_high) * low_values + weight_high * high_values

def to_fine(field, counts, factor, plane_ids, line_ids, column_ids, first_z, first_y):
    section = interp_axis(field, 0, plane_ids, counts[0], factor, first_z)
    section = interp_axis(section, 1, line_ids, counts[1], factor, first_y)
    return interp_axis(section, 2, column_ids, counts[2], factor, 0)

def top_coords(cell_ids, top_y, top_x):
    return (cell_ids // (top_y * top_x), cell_ids // top_x % top_y, cell_ids % top_x)

def top_potential(targets, charges_flat, top_z, top_y, top_x, strength):
    sources = jnp.arange(top_z * top_y * top_x, dtype=jnp.int32)
    target_xyz = top_coords(targets, top_y, top_x)
    source_xyz = top_coords(sources, top_y, top_x)
    distance = jnp.ones((targets.shape[0], sources.shape[0]), jnp.float32)
    for component in range(3):
        offset = (target_xyz[component][:, None] - source_xyz[component][None, :]).astype(jnp.float32)
        distance = distance + offset * offset
    kernel = strength / jnp.sqrt(distance)
    return jnp.dot(kernel, charges_flat, precision=lax.Precision.HIGHEST)

def gradient_along(padded, direction, plane_count, row_count, row_length):

    def shifted(offset_cells):
        corner = [2, 2, 2]
        corner[direction] = corner[direction] + offset_cells
        return padded[corner[0]:corner[0] + plane_count, corner[1]:corner[1] + row_count, corner[2]:corner[2] + row_length]
    return (8.0 * (shifted(1) - shifted(-1)) - (shifted(2) - shifted(-2))) / 12.0

def reference(atom_cell, charge):
    cell_index = (atom_cell[0] * NY + atom_cell[1]) * NX + atom_cell[2]
    charge_grid = jax.ops.segment_sum(charge, cell_index, num_segments=NZ * NY * NX).reshape(NZ, NY, NX)
    plane_ids = jnp.arange(NZ, dtype=jnp.int32)
    line_ids = jnp.arange(NY, dtype=jnp.int32)
    column_ids = jnp.arange(NX, dtype=jnp.int32)
    potential = level_field(charge_grid, kernel_weight)
    level_charge = charge_grid
    for level in range(1, LEVELS):
        level_charge = restrict(level_charge)
        field = level_field(level_charge, partial(level_weight, 1.0 / 2 ** level))
        potential = potential + to_fine(field, field.shape, 2 ** level, plane_ids, line_ids, column_ids, 0, 0)
    top_charge = restrict(level_charge)
    charges_flat = top_charge.reshape(TOPS)
    block_rows = math.gcd(TOPS, 512)
    target_blocks = jnp.arange(TOPS, dtype=jnp.int32).reshape(TOPS // block_rows, block_rows)
    strength = 1.0 / F
    top_field = lax.map(lambda targets: top_potential(targets, charges_flat, TZ, TY, TX, strength), target_blocks).reshape(TZ, TY, TX)
    potential = potential + to_fine(top_field, top_field.shape, F, plane_ids, line_ids, column_ids, 0, 0)
    rimmed = jnp.pad(potential, 2)
    gradients = jnp.stack([gradient_along(rimmed, direction, NZ, NY, NX) for direction in range(3)]).reshape(3, NZ * NY * NX)
    forces = -charge[None, :] * jnp.take(gradients, cell_index, axis=1)
    return (potential, forces)
```

```python
import functools
import math

import jax
import jax.numpy as jnp
import numpy as np
from jax import lax
from jax.experimental import pallas as pl
from jax.experimental.pallas import tpu as pltpu
from jax.sharding import PartitionSpec as P

CZ = 8
CY = 32
NX = 512
F = 32
ROWS = CZ * CY
CHUNK = 1024
MESH = pl.DeviceIdType.MESH
VMEM = pl.BlockSpec(memory_space=pltpu.VMEM)
HBM = pl.BlockSpec(memory_space=pltpu.HBM)
SQUARES = (0, 1, 2, 4, 5, 8)


def iota(shape, dim):
    return lax.broadcasted_iota(jnp.int32, shape, dim)


def near_weight(squared):
    return 1.0 / math.sqrt(squared + 0.25) - 1.0 / math.sqrt(squared + 4.0)


def level_weight(level, squared):
    return (1.0 / math.sqrt(squared + 1.0) - 1.0 / math.sqrt(squared + 4.0)) / 2**level


def split_two(values):
    high = values.astype(jnp.bfloat16)
    return high, (values - high.astype(jnp.float32)).astype(jnp.bfloat16)


def dot32(left, right):
    left_high, left_low = split_two(left)
    right_high, right_low = split_two(right)
    total = jnp.dot(left_high, right_high, preferred_element_type=jnp.float32)
    total += jnp.dot(left_high, right_low, preferred_element_type=jnp.float32)
    return total + jnp.dot(left_low, right_high, preferred_element_type=jnp.float32)


def local_rows(own_ref, half, start, width):
    z0 = lax.axis_index("slab") * CZ
    y0 = lax.axis_index("pencil") * CY
    row = 4 * half
    plane = own_ref[row : row + 1, pl.ds(start, width)].astype(jnp.int32) - z0
    line = own_ref[row + 1 : row + 2, pl.ds(start, width)].astype(jnp.int32) - y0
    columns = own_ref[row + 2 : row + 3, pl.ds(start, width)].astype(jnp.int32)
    return plane * CY + line, columns, own_ref[row + 3 : row + 4, pl.ds(start, width)]


def halve_rows(rows_out, rows_in, line_bits):
    out_row = iota((rows_out, rows_in), 0)
    in_row = iota((rows_out, rows_in), 1)
    plane = in_row >> (line_bits + 1)
    line = (in_row & (2**line_bits - 1)) >> 1
    return jnp.where((plane << (line_bits - 1)) + line == out_row, 1.0, 0.0).astype(jnp.bfloat16)


def halve_columns(columns_in, columns_out):
    return jnp.where(
        iota((columns_in, columns_out), 0) >> 1 == iota((columns_in, columns_out), 1), 1.0, 0.0
    ).astype(jnp.bfloat16)


def halve(values, rows_out, line_bits, columns_out):
    rows, columns = values.shape
    left = halve_rows(rows_out, rows, line_bits)
    high, low = split_two(values)
    part = jnp.dot(left, high, preferred_element_type=jnp.float32)
    part += jnp.dot(left, low, preferred_element_type=jnp.float32)
    right = halve_columns(columns, columns_out)
    high, low = split_two(part)
    whole = jnp.dot(high, right, preferred_element_type=jnp.float32)
    return whole + jnp.dot(low, right, preferred_element_type=jnp.float32)


def deposit(atoms_ref, total_ref, first_plane, planes):
    rows = planes * CY
    width = math.gcd(atoms_ref.shape[1], CHUNK)
    y0 = lax.axis_index("pencil") * CY
    total_ref[0:rows, :] = jnp.zeros((rows, NX), jnp.float32)

    @pl.loop(0, atoms_ref.shape[1] // width)
    def _(step):
        for half in range(2):
            here = pl.ds(pl.multiple_of(step * width, width), width)
            row = 4 * half
            plane = atoms_ref[row : row + 1, here].astype(jnp.int32) - first_plane
            line = atoms_ref[row + 1 : row + 2, here].astype(jnp.int32) - y0
            columns = atoms_ref[row + 2 : row + 3, here].astype(jnp.int32)
            charges = atoms_ref[row + 3 : row + 4, here]
            high = charges.astype(jnp.bfloat16).astype(jnp.float32)
            low = charges - high
            at_row = iota((rows, width), 0) == plane * CY + line
            table = jnp.where(iota((NX, width), 0) == columns, 1.0, 0.0).astype(jnp.bfloat16)
            stacked = jnp.concatenate(
                [
                    jnp.where(at_row, high, 0.0).astype(jnp.bfloat16),
                    jnp.where(at_row, low, 0.0).astype(jnp.bfloat16),
                ],
                axis=0,
            )
            added = lax.dot_general(
                stacked, table, (((1,), (1,)), ((), ())), preferred_element_type=jnp.float32
            )
            total_ref[0:rows, :] += added[:rows] + added[rows:]


def exchange_kernel(
    slabs,
    pencils,
    cell_hbm,
    charge_hbm,
    wide0,
    wide1,
    wide2,
    wide3,
    own,
    cell_ref,
    charge_ref,
    below,
    above,
    total,
    three,
    local,
    send,
    recv,
    send3,
    recv3,
):
    slab = lax.axis_index("slab")
    pencil = lax.axis_index("pencil")
    devices = slabs * pencils
    me = slab * pencils + pencil
    half = own.shape[1]
    loads = [
        pltpu.make_async_copy(cell_hbm, cell_ref, local.at[0]),
        pltpu.make_async_copy(charge_hbm, charge_ref, local.at[1]),
    ]
    for load in loads:
        load.start()
    for ref in (wide0, wide1, wide2):
        ref[...] = jnp.zeros_like(ref)

    def place(step):
        other = lax.rem(me + step, devices)
        return (other // pencils, lax.rem(other, pencils))

    barrier = pltpu.get_barrier_semaphore()

    @pl.loop(1, devices)
    def _(step):
        pl.semaphore_signal(barrier, inc=1, device_id=place(step), device_id_type=MESH)

    for load in loads:
        load.wait()
    for part in range(2):
        there = slice(part * half, (part + 1) * half)
        for row in range(3):
            own[4 * part + row : 4 * part + row + 1, :] = cell_ref[row : row + 1, there].astype(
                jnp.float32
            )
        own[4 * part + 3 : 4 * part + 4, :] = charge_ref[:, there]
    pl.semaphore_wait(barrier, devices - 1)

    def inside(dz, dy):
        z = slab + dz
        y = pencil + dy
        return (z >= 0) & (z < slabs) & (y >= 0) & (y < pencils)

    copies = []

    def add(source, target, dz, dy):
        copies.append((source, target, dz, dy))
        return len(copies) - 1

    to_above = add(own, below, 1, 0)
    to_below = add(own, above, -1, 0)
    lines0 = {1: (32, 0), -1: (8, 40)}
    middle_y = [
        add(wide0.at[4:12, a : a + 8], wide0.at[4:12, b : b + 8], 0, dy)
        for dy, (a, b) in lines0.items()
    ]
    below_y = [
        add(wide0.at[0:4, a : a + 8], wide0.at[0:4, b : b + 8], 0, dy)
        for dy, (a, b) in lines0.items()
    ]
    above_y = [
        add(wide0.at[12:16, a : a + 8], wide0.at[12:16, b : b + 8], 0, dy)
        for dy, (a, b) in lines0.items()
    ]
    one_z = [
        add(wide1.at[4:8, 8:24], wide1.at[a : a + 4, 8:24], dz, 0) for dz, a in ((1, 0), (-1, 8))
    ]
    one_y = [
        add(wide1.at[:, a : a + 8], wide1.at[:, b : b + 8], 0, dy)
        for dy, a, b in ((1, 16, 0), (-1, 8, 24))
    ]
    two_all = [
        add(
            wide2.at[4:6, 8:16],
            wide2.at[4 - 2 * dz : 6 - 2 * dz, 8 - 8 * dy : 16 - 8 * dy],
            dz,
            dy,
        )
        for dz in range(-2, 3)
        for dy in (-1, 0, 1)
        if dz or dy
    ]

    def copy_of(index, device):
        source, target, _, _ = copies[index]
        return pltpu.make_async_remote_copy(
            src_ref=source,
            dst_ref=target,
            send_sem=send.at[index],
            recv_sem=recv.at[index],
            device_id=device,
            device_id_type=MESH,
        )

    def start(indices, also=True):
        for index in indices:
            _, _, dz, dy = copies[index]

            @pl.when(inside(dz, dy) & also)
            def _(index=index, dz=dz, dy=dy):
                copy_of(index, (slab + dz, pencil + dy)).start()

    def arrived(indices, also=True):
        for index in indices:
            _, _, dz, dy = copies[index]

            @pl.when(inside(-dz, -dy) & also)
            def _(index=index, dz=dz, dy=dy):
                copy_of(index, (slab - dz, pencil - dy)).wait_recv()

    def sent(indices, also=True):
        for index in indices:
            _, _, dz, dy = copies[index]

            @pl.when(inside(dz, dy) & also)
            def _(index=index, dz=dz, dy=dy):
                copy_of(index, (slab + dz, pencil + dy)).wait_send()

    def top_copy(step, slot):
        return pltpu.make_async_remote_copy(
            src_ref=three,
            dst_ref=wide3.at[slot],
            send_sem=send3.at[step],
            recv_sem=recv3.at[step],
            device_id=place(step),
            device_id_type=MESH,
        )

    start([to_above, to_below])
    deposit(own, total, CZ * slab, CZ)
    grid = total[...]
    wide0[4:12, 8:40, :] = grid.reshape(CZ, CY, NX)
    start(middle_y)
    one = halve(grid, ROWS // 4, 5, NX // 2)
    wide1[4:8, 8:24, :] = one.reshape(CZ // 2, CY // 2, NX // 2)
    start(one_z)
    two = halve(one, ROWS // 16, 4, NX // 4)
    wide2[4:6, 8:16, :] = two.reshape(CZ // 4, CY // 4, NX // 4)
    start(two_all)
    lowest = halve(two, 8, 3, NX // 4)
    three[...] = lowest
    wide3[pl.ds(me, 1)] = lowest[None]

    @pl.loop(1, devices)
    def _(step):
        top_copy(step, me).start()

    has_below = slab > 0
    has_above = slab < slabs - 1
    arrived([to_above])

    @pl.when(has_below)
    def _():
        deposit(below, total, CZ * slab - 4, 4)
        wide0[0:4, 8:40, :] = total[0 : 4 * CY, :].reshape(4, CY, NX)

    start(below_y, has_below)
    arrived(one_z)
    start(one_y)
    arrived([to_below])

    @pl.when(has_above)
    def _():
        deposit(above, total, CZ * slab + CZ, 4)
        wide0[12:16, 8:40, :] = total[0 : 4 * CY, :].reshape(4, CY, NX)

    start(above_y, has_above)
    sent([to_above, to_below, *middle_y, *one_z, *two_all])
    arrived([*middle_y, *two_all])
    arrived(one_y)
    sent(one_y)

    @pl.loop(1, devices)
    def _(step):
        copy = top_copy(step, lax.rem(me + devices - step, devices))
        copy.wait_send()
        copy.wait_recv()

    arrived(below_y, has_below)
    sent(below_y, has_below)
    arrived(above_y, has_above)
    sent(above_y, has_above)


def exchange_call(slabs, pencils, atom_cell, charge):
    devices = slabs * pencils
    atoms = atom_cell.shape[1]
    shapes = (
        (16, 48, NX),
        (12, 32, NX // 2),
        (10, 32, NX // 4),
        (devices, 8, 128),
        (8, atoms // 2),
    )
    return pl.pallas_call(
        functools.partial(exchange_kernel, slabs, pencils),
        out_shape=[jax.ShapeDtypeStruct(shape, jnp.float32) for shape in shapes],
        in_specs=[HBM] * 2,
        out_specs=[VMEM] * 5,
        scratch_shapes=[
            pltpu.VMEM(atom_cell.shape, jnp.int32),
            pltpu.VMEM((1, atoms), jnp.float32),
            pltpu.VMEM((8, atoms // 2), jnp.float32),
            pltpu.VMEM((8, atoms // 2), jnp.float32),
            pltpu.VMEM((ROWS, NX), jnp.float32),
            pltpu.VMEM((8, 128), jnp.float32),
            pltpu.SemaphoreType.DMA((2,)),
            pltpu.SemaphoreType.DMA((26,)),
            pltpu.SemaphoreType.DMA((26,)),
            pltpu.SemaphoreType.DMA((devices,)),
            pltpu.SemaphoreType.DMA((devices,)),
        ],
        compiler_params=pltpu.CompilerParams(
            collective_id=0, has_side_effects=True, vmem_limit_bytes=40 * 2**20
        ),
    )(atom_cell, charge.reshape(1, -1))


def shift_x(values, step):
    width = values.shape[-1]
    axis = values.ndim - 1
    column = iota(values.shape, axis)
    moved = pltpu.roll(values, (-step) % width, axis)
    return jnp.where((column + step >= 0) & (column + step < width), moved, 0.0)


def pair_x(values, step):
    return shift_x(values, step) + shift_x(values, -step)


def hat(fine, cell, factor, count):
    bits = factor.bit_length()
    numerator = jnp.clip(2 * fine + 1 - factor, 0, 2 * factor * (count - 1))
    lower = jnp.minimum(numerator >> bits, count - 2)
    fraction = (numerator - (lower << bits)).astype(jnp.float32) * (0.5 / factor)
    return jnp.where(
        cell == lower, 1.0 - fraction, jnp.where(cell == lower + 1, fraction, 0.0)
    )


def window_stencil(level, planes_in, planes_out, lines, shift):
    blocks = []
    dz = np.arange(planes_in)[None, :] - np.arange(planes_out)[:, None] + shift
    dy = np.arange(lines)[None, :] - np.arange(lines)[:, None]
    dz = dz[:, None, :, None]
    dy = dy[None, :, None, :]
    near = (np.abs(dz) <= 2) & (np.abs(dy) <= 2)
    for c in range(3):
        squared = (dz * dz + dy * dy + c * c).astype(np.float64)
        weight = (1.0 / np.sqrt(squared + 1.0) - 1.0 / np.sqrt(squared + 4.0)) / 2**level
        weight = np.where(near, weight, 0.0)
        blocks.append(weight.reshape(planes_out * lines, planes_in * lines))
    return np.concatenate(blocks, axis=1).astype(np.float32)


def field_kernel(
    slabs,
    pencils,
    own_ref,
    wide0,
    wide1,
    wide2,
    wide3,
    stencil1,
    stencil2,
    pot_ref,
    force_ref,
    sums,
    wide_pot,
    field1,
    field2,
    field3,
    along_x,
    high_ref,
    low_ref,
):
    slab = lax.axis_index("slab")
    pencil = lax.axis_index("pencil")
    pencil_bits = pencils.bit_length() - 1

    grid1 = wide1[...].reshape(12 * 32, NX // 2)
    field1[...] = dot32(
        stencil1[...], jnp.concatenate([grid1, pair_x(grid1, 1), pair_x(grid1, 2)], axis=0)
    )
    grid2 = wide2[...].reshape(10 * 32, NX // 4)
    field2[...] = dot32(
        stencil2[...], jnp.concatenate([grid2, pair_x(grid2, 1), pair_x(grid2, 2)], axis=0)
    )
    rows3 = slabs * pencils * 8
    grid3 = wide3[...].reshape(rows3, 128)
    coarse = []
    first_row = 0
    first_lane = 0
    for level in (3, 4, 5):
        down = level - 3
        line_bits = pencil_bits + 2 - down
        lines = 2**line_bits
        planes = slabs >> down
        count = planes * lines
        length = NX >> level
        shape = (count, rows3)
        out_row = iota(shape, 0)
        in_row = iota(shape, 1)
        in_plane = in_row >> (3 + pencil_bits)
        in_line = (((in_row >> 3) & (pencils - 1)) << 2) + (in_row & 7)
        cell = ((in_plane >> down) << line_bits) + (in_line >> down)
        chosen = jnp.where((cell == out_row) & ((in_row & 7) < 4), 1.0, 0.0)
        charges = dot32(chosen, grid3)
        reach = 3 if level < 5 else length
        source = iota((128, 128), 0) >> down
        column = iota((128, 128), 1) - first_lane
        valid = (column >= 0) & (column < length)
        pairs = jnp.concatenate(
            [
                jnp.where(valid & (jnp.abs(source - column) == c), 1.0, 0.0)
                for c in range(reach)
            ],
            axis=1,
        )
        moved = dot32(charges, pairs)
        stacked = jnp.concatenate(
            [moved[:, c * 128 : (c + 1) * 128] for c in range(reach)], axis=0
        )
        blocks = []
        for c in range(reach):
            shape = (4 * lines, count)
            dz = (iota(shape, 1) >> line_bits) - (iota(shape, 0) >> line_bits)
            dz = dz - ((slab >> down) - 1)
            dy = (iota(shape, 1) & (lines - 1)) - (iota(shape, 0) & (lines - 1))
            squared = dz * dz + dy * dy
            if level < 5:
                weight = jnp.zeros(shape, jnp.float32)
                for value in SQUARES:
                    weight = jnp.where(
                        squared == value, level_weight(level, value + c * c), weight
                    )
                weight = jnp.where((jnp.abs(dz) <= 2) & (jnp.abs(dy) <= 2), weight, 0.0)
            else:
                weight = (1.0 / F) / jnp.sqrt((squared + (c * c + 1)).astype(jnp.float32))
            blocks.append(dot32(weight, stacked[c * count : (c + 1) * count]))
        field3[first_row : first_row + 4 * lines, :] = sum(blocks[1:], blocks[0])
        first_row = first_row + 4 * lines
        first_lane = first_lane + length

    lane = 0
    for level in range(1, 6):
        length = NX >> level
        rows = length if level < 5 else NX - lane
        weights = hat(iota((rows, NX), 1), iota((rows, NX), 0), 2**level, length)
        weights = jnp.where(iota((rows, NX), 0) < length, weights, 0.0)
        along_x[lane : lane + rows, :] = weights.astype(jnp.bfloat16)
        lane = lane + rows

    @pl.loop(0, 4)
    def _(step):

        def along_zy(level, planes, lines, plane0, line0):
            shape = (3, 48, planes * lines)
            bits = lines.bit_length() - 1
            fine_z = CZ * slab - 2 + 3 * step + iota(shape, 0)
            fine_y = CY * pencil - 8 + iota(shape, 1)
            plane = plane0 + (iota(shape, 2) >> bits)
            line = line0 + (iota(shape, 2) & (lines - 1))
            weights = hat(fine_z, plane, 2**level, (slabs * CZ) >> level) * hat(
                fine_y, line, 2**level, (pencils * CY) >> level
            )
            return weights.reshape(3 * 48, planes * lines)

        parts = [
            dot32(along_zy(1, 8, 32, 4 * slab - 2, 16 * pencil - 8), field1[...]),
            dot32(along_zy(2, 4, 32, 2 * slab - 1, 8 * pencil - 8), field2[...]),
        ]
        first_row = 0
        last = jnp.zeros((3 * 48, 128), jnp.float32)
        for level in (3, 4, 5):
            lines = (pencils * CY) >> level
            weights = along_zy(level, 4, lines, (slab >> (level - 3)) - 1, 0)
            last = last + dot32(weights, field3[first_row : first_row + 4 * lines, :])
            first_row = first_row + 4 * lines
        parts.append(last)
        high, low = split_two(jnp.concatenate(parts, axis=1))
        fine = jnp.dot(high, along_x[...], preferred_element_type=jnp.float32)
        fine += jnp.dot(low, along_x[...], preferred_element_type=jnp.float32)
        wide_pot[pl.ds(4 + 3 * step, 3)] = fine.reshape(3, 48, NX)

    for edge in (0, 1, 2, 3, 16, 17, 18, 19):
        wide_pot[edge] = jnp.zeros((48, NX), jnp.float32)

    @pl.loop(0, 16)
    def _(plane):
        values = wide0[plane]
        sums[0] = values
        sums[1] = pair_x(values, 1)
        sums[2] = pair_x(values, 2)
        for block in range(NX // 128):
            lanes = pl.ds(block * 128, 128)
            table = {}
            for c in range(3):
                part = sums[c, :, lanes]
                table[0, c] = part
                for b in (1, 2):
                    table[b, c] = pltpu.roll(part, b, 0) + pltpu.roll(part, 48 - b, 0)
            groups = {
                0: table[0, 0],
                1: table[0, 1] + table[1, 0],
                2: table[1, 1],
                4: table[0, 2] + table[2, 0],
                5: table[1, 2] + table[2, 1],
                8: table[2, 2],
            }
            for a in range(3):
                total = sum(near_weight(a * a + k) * groups[k] for k in SQUARES)
                for target in {a, -a}:
                    wide_pot[plane + 2 + target, :, lanes] += total

    @pl.loop(0, 12)
    def _(plane):
        shape = (48, NX)
        row = CY * pencil - 8 + iota(shape, 0)
        whole_plane = CZ * slab - 2 + plane + jnp.zeros(shape, jnp.int32)
        valid = (row >= 0) & (row < pencils * CY)
        valid = valid & (whole_plane >= 0) & (whole_plane < slabs * CZ)
        wide_pot[plane + 4] = jnp.where(valid, wide_pot[plane + 4], 0.0)

    def slope(after1, before1, after2, before2):
        return (8.0 * (after1 - before1) - (after2 - before2)) * (1.0 / 12.0)

    @pl.loop(0, CZ)
    def _(plane):
        middle = wide_pot[plane + 6]
        own = middle[8:40]
        pot_ref[plane] = own
        at = [wide_pot[plane + 6 + k, 8:40, :] for k in (1, -1, 2, -2)]
        across = [pltpu.roll(middle, (-k) % 48, 0)[8:40] for k in (1, -1, 2, -2)]
        along = [shift_x(own, k) for k in (1, -1, 2, -2)]
        for direction, four in enumerate((at, across, along)):
            high, low = split_two(slope(*four))
            start = pl.multiple_of(direction * ROWS + plane * CY, CY)
            high_ref[pl.ds(start, CY), :] = high
            low_ref[pl.ds(start, CY), :] = low

    half_atoms = own_ref.shape[1]
    width = math.gcd(half_atoms, 512)

    @pl.loop(0, half_atoms // width)
    def _(step):
        start = pl.multiple_of(step * width, width)
        for half in range(2):
            rows, columns, charges = local_rows(own_ref, half, start, width)
            at_row = iota((ROWS, width), 0) == rows
            table = jnp.where(iota((NX, width), 0) == columns, 1.0, 0.0).astype(jnp.bfloat16)
            place = pl.ds(pl.multiple_of(half * half_atoms + start, width), width)
            for direction in range(3):
                part = pl.ds(direction * ROWS, ROWS)
                at_cell = jnp.dot(high_ref[part, :], table, preferred_element_type=jnp.float32)
                at_cell += jnp.dot(low_ref[part, :], table, preferred_element_type=jnp.float32)
                chosen = jnp.sum(jnp.where(at_row, at_cell, 0.0), axis=0, keepdims=True)
                force_ref[direction : direction + 1, place] = -charges * chosen


def field_call(slabs, pencils, wide, own):
    stencil1 = window_stencil(1, 12, 8, 32, -2)
    stencil2 = window_stencil(2, 10, 4, 32, -3)
    field3_rows = sum(4 * ((pencils * CY) >> level) for level in (3, 4, 5))
    return pl.pallas_call(
        functools.partial(field_kernel, slabs, pencils),
        out_shape=[
            jax.ShapeDtypeStruct((CZ, CY, NX), jnp.float32),
            jax.ShapeDtypeStruct((3, 2 * own.shape[1]), jnp.float32),
        ],
        in_specs=[VMEM] * 7,
        out_specs=[VMEM] * 2,
        scratch_shapes=[
            pltpu.VMEM((3, 48, NX), jnp.float32),
            pltpu.VMEM((20, 48, NX), jnp.float32),
            pltpu.VMEM((8 * 32, NX // 2), jnp.float32),
            pltpu.VMEM((4 * 32, NX // 4), jnp.float32),
            pltpu.VMEM((field3_rows, 128), jnp.float32),
            pltpu.VMEM((NX, NX), jnp.bfloat16),
            pltpu.VMEM((3 * ROWS, NX), jnp.bfloat16),
            pltpu.VMEM((3 * ROWS, NX), jnp.bfloat16),
        ],
        compiler_params=pltpu.CompilerParams(vmem_limit_bytes=24 * 2**20),
    )(
        own,
        *wide,
        jnp.asarray(stencil1),
        jnp.asarray(stencil2),
    )


def solution(mesh):
    slabs = mesh.shape["slab"]
    pencils = mesh.shape["pencil"]

    def body(atom_cell, charge):
        *wide, own = exchange_call(slabs, pencils, atom_cell, charge)
        potential, forces = field_call(slabs, pencils, wide, own)
        return (potential, forces)

    return jax.shard_map(
        body,
        mesh=mesh,
        in_specs=(P(None, ("slab", "pencil")), P(("slab", "pencil"))),
        out_specs=(P("slab", "pencil", None), P(None, ("slab", "pencil"))),
        check_vma=False,
    )
```

```python
import functools
import math

import jax
import jax.numpy as jnp
import numpy as np
from jax import lax
from jax.experimental import pallas as pl
from jax.experimental.pallas import tpu as pltpu
from jax.sharding import PartitionSpec as P

CZ = 8
CY = 32
NX = 512
F = 32
ROWS = CZ * CY
CHUNK = 2048
MESH = pl.DeviceIdType.MESH
VMEM = pl.BlockSpec(memory_space=pltpu.VMEM)
HBM = pl.BlockSpec(memory_space=pltpu.HBM)
SQUARES = (0, 1, 2, 4, 5, 8)


def iota(shape, dim):
    return lax.broadcasted_iota(jnp.int32, shape, dim)


def iota16(shape, dim):
    return iota(shape, dim).astype(jnp.int16)


def one_hot(places, size):
    here = iota16((size, places.shape[1]), 0) == places
    return jnp.where(here, jnp.ones((), jnp.bfloat16), jnp.zeros((), jnp.bfloat16))


def near_weight(squared):
    return 1.0 / math.sqrt(squared + 0.25) - 1.0 / math.sqrt(squared + 4.0)


def level_weight(level, squared):
    return (1.0 / math.sqrt(squared + 1.0) - 1.0 / math.sqrt(squared + 4.0)) / 2**level


def split_two(values):
    high = values.astype(jnp.bfloat16)
    return high, (values - high.astype(jnp.float32)).astype(jnp.bfloat16)


def dot32(left, right):
    left_high, left_low = split_two(left)
    right_high, right_low = split_two(right)
    total = jnp.dot(left_high, right_high, preferred_element_type=jnp.float32)
    total += jnp.dot(left_high, right_low, preferred_element_type=jnp.float32)
    return total + jnp.dot(left_low, right_high, preferred_element_type=jnp.float32)


def local_rows(own_ref, half, start, width):
    z0 = lax.axis_index("slab") * CZ
    y0 = lax.axis_index("pencil") * CY
    row = 4 * half
    plane = own_ref[row : row + 1, pl.ds(start, width)].astype(jnp.int32) - z0
    line = own_ref[row + 1 : row + 2, pl.ds(start, width)].astype(jnp.int32) - y0
    columns = own_ref[row + 2 : row + 3, pl.ds(start, width)].astype(jnp.int32)
    return plane * CY + line, columns, own_ref[row + 3 : row + 4, pl.ds(start, width)]


def halve_rows(rows_out, rows_in, line_bits):
    out_row = iota((rows_out, rows_in), 0)
    in_row = iota((rows_out, rows_in), 1)
    plane = in_row >> (line_bits + 1)
    line = (in_row & (2**line_bits - 1)) >> 1
    return jnp.where((plane << (line_bits - 1)) + line == out_row, 1.0, 0.0).astype(jnp.bfloat16)


def halve_columns(columns_in, columns_out):
    return jnp.where(
        iota((columns_in, columns_out), 0) >> 1 == iota((columns_in, columns_out), 1), 1.0, 0.0
    ).astype(jnp.bfloat16)


def halve(values, rows_out, line_bits, columns_out):
    rows, columns = values.shape
    left = halve_rows(rows_out, rows, line_bits)
    high, low = split_two(values)
    part = jnp.dot(left, high, preferred_element_type=jnp.float32)
    part += jnp.dot(left, low, preferred_element_type=jnp.float32)
    right = halve_columns(columns, columns_out)
    high, low = split_two(part)
    whole = jnp.dot(high, right, preferred_element_type=jnp.float32)
    return whole + jnp.dot(low, right, preferred_element_type=jnp.float32)


def deposit(atoms_ref, total_ref, first_plane, planes):
    rows = planes * CY
    width = math.gcd(atoms_ref.shape[1], CHUNK)
    y0 = lax.axis_index("pencil") * CY
    total_ref[0:rows, :] = jnp.zeros((rows, NX), jnp.float32)

    @pl.loop(0, atoms_ref.shape[1] // width)
    def _(step):
        for half in range(2):
            here = pl.ds(pl.multiple_of(step * width, width), width)
            row = 4 * half
            plane = atoms_ref[row : row + 1, here].astype(jnp.int32) - first_plane
            line = atoms_ref[row + 1 : row + 2, here].astype(jnp.int32) - y0
            columns = atoms_ref[row + 2 : row + 3, here].astype(jnp.int16)
            high, low = split_two(atoms_ref[row + 3 : row + 4, here])
            at_row = iota16((rows, width), 0) == (plane * CY + line).astype(jnp.int16)
            table = one_hot(columns, NX)
            none = jnp.zeros((), jnp.bfloat16)
            stacked = jnp.concatenate(
                [jnp.where(at_row, high, none), jnp.where(at_row, low, none)], axis=0
            )
            added = lax.dot_general(
                stacked, table, (((1,), (1,)), ((), ())), preferred_element_type=jnp.float32
            )
            total_ref[0:rows, :] += added[:rows] + added[rows:]


def exchange_kernel(
    slabs,
    pencils,
    cell_hbm,
    charge_hbm,
    wide0,
    wide1,
    wide2,
    wide3,
    own,
    cell_ref,
    charge_ref,
    below,
    above,
    total,
    three,
    local,
    send,
    recv,
    send3,
    recv3,
):
    slab = lax.axis_index("slab")
    pencil = lax.axis_index("pencil")
    devices = slabs * pencils
    me = slab * pencils + pencil
    half = own.shape[1]
    loads = [
        pltpu.make_async_copy(cell_hbm, cell_ref, local.at[0]),
        pltpu.make_async_copy(charge_hbm, charge_ref, local.at[1]),
    ]
    for load in loads:
        load.start()
    for ref in (wide0, wide1, wide2):
        ref[...] = jnp.zeros_like(ref)

    def place(step):
        other = lax.rem(me + step, devices)
        return (other // pencils, lax.rem(other, pencils))

    barrier = pltpu.get_barrier_semaphore()

    @pl.loop(1, devices)
    def _(step):
        pl.semaphore_signal(barrier, inc=1, device_id=place(step), device_id_type=MESH)

    for load in loads:
        load.wait()
    for part in range(2):
        there = slice(part * half, (part + 1) * half)
        for row in range(3):
            own[4 * part + row : 4 * part + row + 1, :] = cell_ref[row : row + 1, there].astype(
                jnp.float32
            )
        own[4 * part + 3 : 4 * part + 4, :] = charge_ref[:, there]
    pl.semaphore_wait(barrier, devices - 1)

    def inside(dz, dy):
        z = slab + dz
        y = pencil + dy
        return (z >= 0) & (z < slabs) & (y >= 0) & (y < pencils)

    copies = []

    def add(source, target, dz, dy):
        copies.append((source, target, dz, dy))
        return len(copies) - 1

    to_above = add(own, below, 1, 0)
    to_below = add(own, above, -1, 0)
    lines0 = {1: (32, 0), -1: (8, 40)}
    middle_y = [
        add(wide0.at[4:12, a : a + 8], wide0.at[4:12, b : b + 8], 0, dy)
        for dy, (a, b) in lines0.items()
    ]
    below_y = [
        add(wide0.at[0:4, a : a + 8], wide0.at[0:4, b : b + 8], 0, dy)
        for dy, (a, b) in lines0.items()
    ]
    above_y = [
        add(wide0.at[12:16, a : a + 8], wide0.at[12:16, b : b + 8], 0, dy)
        for dy, (a, b) in lines0.items()
    ]
    one_z = [
        add(wide1.at[4:8, 8:24], wide1.at[a : a + 4, 8:24], dz, 0) for dz, a in ((1, 0), (-1, 8))
    ]
    one_y = [
        add(wide1.at[:, a : a + 8], wide1.at[:, b : b + 8], 0, dy)
        for dy, a, b in ((1, 16, 0), (-1, 8, 24))
    ]
    two_all = [
        add(
            wide2.at[4:6, 8:16],
            wide2.at[4 - 2 * dz : 6 - 2 * dz, 8 - 8 * dy : 16 - 8 * dy],
            dz,
            dy,
        )
        for dz in range(-2, 3)
        for dy in (-1, 0, 1)
        if dz or dy
    ]

    def copy_of(index, device):
        source, target, _, _ = copies[index]
        return pltpu.make_async_remote_copy(
            src_ref=source,
            dst_ref=target,
            send_sem=send.at[index],
            recv_sem=recv.at[index],
            device_id=device,
            device_id_type=MESH,
        )

    def start(indices, also=True):
        for index in indices:
            _, _, dz, dy = copies[index]

            @pl.when(inside(dz, dy) & also)
            def _(index=index, dz=dz, dy=dy):
                copy_of(index, (slab + dz, pencil + dy)).start()

    def arrived(indices, also=True):
        for index in indices:
            _, _, dz, dy = copies[index]

            @pl.when(inside(-dz, -dy) & also)
            def _(index=index, dz=dz, dy=dy):
                copy_of(index, (slab - dz, pencil - dy)).wait_recv()

    def sent(indices, also=True):
        for index in indices:
            _, _, dz, dy = copies[index]

            @pl.when(inside(dz, dy) & also)
            def _(index=index, dz=dz, dy=dy):
                copy_of(index, (slab + dz, pencil + dy)).wait_send()

    def top_copy(step, slot):
        return pltpu.make_async_remote_copy(
            src_ref=three,
            dst_ref=wide3.at[slot],
            send_sem=send3.at[step],
            recv_sem=recv3.at[step],
            device_id=place(step),
            device_id_type=MESH,
        )

    start([to_above, to_below])
    deposit(own, total, CZ * slab, CZ)
    grid = total[...]
    wide0[4:12, 8:40, :] = grid.reshape(CZ, CY, NX)
    start(middle_y)
    one = halve(grid, ROWS // 4, 5, NX // 2)
    wide1[4:8, 8:24, :] = one.reshape(CZ // 2, CY // 2, NX // 2)
    start(one_z)
    two = halve(one, ROWS // 16, 4, NX // 4)
    wide2[4:6, 8:16, :] = two.reshape(CZ // 4, CY // 4, NX // 4)
    start(two_all)
    lowest = halve(two, 8, 3, NX // 4)
    three[...] = lowest
    wide3[pl.ds(me, 1)] = lowest[None]

    @pl.loop(1, devices)
    def _(step):
        top_copy(step, me).start()

    has_below = slab > 0
    has_above = slab < slabs - 1
    arrived([to_above])

    @pl.when(has_below)
    def _():
        deposit(below, total, CZ * slab - 4, 4)
        wide0[0:4, 8:40, :] = total[0 : 4 * CY, :].reshape(4, CY, NX)

    start(below_y, has_below)
    arrived(one_z)
    start(one_y)
    arrived([to_below])

    @pl.when(has_above)
    def _():
        deposit(above, total, CZ * slab + CZ, 4)
        wide0[12:16, 8:40, :] = total[0 : 4 * CY, :].reshape(4, CY, NX)

    start(above_y, has_above)
    sent([to_above, to_below, *middle_y, *one_z, *two_all])
    arrived([*middle_y, *two_all])
    arrived(one_y)
    sent(one_y)

    @pl.loop(1, devices)
    def _(step):
        copy = top_copy(step, lax.rem(me + devices - step, devices))
        copy.wait_send()
        copy.wait_recv()

    arrived(below_y, has_below)
    sent(below_y, has_below)
    arrived(above_y, has_above)
    sent(above_y, has_above)


def exchange_call(slabs, pencils, atom_cell, charge):
    devices = slabs * pencils
    atoms = atom_cell.shape[1]
    shapes = (
        (16, 48, NX),
        (12, 32, NX // 2),
        (10, 32, NX // 4),
        (devices, 8, 128),
        (8, atoms // 2),
    )
    return pl.pallas_call(
        functools.partial(exchange_kernel, slabs, pencils),
        out_shape=[jax.ShapeDtypeStruct(shape, jnp.float32) for shape in shapes],
        in_specs=[HBM] * 2,
        out_specs=[VMEM] * 5,
        scratch_shapes=[
            pltpu.VMEM(atom_cell.shape, jnp.int32),
            pltpu.VMEM((1, atoms), jnp.float32),
            pltpu.VMEM((8, atoms // 2), jnp.float32),
            pltpu.VMEM((8, atoms // 2), jnp.float32),
            pltpu.VMEM((ROWS, NX), jnp.float32),
            pltpu.VMEM((8, 128), jnp.float32),
            pltpu.SemaphoreType.DMA((2,)),
            pltpu.SemaphoreType.DMA((26,)),
            pltpu.SemaphoreType.DMA((26,)),
            pltpu.SemaphoreType.DMA((devices,)),
            pltpu.SemaphoreType.DMA((devices,)),
        ],
        cost_estimate=pl.CostEstimate(flops=10**10, bytes_accessed=2**23, transcendentals=0),
        compiler_params=pltpu.CompilerParams(
            collective_id=0, has_side_effects=True, vmem_limit_bytes=40 * 2**20
        ),
    )(atom_cell, charge.reshape(1, -1))


def shift_x(values, step):
    width = values.shape[-1]
    axis = values.ndim - 1
    column = iota(values.shape, axis)
    moved = pltpu.roll(values, (-step) % width, axis)
    return jnp.where((column + step >= 0) & (column + step < width), moved, 0.0)


def pair_x(values, step):
    return shift_x(values, step) + shift_x(values, -step)


def hat(fine, cell, factor, count):
    bits = factor.bit_length()
    numerator = jnp.clip(2 * fine + 1 - factor, 0, 2 * factor * (count - 1))
    lower = jnp.minimum(numerator >> bits, count - 2)
    fraction = (numerator - (lower << bits)).astype(jnp.float32) * (0.5 / factor)
    return jnp.where(
        cell == lower, 1.0 - fraction, jnp.where(cell == lower + 1, fraction, 0.0)
    )


def window_stencil(level, planes_in, planes_out, lines, shift):
    blocks = []
    dz = np.arange(planes_in)[None, :] - np.arange(planes_out)[:, None] + shift
    dy = np.arange(lines)[None, :] - np.arange(lines)[:, None]
    dz = dz[:, None, :, None]
    dy = dy[None, :, None, :]
    near = (np.abs(dz) <= 2) & (np.abs(dy) <= 2)
    for c in range(3):
        squared = (dz * dz + dy * dy + c * c).astype(np.float64)
        weight = (1.0 / np.sqrt(squared + 1.0) - 1.0 / np.sqrt(squared + 4.0)) / 2**level
        weight = np.where(near, weight, 0.0)
        blocks.append(weight.reshape(planes_out * lines, planes_in * lines))
    return np.concatenate(blocks, axis=1).astype(np.float32)


def field_kernel(
    slabs,
    pencils,
    own_ref,
    wide0,
    wide1,
    wide2,
    wide3,
    stencil1,
    stencil2,
    pot_ref,
    force_ref,
    sums,
    wide_pot,
    field1,
    field2,
    field3,
    along_x,
    high_ref,
    low_ref,
):
    slab = lax.axis_index("slab")
    pencil = lax.axis_index("pencil")
    pencil_bits = pencils.bit_length() - 1

    grid1 = wide1[...].reshape(12 * 32, NX // 2)
    field1[...] = dot32(
        stencil1[...], jnp.concatenate([grid1, pair_x(grid1, 1), pair_x(grid1, 2)], axis=0)
    )
    grid2 = wide2[...].reshape(10 * 32, NX // 4)
    field2[...] = dot32(
        stencil2[...], jnp.concatenate([grid2, pair_x(grid2, 1), pair_x(grid2, 2)], axis=0)
    )
    rows3 = slabs * pencils * 8
    grid3 = wide3[...].reshape(rows3, 128)
    coarse = []
    first_row = 0
    first_lane = 0
    for level in (3, 4, 5):
        down = level - 3
        line_bits = pencil_bits + 2 - down
        lines = 2**line_bits
        planes = slabs >> down
        count = planes * lines
        length = NX >> level
        shape = (count, rows3)
        out_row = iota(shape, 0)
        in_row = iota(shape, 1)
        in_plane = in_row >> (3 + pencil_bits)
        in_line = (((in_row >> 3) & (pencils - 1)) << 2) + (in_row & 7)
        cell = ((in_plane >> down) << line_bits) + (in_line >> down)
        chosen = jnp.where((cell == out_row) & ((in_row & 7) < 4), 1.0, 0.0)
        charges = dot32(chosen, grid3)
        reach = 3 if level < 5 else length
        source = iota((128, 128), 0) >> down
        column = iota((128, 128), 1) - first_lane
        valid = (column >= 0) & (column < length)
        pairs = jnp.concatenate(
            [
                jnp.where(valid & (jnp.abs(source - column) == c), 1.0, 0.0)
                for c in range(reach)
            ],
            axis=1,
        )
        moved = dot32(charges, pairs)
        stacked = jnp.concatenate(
            [moved[:, c * 128 : (c + 1) * 128] for c in range(reach)], axis=0
        )
        blocks = []
        for c in range(reach):
            shape = (4 * lines, count)
            dz = (iota(shape, 1) >> line_bits) - (iota(shape, 0) >> line_bits)
            dz = dz - ((slab >> down) - 1)
            dy = (iota(shape, 1) & (lines - 1)) - (iota(shape, 0) & (lines - 1))
            squared = dz * dz + dy * dy
            if level < 5:
                weight = jnp.zeros(shape, jnp.float32)
                for value in SQUARES:
                    weight = jnp.where(
                        squared == value, level_weight(level, value + c * c), weight
                    )
                weight = jnp.where((jnp.abs(dz) <= 2) & (jnp.abs(dy) <= 2), weight, 0.0)
            else:
                weight = (1.0 / F) / jnp.sqrt((squared + (c * c + 1)).astype(jnp.float32))
            blocks.append(dot32(weight, stacked[c * count : (c + 1) * count]))
        field3[first_row : first_row + 4 * lines, :] = sum(blocks[1:], blocks[0])
        first_row = first_row + 4 * lines
        first_lane = first_lane + length

    lane = 0
    for level in range(1, 6):
        length = NX >> level
        rows = length if level < 5 else NX - lane
        weights = hat(iota((rows, NX), 1), iota((rows, NX), 0), 2**level, length)
        weights = jnp.where(iota((rows, NX), 0) < length, weights, 0.0)
        along_x[lane : lane + rows, :] = weights.astype(jnp.bfloat16)
        lane = lane + rows

    @pl.loop(0, 4)
    def _(step):

        def along_zy(level, planes, lines, plane0, line0):
            shape = (3, 48, planes * lines)
            bits = lines.bit_length() - 1
            fine_z = CZ * slab - 2 + 3 * step + iota(shape, 0)
            fine_y = CY * pencil - 8 + iota(shape, 1)
            plane = plane0 + (iota(shape, 2) >> bits)
            line = line0 + (iota(shape, 2) & (lines - 1))
            weights = hat(fine_z, plane, 2**level, (slabs * CZ) >> level) * hat(
                fine_y, line, 2**level, (pencils * CY) >> level
            )
            return weights.reshape(3 * 48, planes * lines)

        parts = [
            dot32(along_zy(1, 8, 32, 4 * slab - 2, 16 * pencil - 8), field1[...]),
            dot32(along_zy(2, 4, 32, 2 * slab - 1, 8 * pencil - 8), field2[...]),
        ]
        first_row = 0
        last = jnp.zeros((3 * 48, 128), jnp.float32)
        for level in (3, 4, 5):
            lines = (pencils * CY) >> level
            weights = along_zy(level, 4, lines, (slab >> (level - 3)) - 1, 0)
            last = last + dot32(weights, field3[first_row : first_row + 4 * lines, :])
            first_row = first_row + 4 * lines
        parts.append(last)
        high, low = split_two(jnp.concatenate(parts, axis=1))
        fine = jnp.dot(high, along_x[...], preferred_element_type=jnp.float32)
        fine += jnp.dot(low, along_x[...], preferred_element_type=jnp.float32)
        wide_pot[pl.ds(4 + 3 * step, 3)] = fine.reshape(3, 48, NX)

    for edge in (0, 1, 2, 3, 16, 17, 18, 19):
        wide_pot[edge] = jnp.zeros((48, NX), jnp.float32)

    @pl.loop(0, 16)
    def _(plane):
        values = wide0[plane]
        sums[0] = values
        sums[1] = pair_x(values, 1)
        sums[2] = pair_x(values, 2)
        for block in range(NX // 128):
            lanes = pl.ds(block * 128, 128)
            table = {}
            for c in range(3):
                part = sums[c, :, lanes]
                table[0, c] = part
                for b in (1, 2):
                    table[b, c] = pltpu.roll(part, b, 0) + pltpu.roll(part, 48 - b, 0)
            groups = {
                0: table[0, 0],
                1: table[0, 1] + table[1, 0],
                2: table[1, 1],
                4: table[0, 2] + table[2, 0],
                5: table[1, 2] + table[2, 1],
                8: table[2, 2],
            }
            for a in range(3):
                total = sum(near_weight(a * a + k) * groups[k] for k in SQUARES)
                for target in {a, -a}:
                    wide_pot[plane + 2 + target, :, lanes] += total

    @pl.loop(0, 12)
    def _(plane):
        shape = (48, NX)
        row = CY * pencil - 8 + iota(shape, 0)
        whole_plane = CZ * slab - 2 + plane + jnp.zeros(shape, jnp.int32)
        valid = (row >= 0) & (row < pencils * CY)
        valid = valid & (whole_plane >= 0) & (whole_plane < slabs * CZ)
        wide_pot[plane + 4] = jnp.where(valid, wide_pot[plane + 4], 0.0)

    def slope(after1, before1, after2, before2):
        return (8.0 * (after1 - before1) - (after2 - before2)) * (1.0 / 12.0)

    @pl.loop(0, CZ)
    def _(plane):
        middle = wide_pot[plane + 6]
        own = middle[8:40]
        pot_ref[plane] = own
        at = [wide_pot[plane + 6 + k, 8:40, :] for k in (1, -1, 2, -2)]
        across = [pltpu.roll(middle, (-k) % 48, 0)[8:40] for k in (1, -1, 2, -2)]
        along = [shift_x(own, k) for k in (1, -1, 2, -2)]
        for direction, four in enumerate((at, across, along)):
            high, low = split_two(slope(*four))
            start = pl.multiple_of(direction * ROWS + plane * CY, CY)
            high_ref[pl.ds(start, CY), :] = high
            low_ref[pl.ds(start, CY), :] = low

    half_atoms = own_ref.shape[1]
    width = math.gcd(half_atoms, 512)

    @pl.loop(0, half_atoms // width)
    def _(step):
        start = pl.multiple_of(step * width, width)
        for half in range(2):
            rows, columns, charges = local_rows(own_ref, half, start, width)
            at_row = iota((ROWS, width), 0) == rows
            table = one_hot(columns.astype(jnp.int16), NX)
            place = pl.ds(pl.multiple_of(half * half_atoms + start, width), width)
            for direction in range(3):
                part = pl.ds(direction * ROWS, ROWS)
                at_cell = jnp.dot(high_ref[part, :], table, preferred_element_type=jnp.float32)
                at_cell += jnp.dot(low_ref[part, :], table, preferred_element_type=jnp.float32)
                chosen = jnp.sum(jnp.where(at_row, at_cell, 0.0), axis=0, keepdims=True)
                force_ref[direction : direction + 1, place] = -charges * chosen


def field_call(slabs, pencils, wide, own):
    stencil1 = window_stencil(1, 12, 8, 32, -2)
    stencil2 = window_stencil(2, 10, 4, 32, -3)
    field3_rows = sum(4 * ((pencils * CY) >> level) for level in (3, 4, 5))
    return pl.pallas_call(
        functools.partial(field_kernel, slabs, pencils),
        out_shape=[
            jax.ShapeDtypeStruct((CZ, CY, NX), jnp.float32),
            jax.ShapeDtypeStruct((3, 2 * own.shape[1]), jnp.float32),
        ],
        in_specs=[VMEM] * 7,
        out_specs=[VMEM] * 2,
        scratch_shapes=[
            pltpu.VMEM((3, 48, NX), jnp.float32),
            pltpu.VMEM((20, 48, NX), jnp.float32),
            pltpu.VMEM((8 * 32, NX // 2), jnp.float32),
            pltpu.VMEM((4 * 32, NX // 4), jnp.float32),
            pltpu.VMEM((field3_rows, 128), jnp.float32),
            pltpu.VMEM((NX, NX), jnp.bfloat16),
            pltpu.VMEM((3 * ROWS, NX), jnp.bfloat16),
            pltpu.VMEM((3 * ROWS, NX), jnp.bfloat16),
        ],
        cost_estimate=pl.CostEstimate(flops=2 * 10**10, bytes_accessed=2**23, transcendentals=0),
        compiler_params=pltpu.CompilerParams(vmem_limit_bytes=24 * 2**20),
    )(
        own,
        *wide,
        jnp.asarray(stencil1),
        jnp.asarray(stencil2),
    )


def solution(mesh):
    slabs = mesh.shape["slab"]
    pencils = mesh.shape["pencil"]

    def body(atom_cell, charge):
        *wide, own = exchange_call(slabs, pencils, atom_cell, charge)
        potential, forces = field_call(slabs, pencils, wide, own)
        return (potential, forces)

    return jax.shard_map(
        body,
        mesh=mesh,
        in_specs=(P(None, ("slab", "pencil")), P(("slab", "pencil"))),
        out_specs=(P("slab", "pencil", None), P(None, ("slab", "pencil"))),
        check_vma=False,
    )
```

```python
import functools
import math

import jax
import jax.numpy as jnp
import numpy as np
from jax import lax
from jax.experimental import pallas as pl
from jax.experimental.pallas import tpu as pltpu
from jax.sharding import PartitionSpec as P

CZ = 8
CY = 32
NX = 512
F = 32
ROWS = CZ * CY
CHUNK = 2048
MESH = pl.DeviceIdType.MESH
VMEM = pl.BlockSpec(memory_space=pltpu.VMEM)
SQUARES = (0, 1, 2, 4, 5, 8)


def iota(shape, dim):
    return lax.broadcasted_iota(jnp.int32, shape, dim)


def iota16(shape, dim):
    return iota(shape, dim).astype(jnp.int16)


def one_hot(places, size):
    here = iota16((size, places.shape[1]), 0) == places
    return jnp.where(here, jnp.ones((), jnp.bfloat16), jnp.zeros((), jnp.bfloat16))


def near_weight(squared):
    return 1.0 / math.sqrt(squared + 0.25) - 1.0 / math.sqrt(squared + 4.0)


def level_weight(level, squared):
    return (1.0 / math.sqrt(squared + 1.0) - 1.0 / math.sqrt(squared + 4.0)) / 2**level


def split_two(values):
    high = values.astype(jnp.bfloat16)
    return high, (values - high.astype(jnp.float32)).astype(jnp.bfloat16)


def dot32(left, right):
    left_high, left_low = split_two(left)
    right_high, right_low = split_two(right)
    total = jnp.dot(left_high, right_high, preferred_element_type=jnp.float32)
    total += jnp.dot(left_high, right_low, preferred_element_type=jnp.float32)
    return total + jnp.dot(left_low, right_high, preferred_element_type=jnp.float32)


def local_rows(own_ref, half, start, width):
    z0 = lax.axis_index("slab") * CZ
    y0 = lax.axis_index("pencil") * CY
    row = 4 * half
    plane = own_ref[row : row + 1, pl.ds(start, width)].astype(jnp.int32) - z0
    line = own_ref[row + 1 : row + 2, pl.ds(start, width)].astype(jnp.int32) - y0
    columns = own_ref[row + 2 : row + 3, pl.ds(start, width)].astype(jnp.int32)
    return plane * CY + line, columns, own_ref[row + 3 : row + 4, pl.ds(start, width)]


def halve_rows(rows_out, rows_in, line_bits):
    out_row = iota((rows_out, rows_in), 0)
    in_row = iota((rows_out, rows_in), 1)
    plane = in_row >> (line_bits + 1)
    line = (in_row & (2**line_bits - 1)) >> 1
    return jnp.where((plane << (line_bits - 1)) + line == out_row, 1.0, 0.0).astype(jnp.bfloat16)


def halve_columns(columns_in, columns_out):
    return jnp.where(
        iota((columns_in, columns_out), 0) >> 1 == iota((columns_in, columns_out), 1), 1.0, 0.0
    ).astype(jnp.bfloat16)


def halve(values, rows_out, line_bits, columns_out):
    rows, columns = values.shape
    left = halve_rows(rows_out, rows, line_bits)
    high, low = split_two(values)
    part = jnp.dot(left, high, preferred_element_type=jnp.float32)
    part += jnp.dot(left, low, preferred_element_type=jnp.float32)
    right = halve_columns(columns, columns_out)
    high, low = split_two(part)
    whole = jnp.dot(high, right, preferred_element_type=jnp.float32)
    return whole + jnp.dot(low, right, preferred_element_type=jnp.float32)


def deposit(atoms_ref, total_ref, first_plane, planes):
    rows = planes * CY
    width = math.gcd(atoms_ref.shape[1], CHUNK)
    y0 = lax.axis_index("pencil") * CY
    total_ref[0:rows, :] = jnp.zeros((rows, NX), jnp.float32)

    @pl.loop(0, atoms_ref.shape[1] // width)
    def _(step):
        for half in range(2):
            here = pl.ds(pl.multiple_of(step * width, width), width)
            row = 4 * half
            plane = atoms_ref[row : row + 1, here].astype(jnp.int32) - first_plane
            line = atoms_ref[row + 1 : row + 2, here].astype(jnp.int32) - y0
            columns = atoms_ref[row + 2 : row + 3, here].astype(jnp.int16)
            high, low = split_two(atoms_ref[row + 3 : row + 4, here])
            at_row = iota16((rows, width), 0) == (plane * CY + line).astype(jnp.int16)
            table = one_hot(columns, NX)
            none = jnp.zeros((), jnp.bfloat16)
            stacked = jnp.concatenate(
                [jnp.where(at_row, high, none), jnp.where(at_row, low, none)], axis=0
            )
            added = lax.dot_general(
                stacked, table, (((1,), (1,)), ((), ())), preferred_element_type=jnp.float32
            )
            total_ref[0:rows, :] += added[:rows] + added[rows:]


def exchange_kernel(
    slabs,
    pencils,
    cell_ref,
    charge_ref,
    wide0,
    wide1,
    wide2,
    wide3,
    own,
    below,
    above,
    total,
    send,
    recv,
    send2,
    recv2,
    send3,
    recv3,
):
    slab = lax.axis_index("slab")
    pencil = lax.axis_index("pencil")
    half = own.shape[1]
    for ref in (wide0, wide1, wide2):
        ref[...] = jnp.zeros_like(ref)
    for part in range(2):
        there = slice(part * half, (part + 1) * half)
        for row in range(3):
            own[4 * part + row : 4 * part + row + 1, :] = cell_ref[row : row + 1, there].astype(
                jnp.float32
            )
        own[4 * part + 3 : 4 * part + 4, :] = charge_ref[:, there]

    def along_pencil(step):
        return (slab, lax.rem(pencil + step, pencils))

    def along_slab(step):
        return (lax.rem(slab + step, slabs), pencil)

    barrier = pltpu.get_barrier_semaphore()

    @pl.loop(1, pencils)
    def _(step):
        pl.semaphore_signal(barrier, inc=1, device_id=along_pencil(step), device_id_type=MESH)

    @pl.loop(1, slabs)
    def _(step):
        pl.semaphore_signal(barrier, inc=1, device_id=along_slab(step), device_id_type=MESH)

    pl.semaphore_wait(barrier, slabs + pencils - 2)

    def inside(dz, dy):
        z = slab + dz
        y = pencil + dy
        return (z >= 0) & (z < slabs) & (y >= 0) & (y < pencils)

    copies = []

    def add(source, target, dz, dy):
        copies.append((source, target, dz, dy))
        return len(copies) - 1

    to_above = add(own, below, 1, 0)
    to_below = add(own, above, -1, 0)
    lines0 = {1: (32, 0), -1: (8, 40)}
    middle_y = [
        add(wide0.at[4:12, a : a + 8], wide0.at[4:12, b : b + 8], 0, dy)
        for dy, (a, b) in lines0.items()
    ]
    below_y = [
        add(wide0.at[0:4, a : a + 8], wide0.at[0:4, b : b + 8], 0, dy)
        for dy, (a, b) in lines0.items()
    ]
    above_y = [
        add(wide0.at[12:16, a : a + 8], wide0.at[12:16, b : b + 8], 0, dy)
        for dy, (a, b) in lines0.items()
    ]
    one_z = [
        add(wide1.at[4:8, 8:24], wide1.at[a : a + 4, 8:24], dz, 0) for dz, a in ((1, 0), (-1, 8))
    ]
    one_y = [
        add(wide1.at[:, a : a + 8], wide1.at[:, b : b + 8], 0, dy)
        for dy, a, b in ((1, 16, 0), (-1, 8, 24))
    ]
    two_z = [
        add(wide2.at[4:6], wide2.at[4 - 2 * dz : 6 - 2 * dz], dz, 0) for dz in (-2, -1, 1, 2)
    ]

    def copy_of(index, device):
        source, target, _, _ = copies[index]
        return pltpu.make_async_remote_copy(
            src_ref=source,
            dst_ref=target,
            send_sem=send.at[index],
            recv_sem=recv.at[index],
            device_id=device,
            device_id_type=MESH,
        )

    def start(indices, also=True):
        for index in indices:
            _, _, dz, dy = copies[index]

            @pl.when(inside(dz, dy) & also)
            def _(index=index, dz=dz, dy=dy):
                copy_of(index, (slab + dz, pencil + dy)).start()

    def arrived(indices, also=True):
        for index in indices:
            _, _, dz, dy = copies[index]

            @pl.when(inside(-dz, -dy) & also)
            def _(index=index, dz=dz, dy=dy):
                copy_of(index, (slab - dz, pencil - dy)).wait_recv()

    def sent(indices, also=True):
        for index in indices:
            _, _, dz, dy = copies[index]

            @pl.when(inside(dz, dy) & also)
            def _(index=index, dz=dz, dy=dy):
                copy_of(index, (slab + dz, pencil + dy)).wait_send()

    def pencil_copy(step):
        lines = pl.ds(pl.multiple_of(8 * pencil, 8), 8)
        return pltpu.make_async_remote_copy(
            src_ref=wide2.at[4:6, lines],
            dst_ref=wide2.at[4:6, lines],
            send_sem=send2.at[step],
            recv_sem=recv2.at[step],
            device_id=along_pencil(step),
            device_id_type=MESH,
        )

    def pencil_arrival(step):
        lines = pl.ds(pl.multiple_of(8 * lax.rem(pencil + pencils - step, pencils), 8), 8)
        return pltpu.make_async_remote_copy(
            src_ref=wide2.at[4:6, lines],
            dst_ref=wide2.at[4:6, lines],
            send_sem=send2.at[step],
            recv_sem=recv2.at[step],
            device_id=along_pencil(step),
            device_id_type=MESH,
        )

    def top_copy(step, slot):
        return pltpu.make_async_remote_copy(
            src_ref=wide3.at[slot],
            dst_ref=wide3.at[slot],
            send_sem=send3.at[step],
            recv_sem=recv3.at[step],
            device_id=along_slab(step),
            device_id_type=MESH,
        )

    start([to_above, to_below])
    deposit(own, total, CZ * slab, CZ)
    grid = total[...]
    wide0[4:12, 8:40, :] = grid.reshape(CZ, CY, NX)
    start(middle_y)
    one = halve(grid, ROWS // 4, 5, NX // 2)
    wide1[4:8, 8:24, :] = one.reshape(CZ // 2, CY // 2, NX // 2)
    start(one_z)
    two = halve(one, ROWS // 16, 4, NX // 4)
    wide2[4:6, pl.ds(pl.multiple_of(8 * pencil, 8), 8), :] = two.reshape(
        CZ // 4, CY // 4, NX // 4
    )
    for step in range(1, pencils):
        pencil_copy(step).start()

    has_below = slab > 0
    has_above = slab < slabs - 1
    arrived([to_above])

    @pl.when(has_below)
    def _():
        deposit(below, total, CZ * slab - 4, 4)
        wide0[0:4, 8:40, :] = total[0 : 4 * CY, :].reshape(4, CY, NX)

    start(below_y, has_below)
    for step in range(1, pencils):
        pencil_arrival(step).wait_recv()
    start(two_z)
    lines2 = 8 * pencils
    three = halve(
        wide2[4:6].reshape(2 * lines2, NX // 4), lines2 // 2, lines2.bit_length() - 1, NX // 4
    )
    wide3[pl.ds(slab, 1)] = three[None]

    @pl.loop(1, slabs)
    def _(step):
        top_copy(step, slab).start()

    arrived(one_z)
    start(one_y)
    arrived([to_below])

    @pl.when(has_above)
    def _():
        deposit(above, total, CZ * slab + CZ, 4)
        wide0[12:16, 8:40, :] = total[0 : 4 * CY, :].reshape(4, CY, NX)

    start(above_y, has_above)
    for step in range(1, pencils):
        pencil_copy(step).wait_send()
    sent([to_above, to_below, *middle_y, *one_z, *two_z])
    arrived([*middle_y, *two_z])
    arrived(one_y)
    sent(one_y)

    @pl.loop(1, slabs)
    def _(step):
        copy = top_copy(step, lax.rem(slab + slabs - step, slabs))
        copy.wait_send()
        copy.wait_recv()

    arrived(below_y, has_below)
    sent(below_y, has_below)
    arrived(above_y, has_above)
    sent(above_y, has_above)


def exchange_call(slabs, pencils, atom_cell, charge):
    atoms = atom_cell.shape[1]
    shapes = (
        (16, 48, NX),
        (12, 32, NX // 2),
        (10, 8 * pencils, NX // 4),
        (slabs, 4 * pencils, 128),
        (8, atoms // 2),
    )
    return pl.pallas_call(
        functools.partial(exchange_kernel, slabs, pencils),
        out_shape=[jax.ShapeDtypeStruct(shape, jnp.float32) for shape in shapes],
        in_specs=[VMEM] * 2,
        out_specs=[VMEM] * 5,
        scratch_shapes=[
            pltpu.VMEM((8, atoms // 2), jnp.float32),
            pltpu.VMEM((8, atoms // 2), jnp.float32),
            pltpu.VMEM((ROWS, NX), jnp.float32),
            pltpu.SemaphoreType.DMA((16,)),
            pltpu.SemaphoreType.DMA((16,)),
            pltpu.SemaphoreType.DMA((pencils,)),
            pltpu.SemaphoreType.DMA((pencils,)),
            pltpu.SemaphoreType.DMA((slabs,)),
            pltpu.SemaphoreType.DMA((slabs,)),
        ],
        cost_estimate=pl.CostEstimate(flops=10**10, bytes_accessed=2**23, transcendentals=0),
        compiler_params=pltpu.CompilerParams(
            collective_id=0, has_side_effects=True, vmem_limit_bytes=40 * 2**20
        ),
    )(atom_cell, charge.reshape(1, -1))


def shift_x(values, step):
    width = values.shape[-1]
    axis = values.ndim - 1
    column = iota(values.shape, axis)
    moved = pltpu.roll(values, (-step) % width, axis)
    return jnp.where((column + step >= 0) & (column + step < width), moved, 0.0)


def pair_x(values, step):
    return shift_x(values, step) + shift_x(values, -step)


def hat(fine, cell, factor, count):
    bits = factor.bit_length()
    numerator = jnp.clip(2 * fine + 1 - factor, 0, 2 * factor * (count - 1))
    lower = jnp.minimum(numerator >> bits, count - 2)
    fraction = (numerator - (lower << bits)).astype(jnp.float32) * (0.5 / factor)
    return jnp.where(
        cell == lower, 1.0 - fraction, jnp.where(cell == lower + 1, fraction, 0.0)
    )


def window_stencil(level, planes_in, planes_out, lines, shift):
    blocks = []
    dz = np.arange(planes_in)[None, :] - np.arange(planes_out)[:, None] + shift
    dy = np.arange(lines)[None, :] - np.arange(lines)[:, None]
    dz = dz[:, None, :, None]
    dy = dy[None, :, None, :]
    near = (np.abs(dz) <= 2) & (np.abs(dy) <= 2)
    for c in range(3):
        squared = (dz * dz + dy * dy + c * c).astype(np.float64)
        weight = (1.0 / np.sqrt(squared + 1.0) - 1.0 / np.sqrt(squared + 4.0)) / 2**level
        weight = np.where(near, weight, 0.0)
        blocks.append(weight.reshape(planes_out * lines, planes_in * lines))
    return np.concatenate(blocks, axis=1).astype(np.float32)


def field_kernel(
    slabs,
    pencils,
    own_ref,
    wide0,
    wide1,
    wide2,
    wide3,
    stencil1,
    stencil2,
    pot_ref,
    force_ref,
    sums,
    wide_pot,
    field1,
    field2,
    field3,
    along_x,
    high_ref,
    low_ref,
):
    slab = lax.axis_index("slab")
    pencil = lax.axis_index("pencil")
    pencil_bits = pencils.bit_length() - 1

    grid1 = wide1[...].reshape(12 * 32, NX // 2)
    field1[...] = dot32(
        stencil1[...], jnp.concatenate([grid1, pair_x(grid1, 1), pair_x(grid1, 2)], axis=0)
    )
    grid2 = wide2[...].reshape(10 * 8 * pencils, NX // 4)
    field2[...] = dot32(
        stencil2[...], jnp.concatenate([grid2, pair_x(grid2, 1), pair_x(grid2, 2)], axis=0)
    )
    rows3 = slabs * pencils * 4
    grid3 = wide3[...].reshape(rows3, 128)
    coarse = []
    first_row = 0
    first_lane = 0
    for level in (3, 4, 5):
        down = level - 3
        line_bits = pencil_bits + 2 - down
        lines = 2**line_bits
        planes = slabs >> down
        count = planes * lines
        length = NX >> level
        if level == 3:
            charges = grid3
        else:
            shape = (count, rows3)
            out_row = iota(shape, 0)
            in_row = iota(shape, 1)
            in_plane = in_row >> (2 + pencil_bits)
            in_line = in_row & (4 * pencils - 1)
            cell = ((in_plane >> down) << line_bits) + (in_line >> down)
            charges = dot32(jnp.where(cell == out_row, 1.0, 0.0), grid3)
        reach = 3 if level < 5 else length
        source = iota((128, 128), 0) >> down
        column = iota((128, 128), 1) - first_lane
        valid = (column >= 0) & (column < length)
        pairs = jnp.concatenate(
            [
                jnp.where(valid & (jnp.abs(source - column) == c), 1.0, 0.0)
                for c in range(reach)
            ],
            axis=1,
        )
        moved = dot32(charges, pairs)
        stacked = jnp.concatenate(
            [moved[:, c * 128 : (c + 1) * 128] for c in range(reach)], axis=0
        )
        blocks = []
        for c in range(reach):
            shape = (4 * lines, count)
            dz = (iota(shape, 1) >> line_bits) - (iota(shape, 0) >> line_bits)
            dz = dz - ((slab >> down) - 1)
            dy = (iota(shape, 1) & (lines - 1)) - (iota(shape, 0) & (lines - 1))
            squared = dz * dz + dy * dy
            if level < 5:
                weight = jnp.zeros(shape, jnp.float32)
                for value in SQUARES:
                    weight = jnp.where(
                        squared == value, level_weight(level, value + c * c), weight
                    )
                weight = jnp.where((jnp.abs(dz) <= 2) & (jnp.abs(dy) <= 2), weight, 0.0)
            else:
                weight = (1.0 / F) / jnp.sqrt((squared + (c * c + 1)).astype(jnp.float32))
            blocks.append(dot32(weight, stacked[c * count : (c + 1) * count]))
        field3[first_row : first_row + 4 * lines, :] = sum(blocks[1:], blocks[0])
        first_row = first_row + 4 * lines
        first_lane = first_lane + length

    lane = 0
    for level in range(1, 6):
        length = NX >> level
        rows = length if level < 5 else NX - lane
        weights = hat(iota((rows, NX), 1), iota((rows, NX), 0), 2**level, length)
        weights = jnp.where(iota((rows, NX), 0) < length, weights, 0.0)
        along_x[lane : lane + rows, :] = weights.astype(jnp.bfloat16)
        lane = lane + rows

    @pl.loop(0, 4)
    def _(step):

        def along_zy(level, planes, lines, plane0, line0):
            shape = (3, 48, planes * lines)
            bits = lines.bit_length() - 1
            fine_z = CZ * slab - 2 + 3 * step + iota(shape, 0)
            fine_y = CY * pencil - 8 + iota(shape, 1)
            plane = plane0 + (iota(shape, 2) >> bits)
            line = line0 + (iota(shape, 2) & (lines - 1))
            weights = hat(fine_z, plane, 2**level, (slabs * CZ) >> level) * hat(
                fine_y, line, 2**level, (pencils * CY) >> level
            )
            return weights.reshape(3 * 48, planes * lines)

        parts = [
            dot32(along_zy(1, 8, 32, 4 * slab - 2, 16 * pencil - 8), field1[...]),
            dot32(along_zy(2, 4, 8 * pencils, 2 * slab - 1, 0), field2[...]),
        ]
        first_row = 0
        last = jnp.zeros((3 * 48, 128), jnp.float32)
        for level in (3, 4, 5):
            lines = (pencils * CY) >> level
            weights = along_zy(level, 4, lines, (slab >> (level - 3)) - 1, 0)
            last = last + dot32(weights, field3[first_row : first_row + 4 * lines, :])
            first_row = first_row + 4 * lines
        parts.append(last)
        high, low = split_two(jnp.concatenate(parts, axis=1))
        fine = jnp.dot(high, along_x[...], preferred_element_type=jnp.float32)
        fine += jnp.dot(low, along_x[...], preferred_element_type=jnp.float32)
        wide_pot[pl.ds(4 + 3 * step, 3)] = fine.reshape(3, 48, NX)

    for edge in (0, 1, 2, 3, 16, 17, 18, 19):
        wide_pot[edge] = jnp.zeros((48, NX), jnp.float32)

    @pl.loop(0, 16)
    def _(plane):
        values = wide0[plane]
        sums[0] = values
        sums[1] = pair_x(values, 1)
        sums[2] = pair_x(values, 2)
        for block in range(NX // 128):
            lanes = pl.ds(block * 128, 128)
            table = {}
            for c in range(3):
                part = sums[c, :, lanes]
                table[0, c] = part
                for b in (1, 2):
                    table[b, c] = pltpu.roll(part, b, 0) + pltpu.roll(part, 48 - b, 0)
            groups = {
                0: table[0, 0],
                1: table[0, 1] + table[1, 0],
                2: table[1, 1],
                4: table[0, 2] + table[2, 0],
                5: table[1, 2] + table[2, 1],
                8: table[2, 2],
            }
            for a in range(3):
                total = sum(near_weight(a * a + k) * groups[k] for k in SQUARES)
                for target in {a, -a}:
                    wide_pot[plane + 2 + target, :, lanes] += total

    @pl.loop(0, 12)
    def _(plane):
        shape = (48, NX)
        row = CY * pencil - 8 + iota(shape, 0)
        whole_plane = CZ * slab - 2 + plane + jnp.zeros(shape, jnp.int32)
        valid = (row >= 0) & (row < pencils * CY)
        valid = valid & (whole_plane >= 0) & (whole_plane < slabs * CZ)
        wide_pot[plane + 4] = jnp.where(valid, wide_pot[plane + 4], 0.0)

    def slope(after1, before1, after2, before2):
        return (8.0 * (after1 - before1) - (after2 - before2)) * (1.0 / 12.0)

    @pl.loop(0, CZ)
    def _(plane):
        middle = wide_pot[plane + 6]
        own = middle[8:40]
        pot_ref[plane] = own
        at = [wide_pot[plane + 6 + k, 8:40, :] for k in (1, -1, 2, -2)]
        across = [pltpu.roll(middle, (-k) % 48, 0)[8:40] for k in (1, -1, 2, -2)]
        along = [shift_x(own, k) for k in (1, -1, 2, -2)]
        for direction, four in enumerate((at, across, along)):
            high, low = split_two(slope(*four))
            start = pl.multiple_of(direction * ROWS + plane * CY, CY)
            high_ref[pl.ds(start, CY), :] = high
            low_ref[pl.ds(start, CY), :] = low

    half_atoms = own_ref.shape[1]
    width = math.gcd(half_atoms, 512)

    @pl.loop(0, half_atoms // width)
    def _(step):
        start = pl.multiple_of(step * width, width)
        for half in range(2):
            rows, columns, charges = local_rows(own_ref, half, start, width)
            at_row = iota((ROWS, width), 0) == rows
            table = one_hot(columns.astype(jnp.int16), NX)
            place = pl.ds(pl.multiple_of(half * half_atoms + start, width), width)
            for direction in range(3):
                part = pl.ds(direction * ROWS, ROWS)
                at_cell = jnp.dot(high_ref[part, :], table, preferred_element_type=jnp.float32)
                at_cell += jnp.dot(low_ref[part, :], table, preferred_element_type=jnp.float32)
                chosen = jnp.sum(jnp.where(at_row, at_cell, 0.0), axis=0, keepdims=True)
                force_ref[direction : direction + 1, place] = -charges * chosen


def field_call(slabs, pencils, wide, own):
    stencil1 = window_stencil(1, 12, 8, 32, -2)
    stencil2 = window_stencil(2, 10, 4, 8 * pencils, -3)
    field3_rows = sum(4 * ((pencils * CY) >> level) for level in (3, 4, 5))
    return pl.pallas_call(
        functools.partial(field_kernel, slabs, pencils),
        out_shape=[
            jax.ShapeDtypeStruct((CZ, CY, NX), jnp.float32),
            jax.ShapeDtypeStruct((3, 2 * own.shape[1]), jnp.float32),
        ],
        in_specs=[VMEM] * 7,
        out_specs=[VMEM] * 2,
        scratch_shapes=[
            pltpu.VMEM((3, 48, NX), jnp.float32),
            pltpu.VMEM((20, 48, NX), jnp.float32),
            pltpu.VMEM((8 * 32, NX // 2), jnp.float32),
            pltpu.VMEM((4 * 8 * pencils, NX // 4), jnp.float32),
            pltpu.VMEM((field3_rows, 128), jnp.float32),
            pltpu.VMEM((NX, NX), jnp.bfloat16),
            pltpu.VMEM((3 * ROWS, NX), jnp.bfloat16),
            pltpu.VMEM((3 * ROWS, NX), jnp.bfloat16),
        ],
        cost_estimate=pl.CostEstimate(flops=2 * 10**10, bytes_accessed=2**23, transcendentals=0),
        compiler_params=pltpu.CompilerParams(vmem_limit_bytes=24 * 2**20),
    )(
        own,
        *wide,
        jnp.asarray(stencil1),
        jnp.asarray(stencil2),
    )


def solution(mesh):
    slabs = mesh.shape["slab"]
    pencils = mesh.shape["pencil"]

    def body(atom_cell, charge):
        *wide, own = exchange_call(slabs, pencils, atom_cell, charge)
        potential, forces = field_call(slabs, pencils, wide, own)
        return (potential, forces)

    return jax.shard_map(
        body,
        mesh=mesh,
        in_specs=(P(None, ("slab", "pencil")), P(("slab", "pencil"))),
        out_specs=(P("slab", "pencil", None), P(None, ("slab", "pencil"))),
        check_vma=False,
    )
```

```python
import functools
import math

import jax
import jax.numpy as jnp
import numpy as np
from jax import lax
from jax.experimental import pallas as pl
from jax.experimental.pallas import tpu as pltpu
from jax.sharding import PartitionSpec as P

CZ = 8
CY = 32
NX = 512
F = 32
ROWS = CZ * CY
CHUNK = 2048
MESH = pl.DeviceIdType.MESH
VMEM = pl.BlockSpec(memory_space=pltpu.VMEM)
SQUARES = (0, 1, 2, 4, 5, 8)


def iota(shape, dim):
    return lax.broadcasted_iota(jnp.int32, shape, dim)


def iota16(shape, dim):
    return iota(shape, dim).astype(jnp.int16)


def one_hot(places, size):
    here = iota16((size, places.shape[1]), 0) == places
    return jnp.where(here, jnp.ones((), jnp.bfloat16), jnp.zeros((), jnp.bfloat16))


def near_weight(squared):
    return 1.0 / math.sqrt(squared + 0.25) - 1.0 / math.sqrt(squared + 4.0)


def level_weight(level, squared):
    return (1.0 / math.sqrt(squared + 1.0) - 1.0 / math.sqrt(squared + 4.0)) / 2**level


def split_two(values):
    high = values.astype(jnp.bfloat16)
    return high, (values - high.astype(jnp.float32)).astype(jnp.bfloat16)


def dot32(left, right):
    left_high, left_low = split_two(left)
    right_high, right_low = split_two(right)
    total = jnp.dot(left_high, right_high, preferred_element_type=jnp.float32)
    total += jnp.dot(left_high, right_low, preferred_element_type=jnp.float32)
    return total + jnp.dot(left_low, right_high, preferred_element_type=jnp.float32)


def local_rows(own_ref, half, start, width):
    z0 = lax.axis_index("slab") * CZ
    y0 = lax.axis_index("pencil") * CY
    row = 4 * half
    plane = own_ref[row : row + 1, pl.ds(start, width)].astype(jnp.int32) - z0
    line = own_ref[row + 1 : row + 2, pl.ds(start, width)].astype(jnp.int32) - y0
    columns = own_ref[row + 2 : row + 3, pl.ds(start, width)].astype(jnp.int32)
    return plane * CY + line, columns, own_ref[row + 3 : row + 4, pl.ds(start, width)]


def halve_rows(rows_out, rows_in, line_bits):
    out_row = iota((rows_out, rows_in), 0)
    in_row = iota((rows_out, rows_in), 1)
    plane = in_row >> (line_bits + 1)
    line = (in_row & (2**line_bits - 1)) >> 1
    return jnp.where((plane << (line_bits - 1)) + line == out_row, 1.0, 0.0).astype(jnp.bfloat16)


def halve_columns(columns_in, columns_out):
    return jnp.where(
        iota((columns_in, columns_out), 0) >> 1 == iota((columns_in, columns_out), 1), 1.0, 0.0
    ).astype(jnp.bfloat16)


def halve(values, rows_out, line_bits, columns_out):
    rows, columns = values.shape
    left = halve_rows(rows_out, rows, line_bits)
    high, low = split_two(values)
    part = jnp.dot(left, high, preferred_element_type=jnp.float32)
    part += jnp.dot(left, low, preferred_element_type=jnp.float32)
    right = halve_columns(columns, columns_out)
    high, low = split_two(part)
    whole = jnp.dot(high, right, preferred_element_type=jnp.float32)
    return whole + jnp.dot(low, right, preferred_element_type=jnp.float32)


def deposit(atoms_ref, total_ref, first_plane, planes):
    rows = planes * CY
    width = math.gcd(atoms_ref.shape[1], CHUNK)
    y0 = lax.axis_index("pencil") * CY
    total_ref[0:rows, :] = jnp.zeros((rows, NX), jnp.float32)

    @pl.loop(0, atoms_ref.shape[1] // width)
    def _(step):
        for half in range(2):
            here = pl.ds(pl.multiple_of(step * width, width), width)
            row = 4 * half
            plane = atoms_ref[row : row + 1, here].astype(jnp.int32) - first_plane
            line = atoms_ref[row + 1 : row + 2, here].astype(jnp.int32) - y0
            columns = atoms_ref[row + 2 : row + 3, here].astype(jnp.int16)
            high, low = split_two(atoms_ref[row + 3 : row + 4, here])
            at_row = iota16((rows, width), 0) == (plane * CY + line).astype(jnp.int16)
            table = one_hot(columns, NX)
            none = jnp.zeros((), jnp.bfloat16)
            stacked = jnp.concatenate(
                [jnp.where(at_row, high, none), jnp.where(at_row, low, none)], axis=0
            )
            added = lax.dot_general(
                stacked, table, (((1,), (1,)), ((), ())), preferred_element_type=jnp.float32
            )
            total_ref[0:rows, :] += added[:rows] + added[rows:]


def exchange_kernel(
    slabs,
    pencils,
    cell_ref,
    charge_ref,
    wide0,
    wide1,
    wide2,
    wide3,
    own,
    below,
    above,
    total,
    send,
    recv,
    send2,
    recv2,
    send3,
    recv3,
):
    slab = lax.axis_index("slab")
    pencil = lax.axis_index("pencil")
    half = own.shape[1]
    for ref in (wide0, wide1, wide2):
        ref[...] = jnp.zeros_like(ref)
    for part in range(2):
        there = slice(part * half, (part + 1) * half)
        for row in range(3):
            own[4 * part + row : 4 * part + row + 1, :] = cell_ref[row : row + 1, there].astype(
                jnp.float32
            )
        own[4 * part + 3 : 4 * part + 4, :] = charge_ref[:, there]

    def along_pencil(step):
        return (slab, lax.rem(pencil + step, pencils))

    def along_slab(step):
        return (lax.rem(slab + step, slabs), pencil)

    barrier = pltpu.get_barrier_semaphore()

    @pl.loop(1, pencils)
    def _(step):
        pl.semaphore_signal(barrier, inc=1, device_id=along_pencil(step), device_id_type=MESH)

    @pl.loop(1, slabs)
    def _(step):
        pl.semaphore_signal(barrier, inc=1, device_id=along_slab(step), device_id_type=MESH)

    pl.semaphore_wait(barrier, slabs + pencils - 2)

    def inside(dz, dy):
        z = slab + dz
        y = pencil + dy
        return (z >= 0) & (z < slabs) & (y >= 0) & (y < pencils)

    copies = []

    def add(source, target, dz, dy):
        copies.append((source, target, dz, dy))
        return len(copies) - 1

    to_above = add(own, below, 1, 0)
    to_below = add(own, above, -1, 0)
    lines0 = {1: (32, 0), -1: (8, 40)}
    middle_y = [
        add(wide0.at[4:12, a : a + 8], wide0.at[4:12, b : b + 8], 0, dy)
        for dy, (a, b) in lines0.items()
    ]
    below_y = [
        add(wide0.at[0:4, a : a + 8], wide0.at[0:4, b : b + 8], 0, dy)
        for dy, (a, b) in lines0.items()
    ]
    above_y = [
        add(wide0.at[12:16, a : a + 8], wide0.at[12:16, b : b + 8], 0, dy)
        for dy, (a, b) in lines0.items()
    ]
    one_z = [
        add(wide1.at[4:8, 8:24], wide1.at[a : a + 4, 8:24], dz, 0) for dz, a in ((1, 0), (-1, 8))
    ]
    one_y = [
        add(wide1.at[:, a : a + 8], wide1.at[:, b : b + 8], 0, dy)
        for dy, a, b in ((1, 16, 0), (-1, 8, 24))
    ]
    two_z = [
        add(wide2.at[4:6], wide2.at[4 - 2 * dz : 6 - 2 * dz], dz, 0) for dz in (-2, -1, 1, 2)
    ]

    def copy_of(index, device):
        source, target, _, _ = copies[index]
        return pltpu.make_async_remote_copy(
            src_ref=source,
            dst_ref=target,
            send_sem=send.at[index],
            recv_sem=recv.at[index],
            device_id=device,
            device_id_type=MESH,
        )

    def start(indices, also=True):
        for index in indices:
            _, _, dz, dy = copies[index]

            @pl.when(inside(dz, dy) & also)
            def _(index=index, dz=dz, dy=dy):
                copy_of(index, (slab + dz, pencil + dy)).start()

    def arrived(indices, also=True):
        for index in indices:
            _, _, dz, dy = copies[index]

            @pl.when(inside(-dz, -dy) & also)
            def _(index=index, dz=dz, dy=dy):
                copy_of(index, (slab - dz, pencil - dy)).wait_recv()

    def sent(indices, also=True):
        for index in indices:
            _, _, dz, dy = copies[index]

            @pl.when(inside(dz, dy) & also)
            def _(index=index, dz=dz, dy=dy):
                copy_of(index, (slab + dz, pencil + dy)).wait_send()

    def pencil_copy(step):
        lines = pl.ds(pl.multiple_of(8 * pencil, 8), 8)
        return pltpu.make_async_remote_copy(
            src_ref=wide2.at[4:6, lines],
            dst_ref=wide2.at[4:6, lines],
            send_sem=send2.at[step],
            recv_sem=recv2.at[step],
            device_id=along_pencil(step),
            device_id_type=MESH,
        )

    def pencil_arrival(step):
        lines = pl.ds(pl.multiple_of(8 * lax.rem(pencil + pencils - step, pencils), 8), 8)
        return pltpu.make_async_remote_copy(
            src_ref=wide2.at[4:6, lines],
            dst_ref=wide2.at[4:6, lines],
            send_sem=send2.at[step],
            recv_sem=recv2.at[step],
            device_id=along_pencil(step),
            device_id_type=MESH,
        )

    def top_copy(step, slot):
        return pltpu.make_async_remote_copy(
            src_ref=wide3.at[slot],
            dst_ref=wide3.at[slot],
            send_sem=send3.at[step],
            recv_sem=recv3.at[step],
            device_id=along_slab(step),
            device_id_type=MESH,
        )

    start([to_above, to_below])
    deposit(own, total, CZ * slab, CZ)
    grid = total[...]
    wide0[4:12, 8:40, :] = grid.reshape(CZ, CY, NX)
    start(middle_y)
    one = halve(grid, ROWS // 4, 5, NX // 2)
    wide1[4:8, 8:24, :] = one.reshape(CZ // 2, CY // 2, NX // 2)
    start(one_z)
    two = halve(one, ROWS // 16, 4, NX // 4)
    wide2[4:6, pl.ds(pl.multiple_of(8 * pencil, 8), 8), :] = two.reshape(
        CZ // 4, CY // 4, NX // 4
    )
    for step in range(1, pencils):
        pencil_copy(step).start()

    has_below = slab > 0
    has_above = slab < slabs - 1
    arrived([to_above])

    @pl.when(has_below)
    def _():
        deposit(below, total, CZ * slab - 4, 4)
        wide0[0:4, 8:40, :] = total[0 : 4 * CY, :].reshape(4, CY, NX)

    start(below_y, has_below)
    for step in range(1, pencils):
        pencil_arrival(step).wait_recv()
    start(two_z)
    lines2 = 8 * pencils
    three = halve(
        wide2[4:6].reshape(2 * lines2, NX // 4), lines2 // 2, lines2.bit_length() - 1, NX // 4
    )
    wide3[pl.ds(slab, 1)] = three[None]

    @pl.loop(1, slabs)
    def _(step):
        top_copy(step, slab).start()

    arrived(one_z)
    start(one_y)
    arrived([to_below])

    @pl.when(has_above)
    def _():
        deposit(above, total, CZ * slab + CZ, 4)
        wide0[12:16, 8:40, :] = total[0 : 4 * CY, :].reshape(4, CY, NX)

    start(above_y, has_above)
    for step in range(1, pencils):
        pencil_copy(step).wait_send()
    sent([to_above, to_below, *middle_y, *one_z, *two_z])
    arrived([*middle_y, *two_z])
    arrived(one_y)
    sent(one_y)

    @pl.loop(1, slabs)
    def _(step):
        copy = top_copy(step, lax.rem(slab + slabs - step, slabs))
        copy.wait_send()
        copy.wait_recv()

    arrived(below_y, has_below)
    sent(below_y, has_below)
    arrived(above_y, has_above)
    sent(above_y, has_above)


def exchange_call(slabs, pencils, atom_cell, charge):
    atoms = atom_cell.shape[1]
    shapes = (
        (16, 48, NX),
        (12, 32, NX // 2),
        (10, 8 * pencils, NX // 4),
        (slabs, 4 * pencils, 128),
        (8, atoms // 2),
    )
    return pl.pallas_call(
        functools.partial(exchange_kernel, slabs, pencils),
        out_shape=[jax.ShapeDtypeStruct(shape, jnp.float32) for shape in shapes],
        in_specs=[VMEM] * 2,
        out_specs=[VMEM] * 5,
        scratch_shapes=[
            pltpu.VMEM((8, atoms // 2), jnp.float32),
            pltpu.VMEM((8, atoms // 2), jnp.float32),
            pltpu.VMEM((ROWS, NX), jnp.float32),
            pltpu.SemaphoreType.DMA((16,)),
            pltpu.SemaphoreType.DMA((16,)),
            pltpu.SemaphoreType.DMA((pencils,)),
            pltpu.SemaphoreType.DMA((pencils,)),
            pltpu.SemaphoreType.DMA((slabs,)),
            pltpu.SemaphoreType.DMA((slabs,)),
        ],
        cost_estimate=pl.CostEstimate(flops=10**10, bytes_accessed=2**23, transcendentals=0),
        compiler_params=pltpu.CompilerParams(
            collective_id=0, has_side_effects=True, vmem_limit_bytes=40 * 2**20
        ),
    )(atom_cell, charge.reshape(1, -1))


def shift_x(values, step):
    width = values.shape[-1]
    axis = values.ndim - 1
    column = iota(values.shape, axis)
    moved = pltpu.roll(values, (-step) % width, axis)
    return jnp.where((column + step >= 0) & (column + step < width), moved, 0.0)


def pair_x(values, step):
    return shift_x(values, step) + shift_x(values, -step)


def hat(fine, cell, factor, count):
    bits = factor.bit_length()
    numerator = jnp.clip(2 * fine + 1 - factor, 0, 2 * factor * (count - 1))
    lower = jnp.minimum(numerator >> bits, count - 2)
    fraction = (numerator - (lower << bits)).astype(jnp.float32) * (0.5 / factor)
    return jnp.where(
        cell == lower, 1.0 - fraction, jnp.where(cell == lower + 1, fraction, 0.0)
    )


def window_stencil(level, planes_in, planes_out, lines, shift):
    blocks = []
    dz = np.arange(planes_in)[None, :] - np.arange(planes_out)[:, None] + shift
    dy = np.arange(lines)[None, :] - np.arange(lines)[:, None]
    dz = dz[:, None, :, None]
    dy = dy[None, :, None, :]
    near = (np.abs(dz) <= 2) & (np.abs(dy) <= 2)
    for c in range(3):
        squared = (dz * dz + dy * dy + c * c).astype(np.float64)
        weight = (1.0 / np.sqrt(squared + 1.0) - 1.0 / np.sqrt(squared + 4.0)) / 2**level
        weight = np.where(near, weight, 0.0)
        blocks.append(weight.reshape(planes_out * lines, planes_in * lines))
    return np.concatenate(blocks, axis=1).astype(np.float32)


def field_kernel(
    slabs,
    pencils,
    own_ref,
    wide0,
    wide1,
    wide2,
    wide3,
    stencil1,
    stencil2,
    pot_ref,
    force_ref,
    paired,
    wide_pot,
    field1,
    field2,
    field3,
    along_x,
    flat1,
    flat2,
    flat3,
    lined_high,
    lined_low,
    high_ref,
    low_ref,
):
    slab = lax.axis_index("slab")
    pencil = lax.axis_index("pencil")
    pencil_bits = pencils.bit_length() - 1

    grid1 = wide1[...].reshape(12 * 32, NX // 2)
    field1[...] = dot32(
        stencil1[...], jnp.concatenate([grid1, pair_x(grid1, 1), pair_x(grid1, 2)], axis=0)
    )
    grid2 = wide2[...].reshape(10 * 8 * pencils, NX // 4)
    field2[...] = dot32(
        stencil2[...], jnp.concatenate([grid2, pair_x(grid2, 1), pair_x(grid2, 2)], axis=0)
    )
    rows3 = slabs * pencils * 4
    grid3 = wide3[...].reshape(rows3, 128)
    coarse = []
    first_row = 0
    first_lane = 0
    for level in (3, 4, 5):
        down = level - 3
        line_bits = pencil_bits + 2 - down
        lines = 2**line_bits
        planes = slabs >> down
        count = planes * lines
        length = NX >> level
        if level == 3:
            charges = grid3
        else:
            shape = (count, rows3)
            out_row = iota(shape, 0)
            in_row = iota(shape, 1)
            in_plane = in_row >> (2 + pencil_bits)
            in_line = in_row & (4 * pencils - 1)
            cell = ((in_plane >> down) << line_bits) + (in_line >> down)
            charges = dot32(jnp.where(cell == out_row, 1.0, 0.0), grid3)
        reach = 3 if level < 5 else length
        source = iota((128, 128), 0) >> down
        column = iota((128, 128), 1) - first_lane
        valid = (column >= 0) & (column < length)
        pairs = jnp.concatenate(
            [
                jnp.where(valid & (jnp.abs(source - column) == c), 1.0, 0.0)
                for c in range(reach)
            ],
            axis=1,
        )
        moved = dot32(charges, pairs)
        stacked = jnp.concatenate(
            [moved[:, c * 128 : (c + 1) * 128] for c in range(reach)], axis=0
        )
        blocks = []
        for c in range(reach):
            out_bits = max(line_bits, 3)
            shape = (4 << out_bits, count)
            dz = (iota(shape, 1) >> line_bits) - (iota(shape, 0) >> out_bits)
            dz = dz - ((slab >> down) - 1)
            dy = (iota(shape, 1) & (lines - 1)) - (iota(shape, 0) & (2**out_bits - 1))
            squared = dz * dz + dy * dy
            if level < 5:
                weight = jnp.zeros(shape, jnp.float32)
                for value in SQUARES:
                    weight = jnp.where(
                        squared == value, level_weight(level, value + c * c), weight
                    )
                weight = jnp.where((jnp.abs(dz) <= 2) & (jnp.abs(dy) <= 2), weight, 0.0)
            else:
                weight = (1.0 / F) / jnp.sqrt((squared + (c * c + 1)).astype(jnp.float32))
            blocks.append(dot32(weight, stacked[c * count : (c + 1) * count]))
        field3[first_row : first_row + (4 << out_bits), :] = sum(blocks[1:], blocks[0])
        first_row = first_row + (4 << out_bits)
        first_lane = first_lane + length

    lane = 0
    for level in range(1, 6):
        length = NX >> level
        rows = length if level < 5 else NX - lane
        weights = hat(iota((rows, NX), 1), iota((rows, NX), 0), 2**level, length)
        weights = jnp.where(iota((rows, NX), 0) < length, weights, 0.0)
        along_x[lane : lane + rows, :] = weights.astype(jnp.bfloat16)
        lane = lane + rows

    upper = pencils * CY
    padded = [max(upper >> level, 8) for level in (3, 4, 5)]
    layers = [
        (1, 4 * slab - 2, 32, 16 * pencil - 8),
        (2, 2 * slab - 1, upper >> 2, 0),
    ]
    layers += [
        (level, (slab >> (level - 3)) - 1, lines, 0)
        for level, lines in zip((3, 4, 5), padded, strict=True)
    ]
    starts = [0, 0, 0, 4 * padded[0], 4 * (padded[0] + padded[1])]
    tops = [0, 0, 0, padded[0], padded[0] + padded[1]]
    fields = [field1, field2, field3, field3, field3]
    flats = [flat1, flat2, flat3, flat3, flat3]

    for plane in range(12):
        fine_z = CZ * slab - 2 + plane
        for (level, plane0, lines, _), begin, top, field, flat in zip(
            layers, starts, tops, fields, flats, strict=True
        ):
            factor = 2**level
            count = (slabs * CZ) >> level
            numerator = jnp.clip(2 * fine_z + 1 - factor, 0, 2 * factor * (count - 1))
            lower = jnp.minimum(numerator >> (level + 1), count - 2)
            fraction = (numerator - (lower << (level + 1))).astype(jnp.float32) * (0.5 / factor)
            row = begin + (lower - plane0) * lines
            row = pl.multiple_of(row, 8)
            mixed = (1.0 - fraction) * field[pl.ds(row, lines), :]
            mixed += fraction * field[pl.ds(row + lines, lines), :]
            high, low = split_two(mixed)
            width = field.shape[1]
            there = slice(plane * width, (plane + 1) * width)
            flat[top : top + lines, there] = high.astype(jnp.float32)
            flat[flat.shape[0] // 2 + top : flat.shape[0] // 2 + top + lines, there] = low.astype(
                jnp.float32
            )

    def along_y(some):
        blocks = []
        for level, _, lines, line0 in some:
            shape = (48, lines)
            fine_y = CY * pencil - 8 + iota(shape, 0)
            blocks.append(hat(fine_y, line0 + iota(shape, 1), 2**level, upper >> level))
        return jnp.concatenate(blocks + blocks, axis=1).astype(jnp.bfloat16)

    for some, flat, first in ((layers[:1], flat1, 0), (layers[1:2], flat2, 256), (layers[2:], flat3, 384)):
        width = flat.shape[1] // 12
        lined = jnp.dot(
            along_y(some), flat[...].astype(jnp.bfloat16), preferred_element_type=jnp.float32
        )
        high, low = split_two(lined)
        for plane in range(12):
            there = slice(plane * width, (plane + 1) * width)
            rows = slice(48 * plane, 48 * plane + 48)
            lined_high[rows, first : first + width] = high[:, there]
            lined_low[rows, first : first + width] = low[:, there]

    fine = jnp.dot(lined_high[...], along_x[...], preferred_element_type=jnp.float32)
    fine += jnp.dot(lined_low[...], along_x[...], preferred_element_type=jnp.float32)
    wide_pot[4:16] = fine.reshape(12, 48, NX)

    @pl.loop(0, 16)
    def _(plane):
        values = wide0[plane]
        for b in (1, 2):
            paired[b - 1, plane] = pltpu.roll(values, b, 0) + pltpu.roll(values, 48 - b, 0)

    @pl.loop(0, 12)
    def _(plane):
        whole_plane = CZ * slab - 2 + plane
        inside_z = (whole_plane >= 0) & (whole_plane < slabs * CZ)
        for block in range(6):
            rows = pl.ds(8 * block, 8)

            def near(b, k):
                if b:
                    return paired[b - 1, plane + 2 + k, rows, :]
                return wide0[plane + 2 + k, rows, :]

            table = {}
            for b in range(3):
                table[0, b] = near(b, 0)
                for a in (1, 2):
                    table[a, b] = near(b, a) + near(b, -a)
            groups = {
                0: table[0, 0],
                1: table[0, 1] + table[1, 0],
                2: table[1, 1],
                4: table[0, 2] + table[2, 0],
                5: table[1, 2] + table[2, 1],
                8: table[2, 2],
            }
            total = wide_pot[plane + 4, rows, :]
            for c in range(3):
                part = sum(near_weight(c * c + k) * groups[k] for k in SQUARES)
                total = total + (pair_x(part, c) if c else part)
            row = CY * pencil - 8 + 8 * block + iota((8, NX), 0)
            valid = (row >= 0) & (row < upper) & inside_z
            wide_pot[plane + 4, rows, :] = jnp.where(valid, total, 0.0)

    def slope(after1, before1, after2, before2):
        return (8.0 * (after1 - before1) - (after2 - before2)) * (1.0 / 12.0)

    @pl.loop(0, CZ)
    def _(plane):
        middle = wide_pot[plane + 6]
        own = middle[8:40]
        pot_ref[plane] = own
        at = [wide_pot[plane + 6 + k, 8:40, :] for k in (1, -1, 2, -2)]
        across = [pltpu.roll(middle, (-k) % 48, 0)[8:40] for k in (1, -1, 2, -2)]
        along = [shift_x(own, k) for k in (1, -1, 2, -2)]
        for direction, four in enumerate((at, across, along)):
            high, low = split_two(slope(*four))
            start = pl.multiple_of(direction * ROWS + plane * CY, CY)
            high_ref[pl.ds(start, CY), :] = high
            low_ref[pl.ds(start, CY), :] = low

    half_atoms = own_ref.shape[1]
    width = math.gcd(half_atoms, 1024)

    @pl.loop(0, half_atoms // width)
    def _(step):
        start = pl.multiple_of(step * width, width)
        for half in range(2):
            rows, columns, charges = local_rows(own_ref, half, start, width)
            at_row = iota((ROWS, width), 0) == rows
            table = one_hot(columns.astype(jnp.int16), NX)
            place = pl.ds(pl.multiple_of(half * half_atoms + start, width), width)
            for direction in range(3):
                part = pl.ds(direction * ROWS, ROWS)
                at_cell = jnp.dot(high_ref[part, :], table, preferred_element_type=jnp.float32)
                at_cell += jnp.dot(low_ref[part, :], table, preferred_element_type=jnp.float32)
                chosen = jnp.sum(jnp.where(at_row, at_cell, 0.0), axis=0, keepdims=True)
                force_ref[direction : direction + 1, place] = -charges * chosen


def field_call(slabs, pencils, wide, own):
    stencil1 = window_stencil(1, 12, 8, 32, -2)
    stencil2 = window_stencil(2, 10, 4, 8 * pencils, -3)
    field3_rows = sum(4 * max((pencils * CY) >> level, 8) for level in (3, 4, 5))
    return pl.pallas_call(
        functools.partial(field_kernel, slabs, pencils),
        out_shape=[
            jax.ShapeDtypeStruct((CZ, CY, NX), jnp.float32),
            jax.ShapeDtypeStruct((3, 2 * own.shape[1]), jnp.float32),
        ],
        in_specs=[VMEM] * 7,
        out_specs=[VMEM] * 2,
        scratch_shapes=[
            pltpu.VMEM((2, 16, 48, NX), jnp.float32),
            pltpu.VMEM((20, 48, NX), jnp.float32),
            pltpu.VMEM((8 * 32, NX // 2), jnp.float32),
            pltpu.VMEM((4 * 8 * pencils, NX // 4), jnp.float32),
            pltpu.VMEM((field3_rows, 128), jnp.float32),
            pltpu.VMEM((NX, NX), jnp.bfloat16),
            pltpu.VMEM((2 * 32, 12 * 256), jnp.float32),
            pltpu.VMEM((2 * 8 * pencils, 12 * 128), jnp.float32),
            pltpu.VMEM((2 * field3_rows // 4, 12 * 128), jnp.float32),
            pltpu.VMEM((12 * 48, NX), jnp.bfloat16),
            pltpu.VMEM((12 * 48, NX), jnp.bfloat16),
            pltpu.VMEM((3 * ROWS, NX), jnp.bfloat16),
            pltpu.VMEM((3 * ROWS, NX), jnp.bfloat16),
        ],
        cost_estimate=pl.CostEstimate(flops=2 * 10**10, bytes_accessed=2**23, transcendentals=0),
        compiler_params=pltpu.CompilerParams(vmem_limit_bytes=40 * 2**20),
    )(
        own,
        *wide,
        jnp.asarray(stencil1),
        jnp.asarray(stencil2),
    )


def solution(mesh):
    slabs = mesh.shape["slab"]
    pencils = mesh.shape["pencil"]

    def body(atom_cell, charge):
        *wide, own = exchange_call(slabs, pencils, atom_cell, charge)
        potential, forces = field_call(slabs, pencils, wide, own)
        return (potential, forces)

    return jax.shard_map(
        body,
        mesh=mesh,
        in_specs=(P(None, ("slab", "pencil")), P(("slab", "pencil"))),
        out_specs=(P("slab", "pencil", None), P(None, ("slab", "pencil"))),
        check_vma=False,
    )
```

```python
import functools
import math

import jax
import jax.numpy as jnp
from jax import lax
from jax.experimental import pallas as pl
from jax.experimental.pallas import tpu as pltpu
from jax.sharding import PartitionSpec as P

CZ = 8
CY = 32
NX = 512
F = 32
ROWS = CZ * CY
CHUNK = 2048
MESH = pl.DeviceIdType.MESH
VMEM = pl.BlockSpec(memory_space=pltpu.VMEM)
SQUARES = (0, 1, 2, 4, 5, 8)


def iota(shape, dim):
    return lax.broadcasted_iota(jnp.int32, shape, dim)


def iota16(shape, dim):
    return iota(shape, dim).astype(jnp.int16)


def one_hot(places, size):
    here = iota16((size, places.shape[1]), 0) == places
    return jnp.where(here, jnp.ones((), jnp.bfloat16), jnp.zeros((), jnp.bfloat16))


def near_weight(squared):
    return 1.0 / math.sqrt(squared + 0.25) - 1.0 / math.sqrt(squared + 4.0)


def level_weight(level, squared):
    return (1.0 / math.sqrt(squared + 1.0) - 1.0 / math.sqrt(squared + 4.0)) / 2**level


def split_two(values):
    high = values.astype(jnp.bfloat16)
    return high, (values - high.astype(jnp.float32)).astype(jnp.bfloat16)


def dot32(left, right):
    left_high, left_low = split_two(left)
    right_high, right_low = split_two(right)
    total = jnp.dot(left_high, right_high, preferred_element_type=jnp.float32)
    total += jnp.dot(left_high, right_low, preferred_element_type=jnp.float32)
    return total + jnp.dot(left_low, right_high, preferred_element_type=jnp.float32)


def local_rows(own_ref, half, start, width):
    z0 = lax.axis_index("slab") * CZ
    y0 = lax.axis_index("pencil") * CY
    row = 4 * half
    plane = own_ref[row : row + 1, pl.ds(start, width)].astype(jnp.int32) - z0
    line = own_ref[row + 1 : row + 2, pl.ds(start, width)].astype(jnp.int32) - y0
    columns = own_ref[row + 2 : row + 3, pl.ds(start, width)].astype(jnp.int32)
    return plane * CY + line, columns, own_ref[row + 3 : row + 4, pl.ds(start, width)]


def halve_rows(rows_out, rows_in, line_bits):
    out_row = iota((rows_out, rows_in), 0)
    in_row = iota((rows_out, rows_in), 1)
    plane = in_row >> (line_bits + 1)
    line = (in_row & (2**line_bits - 1)) >> 1
    return jnp.where((plane << (line_bits - 1)) + line == out_row, 1.0, 0.0).astype(jnp.bfloat16)


def halve_columns(columns_in, columns_out):
    return jnp.where(
        iota((columns_in, columns_out), 0) >> 1 == iota((columns_in, columns_out), 1), 1.0, 0.0
    ).astype(jnp.bfloat16)


def halve(values, rows_out, line_bits, columns_out):
    rows, columns = values.shape
    left = halve_rows(rows_out, rows, line_bits)
    high, low = split_two(values)
    part = jnp.dot(left, high, preferred_element_type=jnp.float32)
    part += jnp.dot(left, low, preferred_element_type=jnp.float32)
    right = halve_columns(columns, columns_out)
    high, low = split_two(part)
    whole = jnp.dot(high, right, preferred_element_type=jnp.float32)
    return whole + jnp.dot(low, right, preferred_element_type=jnp.float32)


def deposit(atoms_ref, total_ref, first_plane, planes, far_plane=None):
    near_rows = planes * CY
    rows = near_rows if far_plane is None else near_rows + CY
    width = math.gcd(atoms_ref.shape[1], CHUNK)
    y0 = lax.axis_index("pencil") * CY
    total_ref[0:rows, :] = jnp.zeros((rows, NX), jnp.float32)

    @pl.loop(0, atoms_ref.shape[1] // width)
    def _(step):
        for half in range(2):
            here = pl.ds(pl.multiple_of(step * width, width), width)
            row = 4 * half
            plane = atoms_ref[row : row + 1, here].astype(jnp.int32) - first_plane
            line = atoms_ref[row + 1 : row + 2, here].astype(jnp.int32) - y0
            columns = atoms_ref[row + 2 : row + 3, here].astype(jnp.int16)
            high, low = split_two(atoms_ref[row + 3 : row + 4, here])
            place = plane * CY + line
            if far_plane is not None:
                far = ((plane + first_plane - far_plane) >> 1) * (CY // 2) + (line >> 1)
                place = jnp.where((plane >= 0) & (plane < planes), place, near_rows + far)
            at_row = iota16((rows, width), 0) == place.astype(jnp.int16)
            table = one_hot(columns, NX)
            none = jnp.zeros((), jnp.bfloat16)
            stacked = jnp.concatenate(
                [jnp.where(at_row, high, none), jnp.where(at_row, low, none)], axis=0
            )
            added = lax.dot_general(
                stacked, table, (((1,), (1,)), ((), ())), preferred_element_type=jnp.float32
            )
            total_ref[0:rows, :] += added[:rows] + added[rows:]


def shift_x(values, step):
    width = values.shape[-1]
    axis = values.ndim - 1
    column = iota(values.shape, axis)
    moved = pltpu.roll(values, (-step) % width, axis)
    return jnp.where((column + step >= 0) & (column + step < width), moved, 0.0)


def pair_x(values, step):
    return shift_x(values, step) + shift_x(values, -step)


def hat(fine, cell, factor, count):
    bits = factor.bit_length()
    numerator = jnp.clip(2 * fine + 1 - factor, 0, 2 * factor * (count - 1))
    lower = jnp.minimum(numerator >> bits, count - 2)
    fraction = (numerator - (lower << bits)).astype(jnp.float32) * (0.5 / factor)
    return jnp.where(
        cell == lower, 1.0 - fraction, jnp.where(cell == lower + 1, fraction, 0.0)
    )


def shift_y(values, step):
    lines = values.shape[0]
    line = iota(values.shape, 0) + step
    return jnp.where((line >= 0) & (line < lines), pltpu.roll(values, (-step) % lines, 0), 0.0)


def field_of(wide, field, shift, level):
    lines = wide.shape[1]

    @pl.loop(0, field.shape[0] // lines)
    def _(plane):
        table = {}
        for a in range(3):
            line = wide[plane + shift]
            if a:
                line = wide[plane + shift + a] + wide[plane + shift - a]
            table[a, 0] = line
            for b in (1, 2):
                table[a, b] = shift_y(line, b) + shift_y(line, -b)
        groups = grouped(table)
        total = None
        for c in range(3):
            part = sum(level_weight(level, c * c + k) * groups[k] for k in SQUARES)
            total = total + pair_x(part, c) if c else part
        field[pl.ds(pl.multiple_of(plane * lines, lines), lines), :] = total


def grouped(table):
    return {
        0: table[0, 0],
        1: table[0, 1] + table[1, 0],
        2: table[1, 1],
        4: table[0, 2] + table[2, 0],
        5: table[1, 2] + table[2, 1],
        8: table[2, 2],
    }


def upper_fields(slabs, pencils, wide3, field3):
    slab = lax.axis_index("slab")
    pencil_bits = pencils.bit_length() - 1
    rows3 = slabs * pencils * 4
    grid3 = wide3[...].reshape(rows3, 128)
    coarse = []
    first_row = 0
    first_lane = 0
    for level in (3, 4, 5):
        down = level - 3
        line_bits = pencil_bits + 2 - down
        lines = 2**line_bits
        planes = slabs >> down
        count = planes * lines
        length = NX >> level
        if level == 3:
            charges = grid3
        else:
            shape = (count, rows3)
            out_row = iota(shape, 0)
            in_row = iota(shape, 1)
            in_plane = in_row >> (2 + pencil_bits)
            in_line = in_row & (4 * pencils - 1)
            cell = ((in_plane >> down) << line_bits) + (in_line >> down)
            charges = dot32(jnp.where(cell == out_row, 1.0, 0.0), grid3)
        reach = 3 if level < 5 else length
        source = iota((128, 128), 0) >> down
        column = iota((128, 128), 1) - first_lane
        valid = (column >= 0) & (column < length)
        pairs = jnp.concatenate(
            [
                jnp.where(valid & (jnp.abs(source - column) == c), 1.0, 0.0)
                for c in range(reach)
            ],
            axis=1,
        )
        moved = dot32(charges, pairs)
        stacked = jnp.concatenate(
            [moved[:, c * 128 : (c + 1) * 128] for c in range(reach)], axis=0
        )
        blocks = []
        for c in range(reach):
            out_bits = max(line_bits, 3)
            shape = (4 << out_bits, count)
            dz = (iota(shape, 1) >> line_bits) - (iota(shape, 0) >> out_bits)
            dz = dz - ((slab >> down) - 1)
            dy = (iota(shape, 1) & (lines - 1)) - (iota(shape, 0) & (2**out_bits - 1))
            squared = dz * dz + dy * dy
            if level < 5:
                weight = jnp.zeros(shape, jnp.float32)
                for value in SQUARES:
                    weight = jnp.where(
                        squared == value, level_weight(level, value + c * c), weight
                    )
                weight = jnp.where((jnp.abs(dz) <= 2) & (jnp.abs(dy) <= 2), weight, 0.0)
            else:
                weight = (1.0 / F) / jnp.sqrt((squared + (c * c + 1)).astype(jnp.float32))
            blocks.append(dot32(weight, stacked[c * count : (c + 1) * count]))
        field3[first_row : first_row + (4 << out_bits), :] = sum(blocks[1:], blocks[0])
        first_row = first_row + (4 << out_bits)
        first_lane = first_lane + length


def interpolate_x(along_x):
    lane = 0
    for level in range(1, 6):
        length = NX >> level
        rows = length if level < 5 else NX - lane
        weights = hat(iota((rows, NX), 1), iota((rows, NX), 0), 2**level, length)
        weights = jnp.where(iota((rows, NX), 0) < length, weights, 0.0)
        along_x[lane : lane + rows, :] = weights.astype(jnp.bfloat16)
        lane = lane + rows


def interpolate(slabs, pencils, fields, flats, along_x, lined_high, lined_low, base):
    slab = lax.axis_index("slab")
    pencil = lax.axis_index("pencil")
    upper = pencils * CY
    padded = [max(upper >> level, 8) for level in (3, 4, 5)]
    layers = [
        (1, 4 * slab - 2, 32, 16 * pencil - 8),
        (2, 2 * slab - 1, upper >> 2, 0),
    ]
    layers += [
        (level, (slab >> (level - 3)) - 1, lines, 0)
        for level, lines in zip((3, 4, 5), padded, strict=True)
    ]
    starts = [0, 0, 0, 4 * padded[0], 4 * (padded[0] + padded[1])]
    tops = [0, 0, 0, padded[0], padded[0] + padded[1]]
    field1, field2, field3 = fields
    flat1, flat2, flat3 = flats
    fields = [field1, field2, field3, field3, field3]
    flats = [flat1, flat2, flat3, flat3, flat3]

    for plane in range(12):
        fine_z = CZ * slab - 2 + plane
        for (level, plane0, lines, _), begin, top, field, flat in zip(
            layers, starts, tops, fields, flats, strict=True
        ):
            factor = 2**level
            count = (slabs * CZ) >> level
            numerator = jnp.clip(2 * fine_z + 1 - factor, 0, 2 * factor * (count - 1))
            lower = jnp.minimum(numerator >> (level + 1), count - 2)
            fraction = (numerator - (lower << (level + 1))).astype(jnp.float32) * (0.5 / factor)
            row = begin + (lower - plane0) * lines
            row = pl.multiple_of(row, 8)
            mixed = (1.0 - fraction) * field[pl.ds(row, lines), :]
            mixed += fraction * field[pl.ds(row + lines, lines), :]
            high, low = split_two(mixed)
            width = field.shape[1]
            there = slice(plane * width, (plane + 1) * width)
            flat[top : top + lines, there] = high.astype(jnp.float32)
            flat[flat.shape[0] // 2 + top : flat.shape[0] // 2 + top + lines, there] = low.astype(
                jnp.float32
            )

    def along_y(some):
        blocks = []
        for level, _, lines, line0 in some:
            shape = (48, lines)
            fine_y = CY * pencil - 8 + iota(shape, 0)
            blocks.append(hat(fine_y, line0 + iota(shape, 1), 2**level, upper >> level))
        return jnp.concatenate(blocks + blocks, axis=1).astype(jnp.bfloat16)

    for some, flat, first in ((layers[:1], flat1, 0), (layers[1:2], flat2, 256), (layers[2:], flat3, 384)):
        width = flat.shape[1] // 12
        lined = jnp.dot(
            along_y(some), flat[...].astype(jnp.bfloat16), preferred_element_type=jnp.float32
        )
        high, low = split_two(lined)
        for plane in range(12):
            there = slice(plane * width, (plane + 1) * width)
            rows = slice(48 * plane, 48 * plane + 48)
            lined_high[rows, first : first + width] = high[:, there]
            lined_low[rows, first : first + width] = low[:, there]

    fine = jnp.dot(lined_high[...], along_x[...], preferred_element_type=jnp.float32)
    fine += jnp.dot(lined_low[...], along_x[...], preferred_element_type=jnp.float32)
    base[...] = fine.reshape(12, 48, NX)


def halve_halo(total, near_first):
    out_row = iota((2 * CY, 5 * CY), 0)
    in_row = iota((2 * CY, 5 * CY), 1)
    near = ((in_row >> 6) << 4) + ((in_row & (CY - 1)) >> 1) + near_first
    far = in_row - 4 * CY + (CY - near_first)
    chosen = jnp.where(in_row < 4 * CY, near, far) == out_row
    left = jnp.where(chosen, 1.0, 0.0).astype(jnp.bfloat16)
    high, low = split_two(total)
    part = jnp.dot(left, high, preferred_element_type=jnp.float32)
    part += jnp.dot(left, low, preferred_element_type=jnp.float32)
    right = halve_columns(NX, NX // 2)
    high, low = split_two(part)
    whole = jnp.dot(high, right, preferred_element_type=jnp.float32)
    return whole + jnp.dot(low, right, preferred_element_type=jnp.float32)


def exchange_kernel(
    slabs,
    pencils,
    cell_ref,
    charge_ref,
    wide0,
    base,
    own,
    wide1,
    wide2,
    wide3,
    below,
    above,
    total,
    field1,
    field2,
    field3,
    along_x,
    flat1,
    flat2,
    flat3,
    lined_high,
    lined_low,
    send,
    recv,
    send2,
    recv2,
    send3,
    recv3,
):
    slab = lax.axis_index("slab")
    pencil = lax.axis_index("pencil")
    half = own.shape[1]
    for ref in (wide0, wide1, wide2):
        ref[...] = jnp.zeros_like(ref)
    for part in range(2):
        there = slice(part * half, (part + 1) * half)
        for row in range(3):
            own[4 * part + row : 4 * part + row + 1, :] = cell_ref[row : row + 1, there].astype(
                jnp.float32
            )
        own[4 * part + 3 : 4 * part + 4, :] = charge_ref[:, there]

    def along_pencil(step):
        return (slab, lax.rem(pencil + step, pencils))

    def along_slab(step):
        return (lax.rem(slab + step, slabs), pencil)

    barrier = pltpu.get_barrier_semaphore()

    @pl.loop(1, pencils)
    def _(step):
        pl.semaphore_signal(barrier, inc=1, device_id=along_pencil(step), device_id_type=MESH)

    @pl.loop(1, slabs)
    def _(step):
        pl.semaphore_signal(barrier, inc=1, device_id=along_slab(step), device_id_type=MESH)

    pl.semaphore_wait(barrier, slabs + pencils - 2)

    def inside(dz, dy):
        z = slab + dz
        y = pencil + dy
        return (z >= 0) & (z < slabs) & (y >= 0) & (y < pencils)

    copies = []

    def add(source, target, dz, dy):
        copies.append((source, target, dz, dy))
        return len(copies) - 1

    to_above = add(own, below, 1, 0)
    to_below = add(own, above, -1, 0)
    lines0 = {1: (32, 0), -1: (8, 40)}
    middle_y = [
        add(wide0.at[4:12, a : a + 8], wide0.at[4:12, b : b + 8], 0, dy)
        for dy, (a, b) in lines0.items()
    ]
    below_y = [
        add(wide0.at[0:4, a : a + 8], wide0.at[0:4, b : b + 8], 0, dy)
        for dy, (a, b) in lines0.items()
    ]
    above_y = [
        add(wide0.at[12:16, a : a + 8], wide0.at[12:16, b : b + 8], 0, dy)
        for dy, (a, b) in lines0.items()
    ]
    one_y, one_y_above = (
        [
            add(wide1.at[some, a : a + 8], wide1.at[some, b : b + 8], 0, dy)
            for dy, a, b in ((1, 16, 0), (-1, 8, 24))
        ]
        for some in (slice(0, 8), slice(8, 12))
    )
    two_z = [
        add(wide2.at[4:6], wide2.at[4 - 2 * dz : 6 - 2 * dz], dz, 0) for dz in (-2, -1, 1, 2)
    ]

    def copy_of(index, device):
        source, target, _, _ = copies[index]
        return pltpu.make_async_remote_copy(
            src_ref=source,
            dst_ref=target,
            send_sem=send.at[index],
            recv_sem=recv.at[index],
            device_id=device,
            device_id_type=MESH,
        )

    def start(indices, also=True):
        for index in indices:
            _, _, dz, dy = copies[index]

            @pl.when(inside(dz, dy) & also)
            def _(index=index, dz=dz, dy=dy):
                copy_of(index, (slab + dz, pencil + dy)).start()

    def arrived(indices, also=True):
        for index in indices:
            _, _, dz, dy = copies[index]

            @pl.when(inside(-dz, -dy) & also)
            def _(index=index, dz=dz, dy=dy):
                copy_of(index, (slab - dz, pencil - dy)).wait_recv()

    def sent(indices, also=True):
        for index in indices:
            _, _, dz, dy = copies[index]

            @pl.when(inside(dz, dy) & also)
            def _(index=index, dz=dz, dy=dy):
                copy_of(index, (slab + dz, pencil + dy)).wait_send()

    def pencil_copy(step):
        lines = pl.ds(pl.multiple_of(8 * pencil, 8), 8)
        return pltpu.make_async_remote_copy(
            src_ref=wide2.at[4:6, lines],
            dst_ref=wide2.at[4:6, lines],
            send_sem=send2.at[step],
            recv_sem=recv2.at[step],
            device_id=along_pencil(step),
            device_id_type=MESH,
        )

    def pencil_arrival(step):
        lines = pl.ds(pl.multiple_of(8 * lax.rem(pencil + pencils - step, pencils), 8), 8)
        return pltpu.make_async_remote_copy(
            src_ref=wide2.at[4:6, lines],
            dst_ref=wide2.at[4:6, lines],
            send_sem=send2.at[step],
            recv_sem=recv2.at[step],
            device_id=along_pencil(step),
            device_id_type=MESH,
        )

    def top_copy(step, slot):
        return pltpu.make_async_remote_copy(
            src_ref=wide3.at[slot],
            dst_ref=wide3.at[slot],
            send_sem=send3.at[step],
            recv_sem=recv3.at[step],
            device_id=along_slab(step),
            device_id_type=MESH,
        )

    start([to_above, to_below])
    deposit(own, total, CZ * slab, CZ)
    grid = total[...]
    wide0[4:12, 8:40, :] = grid.reshape(CZ, CY, NX)
    start(middle_y)
    one = halve(grid, ROWS // 4, 5, NX // 2)
    wide1[4:8, 8:24, :] = one.reshape(CZ // 2, CY // 2, NX // 2)
    two = halve(one, ROWS // 16, 4, NX // 4)
    wide2[4:6, pl.ds(pl.multiple_of(8 * pencil, 8), 8), :] = two.reshape(
        CZ // 4, CY // 4, NX // 4
    )
    for step in range(1, pencils):
        pencil_copy(step).start()

    has_below = slab > 0
    has_above = slab < slabs - 1
    arrived([to_above])

    @pl.when(has_below)
    def _():
        deposit(below, total, CZ * slab - 4, 4, CZ * slab - 8)
        halo = total[0 : 5 * CY, :]
        wide0[0:4, 8:40, :] = halo[0 : 4 * CY].reshape(4, CY, NX)
        wide1[0:4, 8:24, :] = halve_halo(halo, CY).reshape(4, CY // 2, NX // 2)

    start(below_y, has_below)
    start(one_y)
    for step in range(1, pencils):
        pencil_arrival(step).wait_recv()
    start(two_z)
    lines2 = 8 * pencils
    three = halve(
        wide2[4:6].reshape(2 * lines2, NX // 4), lines2 // 2, lines2.bit_length() - 1, NX // 4
    )
    wide3[pl.ds(slab, 1)] = three[None]

    @pl.loop(1, slabs)
    def _(step):
        top_copy(step, slab).start()

    arrived([to_below])

    @pl.when(has_above)
    def _():
        deposit(above, total, CZ * slab + CZ, 4, CZ * slab + CZ + 4)
        halo = total[0 : 5 * CY, :]
        wide0[12:16, 8:40, :] = halo[0 : 4 * CY].reshape(4, CY, NX)
        wide1[8:12, 8:24, :] = halve_halo(halo, 0).reshape(4, CY // 2, NX // 2)

    start(above_y, has_above)
    start(one_y_above, has_above)
    interpolate_x(along_x)
    arrived(two_z)
    field_of(wide2, field2, 3, 2)

    @pl.loop(1, slabs)
    def _(step):
        copy = top_copy(step, lax.rem(slab + slabs - step, slabs))
        copy.wait_send()
        copy.wait_recv()

    upper_fields(slabs, pencils, wide3, field3)
    arrived(one_y)
    arrived(one_y_above, has_above)
    field_of(wide1, field1, 2, 1)
    interpolate(
        slabs,
        pencils,
        (field1, field2, field3),
        (flat1, flat2, flat3),
        along_x,
        lined_high,
        lined_low,
        base,
    )
    for step in range(1, pencils):
        pencil_copy(step).wait_send()
    sent([to_above, to_below, *middle_y, *two_z, *one_y])
    sent(one_y_above, has_above)
    arrived(middle_y)
    arrived(below_y, has_below)
    sent(below_y, has_below)
    arrived(above_y, has_above)
    sent(above_y, has_above)


def exchange_call(slabs, pencils, atom_cell, charge):
    atoms = atom_cell.shape[1]
    shapes = ((16, 48, NX), (12, 48, NX), (8, atoms // 2))
    field3_rows = sum(4 * max((pencils * CY) >> level, 8) for level in (3, 4, 5))
    return pl.pallas_call(
        functools.partial(exchange_kernel, slabs, pencils),
        out_shape=[jax.ShapeDtypeStruct(shape, jnp.float32) for shape in shapes],
        in_specs=[VMEM] * 2,
        out_specs=[VMEM] * 3,
        scratch_shapes=[
            pltpu.VMEM((12, 32, NX // 2), jnp.float32),
            pltpu.VMEM((10, 8 * pencils, NX // 4), jnp.float32),
            pltpu.VMEM((slabs, 4 * pencils, 128), jnp.float32),
            pltpu.VMEM((8, atoms // 2), jnp.float32),
            pltpu.VMEM((8, atoms // 2), jnp.float32),
            pltpu.VMEM((ROWS, NX), jnp.float32),
            pltpu.VMEM((8 * 32, NX // 2), jnp.float32),
            pltpu.VMEM((4 * 8 * pencils, NX // 4), jnp.float32),
            pltpu.VMEM((field3_rows, 128), jnp.float32),
            pltpu.VMEM((NX, NX), jnp.bfloat16),
            pltpu.VMEM((2 * 32, 12 * 256), jnp.float32),
            pltpu.VMEM((2 * 8 * pencils, 12 * 128), jnp.float32),
            pltpu.VMEM((2 * field3_rows // 4, 12 * 128), jnp.float32),
            pltpu.VMEM((12 * 48, NX), jnp.bfloat16),
            pltpu.VMEM((12 * 48, NX), jnp.bfloat16),
            pltpu.SemaphoreType.DMA((16,)),
            pltpu.SemaphoreType.DMA((16,)),
            pltpu.SemaphoreType.DMA((pencils,)),
            pltpu.SemaphoreType.DMA((pencils,)),
            pltpu.SemaphoreType.DMA((slabs,)),
            pltpu.SemaphoreType.DMA((slabs,)),
        ],
        cost_estimate=pl.CostEstimate(flops=10**10, bytes_accessed=2**23, transcendentals=0),
        compiler_params=pltpu.CompilerParams(
            collective_id=0, has_side_effects=True, vmem_limit_bytes=40 * 2**20
        ),
    )(atom_cell, charge.reshape(1, -1))


def field_kernel(
    slabs,
    pencils,
    own_ref,
    wide0,
    base,
    pot_ref,
    force_ref,
    paired,
    wide_pot,
    high_ref,
    low_ref,
):
    slab = lax.axis_index("slab")
    pencil = lax.axis_index("pencil")
    upper = pencils * CY

    @pl.loop(0, 16)
    def _(plane):
        values = wide0[plane]
        for b in (1, 2):
            paired[b - 1, plane] = pltpu.roll(values, b, 0) + pltpu.roll(values, 48 - b, 0)

    @pl.loop(0, 12)
    def _(plane):
        whole_plane = CZ * slab - 2 + plane
        inside_z = (whole_plane >= 0) & (whole_plane < slabs * CZ)
        for block in range(6):
            rows = pl.ds(8 * block, 8)

            def near(b, k):
                if b:
                    return paired[b - 1, plane + 2 + k, rows, :]
                return wide0[plane + 2 + k, rows, :]

            table = {}
            for b in range(3):
                table[0, b] = near(b, 0)
                for a in (1, 2):
                    table[a, b] = near(b, a) + near(b, -a)
            groups = grouped(table)
            total = base[plane, rows, :]
            for c in range(3):
                part = sum(near_weight(c * c + k) * groups[k] for k in SQUARES)
                total = total + (pair_x(part, c) if c else part)
            row = CY * pencil - 8 + 8 * block + iota((8, NX), 0)
            valid = (row >= 0) & (row < upper) & inside_z
            wide_pot[plane, rows, :] = jnp.where(valid, total, 0.0)

    def slope(after1, before1, after2, before2):
        return (8.0 * (after1 - before1) - (after2 - before2)) * (1.0 / 12.0)

    @pl.loop(0, CZ)
    def _(plane):
        middle = wide_pot[plane + 2]
        own = middle[8:40]
        pot_ref[plane] = own
        at = [wide_pot[plane + 2 + k, 8:40, :] for k in (1, -1, 2, -2)]
        across = [pltpu.roll(middle, (-k) % 48, 0)[8:40] for k in (1, -1, 2, -2)]
        along = [shift_x(own, k) for k in (1, -1, 2, -2)]
        for direction, four in enumerate((at, across, along)):
            high, low = split_two(slope(*four))
            start = pl.multiple_of(direction * ROWS + plane * CY, CY)
            high_ref[pl.ds(start, CY), :] = high
            low_ref[pl.ds(start, CY), :] = low

    half_atoms = own_ref.shape[1]
    width = math.gcd(half_atoms, 1024)

    @pl.loop(0, half_atoms // width)
    def _(step):
        start = pl.multiple_of(step * width, width)
        for half in range(2):
            rows, columns, charges = local_rows(own_ref, half, start, width)
            at_row = iota((ROWS, width), 0) == rows
            table = one_hot(columns.astype(jnp.int16), NX)
            place = pl.ds(pl.multiple_of(half * half_atoms + start, width), width)
            for direction in range(3):
                part = pl.ds(direction * ROWS, ROWS)
                at_cell = jnp.dot(high_ref[part, :], table, preferred_element_type=jnp.float32)
                at_cell += jnp.dot(low_ref[part, :], table, preferred_element_type=jnp.float32)
                chosen = jnp.sum(jnp.where(at_row, at_cell, 0.0), axis=0, keepdims=True)
                force_ref[direction : direction + 1, place] = -charges * chosen


def field_call(slabs, pencils, wide, base, own):
    return pl.pallas_call(
        functools.partial(field_kernel, slabs, pencils),
        out_shape=[
            jax.ShapeDtypeStruct((CZ, CY, NX), jnp.float32),
            jax.ShapeDtypeStruct((3, 2 * own.shape[1]), jnp.float32),
        ],
        in_specs=[VMEM] * 3,
        out_specs=[VMEM] * 2,
        scratch_shapes=[
            pltpu.VMEM((2, 16, 48, NX), jnp.float32),
            pltpu.VMEM((12, 48, NX), jnp.float32),
            pltpu.VMEM((3 * ROWS, NX), jnp.bfloat16),
            pltpu.VMEM((3 * ROWS, NX), jnp.bfloat16),
        ],
        cost_estimate=pl.CostEstimate(flops=2 * 10**10, bytes_accessed=2**23, transcendentals=0),
        compiler_params=pltpu.CompilerParams(vmem_limit_bytes=40 * 2**20),
    )(own, wide, base)


def solution(mesh):
    slabs = mesh.shape["slab"]
    pencils = mesh.shape["pencil"]

    def body(atom_cell, charge):
        wide, base, own = exchange_call(slabs, pencils, atom_cell, charge)
        potential, forces = field_call(slabs, pencils, wide, base, own)
        return (potential, forces)

    return jax.shard_map(
        body,
        mesh=mesh,
        in_specs=(P(None, ("slab", "pencil")), P(("slab", "pencil"))),
        out_specs=(P("slab", "pencil", None), P(None, ("slab", "pencil"))),
        check_vma=False,
    )
```

```python
import functools
import math

import jax
import jax.numpy as jnp
from jax import lax
from jax.experimental import pallas as pl
from jax.experimental.pallas import tpu as pltpu
from jax.sharding import PartitionSpec as P

CZ = 8
CY = 32
NX = 512
F = 32
ROWS = CZ * CY
CHUNK = 2048
MESH = pl.DeviceIdType.MESH
VMEM = pl.BlockSpec(memory_space=pltpu.VMEM)
SQUARES = (0, 1, 2, 4, 5, 8)


def iota(shape, dim):
    return lax.broadcasted_iota(jnp.int32, shape, dim)


def iota16(shape, dim):
    return iota(shape, dim).astype(jnp.int16)


def one_hot(places, size):
    here = iota16((size, places.shape[1]), 0) == places
    return jnp.where(here, jnp.ones((), jnp.bfloat16), jnp.zeros((), jnp.bfloat16))


def near_weight(squared):
    return 1.0 / math.sqrt(squared + 0.25) - 1.0 / math.sqrt(squared + 4.0)


def level_weight(level, squared):
    return (1.0 / math.sqrt(squared + 1.0) - 1.0 / math.sqrt(squared + 4.0)) / 2**level


def split_two(values):
    high = values.astype(jnp.bfloat16)
    return high, (values - high.astype(jnp.float32)).astype(jnp.bfloat16)


def dot32(left, right):
    left_high, left_low = split_two(left)
    right_high, right_low = split_two(right)
    total = jnp.dot(left_high, right_high, preferred_element_type=jnp.float32)
    total += jnp.dot(left_high, right_low, preferred_element_type=jnp.float32)
    return total + jnp.dot(left_low, right_high, preferred_element_type=jnp.float32)


def halve_rows(rows_out, rows_in, line_bits):
    out_row = iota((rows_out, rows_in), 0)
    in_row = iota((rows_out, rows_in), 1)
    plane = in_row >> (line_bits + 1)
    line = (in_row & (2**line_bits - 1)) >> 1
    return jnp.where((plane << (line_bits - 1)) + line == out_row, 1.0, 0.0).astype(jnp.bfloat16)


def halve_columns(columns_in, columns_out):
    return jnp.where(
        iota((columns_in, columns_out), 0) >> 1 == iota((columns_in, columns_out), 1), 1.0, 0.0
    ).astype(jnp.bfloat16)


def halve(values, rows_out, line_bits, columns_out):
    rows, columns = values.shape
    left = halve_rows(rows_out, rows, line_bits)
    high, low = split_two(values)
    part = jnp.dot(left, high, preferred_element_type=jnp.float32)
    part += jnp.dot(left, low, preferred_element_type=jnp.float32)
    right = halve_columns(columns, columns_out)
    high, low = split_two(part)
    whole = jnp.dot(high, right, preferred_element_type=jnp.float32)
    return whole + jnp.dot(low, right, preferred_element_type=jnp.float32)


def deposit(atoms_ref, total_ref, first_plane, planes, far_plane=None):
    near_rows = planes * CY
    rows = near_rows if far_plane is None else near_rows + CY
    width = math.gcd(atoms_ref.shape[1], CHUNK)
    y0 = lax.axis_index("pencil") * CY
    total_ref[0:rows, :] = jnp.zeros((rows, NX), jnp.float32)

    @pl.loop(0, atoms_ref.shape[1] // width)
    def _(step):
        for half in range(2):
            here = pl.ds(pl.multiple_of(step * width, width), width)
            row = 4 * half
            plane = atoms_ref[row : row + 1, here].astype(jnp.int32) - first_plane
            line = atoms_ref[row + 1 : row + 2, here].astype(jnp.int32) - y0
            columns = atoms_ref[row + 2 : row + 3, here].astype(jnp.int16)
            high, low = split_two(atoms_ref[row + 3 : row + 4, here])
            place = plane * CY + line
            if far_plane is not None:
                far = ((plane + first_plane - far_plane) >> 1) * (CY // 2) + (line >> 1)
                place = jnp.where((plane >= 0) & (plane < planes), place, near_rows + far)
            at_row = iota16((rows, width), 0) == place.astype(jnp.int16)
            table = one_hot(columns, NX)
            none = jnp.zeros((), jnp.bfloat16)
            stacked = jnp.concatenate(
                [jnp.where(at_row, high, none), jnp.where(at_row, low, none)], axis=0
            )
            added = lax.dot_general(
                stacked, table, (((1,), (1,)), ((), ())), preferred_element_type=jnp.float32
            )
            total_ref[0:rows, :] += added[:rows] + added[rows:]


def shift_x(values, step):
    width = values.shape[-1]
    axis = values.ndim - 1
    column = iota(values.shape, axis)
    moved = pltpu.roll(values, (-step) % width, axis)
    return jnp.where((column + step >= 0) & (column + step < width), moved, 0.0)


def pair_x(values, step):
    return shift_x(values, step) + shift_x(values, -step)


def hat(fine, cell, factor, count):
    bits = factor.bit_length()
    numerator = jnp.clip(2 * fine + 1 - factor, 0, 2 * factor * (count - 1))
    lower = jnp.minimum(numerator >> bits, count - 2)
    fraction = (numerator - (lower << bits)).astype(jnp.float32) * (0.5 / factor)
    return jnp.where(
        cell == lower, 1.0 - fraction, jnp.where(cell == lower + 1, fraction, 0.0)
    )


def shift_y(values, step):
    lines = values.shape[0]
    line = iota(values.shape, 0) + step
    return jnp.where((line >= 0) & (line < lines), pltpu.roll(values, (-step) % lines, 0), 0.0)


def field_of(wide, field, shift, level):
    lines = wide.shape[1]

    @pl.loop(0, field.shape[0] // lines)
    def _(plane):
        table = {}
        for a in range(3):
            line = wide[plane + shift]
            if a:
                line = wide[plane + shift + a] + wide[plane + shift - a]
            table[a, 0] = line
            for b in (1, 2):
                table[a, b] = shift_y(line, b) + shift_y(line, -b)
        groups = grouped(table)
        total = None
        for c in range(3):
            part = sum(level_weight(level, c * c + k) * groups[k] for k in SQUARES)
            total = total + pair_x(part, c) if c else part
        field[pl.ds(pl.multiple_of(plane * lines, lines), lines), :] = total


def grouped(table):
    return {
        0: table[0, 0],
        1: table[0, 1] + table[1, 0],
        2: table[1, 1],
        4: table[0, 2] + table[2, 0],
        5: table[1, 2] + table[2, 1],
        8: table[2, 2],
    }


def upper_fields(slabs, pencils, wide3, field3):
    slab = lax.axis_index("slab")
    pencil_bits = pencils.bit_length() - 1
    rows3 = slabs * pencils * 4
    grid3 = wide3[...].reshape(rows3, 128)
    coarse = []
    first_row = 0
    first_lane = 0
    for level in (3, 4, 5):
        down = level - 3
        line_bits = pencil_bits + 2 - down
        lines = 2**line_bits
        planes = slabs >> down
        count = planes * lines
        length = NX >> level
        if level == 3:
            charges = grid3
        else:
            shape = (count, rows3)
            out_row = iota(shape, 0)
            in_row = iota(shape, 1)
            in_plane = in_row >> (2 + pencil_bits)
            in_line = in_row & (4 * pencils - 1)
            cell = ((in_plane >> down) << line_bits) + (in_line >> down)
            charges = dot32(jnp.where(cell == out_row, 1.0, 0.0), grid3)
        reach = 3 if level < 5 else length
        source = iota((128, 128), 0) >> down
        column = iota((128, 128), 1) - first_lane
        valid = (column >= 0) & (column < length)
        pairs = jnp.concatenate(
            [
                jnp.where(valid & (jnp.abs(source - column) == c), 1.0, 0.0)
                for c in range(reach)
            ],
            axis=1,
        )
        moved = dot32(charges, pairs)
        stacked = jnp.concatenate(
            [moved[:, c * 128 : (c + 1) * 128] for c in range(reach)], axis=0
        )
        blocks = []
        for c in range(reach):
            out_bits = max(line_bits, 3)
            shape = (4 << out_bits, count)
            dz = (iota(shape, 1) >> line_bits) - (iota(shape, 0) >> out_bits)
            dz = dz - ((slab >> down) - 1)
            dy = (iota(shape, 1) & (lines - 1)) - (iota(shape, 0) & (2**out_bits - 1))
            squared = dz * dz + dy * dy
            if level < 5:
                weight = jnp.zeros(shape, jnp.float32)
                for value in SQUARES:
                    weight = jnp.where(
                        squared == value, level_weight(level, value + c * c), weight
                    )
                weight = jnp.where((jnp.abs(dz) <= 2) & (jnp.abs(dy) <= 2), weight, 0.0)
            else:
                weight = (1.0 / F) / jnp.sqrt((squared + (c * c + 1)).astype(jnp.float32))
            blocks.append(dot32(weight, stacked[c * count : (c + 1) * count]))
        field3[first_row : first_row + (4 << out_bits), :] = sum(blocks[1:], blocks[0])
        first_row = first_row + (4 << out_bits)
        first_lane = first_lane + length


def interpolate_x(along_x):
    lane = 0
    for level in range(1, 6):
        length = NX >> level
        rows = length if level < 5 else NX - lane
        weights = hat(iota((rows, NX), 1), iota((rows, NX), 0), 2**level, length)
        weights = jnp.where(iota((rows, NX), 0) < length, weights, 0.0)
        along_x[lane : lane + rows, :] = weights.astype(jnp.bfloat16)
        lane = lane + rows


def interpolate(slabs, pencils, fields, flats, along_x, lined_high, lined_low, base):
    slab = lax.axis_index("slab")
    pencil = lax.axis_index("pencil")
    upper = pencils * CY
    padded = [max(upper >> level, 8) for level in (3, 4, 5)]
    layers = [
        (1, 4 * slab - 2, 32, 16 * pencil - 8),
        (2, 2 * slab - 1, upper >> 2, 0),
    ]
    layers += [
        (level, (slab >> (level - 3)) - 1, lines, 0)
        for level, lines in zip((3, 4, 5), padded, strict=True)
    ]
    starts = [0, 0, 0, 4 * padded[0], 4 * (padded[0] + padded[1])]
    tops = [0, 0, 0, padded[0], padded[0] + padded[1]]
    field1, field2, field3 = fields
    flat1, flat2, flat3 = flats
    fields = [field1, field2, field3, field3, field3]
    flats = [flat1, flat2, flat3, flat3, flat3]

    for plane in range(12):
        fine_z = CZ * slab - 2 + plane
        for (level, plane0, lines, _), begin, top, field, flat in zip(
            layers, starts, tops, fields, flats, strict=True
        ):
            factor = 2**level
            count = (slabs * CZ) >> level
            numerator = jnp.clip(2 * fine_z + 1 - factor, 0, 2 * factor * (count - 1))
            lower = jnp.minimum(numerator >> (level + 1), count - 2)
            fraction = (numerator - (lower << (level + 1))).astype(jnp.float32) * (0.5 / factor)
            row = begin + (lower - plane0) * lines
            row = pl.multiple_of(row, 8)
            mixed = (1.0 - fraction) * field[pl.ds(row, lines), :]
            mixed += fraction * field[pl.ds(row + lines, lines), :]
            high, low = split_two(mixed)
            width = field.shape[1]
            there = slice(plane * width, (plane + 1) * width)
            flat[top : top + lines, there] = high.astype(jnp.float32)
            flat[flat.shape[0] // 2 + top : flat.shape[0] // 2 + top + lines, there] = low.astype(
                jnp.float32
            )

    def along_y(some):
        blocks = []
        for level, _, lines, line0 in some:
            shape = (48, lines)
            fine_y = CY * pencil - 8 + iota(shape, 0)
            blocks.append(hat(fine_y, line0 + iota(shape, 1), 2**level, upper >> level))
        return jnp.concatenate(blocks + blocks, axis=1).astype(jnp.bfloat16)

    for some, flat, first in ((layers[:1], flat1, 0), (layers[1:2], flat2, 256), (layers[2:], flat3, 384)):
        width = flat.shape[1] // 12
        lined = jnp.dot(
            along_y(some), flat[...].astype(jnp.bfloat16), preferred_element_type=jnp.float32
        )
        high, low = split_two(lined)
        for plane in range(12):
            there = slice(plane * width, (plane + 1) * width)
            rows = slice(48 * plane, 48 * plane + 48)
            lined_high[rows, first : first + width] = high[:, there]
            lined_low[rows, first : first + width] = low[:, there]

    fine = jnp.dot(lined_high[...], along_x[...], preferred_element_type=jnp.float32)
    fine += jnp.dot(lined_low[...], along_x[...], preferred_element_type=jnp.float32)
    base[...] = fine.reshape(12, 48, NX)


def halve_halo(total, near_first):
    out_row = iota((2 * CY, 5 * CY), 0)
    in_row = iota((2 * CY, 5 * CY), 1)
    near = ((in_row >> 6) << 4) + ((in_row & (CY - 1)) >> 1) + near_first
    far = in_row - 4 * CY + (CY - near_first)
    chosen = jnp.where(in_row < 4 * CY, near, far) == out_row
    left = jnp.where(chosen, 1.0, 0.0).astype(jnp.bfloat16)
    high, low = split_two(total)
    part = jnp.dot(left, high, preferred_element_type=jnp.float32)
    part += jnp.dot(left, low, preferred_element_type=jnp.float32)
    right = halve_columns(NX, NX // 2)
    high, low = split_two(part)
    whole = jnp.dot(high, right, preferred_element_type=jnp.float32)
    return whole + jnp.dot(low, right, preferred_element_type=jnp.float32)


def row_slices(atoms):
    half_rows = atoms // 256
    for row in range(2 * half_rows):
        yield row, row // half_rows, row % half_rows * 128


def sort_atoms(own, planes, place_ref, sorted_ref, starts_ref, moved):
    atoms = 2 * own.shape[1]
    rows = atoms // 128
    for row, half, begin in row_slices(atoms):
        planes[row : row + 1, :] = own[4 * half : 4 * half + 1, begin : begin + 128]
    plane = planes[...].astype(jnp.int32) - lax.axis_index("slab") * CZ
    bins = [jnp.where(plane == b, 1.0, 0.0) for b in range(CZ)]
    stacked = jnp.concatenate(bins, axis=0).astype(jnp.bfloat16)
    earlier = iota((128, 128), 0) < iota((128, 128), 1)
    earlier = jnp.where(earlier, 1.0, 0.0).astype(jnp.bfloat16)
    in_row = jnp.dot(stacked, earlier, preferred_element_type=jnp.float32)
    ones = jnp.ones((128, 128), jnp.bfloat16)
    of_row = jnp.dot(stacked, ones, preferred_element_type=jnp.float32).astype(jnp.bfloat16)
    size = (CZ * rows, CZ * rows)
    above = jnp.where(iota(size, 1) < iota(size, 0), 1.0, 0.0).astype(jnp.bfloat16)
    before = jnp.dot(above, of_row, preferred_element_type=jnp.float32)
    both = in_row + before
    place = sum(bins[b] * both[b * rows : (b + 1) * rows] for b in range(CZ))
    for b in range(CZ):
        starts_ref[b : b + 1, :] = before[b * rows : b * rows + 1, :]
    planes[...] = place
    for row, half, begin in row_slices(atoms):
        place_ref[half : half + 1, begin : begin + 128] = planes[row : row + 1, :]

    width = math.gcd(own.shape[1], CHUNK)
    y0 = lax.axis_index("pencil") * CY
    moved[...] = jnp.zeros_like(moved)

    @pl.loop(0, own.shape[1] // width)
    def _(step):
        for half in range(2):
            here = pl.ds(pl.multiple_of(step * width, width), width)
            row = 4 * half
            line = own[row + 1 : row + 2, here].astype(jnp.int32) - y0
            column = own[row + 2 : row + 3, here].astype(jnp.int32)
            to = place_ref[half : half + 1, here].astype(jnp.int32)
            at_row = iota16((rows, width), 0) == (to >> 7).astype(jnp.int16)
            none = jnp.zeros((), jnp.bfloat16)
            fields = [
                jnp.where(at_row, part.astype(jnp.float32).astype(jnp.bfloat16), none)
                for part in (line, column & 255, column >> 8)
            ]
            moved[...] += lax.dot_general(
                jnp.concatenate(fields, axis=0),
                one_hot((to & 127).astype(jnp.int16), 128),
                (((1,), (1,)), ((), ())),
                preferred_element_type=jnp.float32,
            )

    moved[rows : 2 * rows, :] += 256.0 * moved[2 * rows : 3 * rows, :]
    for row in range(rows):
        there = slice(128 * row, 128 * row + 128)
        sorted_ref[0:1, there] = moved[row : row + 1, :]
        sorted_ref[1:2, there] = moved[rows + row : rows + row + 1, :]


def exchange_kernel(
    slabs,
    pencils,
    cell_ref,
    charge_ref,
    wide0,
    base,
    own,
    place_ref,
    sorted_ref,
    starts_ref,
    wide1,
    wide2,
    wide3,
    planes,
    moved,
    below,
    above,
    total,
    field1,
    field2,
    field3,
    along_x,
    flat1,
    flat2,
    flat3,
    lined_high,
    lined_low,
    send,
    recv,
    send2,
    recv2,
    send3,
    recv3,
):
    slab = lax.axis_index("slab")
    pencil = lax.axis_index("pencil")
    half = own.shape[1]
    for ref in (wide0, wide1, wide2):
        ref[...] = jnp.zeros_like(ref)
    for part in range(2):
        there = slice(part * half, (part + 1) * half)
        for row in range(3):
            own[4 * part + row : 4 * part + row + 1, :] = cell_ref[row : row + 1, there].astype(
                jnp.float32
            )
        own[4 * part + 3 : 4 * part + 4, :] = charge_ref[:, there]

    def along_pencil(step):
        return (slab, lax.rem(pencil + step, pencils))

    def along_slab(step):
        return (lax.rem(slab + step, slabs), pencil)

    barrier = pltpu.get_barrier_semaphore()

    @pl.loop(1, pencils)
    def _(step):
        pl.semaphore_signal(barrier, inc=1, device_id=along_pencil(step), device_id_type=MESH)

    @pl.loop(1, slabs)
    def _(step):
        pl.semaphore_signal(barrier, inc=1, device_id=along_slab(step), device_id_type=MESH)

    pl.semaphore_wait(barrier, slabs + pencils - 2)

    def inside(dz, dy):
        z = slab + dz
        y = pencil + dy
        return (z >= 0) & (z < slabs) & (y >= 0) & (y < pencils)

    copies = []

    def add(source, target, dz, dy):
        copies.append((source, target, dz, dy))
        return len(copies) - 1

    to_above = add(own, below, 1, 0)
    to_below = add(own, above, -1, 0)
    lines0 = {1: (32, 0), -1: (8, 40)}
    middle_y = [
        add(wide0.at[4:12, a : a + 8], wide0.at[4:12, b : b + 8], 0, dy)
        for dy, (a, b) in lines0.items()
    ]
    below_y = [
        add(wide0.at[0:4, a : a + 8], wide0.at[0:4, b : b + 8], 0, dy)
        for dy, (a, b) in lines0.items()
    ]
    above_y = [
        add(wide0.at[12:16, a : a + 8], wide0.at[12:16, b : b + 8], 0, dy)
        for dy, (a, b) in lines0.items()
    ]
    one_y, one_y_above = (
        [
            add(wide1.at[some, a : a + 8], wide1.at[some, b : b + 8], 0, dy)
            for dy, a, b in ((1, 16, 0), (-1, 8, 24))
        ]
        for some in (slice(0, 8), slice(8, 12))
    )
    two_z = [
        add(wide2.at[4:6], wide2.at[4 - 2 * dz : 6 - 2 * dz], dz, 0) for dz in (-2, -1, 1, 2)
    ]

    def copy_of(index, device):
        source, target, _, _ = copies[index]
        return pltpu.make_async_remote_copy(
            src_ref=source,
            dst_ref=target,
            send_sem=send.at[index],
            recv_sem=recv.at[index],
            device_id=device,
            device_id_type=MESH,
        )

    def start(indices, also=True):
        for index in indices:
            _, _, dz, dy = copies[index]

            @pl.when(inside(dz, dy) & also)
            def _(index=index, dz=dz, dy=dy):
                copy_of(index, (slab + dz, pencil + dy)).start()

    def arrived(indices, also=True):
        for index in indices:
            _, _, dz, dy = copies[index]

            @pl.when(inside(-dz, -dy) & also)
            def _(index=index, dz=dz, dy=dy):
                copy_of(index, (slab - dz, pencil - dy)).wait_recv()

    def sent(indices, also=True):
        for index in indices:
            _, _, dz, dy = copies[index]

            @pl.when(inside(dz, dy) & also)
            def _(index=index, dz=dz, dy=dy):
                copy_of(index, (slab + dz, pencil + dy)).wait_send()

    def pencil_copy(step):
        lines = pl.ds(pl.multiple_of(8 * pencil, 8), 8)
        return pltpu.make_async_remote_copy(
            src_ref=wide2.at[4:6, lines],
            dst_ref=wide2.at[4:6, lines],
            send_sem=send2.at[step],
            recv_sem=recv2.at[step],
            device_id=along_pencil(step),
            device_id_type=MESH,
        )

    def pencil_arrival(step):
        lines = pl.ds(pl.multiple_of(8 * lax.rem(pencil + pencils - step, pencils), 8), 8)
        return pltpu.make_async_remote_copy(
            src_ref=wide2.at[4:6, lines],
            dst_ref=wide2.at[4:6, lines],
            send_sem=send2.at[step],
            recv_sem=recv2.at[step],
            device_id=along_pencil(step),
            device_id_type=MESH,
        )

    def top_copy(step, slot):
        return pltpu.make_async_remote_copy(
            src_ref=wide3.at[slot],
            dst_ref=wide3.at[slot],
            send_sem=send3.at[step],
            recv_sem=recv3.at[step],
            device_id=along_slab(step),
            device_id_type=MESH,
        )

    start([to_above, to_below])
    deposit(own, total, CZ * slab, CZ)
    grid = total[...]
    wide0[4:12, 8:40, :] = grid.reshape(CZ, CY, NX)
    start(middle_y)
    one = halve(grid, ROWS // 4, 5, NX // 2)
    wide1[4:8, 8:24, :] = one.reshape(CZ // 2, CY // 2, NX // 2)
    two = halve(one, ROWS // 16, 4, NX // 4)
    wide2[4:6, pl.ds(pl.multiple_of(8 * pencil, 8), 8), :] = two.reshape(
        CZ // 4, CY // 4, NX // 4
    )
    for step in range(1, pencils):
        pencil_copy(step).start()

    has_below = slab > 0
    has_above = slab < slabs - 1
    sort_atoms(own, planes, place_ref, sorted_ref, starts_ref, moved)
    for step in range(1, pencils):
        pencil_arrival(step).wait_recv()
    start(two_z)
    lines2 = 8 * pencils
    three = halve(
        wide2[4:6].reshape(2 * lines2, NX // 4), lines2 // 2, lines2.bit_length() - 1, NX // 4
    )
    wide3[pl.ds(slab, 1)] = three[None]

    @pl.loop(1, slabs)
    def _(step):
        top_copy(step, slab).start()

    arrived([to_above])

    @pl.when(has_below)
    def _():
        deposit(below, total, CZ * slab - 4, 4, CZ * slab - 8)
        halo = total[0 : 5 * CY, :]
        wide0[0:4, 8:40, :] = halo[0 : 4 * CY].reshape(4, CY, NX)
        wide1[0:4, 8:24, :] = halve_halo(halo, CY).reshape(4, CY // 2, NX // 2)

    start(below_y, has_below)
    start(one_y)
    arrived([to_below])

    @pl.when(has_above)
    def _():
        deposit(above, total, CZ * slab + CZ, 4, CZ * slab + CZ + 4)
        halo = total[0 : 5 * CY, :]
        wide0[12:16, 8:40, :] = halo[0 : 4 * CY].reshape(4, CY, NX)
        wide1[8:12, 8:24, :] = halve_halo(halo, 0).reshape(4, CY // 2, NX // 2)

    start(above_y, has_above)
    start(one_y_above, has_above)
    interpolate_x(along_x)
    arrived(two_z)
    field_of(wide2, field2, 3, 2)

    @pl.loop(1, slabs)
    def _(step):
        copy = top_copy(step, lax.rem(slab + slabs - step, slabs))
        copy.wait_send()
        copy.wait_recv()

    upper_fields(slabs, pencils, wide3, field3)
    arrived(one_y)
    arrived(one_y_above, has_above)
    field_of(wide1, field1, 2, 1)
    interpolate(
        slabs,
        pencils,
        (field1, field2, field3),
        (flat1, flat2, flat3),
        along_x,
        lined_high,
        lined_low,
        base,
    )
    for step in range(1, pencils):
        pencil_copy(step).wait_send()
    sent([to_above, to_below, *middle_y, *two_z, *one_y])
    sent(one_y_above, has_above)
    arrived(middle_y)
    arrived(below_y, has_below)
    sent(below_y, has_below)
    arrived(above_y, has_above)
    sent(above_y, has_above)


def exchange_call(slabs, pencils, atom_cell, charge):
    atoms = atom_cell.shape[1]
    shapes = (
        (16, 48, NX),
        (12, 48, NX),
        (8, atoms // 2),
        (2, atoms // 2),
        (2, atoms),
        (CZ, 128),
    )
    field3_rows = sum(4 * max((pencils * CY) >> level, 8) for level in (3, 4, 5))
    return pl.pallas_call(
        functools.partial(exchange_kernel, slabs, pencils),
        out_shape=[jax.ShapeDtypeStruct(shape, jnp.float32) for shape in shapes],
        in_specs=[VMEM] * 2,
        out_specs=[VMEM] * 6,
        scratch_shapes=[
            pltpu.VMEM((12, 32, NX // 2), jnp.float32),
            pltpu.VMEM((10, 8 * pencils, NX // 4), jnp.float32),
            pltpu.VMEM((slabs, 4 * pencils, 128), jnp.float32),
            pltpu.VMEM((atoms // 128, 128), jnp.float32),
            pltpu.VMEM((3 * atoms // 128, 128), jnp.float32),
            pltpu.VMEM((8, atoms // 2), jnp.float32),
            pltpu.VMEM((8, atoms // 2), jnp.float32),
            pltpu.VMEM((ROWS, NX), jnp.float32),
            pltpu.VMEM((8 * 32, NX // 2), jnp.float32),
            pltpu.VMEM((4 * 8 * pencils, NX // 4), jnp.float32),
            pltpu.VMEM((field3_rows, 128), jnp.float32),
            pltpu.VMEM((NX, NX), jnp.bfloat16),
            pltpu.VMEM((2 * 32, 12 * 256), jnp.float32),
            pltpu.VMEM((2 * 8 * pencils, 12 * 128), jnp.float32),
            pltpu.VMEM((2 * field3_rows // 4, 12 * 128), jnp.float32),
            pltpu.VMEM((12 * 48, NX), jnp.bfloat16),
            pltpu.VMEM((12 * 48, NX), jnp.bfloat16),
            pltpu.SemaphoreType.DMA((16,)),
            pltpu.SemaphoreType.DMA((16,)),
            pltpu.SemaphoreType.DMA((pencils,)),
            pltpu.SemaphoreType.DMA((pencils,)),
            pltpu.SemaphoreType.DMA((slabs,)),
            pltpu.SemaphoreType.DMA((slabs,)),
        ],
        cost_estimate=pl.CostEstimate(flops=10**10, bytes_accessed=2**23, transcendentals=0),
        compiler_params=pltpu.CompilerParams(
            collective_id=0, has_side_effects=True, vmem_limit_bytes=40 * 2**20
        ),
    )(atom_cell, charge.reshape(1, -1))


def field_kernel(
    slabs,
    pencils,
    own_ref,
    place_ref,
    sorted_ref,
    starts_ref,
    wide0,
    base,
    pot_ref,
    force_ref,
    paired,
    wide_pot,
    slopes,
    bounds,
    found,
    by_row,
):
    slab = lax.axis_index("slab")
    pencil = lax.axis_index("pencil")
    upper = pencils * CY

    @pl.loop(0, 16)
    def _(plane):
        values = wide0[plane]
        for b in (1, 2):
            paired[b - 1, plane] = pltpu.roll(values, b, 0) + pltpu.roll(values, 48 - b, 0)

    @pl.loop(0, 12)
    def _(plane):
        whole_plane = CZ * slab - 2 + plane
        inside_z = (whole_plane >= 0) & (whole_plane < slabs * CZ)
        for block in range(6):
            rows = pl.ds(8 * block, 8)

            def near(b, k):
                if b:
                    return paired[b - 1, plane + 2 + k, rows, :]
                return wide0[plane + 2 + k, rows, :]

            table = {}
            for b in range(3):
                table[0, b] = near(b, 0)
                for a in (1, 2):
                    table[a, b] = near(b, a) + near(b, -a)
            groups = grouped(table)
            total = base[plane, rows, :]
            for c in range(3):
                part = sum(near_weight(c * c + k) * groups[k] for k in SQUARES)
                total = total + (pair_x(part, c) if c else part)
            row = CY * pencil - 8 + 8 * block + iota((8, NX), 0)
            valid = (row >= 0) & (row < upper) & inside_z
            wide_pot[plane, rows, :] = jnp.where(valid, total, 0.0)

    def slope(after1, before1, after2, before2):
        return (8.0 * (after1 - before1) - (after2 - before2)) * (1.0 / 12.0)

    atoms = 2 * own_ref.shape[1]
    for plane in range(CZ):
        bounds[plane] = jnp.max(starts_ref[plane : plane + 1, :]).astype(jnp.int32)
    bounds[CZ] = jnp.int32(atoms)
    found[...] = jnp.zeros_like(found)
    size = math.gcd(atoms, 1024)

    @pl.loop(0, CZ)
    def _(plane):
        middle = wide_pot[plane + 2]
        own = middle[8:40]
        pot_ref[plane] = own
        at = [wide_pot[plane + 2 + k, 8:40, :] for k in (1, -1, 2, -2)]
        across = [pltpu.roll(middle, (-k) % 48, 0)[8:40] for k in (1, -1, 2, -2)]
        along = [shift_x(own, k) for k in (1, -1, 2, -2)]
        for direction, four in enumerate((at, across, along)):
            high, low = split_two(slope(*four))
            slopes[2 * direction * CY : (2 * direction + 1) * CY, :] = high
            slopes[(2 * direction + 1) * CY : (2 * direction + 2) * CY, :] = low
        first = bounds[plane]
        last = bounds[plane + 1]

        def block(step, carry):
            begin = pl.multiple_of(step * size, size)
            here = pl.ds(begin, size)
            table = one_hot(sorted_ref[1:2, here].astype(jnp.int32).astype(jnp.int16), NX)
            at_cell = jnp.dot(slopes[...], table, preferred_element_type=jnp.float32)
            index = begin + iota((1, size), 1)
            line = sorted_ref[0:1, here].astype(jnp.int32)
            line = jnp.where((index >= first) & (index < last), line, -1)
            at_row = iota((CY, size), 0) == line
            for direction in range(3):
                high = at_cell[2 * direction * CY : (2 * direction + 1) * CY]
                low = at_cell[(2 * direction + 1) * CY : (2 * direction + 2) * CY]
                found[direction : direction + 1, here] += jnp.sum(
                    jnp.where(at_row, high + low, 0.0), axis=0, keepdims=True
                )
            return carry

        lax.fori_loop(first // size, (last + size - 1) // size, block, 0)

    rows = atoms // 128
    for direction in range(3):
        for row in range(rows):
            there = slice(128 * row, 128 * row + 128)
            by_row[direction * rows + row : direction * rows + row + 1, :] = found[
                direction : direction + 1, there
            ]
    high, low = split_two(by_row[...])
    split = jnp.concatenate([high, low], axis=0)
    width = math.gcd(own_ref.shape[1], CHUNK)

    @pl.loop(0, own_ref.shape[1] // width)
    def _(step):
        for half in range(2):
            start = pl.multiple_of(step * width, width)
            here = pl.ds(start, width)
            to = place_ref[half : half + 1, here].astype(jnp.int32)
            table = one_hot((to & 127).astype(jnp.int16), 128)
            values = jnp.dot(split, table, preferred_element_type=jnp.float32)
            at_row = iota((rows, width), 0) == to >> 7
            charges = own_ref[4 * half + 3 : 4 * half + 4, here]
            place = pl.ds(pl.multiple_of(half * own_ref.shape[1] + start, width), width)
            for direction in range(3):
                high = values[direction * rows : (direction + 1) * rows]
                low = values[(3 + direction) * rows : (4 + direction) * rows]
                chosen = jnp.sum(jnp.where(at_row, high + low, 0.0), axis=0, keepdims=True)
                force_ref[direction : direction + 1, place] = -charges * chosen


def field_call(slabs, pencils, wide, base, own, order):
    atoms = 2 * own.shape[1]
    return pl.pallas_call(
        functools.partial(field_kernel, slabs, pencils),
        out_shape=[
            jax.ShapeDtypeStruct((CZ, CY, NX), jnp.float32),
            jax.ShapeDtypeStruct((3, 2 * own.shape[1]), jnp.float32),
        ],
        in_specs=[VMEM] * 6,
        out_specs=[VMEM] * 2,
        scratch_shapes=[
            pltpu.VMEM((2, 16, 48, NX), jnp.float32),
            pltpu.VMEM((12, 48, NX), jnp.float32),
            pltpu.VMEM((6 * CY, NX), jnp.bfloat16),
            pltpu.SMEM((CZ + 1,), jnp.int32),
            pltpu.VMEM((3, atoms), jnp.float32),
            pltpu.VMEM((3 * atoms // 128, 128), jnp.float32),
        ],
        cost_estimate=pl.CostEstimate(flops=2 * 10**10, bytes_accessed=2**23, transcendentals=0),
        compiler_params=pltpu.CompilerParams(vmem_limit_bytes=40 * 2**20),
    )(own, *order, wide, base)


def solution(mesh):
    slabs = mesh.shape["slab"]
    pencils = mesh.shape["pencil"]

    def body(atom_cell, charge):
        wide, base, own, *order = exchange_call(slabs, pencils, atom_cell, charge)
        potential, forces = field_call(slabs, pencils, wide, base, own, order)
        return (potential, forces)

    return jax.shard_map(
        body,
        mesh=mesh,
        in_specs=(P(None, ("slab", "pencil")), P(("slab", "pencil"))),
        out_specs=(P("slab", "pencil", None), P(None, ("slab", "pencil"))),
        check_vma=False,
    )
```

```python
import functools
import math

import jax
import jax.numpy as jnp
from jax import lax
from jax.experimental import pallas as pl
from jax.experimental.pallas import tpu as pltpu
from jax.sharding import PartitionSpec as P

CZ = 8
CY = 32
NX = 512
F = 32
ROWS = CZ * CY
CHUNK = 2048
MESH = pl.DeviceIdType.MESH
VMEM = pl.BlockSpec(memory_space=pltpu.VMEM)
SQUARES = (0, 1, 2, 4, 5, 8)


def iota(shape, dim):
    return lax.broadcasted_iota(jnp.int32, shape, dim)


def iota16(shape, dim):
    return iota(shape, dim).astype(jnp.int16)


def one_hot(places, size):
    here = iota16((size, places.shape[1]), 0) == places
    return jnp.where(here, jnp.ones((), jnp.bfloat16), jnp.zeros((), jnp.bfloat16))


def near_weight(squared):
    return 1.0 / math.sqrt(squared + 0.25) - 1.0 / math.sqrt(squared + 4.0)


def level_weight(level, squared):
    return (1.0 / math.sqrt(squared + 1.0) - 1.0 / math.sqrt(squared + 4.0)) / 2**level


def split_two(values):
    high = values.astype(jnp.bfloat16)
    return high, (values - high.astype(jnp.float32)).astype(jnp.bfloat16)


def dot32(left, right):
    left_high, left_low = split_two(left)
    right_high, right_low = split_two(right)
    total = jnp.dot(left_high, right_high, preferred_element_type=jnp.float32)
    total += jnp.dot(left_high, right_low, preferred_element_type=jnp.float32)
    return total + jnp.dot(left_low, right_high, preferred_element_type=jnp.float32)


def halve_rows(rows_out, rows_in, line_bits):
    out_row = iota((rows_out, rows_in), 0)
    in_row = iota((rows_out, rows_in), 1)
    plane = in_row >> (line_bits + 1)
    line = (in_row & (2**line_bits - 1)) >> 1
    return jnp.where((plane << (line_bits - 1)) + line == out_row, 1.0, 0.0).astype(jnp.bfloat16)


def halve_columns(columns_in, columns_out):
    return jnp.where(
        iota((columns_in, columns_out), 0) >> 1 == iota((columns_in, columns_out), 1), 1.0, 0.0
    ).astype(jnp.bfloat16)


def halve(values, rows_out, line_bits, columns_out):
    rows, columns = values.shape
    left = halve_rows(rows_out, rows, line_bits)
    high, low = split_two(values)
    part = jnp.dot(left, high, preferred_element_type=jnp.float32)
    part += jnp.dot(left, low, preferred_element_type=jnp.float32)
    right = halve_columns(columns, columns_out)
    high, low = split_two(part)
    whole = jnp.dot(high, right, preferred_element_type=jnp.float32)
    return whole + jnp.dot(low, right, preferred_element_type=jnp.float32)


def deposit(atoms_ref, begin, end, total_ref, first_plane, planes, far_plane=None):
    near_rows = planes * CY
    rows = near_rows if far_plane is None else near_rows + CY
    width = math.gcd(end - begin, CHUNK)
    y0 = lax.axis_index("pencil") * CY

    @pl.loop(0, (end - begin) // width)
    def _(step):
        here = pl.ds(pl.multiple_of(begin + step * width, width), width)
        plane = atoms_ref[0:1, here].astype(jnp.int32) - first_plane
        line = atoms_ref[1:2, here].astype(jnp.int32) - y0
        columns = atoms_ref[2:3, here].astype(jnp.int32).astype(jnp.int16)
        high, low = split_two(atoms_ref[3:4, here])
        place = plane * CY + line
        if far_plane is not None:
            far = ((plane + first_plane - far_plane) >> 1) * (CY // 2) + (line >> 1)
            place = jnp.where((plane >= 0) & (plane < planes), place, near_rows + far)
        at_row = iota16((rows, width), 0) == place.astype(jnp.int16)
        none = jnp.zeros((), jnp.bfloat16)
        stacked = jnp.concatenate(
            [jnp.where(at_row, high, none), jnp.where(at_row, low, none)], axis=0
        )
        added = lax.dot_general(
            stacked,
            one_hot(columns, NX),
            (((1,), (1,)), ((), ())),
            preferred_element_type=jnp.float32,
        )
        total_ref[0:rows, :] += added[:rows] + added[rows:]


def shift_x(values, step):
    width = values.shape[-1]
    axis = values.ndim - 1
    column = iota(values.shape, axis)
    moved = pltpu.roll(values, (-step) % width, axis)
    return jnp.where((column + step >= 0) & (column + step < width), moved, 0.0)


def pair_x(values, step):
    return shift_x(values, step) + shift_x(values, -step)


def hat(fine, cell, factor, count):
    bits = factor.bit_length()
    numerator = jnp.clip(2 * fine + 1 - factor, 0, 2 * factor * (count - 1))
    lower = jnp.minimum(numerator >> bits, count - 2)
    fraction = (numerator - (lower << bits)).astype(jnp.float32) * (0.5 / factor)
    return jnp.where(
        cell == lower, 1.0 - fraction, jnp.where(cell == lower + 1, fraction, 0.0)
    )


def shift_y(values, step):
    lines = values.shape[0]
    line = iota(values.shape, 0) + step
    return jnp.where((line >= 0) & (line < lines), pltpu.roll(values, (-step) % lines, 0), 0.0)


def field_of(wide, field, shift, level):
    lines = wide.shape[1]

    @pl.loop(0, field.shape[0] // lines)
    def _(plane):
        table = {}
        for a in range(3):
            line = wide[plane + shift]
            if a:
                line = wide[plane + shift + a] + wide[plane + shift - a]
            table[a, 0] = line
            for b in (1, 2):
                table[a, b] = shift_y(line, b) + shift_y(line, -b)
        groups = grouped(table)
        total = None
        for c in range(3):
            part = sum(level_weight(level, c * c + k) * groups[k] for k in SQUARES)
            total = total + pair_x(part, c) if c else part
        field[pl.ds(pl.multiple_of(plane * lines, lines), lines), :] = total


def grouped(table):
    return {
        0: table[0, 0],
        1: table[0, 1] + table[1, 0],
        2: table[1, 1],
        4: table[0, 2] + table[2, 0],
        5: table[1, 2] + table[2, 1],
        8: table[2, 2],
    }


def upper_fields(slabs, pencils, wide3, field3):
    slab = lax.axis_index("slab")
    pencil_bits = pencils.bit_length() - 1
    rows3 = slabs * pencils * 4
    grid3 = wide3[...].reshape(rows3, 128)
    coarse = []
    first_row = 0
    first_lane = 0
    for level in (3, 4, 5):
        down = level - 3
        line_bits = pencil_bits + 2 - down
        lines = 2**line_bits
        planes = slabs >> down
        count = planes * lines
        length = NX >> level
        if level == 3:
            charges = grid3
        else:
            shape = (count, rows3)
            out_row = iota(shape, 0)
            in_row = iota(shape, 1)
            in_plane = in_row >> (2 + pencil_bits)
            in_line = in_row & (4 * pencils - 1)
            cell = ((in_plane >> down) << line_bits) + (in_line >> down)
            charges = dot32(jnp.where(cell == out_row, 1.0, 0.0), grid3)
        reach = 3 if level < 5 else length
        source = iota((128, 128), 0) >> down
        column = iota((128, 128), 1) - first_lane
        valid = (column >= 0) & (column < length)
        pairs = jnp.concatenate(
            [
                jnp.where(valid & (jnp.abs(source - column) == c), 1.0, 0.0)
                for c in range(reach)
            ],
            axis=1,
        )
        moved = dot32(charges, pairs)
        stacked = jnp.concatenate(
            [moved[:, c * 128 : (c + 1) * 128] for c in range(reach)], axis=0
        )
        blocks = []
        for c in range(reach):
            out_bits = max(line_bits, 3)
            shape = (4 << out_bits, count)
            dz = (iota(shape, 1) >> line_bits) - (iota(shape, 0) >> out_bits)
            dz = dz - ((slab >> down) - 1)
            dy = (iota(shape, 1) & (lines - 1)) - (iota(shape, 0) & (2**out_bits - 1))
            squared = dz * dz + dy * dy
            if level < 5:
                weight = jnp.zeros(shape, jnp.float32)
                for value in SQUARES:
                    weight = jnp.where(
                        squared == value, level_weight(level, value + c * c), weight
                    )
                weight = jnp.where((jnp.abs(dz) <= 2) & (jnp.abs(dy) <= 2), weight, 0.0)
            else:
                weight = (1.0 / F) / jnp.sqrt((squared + (c * c + 1)).astype(jnp.float32))
            blocks.append(dot32(weight, stacked[c * count : (c + 1) * count]))
        field3[first_row : first_row + (4 << out_bits), :] = sum(blocks[1:], blocks[0])
        first_row = first_row + (4 << out_bits)
        first_lane = first_lane + length


def interpolate_x(along_x):
    lane = 0
    for level in range(1, 6):
        length = NX >> level
        rows = length if level < 5 else NX - lane
        weights = hat(iota((rows, NX), 1), iota((rows, NX), 0), 2**level, length)
        weights = jnp.where(iota((rows, NX), 0) < length, weights, 0.0)
        along_x[lane : lane + rows, :] = weights.astype(jnp.bfloat16)
        lane = lane + rows


def interpolate(slabs, pencils, fields, flats, along_x, lined_high, lined_low, base):
    slab = lax.axis_index("slab")
    pencil = lax.axis_index("pencil")
    upper = pencils * CY
    padded = [max(upper >> level, 8) for level in (3, 4, 5)]
    layers = [
        (1, 4 * slab - 2, 32, 16 * pencil - 8),
        (2, 2 * slab - 1, upper >> 2, 0),
    ]
    layers += [
        (level, (slab >> (level - 3)) - 1, lines, 0)
        for level, lines in zip((3, 4, 5), padded, strict=True)
    ]
    starts = [0, 0, 0, 4 * padded[0], 4 * (padded[0] + padded[1])]
    tops = [0, 0, 0, padded[0], padded[0] + padded[1]]
    field1, field2, field3 = fields
    flat1, flat2, flat3 = flats
    fields = [field1, field2, field3, field3, field3]
    flats = [flat1, flat2, flat3, flat3, flat3]

    for plane in range(12):
        fine_z = CZ * slab - 2 + plane
        for (level, plane0, lines, _), begin, top, field, flat in zip(
            layers, starts, tops, fields, flats, strict=True
        ):
            factor = 2**level
            count = (slabs * CZ) >> level
            numerator = jnp.clip(2 * fine_z + 1 - factor, 0, 2 * factor * (count - 1))
            lower = jnp.minimum(numerator >> (level + 1), count - 2)
            fraction = (numerator - (lower << (level + 1))).astype(jnp.float32) * (0.5 / factor)
            row = begin + (lower - plane0) * lines
            row = pl.multiple_of(row, 8)
            mixed = (1.0 - fraction) * field[pl.ds(row, lines), :]
            mixed += fraction * field[pl.ds(row + lines, lines), :]
            high, low = split_two(mixed)
            width = field.shape[1]
            there = slice(plane * width, (plane + 1) * width)
            flat[top : top + lines, there] = high.astype(jnp.float32)
            flat[flat.shape[0] // 2 + top : flat.shape[0] // 2 + top + lines, there] = low.astype(
                jnp.float32
            )

    def along_y(some):
        blocks = []
        for level, _, lines, line0 in some:
            shape = (48, lines)
            fine_y = CY * pencil - 8 + iota(shape, 0)
            blocks.append(hat(fine_y, line0 + iota(shape, 1), 2**level, upper >> level))
        return jnp.concatenate(blocks + blocks, axis=1).astype(jnp.bfloat16)

    for some, flat, first in ((layers[:1], flat1, 0), (layers[1:2], flat2, 256), (layers[2:], flat3, 384)):
        width = flat.shape[1] // 12
        lined = jnp.dot(
            along_y(some), flat[...].astype(jnp.bfloat16), preferred_element_type=jnp.float32
        )
        high, low = split_two(lined)
        for plane in range(12):
            there = slice(plane * width, (plane + 1) * width)
            rows = slice(48 * plane, 48 * plane + 48)
            lined_high[rows, first : first + width] = high[:, there]
            lined_low[rows, first : first + width] = low[:, there]

    fine = jnp.dot(lined_high[...], along_x[...], preferred_element_type=jnp.float32)
    fine += jnp.dot(lined_low[...], along_x[...], preferred_element_type=jnp.float32)
    base[...] = fine.reshape(12, 48, NX)


def halve_halo(total, near_first):
    out_row = iota((2 * CY, 5 * CY), 0)
    in_row = iota((2 * CY, 5 * CY), 1)
    near = ((in_row >> 6) << 4) + ((in_row & (CY - 1)) >> 1) + near_first
    far = in_row - 4 * CY + (CY - near_first)
    chosen = jnp.where(in_row < 4 * CY, near, far) == out_row
    left = jnp.where(chosen, 1.0, 0.0).astype(jnp.bfloat16)
    high, low = split_two(total)
    part = jnp.dot(left, high, preferred_element_type=jnp.float32)
    part += jnp.dot(left, low, preferred_element_type=jnp.float32)
    right = halve_columns(NX, NX // 2)
    high, low = split_two(part)
    whole = jnp.dot(high, right, preferred_element_type=jnp.float32)
    return whole + jnp.dot(low, right, preferred_element_type=jnp.float32)


def sort_atoms(own, planes, place_ref, sorted_ref, starts_ref, moved):
    atoms = own.shape[1]
    rows = atoms // 128
    for row in range(rows):
        planes[row : row + 1, :] = own[0:1, 128 * row : 128 * row + 128]
    plane = planes[...].astype(jnp.int32) - lax.axis_index("slab") * CZ
    bins = [jnp.where(plane == b, 1.0, 0.0) for b in range(CZ)]
    stacked = jnp.concatenate(bins, axis=0).astype(jnp.bfloat16)
    earlier = iota((128, 128), 0) < iota((128, 128), 1)
    earlier = jnp.where(earlier, 1.0, 0.0).astype(jnp.bfloat16)
    in_row = jnp.dot(stacked, earlier, preferred_element_type=jnp.float32)
    ones = jnp.ones((128, 128), jnp.bfloat16)
    of_row = jnp.dot(stacked, ones, preferred_element_type=jnp.float32).astype(jnp.bfloat16)
    size = (CZ * rows, CZ * rows)
    above = jnp.where(iota(size, 1) < iota(size, 0), 1.0, 0.0).astype(jnp.bfloat16)
    before = jnp.dot(above, of_row, preferred_element_type=jnp.float32)
    both = in_row + before
    place = sum(bins[b] * both[b * rows : (b + 1) * rows] for b in range(CZ))
    for b in range(CZ):
        starts_ref[b : b + 1, :] = before[b * rows : b * rows + 1, :]
    planes[...] = place
    for row in range(rows):
        place_ref[0:1, 128 * row : 128 * row + 128] = planes[row : row + 1, :]

    width = math.gcd(atoms, CHUNK)
    y0 = lax.axis_index("pencil") * CY
    moved[...] = jnp.zeros_like(moved)

    @pl.loop(0, atoms // width)
    def _(step):
        here = pl.ds(pl.multiple_of(step * width, width), width)
        line = own[1:2, here].astype(jnp.int32) - y0
        column = own[2:3, here].astype(jnp.int32)
        to = place_ref[0:1, here].astype(jnp.int32)
        at_row = iota16((rows, width), 0) == (to >> 7).astype(jnp.int16)
        none = jnp.zeros((), jnp.bfloat16)
        fields = [
            jnp.where(at_row, part.astype(jnp.float32).astype(jnp.bfloat16), none)
            for part in (line, column & 255, column >> 8)
        ]
        moved[...] += lax.dot_general(
            jnp.concatenate(fields, axis=0),
            one_hot((to & 127).astype(jnp.int16), 128),
            (((1,), (1,)), ((), ())),
            preferred_element_type=jnp.float32,
        )

    moved[rows : 2 * rows, :] += 256.0 * moved[2 * rows : 3 * rows, :]
    for row in range(rows):
        there = slice(128 * row, 128 * row + 128)
        sorted_ref[0:1, there] = moved[row : row + 1, :]
        sorted_ref[1:2, there] = moved[rows + row : rows + row + 1, :]


def exchange_kernel(
    slabs,
    pencils,
    own,
    wide0,
    base,
    place_ref,
    sorted_ref,
    starts_ref,
    wide1,
    wide2,
    wide3,
    planes,
    moved,
    below,
    above,
    total,
    total_below,
    total_above,
    field1,
    field2,
    field3,
    along_x,
    flat1,
    flat2,
    flat3,
    lined_high,
    lined_low,
    send,
    recv,
    send2,
    recv2,
    send3,
    recv3,
):
    slab = lax.axis_index("slab")
    pencil = lax.axis_index("pencil")
    atoms = own.shape[1]
    for ref in (wide0, wide1, wide2, total, total_below, total_above):
        ref[...] = jnp.zeros_like(ref)

    def along_pencil(step):
        return (slab, lax.rem(pencil + step, pencils))

    def along_slab(step):
        return (lax.rem(slab + step, slabs), pencil)

    barrier = pltpu.get_barrier_semaphore()

    @pl.loop(1, pencils)
    def _(step):
        pl.semaphore_signal(barrier, inc=1, device_id=along_pencil(step), device_id_type=MESH)

    @pl.loop(1, slabs)
    def _(step):
        pl.semaphore_signal(barrier, inc=1, device_id=along_slab(step), device_id_type=MESH)

    pl.semaphore_wait(barrier, slabs + pencils - 2)

    def inside(dz, dy):
        z = slab + dz
        y = pencil + dy
        return (z >= 0) & (z < slabs) & (y >= 0) & (y < pencils)

    copies = []

    def add(source, target, dz, dy):
        copies.append((source, target, dz, dy))
        return len(copies) - 1

    parts = [(0, atoms // 2), (atoms // 2, atoms)]
    to_above = [add(own.at[:, a:b], below.at[:, a:b], 1, 0) for a, b in parts]
    to_below = [add(own.at[:, a:b], above.at[:, a:b], -1, 0) for a, b in parts]
    lines0 = {1: (32, 0), -1: (8, 40)}
    middle_y = [
        add(wide0.at[4:12, a : a + 8], wide0.at[4:12, b : b + 8], 0, dy)
        for dy, (a, b) in lines0.items()
    ]
    below_y = [
        add(wide0.at[0:4, a : a + 8], wide0.at[0:4, b : b + 8], 0, dy)
        for dy, (a, b) in lines0.items()
    ]
    above_y = [
        add(wide0.at[12:16, a : a + 8], wide0.at[12:16, b : b + 8], 0, dy)
        for dy, (a, b) in lines0.items()
    ]
    one_y, one_y_above = (
        [
            add(wide1.at[some, a : a + 8], wide1.at[some, b : b + 8], 0, dy)
            for dy, a, b in ((1, 16, 0), (-1, 8, 24))
        ]
        for some in (slice(0, 8), slice(8, 12))
    )
    two_z = [
        add(wide2.at[4:6], wide2.at[4 - 2 * dz : 6 - 2 * dz], dz, 0) for dz in (-2, -1, 1, 2)
    ]

    def copy_of(index, device):
        source, target, _, _ = copies[index]
        return pltpu.make_async_remote_copy(
            src_ref=source,
            dst_ref=target,
            send_sem=send.at[index],
            recv_sem=recv.at[index],
            device_id=device,
            device_id_type=MESH,
        )

    def start(indices, also=True):
        for index in indices:
            _, _, dz, dy = copies[index]

            @pl.when(inside(dz, dy) & also)
            def _(index=index, dz=dz, dy=dy):
                copy_of(index, (slab + dz, pencil + dy)).start()

    def arrived(indices, also=True):
        for index in indices:
            _, _, dz, dy = copies[index]

            @pl.when(inside(-dz, -dy) & also)
            def _(index=index, dz=dz, dy=dy):
                copy_of(index, (slab - dz, pencil - dy)).wait_recv()

    def sent(indices, also=True):
        for index in indices:
            _, _, dz, dy = copies[index]

            @pl.when(inside(dz, dy) & also)
            def _(index=index, dz=dz, dy=dy):
                copy_of(index, (slab + dz, pencil + dy)).wait_send()

    def pencil_copy(step):
        lines = pl.ds(pl.multiple_of(8 * pencil, 8), 8)
        return pltpu.make_async_remote_copy(
            src_ref=wide2.at[4:6, lines],
            dst_ref=wide2.at[4:6, lines],
            send_sem=send2.at[step],
            recv_sem=recv2.at[step],
            device_id=along_pencil(step),
            device_id_type=MESH,
        )

    def pencil_arrival(step):
        lines = pl.ds(pl.multiple_of(8 * lax.rem(pencil + pencils - step, pencils), 8), 8)
        return pltpu.make_async_remote_copy(
            src_ref=wide2.at[4:6, lines],
            dst_ref=wide2.at[4:6, lines],
            send_sem=send2.at[step],
            recv_sem=recv2.at[step],
            device_id=along_pencil(step),
            device_id_type=MESH,
        )

    def top_copy(step, slot):
        return pltpu.make_async_remote_copy(
            src_ref=wide3.at[slot],
            dst_ref=wide3.at[slot],
            send_sem=send3.at[step],
            recv_sem=recv3.at[step],
            device_id=along_slab(step),
            device_id_type=MESH,
        )

    for part in zip(to_above, to_below, strict=True):
        start(part)
    deposit(own, 0, atoms, total, CZ * slab, CZ)
    grid = total[...]
    wide0[4:12, 8:40, :] = grid.reshape(CZ, CY, NX)
    start(middle_y)
    one = halve(grid, ROWS // 4, 5, NX // 2)
    wide1[4:8, 8:24, :] = one.reshape(CZ // 2, CY // 2, NX // 2)
    two = halve(one, ROWS // 16, 4, NX // 4)
    wide2[4:6, pl.ds(pl.multiple_of(8 * pencil, 8), 8), :] = two.reshape(
        CZ // 4, CY // 4, NX // 4
    )
    for step in range(1, pencils):
        pencil_copy(step).start()

    has_below = slab > 0
    has_above = slab < slabs - 1

    def neighbours(part):
        begin, end = parts[part]
        arrived([to_above[part]])

        @pl.when(has_below)
        def _():
            deposit(below, begin, end, total_below, CZ * slab - 4, 4, CZ * slab - 8)

        arrived([to_below[part]])

        @pl.when(has_above)
        def _():
            deposit(above, begin, end, total_above, CZ * slab + CZ, 4, CZ * slab + CZ + 4)

    neighbours(0)
    for step in range(1, pencils):
        pencil_arrival(step).wait_recv()
    start(two_z)
    lines2 = 8 * pencils
    three = halve(
        wide2[4:6].reshape(2 * lines2, NX // 4), lines2 // 2, lines2.bit_length() - 1, NX // 4
    )
    wide3[pl.ds(slab, 1)] = three[None]

    @pl.loop(1, slabs)
    def _(step):
        top_copy(step, slab).start()

    neighbours(1)

    @pl.when(has_below)
    def _():
        halo = total_below[...]
        wide0[0:4, 8:40, :] = halo[0 : 4 * CY].reshape(4, CY, NX)
        wide1[0:4, 8:24, :] = halve_halo(halo, CY).reshape(4, CY // 2, NX // 2)

    start(below_y, has_below)
    start(one_y)

    @pl.when(has_above)
    def _():
        halo = total_above[...]
        wide0[12:16, 8:40, :] = halo[0 : 4 * CY].reshape(4, CY, NX)
        wide1[8:12, 8:24, :] = halve_halo(halo, 0).reshape(4, CY // 2, NX // 2)

    start(above_y, has_above)
    start(one_y_above, has_above)
    sort_atoms(own, planes, place_ref, sorted_ref, starts_ref, moved)
    interpolate_x(along_x)
    arrived(two_z)
    field_of(wide2, field2, 3, 2)

    @pl.loop(1, slabs)
    def _(step):
        copy = top_copy(step, lax.rem(slab + slabs - step, slabs))
        copy.wait_send()
        copy.wait_recv()

    upper_fields(slabs, pencils, wide3, field3)
    arrived(one_y)
    arrived(one_y_above, has_above)
    field_of(wide1, field1, 2, 1)
    interpolate(
        slabs,
        pencils,
        (field1, field2, field3),
        (flat1, flat2, flat3),
        along_x,
        lined_high,
        lined_low,
        base,
    )
    for step in range(1, pencils):
        pencil_copy(step).wait_send()
    sent([*to_above, *to_below, *middle_y, *two_z, *one_y])
    sent(one_y_above, has_above)
    arrived(middle_y)
    arrived(below_y, has_below)
    sent(below_y, has_below)
    arrived(above_y, has_above)
    sent(above_y, has_above)


def exchange_call(slabs, pencils, own):
    atoms = own.shape[1]
    shapes = (
        (16, 48, NX),
        (12, 48, NX),
        (1, atoms),
        (2, atoms),
        (CZ, 128),
    )
    field3_rows = sum(4 * max((pencils * CY) >> level, 8) for level in (3, 4, 5))
    return pl.pallas_call(
        functools.partial(exchange_kernel, slabs, pencils),
        out_shape=[jax.ShapeDtypeStruct(shape, jnp.float32) for shape in shapes],
        in_specs=[VMEM],
        out_specs=[VMEM] * 5,
        scratch_shapes=[
            pltpu.VMEM((12, 32, NX // 2), jnp.float32),
            pltpu.VMEM((10, 8 * pencils, NX // 4), jnp.float32),
            pltpu.VMEM((slabs, 4 * pencils, 128), jnp.float32),
            pltpu.VMEM((atoms // 128, 128), jnp.float32),
            pltpu.VMEM((3 * atoms // 128, 128), jnp.float32),
            pltpu.VMEM((4, atoms), jnp.float32),
            pltpu.VMEM((4, atoms), jnp.float32),
            pltpu.VMEM((ROWS, NX), jnp.float32),
            pltpu.VMEM((5 * CY, NX), jnp.float32),
            pltpu.VMEM((5 * CY, NX), jnp.float32),
            pltpu.VMEM((8 * 32, NX // 2), jnp.float32),
            pltpu.VMEM((4 * 8 * pencils, NX // 4), jnp.float32),
            pltpu.VMEM((field3_rows, 128), jnp.float32),
            pltpu.VMEM((NX, NX), jnp.bfloat16),
            pltpu.VMEM((2 * 32, 12 * 256), jnp.float32),
            pltpu.VMEM((2 * 8 * pencils, 12 * 128), jnp.float32),
            pltpu.VMEM((2 * field3_rows // 4, 12 * 128), jnp.float32),
            pltpu.VMEM((12 * 48, NX), jnp.bfloat16),
            pltpu.VMEM((12 * 48, NX), jnp.bfloat16),
            pltpu.SemaphoreType.DMA((18,)),
            pltpu.SemaphoreType.DMA((18,)),
            pltpu.SemaphoreType.DMA((pencils,)),
            pltpu.SemaphoreType.DMA((pencils,)),
            pltpu.SemaphoreType.DMA((slabs,)),
            pltpu.SemaphoreType.DMA((slabs,)),
        ],
        cost_estimate=pl.CostEstimate(flops=10**10, bytes_accessed=2**23, transcendentals=0),
        compiler_params=pltpu.CompilerParams(
            collective_id=0, has_side_effects=True, vmem_limit_bytes=40 * 2**20
        ),
    )(own)


def field_kernel(
    slabs,
    pencils,
    own_ref,
    place_ref,
    sorted_ref,
    starts_ref,
    wide0,
    base,
    pot_ref,
    force_ref,
    paired,
    wide_pot,
    slopes,
    bounds,
    found,
    by_row,
):
    slab = lax.axis_index("slab")
    pencil = lax.axis_index("pencil")
    upper = pencils * CY

    @pl.loop(0, 16)
    def _(plane):
        values = wide0[plane]
        for b in (1, 2):
            paired[b - 1, plane] = pltpu.roll(values, b, 0) + pltpu.roll(values, 48 - b, 0)

    @pl.loop(0, 12)
    def _(plane):
        whole_plane = CZ * slab - 2 + plane
        inside_z = (whole_plane >= 0) & (whole_plane < slabs * CZ)
        for block in range(6):
            rows = pl.ds(8 * block, 8)

            def near(b, k):
                if b:
                    return paired[b - 1, plane + 2 + k, rows, :]
                return wide0[plane + 2 + k, rows, :]

            table = {}
            for b in range(3):
                table[0, b] = near(b, 0)
                for a in (1, 2):
                    table[a, b] = near(b, a) + near(b, -a)
            groups = grouped(table)
            total = base[plane, rows, :]
            for c in range(3):
                part = sum(near_weight(c * c + k) * groups[k] for k in SQUARES)
                total = total + (pair_x(part, c) if c else part)
            row = CY * pencil - 8 + 8 * block + iota((8, NX), 0)
            valid = (row >= 0) & (row < upper) & inside_z
            wide_pot[plane, rows, :] = jnp.where(valid, total, 0.0)

    def slope(after1, before1, after2, before2):
        return (8.0 * (after1 - before1) - (after2 - before2)) * (1.0 / 12.0)

    atoms = own_ref.shape[1]
    for plane in range(CZ):
        bounds[plane] = jnp.max(starts_ref[plane : plane + 1, :]).astype(jnp.int32)
    bounds[CZ] = jnp.int32(atoms)
    found[...] = jnp.zeros_like(found)
    size = math.gcd(atoms, 1024)

    @pl.loop(0, CZ)
    def _(plane):
        middle = wide_pot[plane + 2]
        own = middle[8:40]
        pot_ref[plane] = own
        at = [wide_pot[plane + 2 + k, 8:40, :] for k in (1, -1, 2, -2)]
        across = [pltpu.roll(middle, (-k) % 48, 0)[8:40] for k in (1, -1, 2, -2)]
        along = [shift_x(own, k) for k in (1, -1, 2, -2)]
        for direction, four in enumerate((at, across, along)):
            high, low = split_two(slope(*four))
            slopes[2 * direction * CY : (2 * direction + 1) * CY, :] = high
            slopes[(2 * direction + 1) * CY : (2 * direction + 2) * CY, :] = low
        first = bounds[plane]
        last = bounds[plane + 1]

        def block(step, carry):
            begin = pl.multiple_of(step * size, size)
            here = pl.ds(begin, size)
            table = one_hot(sorted_ref[1:2, here].astype(jnp.int32).astype(jnp.int16), NX)
            at_cell = jnp.dot(slopes[...], table, preferred_element_type=jnp.float32)
            index = begin + iota((1, size), 1)
            line = sorted_ref[0:1, here].astype(jnp.int32)
            line = jnp.where((index >= first) & (index < last), line, -1)
            at_row = iota((CY, size), 0) == line
            for direction in range(3):
                high = at_cell[2 * direction * CY : (2 * direction + 1) * CY]
                low = at_cell[(2 * direction + 1) * CY : (2 * direction + 2) * CY]
                found[direction : direction + 1, here] += jnp.sum(
                    jnp.where(at_row, high + low, 0.0), axis=0, keepdims=True
                )
            return carry

        lax.fori_loop(first // size, (last + size - 1) // size, block, 0)

    rows = atoms // 128
    for direction in range(3):
        for row in range(rows):
            there = slice(128 * row, 128 * row + 128)
            by_row[direction * rows + row : direction * rows + row + 1, :] = found[
                direction : direction + 1, there
            ]
    high, low = split_two(by_row[...])
    split = jnp.concatenate([high, low], axis=0)
    width = math.gcd(atoms, CHUNK)

    @pl.loop(0, atoms // width)
    def _(step):
        here = pl.ds(pl.multiple_of(step * width, width), width)
        to = place_ref[0:1, here].astype(jnp.int32)
        table = one_hot((to & 127).astype(jnp.int16), 128)
        values = jnp.dot(split, table, preferred_element_type=jnp.float32)
        at_row = iota((rows, width), 0) == to >> 7
        charges = own_ref[3:4, here]
        for direction in range(3):
            high = values[direction * rows : (direction + 1) * rows]
            low = values[(3 + direction) * rows : (4 + direction) * rows]
            chosen = jnp.sum(jnp.where(at_row, high + low, 0.0), axis=0, keepdims=True)
            force_ref[direction : direction + 1, here] = -charges * chosen


def field_call(slabs, pencils, wide, base, own, order):
    atoms = own.shape[1]
    return pl.pallas_call(
        functools.partial(field_kernel, slabs, pencils),
        out_shape=[
            jax.ShapeDtypeStruct((CZ, CY, NX), jnp.float32),
            jax.ShapeDtypeStruct((3, atoms), jnp.float32),
        ],
        in_specs=[VMEM] * 6,
        out_specs=[VMEM] * 2,
        scratch_shapes=[
            pltpu.VMEM((2, 16, 48, NX), jnp.float32),
            pltpu.VMEM((12, 48, NX), jnp.float32),
            pltpu.VMEM((6 * CY, NX), jnp.bfloat16),
            pltpu.SMEM((CZ + 1,), jnp.int32),
            pltpu.VMEM((3, atoms), jnp.float32),
            pltpu.VMEM((3 * atoms // 128, 128), jnp.float32),
        ],
        cost_estimate=pl.CostEstimate(flops=2 * 10**10, bytes_accessed=2**23, transcendentals=0),
        compiler_params=pltpu.CompilerParams(vmem_limit_bytes=40 * 2**20),
    )(own, *order, wide, base)


def solution(mesh):
    slabs = mesh.shape["slab"]
    pencils = mesh.shape["pencil"]

    def body(atom_cell, charge):
        own = jnp.concatenate([atom_cell.astype(jnp.float32), charge[None]], axis=0)
        wide, base, *order = exchange_call(slabs, pencils, own)
        potential, forces = field_call(slabs, pencils, wide, base, own, order)
        return (potential, forces)

    return jax.shard_map(
        body,
        mesh=mesh,
        in_specs=(P(None, ("slab", "pencil")), P(("slab", "pencil"))),
        out_specs=(P("slab", "pencil", None), P(None, ("slab", "pencil"))),
        check_vma=False,
    )
```

```python
import functools
import math

import jax
import jax.numpy as jnp
from jax import lax
from jax.experimental import pallas as pl
from jax.experimental.pallas import tpu as pltpu
from jax.sharding import PartitionSpec as P

CZ = 8
CY = 32
NX = 512
F = 32
ROWS = CZ * CY
CHUNK = 2048
MESH = pl.DeviceIdType.MESH
VMEM = pl.BlockSpec(memory_space=pltpu.VMEM)
SQUARES = (0, 1, 2, 4, 5, 8)


def iota(shape, dim):
    return lax.broadcasted_iota(jnp.int32, shape, dim)


def iota16(shape, dim):
    return iota(shape, dim).astype(jnp.int16)


def one_hot(places, size):
    here = iota16((size, places.shape[1]), 0) == places
    return jnp.where(here, jnp.ones((), jnp.bfloat16), jnp.zeros((), jnp.bfloat16))


def near_weight(squared):
    return 1.0 / math.sqrt(squared + 0.25) - 1.0 / math.sqrt(squared + 4.0)


def level_weight(level, squared):
    return (1.0 / math.sqrt(squared + 1.0) - 1.0 / math.sqrt(squared + 4.0)) / 2**level


def split_two(values):
    high = values.astype(jnp.bfloat16)
    return high, (values - high.astype(jnp.float32)).astype(jnp.bfloat16)


def dot32(left, right):
    left_high, left_low = split_two(left)
    right_high, right_low = split_two(right)
    total = jnp.dot(left_high, right_high, preferred_element_type=jnp.float32)
    total += jnp.dot(left_high, right_low, preferred_element_type=jnp.float32)
    return total + jnp.dot(left_low, right_high, preferred_element_type=jnp.float32)


def halve_rows(rows_out, rows_in, line_bits):
    out_row = iota((rows_out, rows_in), 0)
    in_row = iota((rows_out, rows_in), 1)
    plane = in_row >> (line_bits + 1)
    line = (in_row & (2**line_bits - 1)) >> 1
    return jnp.where((plane << (line_bits - 1)) + line == out_row, 1.0, 0.0).astype(jnp.bfloat16)


def halve_columns(columns_in, columns_out):
    return jnp.where(
        iota((columns_in, columns_out), 0) >> 1 == iota((columns_in, columns_out), 1), 1.0, 0.0
    ).astype(jnp.bfloat16)


def halve(values, rows_out, line_bits, columns_out):
    rows, columns = values.shape
    left = halve_rows(rows_out, rows, line_bits)
    high, low = split_two(values)
    part = jnp.dot(left, high, preferred_element_type=jnp.float32)
    part += jnp.dot(left, low, preferred_element_type=jnp.float32)
    right = halve_columns(columns, columns_out)
    high, low = split_two(part)
    whole = jnp.dot(high, right, preferred_element_type=jnp.float32)
    return whole + jnp.dot(low, right, preferred_element_type=jnp.float32)


def deposit(atoms_ref, begin, end, total_ref, first_plane, planes, far_plane=None):
    near_rows = planes * CY
    rows = near_rows if far_plane is None else near_rows + CY
    width = math.gcd(end - begin, CHUNK)
    y0 = lax.axis_index("pencil") * CY

    @pl.loop(0, (end - begin) // width)
    def _(step):
        here = pl.ds(pl.multiple_of(begin + step * width, width), width)
        plane = atoms_ref[0:1, here].astype(jnp.int32) - first_plane
        line = atoms_ref[1:2, here].astype(jnp.int32) - y0
        columns = atoms_ref[2:3, here].astype(jnp.int32).astype(jnp.int16)
        high, low = split_two(atoms_ref[3:4, here])
        place = plane * CY + line
        if far_plane is not None:
            far = ((plane + first_plane - far_plane) >> 1) * (CY // 2) + (line >> 1)
            place = jnp.where((plane >= 0) & (plane < planes), place, near_rows + far)
        at_row = iota16((rows, width), 0) == place.astype(jnp.int16)
        none = jnp.zeros((), jnp.bfloat16)
        stacked = jnp.concatenate(
            [jnp.where(at_row, high, none), jnp.where(at_row, low, none)], axis=0
        )
        added = lax.dot_general(
            stacked,
            one_hot(columns, NX),
            (((1,), (1,)), ((), ())),
            preferred_element_type=jnp.float32,
        )
        total_ref[0:rows, :] += added[:rows] + added[rows:]


def shift_x(values, step):
    width = values.shape[-1]
    axis = values.ndim - 1
    column = iota(values.shape, axis)
    moved = pltpu.roll(values, (-step) % width, axis)
    return jnp.where((column + step >= 0) & (column + step < width), moved, 0.0)


def pair_x(values, step):
    return shift_x(values, step) + shift_x(values, -step)


def hat(fine, cell, factor, count):
    bits = factor.bit_length()
    numerator = jnp.clip(2 * fine + 1 - factor, 0, 2 * factor * (count - 1))
    lower = jnp.minimum(numerator >> bits, count - 2)
    fraction = (numerator - (lower << bits)).astype(jnp.float32) * (0.5 / factor)
    return jnp.where(
        cell == lower, 1.0 - fraction, jnp.where(cell == lower + 1, fraction, 0.0)
    )


def shift_y(values, step):
    lines = values.shape[0]
    line = iota(values.shape, 0) + step
    return jnp.where((line >= 0) & (line < lines), pltpu.roll(values, (-step) % lines, 0), 0.0)


def field_of(wide, field, shift, level):
    lines = wide.shape[1]

    @pl.loop(0, field.shape[0] // lines)
    def _(plane):
        table = {}
        for a in range(3):
            line = wide[plane + shift]
            if a:
                line = wide[plane + shift + a] + wide[plane + shift - a]
            table[a, 0] = line
            for b in (1, 2):
                table[a, b] = shift_y(line, b) + shift_y(line, -b)
        groups = grouped(table)
        total = None
        for c in range(3):
            part = sum(level_weight(level, c * c + k) * groups[k] for k in SQUARES)
            total = total + pair_x(part, c) if c else part
        field[pl.ds(pl.multiple_of(plane * lines, lines), lines), :] = total


def grouped(table):
    return {
        0: table[0, 0],
        1: table[0, 1] + table[1, 0],
        2: table[1, 1],
        4: table[0, 2] + table[2, 0],
        5: table[1, 2] + table[2, 1],
        8: table[2, 2],
    }


def upper_fields(slabs, pencils, wide3, field3):
    slab = lax.axis_index("slab")
    pencil_bits = pencils.bit_length() - 1
    rows3 = slabs * pencils * 4
    grid3 = wide3[...].reshape(rows3, 128)
    first_row = 0
    first_lane = 0
    for level in (3, 4, 5):
        down = level - 3
        line_bits = pencil_bits + 2 - down
        lines = 2**line_bits
        planes = slabs >> down
        count = planes * lines
        length = NX >> level
        if level == 3:
            charges = grid3
        else:
            shape = (count, rows3)
            out_row = iota(shape, 0)
            in_row = iota(shape, 1)
            in_plane = in_row >> (2 + pencil_bits)
            in_line = in_row & (4 * pencils - 1)
            cell = ((in_plane >> down) << line_bits) + (in_line >> down)
            charges = dot32(jnp.where(cell == out_row, 1.0, 0.0), grid3)
        reach = 3 if level < 5 else length
        source = iota((128, 128), 0) >> down
        column = iota((128, 128), 1) - first_lane
        valid = (column >= 0) & (column < length)
        pairs = jnp.concatenate(
            [
                jnp.where(valid & (jnp.abs(source - column) == c), 1.0, 0.0)
                for c in range(reach)
            ],
            axis=1,
        )
        moved = dot32(charges, pairs)
        stacked = jnp.concatenate(
            [moved[:, c * 128 : (c + 1) * 128] for c in range(reach)], axis=0
        )
        out_bits = max(line_bits, 3)
        shape = (4 << out_bits, reach * count)
        across = iota(shape, 1) >> (count.bit_length() - 1)
        source = iota(shape, 1) & (count - 1)
        dz = (source >> line_bits) - (iota(shape, 0) >> out_bits) - ((slab >> down) - 1)
        dy = (source & (lines - 1)) - (iota(shape, 0) & (2**out_bits - 1))
        squared = (dz * dz + dy * dy + across * across).astype(jnp.float32)
        weight = 1.0 / jnp.sqrt(squared + 1.0)
        if level < 5:
            weight = (weight - 1.0 / jnp.sqrt(squared + 4.0)) / 2**level
            weight = jnp.where((jnp.abs(dz) <= 2) & (jnp.abs(dy) <= 2), weight, 0.0)
        else:
            weight = weight / F
        field3[first_row : first_row + (4 << out_bits), :] = dot32(weight, stacked)
        first_row = first_row + (4 << out_bits)
        first_lane = first_lane + length


def interpolate_x(along_x):
    lane = 0
    for level in range(1, 6):
        length = NX >> level
        rows = length if level < 5 else NX - lane
        weights = hat(iota((rows, NX), 1), iota((rows, NX), 0), 2**level, length)
        weights = jnp.where(iota((rows, NX), 0) < length, weights, 0.0)
        along_x[lane : lane + rows, :] = weights.astype(jnp.bfloat16)
        lane = lane + rows


def interpolate(slabs, pencils, fields, flats, along_x, lined_high, lined_low, base):
    slab = lax.axis_index("slab")
    pencil = lax.axis_index("pencil")
    upper = pencils * CY
    padded = [max(upper >> level, 8) for level in (3, 4, 5)]
    layers = [
        (1, 4 * slab - 2, 32, 16 * pencil - 8),
        (2, 2 * slab - 1, upper >> 2, 0),
    ]
    layers += [
        (level, (slab >> (level - 3)) - 1, lines, 0)
        for level, lines in zip((3, 4, 5), padded, strict=True)
    ]
    starts = [0, 0, 0, 4 * padded[0], 4 * (padded[0] + padded[1])]
    tops = [0, 0, 0, padded[0], padded[0] + padded[1]]
    field1, field2, field3 = fields
    flat1, flat2, flat3 = flats
    fields = [field1, field2, field3, field3, field3]
    flats = [flat1, flat2, flat3, flat3, flat3]

    for plane in range(12):
        fine_z = CZ * slab - 2 + plane
        for (level, plane0, lines, _), begin, top, field, flat in zip(
            layers, starts, tops, fields, flats, strict=True
        ):
            factor = 2**level
            count = (slabs * CZ) >> level
            numerator = jnp.clip(2 * fine_z + 1 - factor, 0, 2 * factor * (count - 1))
            lower = jnp.minimum(numerator >> (level + 1), count - 2)
            fraction = (numerator - (lower << (level + 1))).astype(jnp.float32) * (0.5 / factor)
            row = begin + (lower - plane0) * lines
            row = pl.multiple_of(row, 8)
            mixed = (1.0 - fraction) * field[pl.ds(row, lines), :]
            mixed += fraction * field[pl.ds(row + lines, lines), :]
            high, low = split_two(mixed)
            width = field.shape[1]
            there = slice(plane * width, (plane + 1) * width)
            flat[top : top + lines, there] = high.astype(jnp.float32)
            flat[flat.shape[0] // 2 + top : flat.shape[0] // 2 + top + lines, there] = low.astype(
                jnp.float32
            )

    def along_y(some):
        blocks = []
        for level, _, lines, line0 in some:
            shape = (48, lines)
            fine_y = CY * pencil - 8 + iota(shape, 0)
            blocks.append(hat(fine_y, line0 + iota(shape, 1), 2**level, upper >> level))
        return jnp.concatenate(blocks + blocks, axis=1).astype(jnp.bfloat16)

    for some, flat, first in ((layers[:1], flat1, 0), (layers[1:2], flat2, 256), (layers[2:], flat3, 384)):
        width = flat.shape[1] // 12
        lined = jnp.dot(
            along_y(some), flat[...].astype(jnp.bfloat16), preferred_element_type=jnp.float32
        )
        high, low = split_two(lined)
        for plane in range(12):
            there = slice(plane * width, (plane + 1) * width)
            rows = slice(48 * plane, 48 * plane + 48)
            lined_high[rows, first : first + width] = high[:, there]
            lined_low[rows, first : first + width] = low[:, there]

    fine = jnp.dot(lined_high[...], along_x[...], preferred_element_type=jnp.float32)
    fine += jnp.dot(lined_low[...], along_x[...], preferred_element_type=jnp.float32)
    base[...] = fine.reshape(12, 48, NX)


def halve_halo(total, near_first):
    out_row = iota((2 * CY, 5 * CY), 0)
    in_row = iota((2 * CY, 5 * CY), 1)
    near = ((in_row >> 6) << 4) + ((in_row & (CY - 1)) >> 1) + near_first
    far = in_row - 4 * CY + (CY - near_first)
    chosen = jnp.where(in_row < 4 * CY, near, far) == out_row
    left = jnp.where(chosen, 1.0, 0.0).astype(jnp.bfloat16)
    high, low = split_two(total)
    part = jnp.dot(left, high, preferred_element_type=jnp.float32)
    part += jnp.dot(left, low, preferred_element_type=jnp.float32)
    right = halve_columns(NX, NX // 2)
    high, low = split_two(part)
    whole = jnp.dot(high, right, preferred_element_type=jnp.float32)
    return whole + jnp.dot(low, right, preferred_element_type=jnp.float32)


def sort_atoms(own, planes, place_ref, sorted_ref, starts_ref, moved):
    atoms = own.shape[1]
    rows = atoms // 128
    for row in range(rows):
        planes[row : row + 1, :] = own[0:1, 128 * row : 128 * row + 128]
    plane = planes[...].astype(jnp.int32) - lax.axis_index("slab") * CZ
    bins = [jnp.where(plane == b, 1.0, 0.0) for b in range(CZ)]
    stacked = jnp.concatenate(bins, axis=0).astype(jnp.bfloat16)
    earlier = iota((128, 128), 0) < iota((128, 128), 1)
    earlier = jnp.where(earlier, 1.0, 0.0).astype(jnp.bfloat16)
    in_row = jnp.dot(stacked, earlier, preferred_element_type=jnp.float32)
    ones = jnp.ones((128, 128), jnp.bfloat16)
    of_row = jnp.dot(stacked, ones, preferred_element_type=jnp.float32).astype(jnp.bfloat16)
    size = (CZ * rows, CZ * rows)
    above = jnp.where(iota(size, 1) < iota(size, 0), 1.0, 0.0).astype(jnp.bfloat16)
    before = jnp.dot(above, of_row, preferred_element_type=jnp.float32)
    both = in_row + before
    place = sum(bins[b] * both[b * rows : (b + 1) * rows] for b in range(CZ))
    for b in range(CZ):
        starts_ref[b : b + 1, :] = before[b * rows : b * rows + 1, :]
    planes[...] = place
    for row in range(rows):
        place_ref[0:1, 128 * row : 128 * row + 128] = planes[row : row + 1, :]

    width = math.gcd(atoms, CHUNK)
    y0 = lax.axis_index("pencil") * CY
    moved[...] = jnp.zeros_like(moved)

    @pl.loop(0, atoms // width)
    def _(step):
        here = pl.ds(pl.multiple_of(step * width, width), width)
        line = own[1:2, here].astype(jnp.int32) - y0
        column = own[2:3, here].astype(jnp.int32)
        to = place_ref[0:1, here].astype(jnp.int32)
        at_row = iota16((rows, width), 0) == (to >> 7).astype(jnp.int16)
        none = jnp.zeros((), jnp.bfloat16)
        fields = [
            jnp.where(at_row, part.astype(jnp.float32).astype(jnp.bfloat16), none)
            for part in (line, column & 255, column >> 8)
        ]
        moved[...] += lax.dot_general(
            jnp.concatenate(fields, axis=0),
            one_hot((to & 127).astype(jnp.int16), 128),
            (((1,), (1,)), ((), ())),
            preferred_element_type=jnp.float32,
        )

    moved[rows : 2 * rows, :] += 256.0 * moved[2 * rows : 3 * rows, :]
    for row in range(rows):
        there = slice(128 * row, 128 * row + 128)
        sorted_ref[0:1, there] = moved[row : row + 1, :]
        sorted_ref[1:2, there] = moved[rows + row : rows + row + 1, :]


def exchange_kernel(
    slabs,
    pencils,
    own,
    wide0,
    base,
    place_ref,
    sorted_ref,
    starts_ref,
    wide1,
    wide2,
    wide3,
    planes,
    moved,
    below,
    above,
    total,
    total_below,
    total_above,
    field1,
    field2,
    field3,
    along_x,
    flat1,
    flat2,
    flat3,
    lined_high,
    lined_low,
    send,
    recv,
    send2,
    recv2,
    send3,
    recv3,
):
    slab = lax.axis_index("slab")
    pencil = lax.axis_index("pencil")
    atoms = own.shape[1]
    for ref in (wide0, wide1, wide2, total, total_below, total_above):
        ref[...] = jnp.zeros_like(ref)

    def along_pencil(step):
        return (slab, lax.rem(pencil + step, pencils))

    def along_slab(step):
        return (lax.rem(slab + step, slabs), pencil)

    barrier = pltpu.get_barrier_semaphore()

    @pl.loop(1, pencils)
    def _(step):
        pl.semaphore_signal(barrier, inc=1, device_id=along_pencil(step), device_id_type=MESH)

    @pl.loop(1, slabs)
    def _(step):
        pl.semaphore_signal(barrier, inc=1, device_id=along_slab(step), device_id_type=MESH)

    sort_atoms(own, planes, place_ref, sorted_ref, starts_ref, moved)
    pl.semaphore_wait(barrier, slabs + pencils - 2)

    def inside(dz, dy):
        z = slab + dz
        y = pencil + dy
        return (z >= 0) & (z < slabs) & (y >= 0) & (y < pencils)

    copies = []

    def add(source, target, dz, dy):
        copies.append((source, target, dz, dy))
        return len(copies) - 1

    parts = [(0, atoms // 2), (atoms // 2, atoms)]
    to_above = [add(own.at[:, a:b], below.at[:, a:b], 1, 0) for a, b in parts]
    to_below = [add(own.at[:, a:b], above.at[:, a:b], -1, 0) for a, b in parts]
    lines0 = {1: (32, 0), -1: (8, 40)}
    middle_y = [
        add(wide0.at[4:12, a : a + 8], wide0.at[4:12, b : b + 8], 0, dy)
        for dy, (a, b) in lines0.items()
    ]
    below_y = [
        add(wide0.at[0:4, a : a + 8], wide0.at[0:4, b : b + 8], 0, dy)
        for dy, (a, b) in lines0.items()
    ]
    above_y = [
        add(wide0.at[12:16, a : a + 8], wide0.at[12:16, b : b + 8], 0, dy)
        for dy, (a, b) in lines0.items()
    ]
    one_y, one_y_above = (
        [
            add(wide1.at[some, a : a + 8], wide1.at[some, b : b + 8], 0, dy)
            for dy, a, b in ((1, 16, 0), (-1, 8, 24))
        ]
        for some in (slice(0, 8), slice(8, 12))
    )
    two_z = [
        add(wide2.at[4:6], wide2.at[4 - 2 * dz : 6 - 2 * dz], dz, 0) for dz in (-2, -1, 1, 2)
    ]

    def copy_of(index, device):
        source, target, _, _ = copies[index]
        return pltpu.make_async_remote_copy(
            src_ref=source,
            dst_ref=target,
            send_sem=send.at[index],
            recv_sem=recv.at[index],
            device_id=device,
            device_id_type=MESH,
        )

    def start(indices, also=True):
        for index in indices:
            _, _, dz, dy = copies[index]

            @pl.when(inside(dz, dy) & also)
            def _(index=index, dz=dz, dy=dy):
                copy_of(index, (slab + dz, pencil + dy)).start()

    def arrived(indices, also=True):
        for index in indices:
            _, _, dz, dy = copies[index]

            @pl.when(inside(-dz, -dy) & also)
            def _(index=index, dz=dz, dy=dy):
                copy_of(index, (slab - dz, pencil - dy)).wait_recv()

    def sent(indices, also=True):
        for index in indices:
            _, _, dz, dy = copies[index]

            @pl.when(inside(dz, dy) & also)
            def _(index=index, dz=dz, dy=dy):
                copy_of(index, (slab + dz, pencil + dy)).wait_send()

    def pencil_copy(step):
        lines = pl.ds(pl.multiple_of(8 * pencil, 8), 8)
        return pltpu.make_async_remote_copy(
            src_ref=wide2.at[4:6, lines],
            dst_ref=wide2.at[4:6, lines],
            send_sem=send2.at[step],
            recv_sem=recv2.at[step],
            device_id=along_pencil(step),
            device_id_type=MESH,
        )

    def pencil_arrival(step):
        lines = pl.ds(pl.multiple_of(8 * lax.rem(pencil + pencils - step, pencils), 8), 8)
        return pltpu.make_async_remote_copy(
            src_ref=wide2.at[4:6, lines],
            dst_ref=wide2.at[4:6, lines],
            send_sem=send2.at[step],
            recv_sem=recv2.at[step],
            device_id=along_pencil(step),
            device_id_type=MESH,
        )

    def top_copy(step, slot):
        return pltpu.make_async_remote_copy(
            src_ref=wide3.at[slot],
            dst_ref=wide3.at[slot],
            send_sem=send3.at[step],
            recv_sem=recv3.at[step],
            device_id=along_slab(step),
            device_id_type=MESH,
        )

    for part in zip(to_above, to_below, strict=True):
        start(part)
    deposit(own, 0, atoms, total, CZ * slab, CZ)
    grid = total[...]
    wide0[4:12, 8:40, :] = grid.reshape(CZ, CY, NX)
    start(middle_y)
    one = halve(grid, ROWS // 4, 5, NX // 2)
    wide1[4:8, 8:24, :] = one.reshape(CZ // 2, CY // 2, NX // 2)
    two = halve(one, ROWS // 16, 4, NX // 4)
    wide2[4:6, pl.ds(pl.multiple_of(8 * pencil, 8), 8), :] = two.reshape(
        CZ // 4, CY // 4, NX // 4
    )
    for step in range(1, pencils):
        pencil_copy(step).start()

    has_below = slab > 0
    has_above = slab < slabs - 1

    def neighbours(part):
        begin, end = parts[part]
        arrived([to_above[part]])

        @pl.when(has_below)
        def _():
            deposit(below, begin, end, total_below, CZ * slab - 4, 4, CZ * slab - 8)

        arrived([to_below[part]])

        @pl.when(has_above)
        def _():
            deposit(above, begin, end, total_above, CZ * slab + CZ, 4, CZ * slab + CZ + 4)

    neighbours(0)
    for step in range(1, pencils):
        pencil_arrival(step).wait_recv()
    start(two_z)
    lines2 = 8 * pencils
    three = halve(
        wide2[4:6].reshape(2 * lines2, NX // 4), lines2 // 2, lines2.bit_length() - 1, NX // 4
    )
    wide3[pl.ds(slab, 1)] = three[None]

    @pl.loop(1, slabs)
    def _(step):
        top_copy(step, slab).start()

    neighbours(1)

    @pl.when(has_below)
    def _():
        halo = total_below[...]
        wide0[0:4, 8:40, :] = halo[0 : 4 * CY].reshape(4, CY, NX)
        wide1[0:4, 8:24, :] = halve_halo(halo, CY).reshape(4, CY // 2, NX // 2)

    start(below_y, has_below)
    start(one_y)

    @pl.when(has_above)
    def _():
        halo = total_above[...]
        wide0[12:16, 8:40, :] = halo[0 : 4 * CY].reshape(4, CY, NX)
        wide1[8:12, 8:24, :] = halve_halo(halo, 0).reshape(4, CY // 2, NX // 2)

    start(above_y, has_above)
    start(one_y_above, has_above)
    interpolate_x(along_x)
    arrived(two_z)
    field_of(wide2, field2, 3, 2)

    @pl.loop(1, slabs)
    def _(step):
        copy = top_copy(step, lax.rem(slab + slabs - step, slabs))
        copy.wait_send()
        copy.wait_recv()

    upper_fields(slabs, pencils, wide3, field3)
    arrived(one_y)
    arrived(one_y_above, has_above)
    field_of(wide1, field1, 2, 1)
    interpolate(
        slabs,
        pencils,
        (field1, field2, field3),
        (flat1, flat2, flat3),
        along_x,
        lined_high,
        lined_low,
        base,
    )
    for step in range(1, pencils):
        pencil_copy(step).wait_send()
    sent([*to_above, *to_below, *middle_y, *two_z, *one_y])
    sent(one_y_above, has_above)
    arrived(middle_y)
    arrived(below_y, has_below)
    sent(below_y, has_below)
    arrived(above_y, has_above)
    sent(above_y, has_above)


def exchange_call(slabs, pencils, own):
    atoms = own.shape[1]
    shapes = (
        (16, 48, NX),
        (12, 48, NX),
        (1, atoms),
        (2, atoms),
        (CZ, 128),
    )
    field3_rows = sum(4 * max((pencils * CY) >> level, 8) for level in (3, 4, 5))
    return pl.pallas_call(
        functools.partial(exchange_kernel, slabs, pencils),
        out_shape=[jax.ShapeDtypeStruct(shape, jnp.float32) for shape in shapes],
        in_specs=[VMEM],
        out_specs=[VMEM] * 5,
        scratch_shapes=[
            pltpu.VMEM((12, 32, NX // 2), jnp.float32),
            pltpu.VMEM((10, 8 * pencils, NX // 4), jnp.float32),
            pltpu.VMEM((slabs, 4 * pencils, 128), jnp.float32),
            pltpu.VMEM((atoms // 128, 128), jnp.float32),
            pltpu.VMEM((3 * atoms // 128, 128), jnp.float32),
            pltpu.VMEM((4, atoms), jnp.float32),
            pltpu.VMEM((4, atoms), jnp.float32),
            pltpu.VMEM((ROWS, NX), jnp.float32),
            pltpu.VMEM((5 * CY, NX), jnp.float32),
            pltpu.VMEM((5 * CY, NX), jnp.float32),
            pltpu.VMEM((8 * 32, NX // 2), jnp.float32),
            pltpu.VMEM((4 * 8 * pencils, NX // 4), jnp.float32),
            pltpu.VMEM((field3_rows, 128), jnp.float32),
            pltpu.VMEM((NX, NX), jnp.bfloat16),
            pltpu.VMEM((2 * 32, 12 * 256), jnp.float32),
            pltpu.VMEM((2 * 8 * pencils, 12 * 128), jnp.float32),
            pltpu.VMEM((2 * field3_rows // 4, 12 * 128), jnp.float32),
            pltpu.VMEM((12 * 48, NX), jnp.bfloat16),
            pltpu.VMEM((12 * 48, NX), jnp.bfloat16),
            pltpu.SemaphoreType.DMA((18,)),
            pltpu.SemaphoreType.DMA((18,)),
            pltpu.SemaphoreType.DMA((pencils,)),
            pltpu.SemaphoreType.DMA((pencils,)),
            pltpu.SemaphoreType.DMA((slabs,)),
            pltpu.SemaphoreType.DMA((slabs,)),
        ],
        cost_estimate=pl.CostEstimate(flops=10**10, bytes_accessed=2**23, transcendentals=0),
        compiler_params=pltpu.CompilerParams(
            collective_id=0, has_side_effects=True, vmem_limit_bytes=40 * 2**20
        ),
    )(own)


def field_kernel(
    slabs,
    pencils,
    own_ref,
    place_ref,
    sorted_ref,
    starts_ref,
    wide0,
    base,
    pot_ref,
    force_ref,
    paired,
    wide_pot,
    slopes,
    bounds,
    found,
    by_row,
):
    slab = lax.axis_index("slab")
    pencil = lax.axis_index("pencil")
    upper = pencils * CY

    @pl.loop(0, 16)
    def _(plane):
        values = wide0[plane]
        for b in (1, 2):
            paired[b - 1, plane] = pltpu.roll(values, b, 0) + pltpu.roll(values, 48 - b, 0)

    @pl.loop(0, 12)
    def _(plane):
        whole_plane = CZ * slab - 2 + plane
        inside_z = (whole_plane >= 0) & (whole_plane < slabs * CZ)
        for block in range(6):
            rows = pl.ds(8 * block, 8)

            def near(b, k):
                if b:
                    return paired[b - 1, plane + 2 + k, rows, :]
                return wide0[plane + 2 + k, rows, :]

            table = {}
            for b in range(3):
                table[0, b] = near(b, 0)
                for a in (1, 2):
                    table[a, b] = near(b, a) + near(b, -a)
            groups = grouped(table)
            total = base[plane, rows, :]
            for c in range(3):
                part = sum(near_weight(c * c + k) * groups[k] for k in SQUARES)
                total = total + (pair_x(part, c) if c else part)
            row = CY * pencil - 8 + 8 * block + iota((8, NX), 0)
            valid = (row >= 0) & (row < upper) & inside_z
            wide_pot[plane, rows, :] = jnp.where(valid, total, 0.0)

    def slope(after1, before1, after2, before2):
        return (8.0 * (after1 - before1) - (after2 - before2)) * (1.0 / 12.0)

    atoms = own_ref.shape[1]
    for plane in range(CZ):
        bounds[plane] = jnp.max(starts_ref[plane : plane + 1, :]).astype(jnp.int32)
    bounds[CZ] = jnp.int32(atoms)
    found[...] = jnp.zeros_like(found)
    size = math.gcd(atoms, 1024)

    @pl.loop(0, CZ)
    def _(plane):
        middle = wide_pot[plane + 2]
        own = middle[8:40]
        pot_ref[plane] = own
        at = [wide_pot[plane + 2 + k, 8:40, :] for k in (1, -1, 2, -2)]
        across = [pltpu.roll(middle, (-k) % 48, 0)[8:40] for k in (1, -1, 2, -2)]
        along = [shift_x(own, k) for k in (1, -1, 2, -2)]
        for direction, four in enumerate((at, across, along)):
            high, low = split_two(slope(*four))
            slopes[2 * direction * CY : (2 * direction + 1) * CY, :] = high
            slopes[(2 * direction + 1) * CY : (2 * direction + 2) * CY, :] = low
        first = bounds[plane]
        last = bounds[plane + 1]

        def block(step, carry):
            begin = pl.multiple_of(step * size, size)
            here = pl.ds(begin, size)
            table = one_hot(sorted_ref[1:2, here].astype(jnp.int32).astype(jnp.int16), NX)
            at_cell = jnp.dot(slopes[...], table, preferred_element_type=jnp.float32)
            index = begin + iota((1, size), 1)
            line = sorted_ref[0:1, here].astype(jnp.int32)
            line = jnp.where((index >= first) & (index < last), line, -1)
            at_row = iota((CY, size), 0) == line
            for direction in range(3):
                high = at_cell[2 * direction * CY : (2 * direction + 1) * CY]
                low = at_cell[(2 * direction + 1) * CY : (2 * direction + 2) * CY]
                found[direction : direction + 1, here] += jnp.sum(
                    jnp.where(at_row, high + low, 0.0), axis=0, keepdims=True
                )
            return carry

        lax.fori_loop(first // size, (last + size - 1) // size, block, 0)

    rows = atoms // 128
    for direction in range(3):
        for row in range(rows):
            there = slice(128 * row, 128 * row + 128)
            by_row[direction * rows + row : direction * rows + row + 1, :] = found[
                direction : direction + 1, there
            ]
    high, low = split_two(by_row[...])
    split = jnp.concatenate([high, low], axis=0)
    width = math.gcd(atoms, CHUNK)

    @pl.loop(0, atoms // width)
    def _(step):
        here = pl.ds(pl.multiple_of(step * width, width), width)
        to = place_ref[0:1, here].astype(jnp.int32)
        table = one_hot((to & 127).astype(jnp.int16), 128)
        values = jnp.dot(split, table, preferred_element_type=jnp.float32)
        at_row = iota((rows, width), 0) == to >> 7
        charges = own_ref[3:4, here]
        for direction in range(3):
            high = values[direction * rows : (direction + 1) * rows]
            low = values[(3 + direction) * rows : (4 + direction) * rows]
            chosen = jnp.sum(jnp.where(at_row, high + low, 0.0), axis=0, keepdims=True)
            force_ref[direction : direction + 1, here] = -charges * chosen


def field_call(slabs, pencils, wide, base, own, order):
    atoms = own.shape[1]
    return pl.pallas_call(
        functools.partial(field_kernel, slabs, pencils),
        out_shape=[
            jax.ShapeDtypeStruct((CZ, CY, NX), jnp.float32),
            jax.ShapeDtypeStruct((3, atoms), jnp.float32),
        ],
        in_specs=[VMEM] * 6,
        out_specs=[VMEM] * 2,
        scratch_shapes=[
            pltpu.VMEM((2, 16, 48, NX), jnp.float32),
            pltpu.VMEM((12, 48, NX), jnp.float32),
            pltpu.VMEM((6 * CY, NX), jnp.bfloat16),
            pltpu.SMEM((CZ + 1,), jnp.int32),
            pltpu.VMEM((3, atoms), jnp.float32),
            pltpu.VMEM((3 * atoms // 128, 128), jnp.float32),
        ],
        cost_estimate=pl.CostEstimate(flops=2 * 10**10, bytes_accessed=2**23, transcendentals=0),
        compiler_params=pltpu.CompilerParams(vmem_limit_bytes=40 * 2**20),
    )(own, *order, wide, base)


def solution(mesh):
    slabs = mesh.shape["slab"]
    pencils = mesh.shape["pencil"]

    def body(atom_cell, charge):
        own = jnp.concatenate([atom_cell.astype(jnp.float32), charge[None]], axis=0)
        wide, base, *order = exchange_call(slabs, pencils, own)
        potential, forces = field_call(slabs, pencils, wide, base, own, order)
        return (potential, forces)

    return jax.shard_map(
        body,
        mesh=mesh,
        in_specs=(P(None, ("slab", "pencil")), P(("slab", "pencil"))),
        out_specs=(P("slab", "pencil", None), P(None, ("slab", "pencil"))),
        check_vma=False,
    )
```

```python
import functools
import math

import jax
import jax.numpy as jnp
from jax import lax
from jax.experimental import pallas as pl
from jax.experimental.pallas import tpu as pltpu
from jax.sharding import PartitionSpec as P

CZ = 8
CY = 32
NX = 512
F = 32
ROWS = CZ * CY
CHUNK = 2048
MESH = pl.DeviceIdType.MESH
VMEM = pl.BlockSpec(memory_space=pltpu.VMEM)
SQUARES = (0, 1, 2, 4, 5, 8)


def iota(shape, dim):
    return lax.broadcasted_iota(jnp.int32, shape, dim)


def iota16(shape, dim):
    return iota(shape, dim).astype(jnp.int16)


def one_hot(places, size):
    here = iota16((size, places.shape[1]), 0) == places
    return jnp.where(here, jnp.ones((), jnp.bfloat16), jnp.zeros((), jnp.bfloat16))


def near_weight(squared):
    return 1.0 / math.sqrt(squared + 0.25) - 1.0 / math.sqrt(squared + 4.0)


def level_weight(level, squared):
    return (1.0 / math.sqrt(squared + 1.0) - 1.0 / math.sqrt(squared + 4.0)) / 2**level


def split_two(values):
    high = values.astype(jnp.bfloat16)
    return high, (values - high.astype(jnp.float32)).astype(jnp.bfloat16)


def dot32(left, right):
    left_high, left_low = split_two(left)
    right_high, right_low = split_two(right)
    total = jnp.dot(left_high, right_high, preferred_element_type=jnp.float32)
    total += jnp.dot(left_high, right_low, preferred_element_type=jnp.float32)
    return total + jnp.dot(left_low, right_high, preferred_element_type=jnp.float32)


def halve_rows(rows_out, rows_in, line_bits):
    out_row = iota((rows_out, rows_in), 0)
    in_row = iota((rows_out, rows_in), 1)
    plane = in_row >> (line_bits + 1)
    line = (in_row & (2**line_bits - 1)) >> 1
    return jnp.where((plane << (line_bits - 1)) + line == out_row, 1.0, 0.0).astype(jnp.bfloat16)


def halve_columns(columns_in, columns_out):
    return jnp.where(
        iota((columns_in, columns_out), 0) >> 1 == iota((columns_in, columns_out), 1), 1.0, 0.0
    ).astype(jnp.bfloat16)


def halve(values, rows_out, line_bits, columns_out):
    rows, columns = values.shape
    left = halve_rows(rows_out, rows, line_bits)
    high, low = split_two(values)
    part = jnp.dot(left, high, preferred_element_type=jnp.float32)
    part += jnp.dot(left, low, preferred_element_type=jnp.float32)
    right = halve_columns(columns, columns_out)
    high, low = split_two(part)
    whole = jnp.dot(high, right, preferred_element_type=jnp.float32)
    return whole + jnp.dot(low, right, preferred_element_type=jnp.float32)


def deposit(atoms_ref, begin, end, total_ref, first_plane, planes, far_plane=None):
    near_rows = planes * CY
    rows = near_rows if far_plane is None else near_rows + CY
    width = math.gcd(end - begin, CHUNK)
    y0 = lax.axis_index("pencil") * CY

    @pl.loop(0, (end - begin) // width)
    def _(step):
        here = pl.ds(pl.multiple_of(begin + step * width, width), width)
        plane = atoms_ref[0:1, here].astype(jnp.int32) - first_plane
        line = atoms_ref[1:2, here].astype(jnp.int32) - y0
        columns = atoms_ref[2:3, here].astype(jnp.int32).astype(jnp.int16)
        high, low = split_two(atoms_ref[3:4, here])
        place = plane * CY + line
        if far_plane is not None:
            far = ((plane + first_plane - far_plane) >> 1) * (CY // 2) + (line >> 1)
            place = jnp.where((plane >= 0) & (plane < planes), place, near_rows + far)
        at_row = iota16((rows, width), 0) == place.astype(jnp.int16)
        none = jnp.zeros((), jnp.bfloat16)
        stacked = jnp.concatenate(
            [jnp.where(at_row, high, none), jnp.where(at_row, low, none)], axis=0
        )
        added = lax.dot_general(
            stacked,
            one_hot(columns, NX),
            (((1,), (1,)), ((), ())),
            preferred_element_type=jnp.float32,
        )
        total_ref[0:rows, :] += added[:rows] + added[rows:]


def shift_x(values, step):
    width = values.shape[-1]
    axis = values.ndim - 1
    column = iota(values.shape, axis)
    moved = pltpu.roll(values, (-step) % width, axis)
    return jnp.where((column + step >= 0) & (column + step < width), moved, 0.0)


def pair_x(values, step):
    return shift_x(values, step) + shift_x(values, -step)


def hat(fine, cell, factor, count):
    bits = factor.bit_length()
    numerator = jnp.clip(2 * fine + 1 - factor, 0, 2 * factor * (count - 1))
    lower = jnp.minimum(numerator >> bits, count - 2)
    fraction = (numerator - (lower << bits)).astype(jnp.float32) * (0.5 / factor)
    return jnp.where(
        cell == lower, 1.0 - fraction, jnp.where(cell == lower + 1, fraction, 0.0)
    )


def shift_y(values, step):
    lines = values.shape[0]
    line = iota(values.shape, 0) + step
    return jnp.where((line >= 0) & (line < lines), pltpu.roll(values, (-step) % lines, 0), 0.0)


def field_of(wide, field, shift, level):
    lines = wide.shape[1]

    @pl.loop(0, field.shape[0] // lines)
    def _(plane):
        table = {}
        for a in range(3):
            line = wide[plane + shift]
            if a:
                line = wide[plane + shift + a] + wide[plane + shift - a]
            table[a, 0] = line
            for b in (1, 2):
                table[a, b] = shift_y(line, b) + shift_y(line, -b)
        groups = grouped(table)
        total = None
        for c in range(3):
            part = sum(level_weight(level, c * c + k) * groups[k] for k in SQUARES)
            total = total + pair_x(part, c) if c else part
        field[pl.ds(pl.multiple_of(plane * lines, lines), lines), :] = total


def grouped(table):
    return {
        0: table[0, 0],
        1: table[0, 1] + table[1, 0],
        2: table[1, 1],
        4: table[0, 2] + table[2, 0],
        5: table[1, 2] + table[2, 1],
        8: table[2, 2],
    }


def upper_fields(slabs, pencils, wide3, field3):
    slab = lax.axis_index("slab")
    pencil_bits = pencils.bit_length() - 1
    rows3 = slabs * pencils * 4
    grid3 = wide3[...].reshape(rows3, 128)
    first_row = 0
    first_lane = 0
    for level in (3, 4, 5):
        down = level - 3
        line_bits = pencil_bits + 2 - down
        lines = 2**line_bits
        planes = slabs >> down
        count = planes * lines
        length = NX >> level
        if level == 3:
            charges = grid3
        else:
            shape = (count, rows3)
            out_row = iota(shape, 0)
            in_row = iota(shape, 1)
            in_plane = in_row >> (2 + pencil_bits)
            in_line = in_row & (4 * pencils - 1)
            cell = ((in_plane >> down) << line_bits) + (in_line >> down)
            charges = dot32(jnp.where(cell == out_row, 1.0, 0.0), grid3)
        reach = 3 if level < 5 else length
        source = iota((128, 128), 0) >> down
        column = iota((128, 128), 1) - first_lane
        valid = (column >= 0) & (column < length)
        pairs = jnp.concatenate(
            [
                jnp.where(valid & (jnp.abs(source - column) == c), 1.0, 0.0)
                for c in range(reach)
            ],
            axis=1,
        )
        moved = dot32(charges, pairs)
        stacked = jnp.concatenate(
            [moved[:, c * 128 : (c + 1) * 128] for c in range(reach)], axis=0
        )
        out_bits = max(line_bits, 3)
        shape = (4 << out_bits, reach * count)
        across = iota(shape, 1) >> (count.bit_length() - 1)
        source = iota(shape, 1) & (count - 1)
        dz = (source >> line_bits) - (iota(shape, 0) >> out_bits) - ((slab >> down) - 1)
        dy = (source & (lines - 1)) - (iota(shape, 0) & (2**out_bits - 1))
        squared = (dz * dz + dy * dy + across * across).astype(jnp.float32)
        weight = 1.0 / jnp.sqrt(squared + 1.0)
        if level < 5:
            weight = (weight - 1.0 / jnp.sqrt(squared + 4.0)) / 2**level
            weight = jnp.where((jnp.abs(dz) <= 2) & (jnp.abs(dy) <= 2), weight, 0.0)
        else:
            weight = weight / F
        field3[first_row : first_row + (4 << out_bits), :] = dot32(weight, stacked)
        first_row = first_row + (4 << out_bits)
        first_lane = first_lane + length


def interpolate_x(along_x):
    lane = 0
    for level in range(1, 6):
        length = NX >> level
        rows = length if level < 5 else NX - lane
        weights = hat(iota((rows, NX), 1), iota((rows, NX), 0), 2**level, length)
        weights = jnp.where(iota((rows, NX), 0) < length, weights, 0.0)
        along_x[lane : lane + rows, :] = weights.astype(jnp.bfloat16)
        lane = lane + rows


def interpolate(slabs, pencils, fields, flats, along_x, lined_high, lined_low, base):
    slab = lax.axis_index("slab")
    pencil = lax.axis_index("pencil")
    upper = pencils * CY
    padded = [max(upper >> level, 8) for level in (3, 4, 5)]
    layers = [
        (1, 4 * slab - 2, 32, 16 * pencil - 8),
        (2, 2 * slab - 1, upper >> 2, 0),
    ]
    layers += [
        (level, (slab >> (level - 3)) - 1, lines, 0)
        for level, lines in zip((3, 4, 5), padded, strict=True)
    ]
    starts = [0, 0, 0, 4 * padded[0], 4 * (padded[0] + padded[1])]
    tops = [0, 0, 0, padded[0], padded[0] + padded[1]]
    field1, field2, field3 = fields
    flat1, flat2, flat3 = flats
    fields = [field1, field2, field3, field3, field3]
    flats = [flat1, flat2, flat3, flat3, flat3]

    for plane in range(12):
        fine_z = CZ * slab - 2 + plane
        for (level, plane0, lines, _), begin, top, field, flat in zip(
            layers, starts, tops, fields, flats, strict=True
        ):
            factor = 2**level
            count = (slabs * CZ) >> level
            numerator = jnp.clip(2 * fine_z + 1 - factor, 0, 2 * factor * (count - 1))
            lower = jnp.minimum(numerator >> (level + 1), count - 2)
            fraction = (numerator - (lower << (level + 1))).astype(jnp.float32) * (0.5 / factor)
            row = begin + (lower - plane0) * lines
            row = pl.multiple_of(row, 8)
            mixed = (1.0 - fraction) * field[pl.ds(row, lines), :]
            mixed += fraction * field[pl.ds(row + lines, lines), :]
            high, low = split_two(mixed)
            width = field.shape[1]
            there = slice(plane * width, (plane + 1) * width)
            flat[top : top + lines, there] = high.astype(jnp.float32)
            flat[flat.shape[0] // 2 + top : flat.shape[0] // 2 + top + lines, there] = low.astype(
                jnp.float32
            )

    def along_y(some):
        blocks = []
        for level, _, lines, line0 in some:
            shape = (48, lines)
            fine_y = CY * pencil - 8 + iota(shape, 0)
            blocks.append(hat(fine_y, line0 + iota(shape, 1), 2**level, upper >> level))
        return jnp.concatenate(blocks + blocks, axis=1).astype(jnp.bfloat16)

    for some, flat, first in ((layers[:1], flat1, 0), (layers[1:2], flat2, 256), (layers[2:], flat3, 384)):
        width = flat.shape[1] // 12
        lined = jnp.dot(
            along_y(some), flat[...].astype(jnp.bfloat16), preferred_element_type=jnp.float32
        )
        high, low = split_two(lined)
        for plane in range(12):
            there = slice(plane * width, (plane + 1) * width)
            rows = slice(48 * plane, 48 * plane + 48)
            lined_high[rows, first : first + width] = high[:, there]
            lined_low[rows, first : first + width] = low[:, there]

    fine = jnp.dot(lined_high[...], along_x[...], preferred_element_type=jnp.float32)
    fine += jnp.dot(lined_low[...], along_x[...], preferred_element_type=jnp.float32)
    base[...] = fine.reshape(12, 48, NX)


def halve_halo(total, near_first):
    out_row = iota((2 * CY, 5 * CY), 0)
    in_row = iota((2 * CY, 5 * CY), 1)
    near = ((in_row >> 6) << 4) + ((in_row & (CY - 1)) >> 1) + near_first
    far = in_row - 4 * CY + (CY - near_first)
    chosen = jnp.where(in_row < 4 * CY, near, far) == out_row
    left = jnp.where(chosen, 1.0, 0.0).astype(jnp.bfloat16)
    high, low = split_two(total)
    part = jnp.dot(left, high, preferred_element_type=jnp.float32)
    part += jnp.dot(left, low, preferred_element_type=jnp.float32)
    right = halve_columns(NX, NX // 2)
    high, low = split_two(part)
    whole = jnp.dot(high, right, preferred_element_type=jnp.float32)
    return whole + jnp.dot(low, right, preferred_element_type=jnp.float32)


def sort_atoms(own, planes, place_ref, sorted_ref, starts_ref, moved):
    atoms = own.shape[1]
    rows = atoms // 128
    for row in range(rows):
        planes[row : row + 1, :] = own[0:1, 128 * row : 128 * row + 128]
    plane = planes[...].astype(jnp.int32) - lax.axis_index("slab") * CZ
    bins = [jnp.where(plane == b, 1.0, 0.0) for b in range(CZ)]
    stacked = jnp.concatenate(bins, axis=0).astype(jnp.bfloat16)
    earlier = iota((128, 128), 0) < iota((128, 128), 1)
    earlier = jnp.where(earlier, 1.0, 0.0).astype(jnp.bfloat16)
    in_row = jnp.dot(stacked, earlier, preferred_element_type=jnp.float32)
    ones = jnp.ones((128, 128), jnp.bfloat16)
    of_row = jnp.dot(stacked, ones, preferred_element_type=jnp.float32).astype(jnp.bfloat16)
    size = (CZ * rows, CZ * rows)
    above = jnp.where(iota(size, 1) < iota(size, 0), 1.0, 0.0).astype(jnp.bfloat16)
    before = jnp.dot(above, of_row, preferred_element_type=jnp.float32)
    both = in_row + before
    place = sum(bins[b] * both[b * rows : (b + 1) * rows] for b in range(CZ))
    for b in range(CZ):
        starts_ref[b : b + 1, :] = before[b * rows : b * rows + 1, :]
    planes[...] = place
    for row in range(rows):
        place_ref[0:1, 128 * row : 128 * row + 128] = planes[row : row + 1, :]

    width = math.gcd(atoms, CHUNK)
    y0 = lax.axis_index("pencil") * CY
    moved[...] = jnp.zeros_like(moved)

    @pl.loop(0, atoms // width)
    def _(step):
        here = pl.ds(pl.multiple_of(step * width, width), width)
        line = own[1:2, here].astype(jnp.int32) - y0
        column = own[2:3, here].astype(jnp.int32)
        to = place_ref[0:1, here].astype(jnp.int32)
        at_row = iota16((rows, width), 0) == (to >> 7).astype(jnp.int16)
        none = jnp.zeros((), jnp.bfloat16)
        fields = [
            jnp.where(at_row, part.astype(jnp.float32).astype(jnp.bfloat16), none)
            for part in (line, column & 255, column >> 8)
        ]
        moved[...] += lax.dot_general(
            jnp.concatenate(fields, axis=0),
            one_hot((to & 127).astype(jnp.int16), 128),
            (((1,), (1,)), ((), ())),
            preferred_element_type=jnp.float32,
        )

    moved[rows : 2 * rows, :] += 256.0 * moved[2 * rows : 3 * rows, :]
    for row in range(rows):
        there = slice(128 * row, 128 * row + 128)
        sorted_ref[0:1, there] = moved[row : row + 1, :]
        sorted_ref[1:2, there] = moved[rows + row : rows + row + 1, :]


def exchange_kernel(
    slabs,
    pencils,
    own,
    wide0,
    base,
    place_ref,
    sorted_ref,
    starts_ref,
    wide1,
    wide2,
    wide3,
    planes,
    moved,
    below,
    above,
    total,
    total_below,
    total_above,
    field1,
    field2,
    field3,
    along_x,
    flat1,
    flat2,
    flat3,
    lined_high,
    lined_low,
    send,
    recv,
    send2,
    recv2,
    send3,
    recv3,
):
    slab = lax.axis_index("slab")
    pencil = lax.axis_index("pencil")
    atoms = own.shape[1]
    for ref in (wide0, wide1, wide2, total, total_below, total_above):
        ref[...] = jnp.zeros_like(ref)

    def along_pencil(step):
        return (slab, lax.rem(pencil + step, pencils))

    def along_slab(step):
        return (lax.rem(slab + step, slabs), pencil)

    barrier = pltpu.get_barrier_semaphore()

    @pl.loop(1, pencils)
    def _(step):
        pl.semaphore_signal(barrier, inc=1, device_id=along_pencil(step), device_id_type=MESH)

    @pl.loop(1, slabs)
    def _(step):
        pl.semaphore_signal(barrier, inc=1, device_id=along_slab(step), device_id_type=MESH)

    sort_atoms(own, planes, place_ref, sorted_ref, starts_ref, moved)
    pl.semaphore_wait(barrier, slabs + pencils - 2)

    def inside(dz, dy):
        z = slab + dz
        y = pencil + dy
        return (z >= 0) & (z < slabs) & (y >= 0) & (y < pencils)

    copies = []

    def add(source, target, dz, dy):
        copies.append((source, target, dz, dy))
        return len(copies) - 1

    parts = [(0, atoms // 2), (atoms // 2, atoms)]
    to_above = [add(own.at[:, a:b], below.at[:, a:b], 1, 0) for a, b in parts]
    to_below = [add(own.at[:, a:b], above.at[:, a:b], -1, 0) for a, b in parts]
    lines0 = {1: (36, 4), -1: (8, 40)}
    middle_y = [
        add(wide0.at[4:12, a : a + 4], wide0.at[4:12, b : b + 4], 0, dy)
        for dy, (a, b) in lines0.items()
    ]
    below_y = [
        add(wide0.at[0:4, a : a + 4], wide0.at[0:4, b : b + 4], 0, dy)
        for dy, (a, b) in lines0.items()
    ]
    above_y = [
        add(wide0.at[12:16, a : a + 4], wide0.at[12:16, b : b + 4], 0, dy)
        for dy, (a, b) in lines0.items()
    ]
    one_y, one_y_above = (
        [
            add(wide1.at[some, a : a + 4], wide1.at[some, b : b + 4], 0, dy)
            for dy, a, b in ((1, 20, 4), (-1, 8, 24))
        ]
        for some in (slice(0, 8), slice(8, 12))
    )
    two_z = [
        add(wide2.at[4:6], wide2.at[4 - 2 * dz : 6 - 2 * dz], dz, 0) for dz in (-2, -1, 1, 2)
    ]

    def copy_of(index, device):
        source, target, _, _ = copies[index]
        return pltpu.make_async_remote_copy(
            src_ref=source,
            dst_ref=target,
            send_sem=send.at[index],
            recv_sem=recv.at[index],
            device_id=device,
            device_id_type=MESH,
        )

    def start(indices, also=True):
        for index in indices:
            _, _, dz, dy = copies[index]

            @pl.when(inside(dz, dy) & also)
            def _(index=index, dz=dz, dy=dy):
                copy_of(index, (slab + dz, pencil + dy)).start()

    def arrived(indices, also=True):
        for index in indices:
            _, _, dz, dy = copies[index]

            @pl.when(inside(-dz, -dy) & also)
            def _(index=index, dz=dz, dy=dy):
                copy_of(index, (slab - dz, pencil - dy)).wait_recv()

    def sent(indices, also=True):
        for index in indices:
            _, _, dz, dy = copies[index]

            @pl.when(inside(dz, dy) & also)
            def _(index=index, dz=dz, dy=dy):
                copy_of(index, (slab + dz, pencil + dy)).wait_send()

    def pencil_copy(step):
        lines = pl.ds(pl.multiple_of(8 * pencil, 8), 8)
        return pltpu.make_async_remote_copy(
            src_ref=wide2.at[4:6, lines],
            dst_ref=wide2.at[4:6, lines],
            send_sem=send2.at[step],
            recv_sem=recv2.at[step],
            device_id=along_pencil(step),
            device_id_type=MESH,
        )

    def pencil_arrival(step):
        lines = pl.ds(pl.multiple_of(8 * lax.rem(pencil + pencils - step, pencils), 8), 8)
        return pltpu.make_async_remote_copy(
            src_ref=wide2.at[4:6, lines],
            dst_ref=wide2.at[4:6, lines],
            send_sem=send2.at[step],
            recv_sem=recv2.at[step],
            device_id=along_pencil(step),
            device_id_type=MESH,
        )

    def top_copy(step, slot):
        return pltpu.make_async_remote_copy(
            src_ref=wide3.at[slot],
            dst_ref=wide3.at[slot],
            send_sem=send3.at[step],
            recv_sem=recv3.at[step],
            device_id=along_slab(step),
            device_id_type=MESH,
        )

    for part in zip(to_above, to_below, strict=True):
        start(part)
    deposit(own, 0, atoms, total, CZ * slab, CZ)
    grid = total[...]
    wide0[4:12, 8:40, :] = grid.reshape(CZ, CY, NX)
    start(middle_y)
    one = halve(grid, ROWS // 4, 5, NX // 2)
    wide1[4:8, 8:24, :] = one.reshape(CZ // 2, CY // 2, NX // 2)
    two = halve(one, ROWS // 16, 4, NX // 4)
    wide2[4:6, pl.ds(pl.multiple_of(8 * pencil, 8), 8), :] = two.reshape(
        CZ // 4, CY // 4, NX // 4
    )
    for step in range(1, pencils):
        pencil_copy(step).start()

    has_below = slab > 0
    has_above = slab < slabs - 1

    def from_below(part):
        begin, end = parts[part]
        arrived([to_above[part]])

        @pl.when(has_below)
        def _():
            deposit(below, begin, end, total_below, CZ * slab - 4, 4, CZ * slab - 8)

    def from_above(part):
        begin, end = parts[part]
        arrived([to_below[part]])

        @pl.when(has_above)
        def _():
            deposit(above, begin, end, total_above, CZ * slab + CZ, 4, CZ * slab + CZ + 4)

    from_below(0)
    from_above(0)
    for step in range(1, pencils):
        pencil_arrival(step).wait_recv()
    start(two_z)
    lines2 = 8 * pencils
    three = halve(
        wide2[4:6].reshape(2 * lines2, NX // 4), lines2 // 2, lines2.bit_length() - 1, NX // 4
    )
    wide3[pl.ds(slab, 1)] = three[None]

    @pl.loop(1, slabs)
    def _(step):
        top_copy(step, slab).start()

    from_below(1)

    @pl.when(has_below)
    def _():
        halo = total_below[...]
        wide0[0:4, 8:40, :] = halo[0 : 4 * CY].reshape(4, CY, NX)
        wide1[0:4, 8:24, :] = halve_halo(halo, CY).reshape(4, CY // 2, NX // 2)

    start(below_y, has_below)
    start(one_y)
    from_above(1)

    @pl.when(has_above)
    def _():
        halo = total_above[...]
        wide0[12:16, 8:40, :] = halo[0 : 4 * CY].reshape(4, CY, NX)
        wide1[8:12, 8:24, :] = halve_halo(halo, 0).reshape(4, CY // 2, NX // 2)

    start(above_y, has_above)
    start(one_y_above, has_above)
    interpolate_x(along_x)
    arrived(two_z)
    field_of(wide2, field2, 3, 2)

    @pl.loop(1, slabs)
    def _(step):
        copy = top_copy(step, lax.rem(slab + slabs - step, slabs))
        copy.wait_send()
        copy.wait_recv()

    upper_fields(slabs, pencils, wide3, field3)
    arrived(one_y)
    arrived(one_y_above, has_above)
    field_of(wide1, field1, 2, 1)
    interpolate(
        slabs,
        pencils,
        (field1, field2, field3),
        (flat1, flat2, flat3),
        along_x,
        lined_high,
        lined_low,
        base,
    )
    for step in range(1, pencils):
        pencil_copy(step).wait_send()
    sent([*to_above, *to_below, *middle_y, *two_z, *one_y])
    sent(one_y_above, has_above)
    arrived(middle_y)
    arrived(below_y, has_below)
    sent(below_y, has_below)
    arrived(above_y, has_above)
    sent(above_y, has_above)


def exchange_call(slabs, pencils, own):
    atoms = own.shape[1]
    shapes = (
        (16, 48, NX),
        (12, 48, NX),
        (1, atoms),
        (2, atoms),
        (CZ, 128),
    )
    field3_rows = sum(4 * max((pencils * CY) >> level, 8) for level in (3, 4, 5))
    return pl.pallas_call(
        functools.partial(exchange_kernel, slabs, pencils),
        out_shape=[jax.ShapeDtypeStruct(shape, jnp.float32) for shape in shapes],
        in_specs=[VMEM],
        out_specs=[VMEM] * 5,
        scratch_shapes=[
            pltpu.VMEM((12, 32, NX // 2), jnp.float32),
            pltpu.VMEM((10, 8 * pencils, NX // 4), jnp.float32),
            pltpu.VMEM((slabs, 4 * pencils, 128), jnp.float32),
            pltpu.VMEM((atoms // 128, 128), jnp.float32),
            pltpu.VMEM((3 * atoms // 128, 128), jnp.float32),
            pltpu.VMEM((4, atoms), jnp.float32),
            pltpu.VMEM((4, atoms), jnp.float32),
            pltpu.VMEM((ROWS, NX), jnp.float32),
            pltpu.VMEM((5 * CY, NX), jnp.float32),
            pltpu.VMEM((5 * CY, NX), jnp.float32),
            pltpu.VMEM((8 * 32, NX // 2), jnp.float32),
            pltpu.VMEM((4 * 8 * pencils, NX // 4), jnp.float32),
            pltpu.VMEM((field3_rows, 128), jnp.float32),
            pltpu.VMEM((NX, NX), jnp.bfloat16),
            pltpu.VMEM((2 * 32, 12 * 256), jnp.float32),
            pltpu.VMEM((2 * 8 * pencils, 12 * 128), jnp.float32),
            pltpu.VMEM((2 * field3_rows // 4, 12 * 128), jnp.float32),
            pltpu.VMEM((12 * 48, NX), jnp.bfloat16),
            pltpu.VMEM((12 * 48, NX), jnp.bfloat16),
            pltpu.SemaphoreType.DMA((18,)),
            pltpu.SemaphoreType.DMA((18,)),
            pltpu.SemaphoreType.DMA((pencils,)),
            pltpu.SemaphoreType.DMA((pencils,)),
            pltpu.SemaphoreType.DMA((slabs,)),
            pltpu.SemaphoreType.DMA((slabs,)),
        ],
        cost_estimate=pl.CostEstimate(flops=10**10, bytes_accessed=2**23, transcendentals=0),
        compiler_params=pltpu.CompilerParams(
            collective_id=0, has_side_effects=True, vmem_limit_bytes=40 * 2**20
        ),
    )(own)


def field_kernel(
    slabs,
    pencils,
    own_ref,
    place_ref,
    sorted_ref,
    starts_ref,
    wide0,
    base,
    pot_ref,
    force_ref,
    paired,
    wide_pot,
    slopes,
    bounds,
    found,
    by_row,
):
    slab = lax.axis_index("slab")
    pencil = lax.axis_index("pencil")
    upper = pencils * CY

    @pl.loop(0, 16)
    def _(plane):
        values = wide0[plane]
        for b in (1, 2):
            paired[b - 1, plane] = pltpu.roll(values, b, 0) + pltpu.roll(values, 48 - b, 0)

    @pl.loop(0, 12)
    def _(plane):
        whole_plane = CZ * slab - 2 + plane
        inside_z = (whole_plane >= 0) & (whole_plane < slabs * CZ)
        for block in range(6):
            rows = pl.ds(8 * block, 8)

            def near(b, k):
                if b:
                    return paired[b - 1, plane + 2 + k, rows, :]
                return wide0[plane + 2 + k, rows, :]

            table = {}
            for b in range(3):
                table[0, b] = near(b, 0)
                for a in (1, 2):
                    table[a, b] = near(b, a) + near(b, -a)
            groups = grouped(table)
            total = base[plane, rows, :]
            for c in range(3):
                part = sum(near_weight(c * c + k) * groups[k] for k in SQUARES)
                total = total + (pair_x(part, c) if c else part)
            row = CY * pencil - 8 + 8 * block + iota((8, NX), 0)
            valid = (row >= 0) & (row < upper) & inside_z
            wide_pot[plane, rows, :] = jnp.where(valid, total, 0.0)

    def slope(after1, before1, after2, before2):
        return (8.0 * (after1 - before1) - (after2 - before2)) * (1.0 / 12.0)

    atoms = own_ref.shape[1]
    for plane in range(CZ):
        bounds[plane] = jnp.max(starts_ref[plane : plane + 1, :]).astype(jnp.int32)
    bounds[CZ] = jnp.int32(atoms)
    found[...] = jnp.zeros_like(found)
    size = math.gcd(atoms, 1024)

    @pl.loop(0, CZ)
    def _(plane):
        middle = wide_pot[plane + 2]
        own = middle[8:40]
        pot_ref[plane] = own
        at = [wide_pot[plane + 2 + k, 8:40, :] for k in (1, -1, 2, -2)]
        across = [pltpu.roll(middle, (-k) % 48, 0)[8:40] for k in (1, -1, 2, -2)]
        along = [shift_x(own, k) for k in (1, -1, 2, -2)]
        for direction, four in enumerate((at, across, along)):
            high, low = split_two(slope(*four))
            slopes[2 * direction * CY : (2 * direction + 1) * CY, :] = high
            slopes[(2 * direction + 1) * CY : (2 * direction + 2) * CY, :] = low
        first = bounds[plane]
        last = bounds[plane + 1]

        def block(step, carry):
            begin = pl.multiple_of(step * size, size)
            here = pl.ds(begin, size)
            table = one_hot(sorted_ref[1:2, here].astype(jnp.int32).astype(jnp.int16), NX)
            at_cell = jnp.dot(slopes[...], table, preferred_element_type=jnp.float32)
            index = begin + iota((1, size), 1)
            line = sorted_ref[0:1, here].astype(jnp.int32)
            line = jnp.where((index >= first) & (index < last), line, -1)
            at_row = iota((CY, size), 0) == line
            for direction in range(3):
                high = at_cell[2 * direction * CY : (2 * direction + 1) * CY]
                low = at_cell[(2 * direction + 1) * CY : (2 * direction + 2) * CY]
                found[direction : direction + 1, here] += jnp.sum(
                    jnp.where(at_row, high + low, 0.0), axis=0, keepdims=True
                )
            return carry

        lax.fori_loop(first // size, (last + size - 1) // size, block, 0)

    rows = atoms // 128
    for direction in range(3):
        for row in range(rows):
            there = slice(128 * row, 128 * row + 128)
            by_row[direction * rows + row : direction * rows + row + 1, :] = found[
                direction : direction + 1, there
            ]
    high, low = split_two(by_row[...])
    split = jnp.concatenate([high, low], axis=0)
    width = math.gcd(atoms, CHUNK)

    @pl.loop(0, atoms // width)
    def _(step):
        here = pl.ds(pl.multiple_of(step * width, width), width)
        to = place_ref[0:1, here].astype(jnp.int32)
        table = one_hot((to & 127).astype(jnp.int16), 128)
        values = jnp.dot(split, table, preferred_element_type=jnp.float32)
        at_row = iota((rows, width), 0) == to >> 7
        charges = own_ref[3:4, here]
        for direction in range(3):
            high = values[direction * rows : (direction + 1) * rows]
            low = values[(3 + direction) * rows : (4 + direction) * rows]
            chosen = jnp.sum(jnp.where(at_row, high + low, 0.0), axis=0, keepdims=True)
            force_ref[direction : direction + 1, here] = -charges * chosen


def field_call(slabs, pencils, wide, base, own, order):
    atoms = own.shape[1]
    return pl.pallas_call(
        functools.partial(field_kernel, slabs, pencils),
        out_shape=[
            jax.ShapeDtypeStruct((CZ, CY, NX), jnp.float32),
            jax.ShapeDtypeStruct((3, atoms), jnp.float32),
        ],
        in_specs=[VMEM] * 6,
        out_specs=[VMEM] * 2,
        scratch_shapes=[
            pltpu.VMEM((2, 16, 48, NX), jnp.float32),
            pltpu.VMEM((12, 48, NX), jnp.float32),
            pltpu.VMEM((6 * CY, NX), jnp.bfloat16),
            pltpu.SMEM((CZ + 1,), jnp.int32),
            pltpu.VMEM((3, atoms), jnp.float32),
            pltpu.VMEM((3 * atoms // 128, 128), jnp.float32),
        ],
        cost_estimate=pl.CostEstimate(flops=2 * 10**10, bytes_accessed=2**23, transcendentals=0),
        compiler_params=pltpu.CompilerParams(vmem_limit_bytes=40 * 2**20),
    )(own, *order, wide, base)


def solution(mesh):
    slabs = mesh.shape["slab"]
    pencils = mesh.shape["pencil"]

    def body(atom_cell, charge):
        own = jnp.concatenate([atom_cell.astype(jnp.float32), charge[None]], axis=0)
        wide, base, *order = exchange_call(slabs, pencils, own)
        potential, forces = field_call(slabs, pencils, wide, base, own, order)
        return (potential, forces)

    return jax.shard_map(
        body,
        mesh=mesh,
        in_specs=(P(None, ("slab", "pencil")), P(("slab", "pencil"))),
        out_specs=(P("slab", "pencil", None), P(None, ("slab", "pencil"))),
        check_vma=False,
    )
```

```python
import functools
import math

import jax
import jax.numpy as jnp
from jax import lax
from jax.experimental import pallas as pl
from jax.experimental.pallas import tpu as pltpu
from jax.sharding import PartitionSpec as P

CZ = 8
CY = 32
NX = 512
F = 32
ROWS = CZ * CY
CHUNK = 2048
MESH = pl.DeviceIdType.MESH
VMEM = pl.BlockSpec(memory_space=pltpu.VMEM)
SQUARES = (0, 1, 2, 4, 5, 8)


def iota(shape, dim):
    return lax.broadcasted_iota(jnp.int32, shape, dim)


def iota16(shape, dim):
    return iota(shape, dim).astype(jnp.int16)


def one_hot(places, size):
    here = iota16((size, places.shape[1]), 0) == places
    return jnp.where(here, jnp.ones((), jnp.bfloat16), jnp.zeros((), jnp.bfloat16))


def near_weight(squared):
    return 1.0 / math.sqrt(squared + 0.25) - 1.0 / math.sqrt(squared + 4.0)


def level_weight(level, squared):
    return (1.0 / math.sqrt(squared + 1.0) - 1.0 / math.sqrt(squared + 4.0)) / 2**level


def split_two(values):
    high = values.astype(jnp.bfloat16)
    return high, (values - high.astype(jnp.float32)).astype(jnp.bfloat16)


def dot32(left, right):
    left_high, left_low = split_two(left)
    right_high, right_low = split_two(right)
    total = jnp.dot(left_high, right_high, preferred_element_type=jnp.float32)
    total += jnp.dot(left_high, right_low, preferred_element_type=jnp.float32)
    return total + jnp.dot(left_low, right_high, preferred_element_type=jnp.float32)


def halve_rows(rows_out, rows_in, line_bits):
    out_row = iota((rows_out, rows_in), 0)
    in_row = iota((rows_out, rows_in), 1)
    plane = in_row >> (line_bits + 1)
    line = (in_row & (2**line_bits - 1)) >> 1
    return jnp.where((plane << (line_bits - 1)) + line == out_row, 1.0, 0.0).astype(jnp.bfloat16)


def halve_columns(columns_in, columns_out):
    return jnp.where(
        iota((columns_in, columns_out), 0) >> 1 == iota((columns_in, columns_out), 1), 1.0, 0.0
    ).astype(jnp.bfloat16)


def halve(values, rows_out, line_bits, columns_out):
    rows, columns = values.shape
    left = halve_rows(rows_out, rows, line_bits)
    high, low = split_two(values)
    part = jnp.dot(left, high, preferred_element_type=jnp.float32)
    part += jnp.dot(left, low, preferred_element_type=jnp.float32)
    right = halve_columns(columns, columns_out)
    high, low = split_two(part)
    whole = jnp.dot(high, right, preferred_element_type=jnp.float32)
    return whole + jnp.dot(low, right, preferred_element_type=jnp.float32)


def deposit(atoms_ref, begin, end, total_ref, first_plane, planes, far_plane=None):
    near_rows = planes * CY
    rows = near_rows if far_plane is None else near_rows + CY
    width = math.gcd(end - begin, CHUNK)
    y0 = lax.axis_index("pencil") * CY

    @pl.loop(0, (end - begin) // width)
    def _(step):
        here = pl.ds(pl.multiple_of(begin + step * width, width), width)
        plane = atoms_ref[0:1, here].astype(jnp.int32) - first_plane
        line = atoms_ref[1:2, here].astype(jnp.int32) - y0
        columns = atoms_ref[2:3, here].astype(jnp.int32).astype(jnp.int16)
        high, low = split_two(atoms_ref[3:4, here])
        place = plane * CY + line
        if far_plane is not None:
            far = ((plane + first_plane - far_plane) >> 1) * (CY // 2) + (line >> 1)
            place = jnp.where((plane >= 0) & (plane < planes), place, near_rows + far)
        at_row = iota16((rows, width), 0) == place.astype(jnp.int16)
        none = jnp.zeros((), jnp.bfloat16)
        stacked = jnp.concatenate(
            [jnp.where(at_row, high, none), jnp.where(at_row, low, none)], axis=0
        )
        added = lax.dot_general(
            stacked,
            one_hot(columns, NX),
            (((1,), (1,)), ((), ())),
            preferred_element_type=jnp.float32,
        )
        total_ref[0:rows, :] += added[:rows] + added[rows:]


def shift_x(values, step):
    width = values.shape[-1]
    axis = values.ndim - 1
    column = iota(values.shape, axis)
    moved = pltpu.roll(values, (-step) % width, axis)
    return jnp.where((column + step >= 0) & (column + step < width), moved, 0.0)


def pair_x(values, step):
    return shift_x(values, step) + shift_x(values, -step)


def hat(fine, cell, factor, count):
    bits = factor.bit_length()
    numerator = jnp.clip(2 * fine + 1 - factor, 0, 2 * factor * (count - 1))
    lower = jnp.minimum(numerator >> bits, count - 2)
    fraction = (numerator - (lower << bits)).astype(jnp.float32) * (0.5 / factor)
    return jnp.where(
        cell == lower, 1.0 - fraction, jnp.where(cell == lower + 1, fraction, 0.0)
    )


def shift_y(values, step):
    lines = values.shape[0]
    line = iota(values.shape, 0) + step
    return jnp.where((line >= 0) & (line < lines), pltpu.roll(values, (-step) % lines, 0), 0.0)


def field_of(wide, field, shift, level):
    lines = wide.shape[1]

    @pl.loop(0, field.shape[0] // lines)
    def _(plane):
        table = {}
        for a in range(3):
            line = wide[plane + shift]
            if a:
                line = wide[plane + shift + a] + wide[plane + shift - a]
            table[a, 0] = line
            for b in (1, 2):
                table[a, b] = shift_y(line, b) + shift_y(line, -b)
        groups = grouped(table)
        total = None
        for c in range(3):
            part = sum(level_weight(level, c * c + k) * groups[k] for k in SQUARES)
            total = total + pair_x(part, c) if c else part
        field[pl.ds(pl.multiple_of(plane * lines, lines), lines), :] = total


def grouped(table):
    return {
        0: table[0, 0],
        1: table[0, 1] + table[1, 0],
        2: table[1, 1],
        4: table[0, 2] + table[2, 0],
        5: table[1, 2] + table[2, 1],
        8: table[2, 2],
    }


def upper_fields(slabs, pencils, wide3, field3):
    slab = lax.axis_index("slab")
    pencil_bits = pencils.bit_length() - 1
    rows3 = slabs * pencils * 4
    grid3 = wide3[...].reshape(rows3, 128)
    first_row = 0
    first_lane = 0
    for level in (3, 4, 5):
        down = level - 3
        line_bits = pencil_bits + 2 - down
        lines = 2**line_bits
        planes = slabs >> down
        count = planes * lines
        length = NX >> level
        if level == 3:
            charges = grid3
        else:
            shape = (count, rows3)
            out_row = iota(shape, 0)
            in_row = iota(shape, 1)
            in_plane = in_row >> (2 + pencil_bits)
            in_line = in_row & (4 * pencils - 1)
            cell = ((in_plane >> down) << line_bits) + (in_line >> down)
            charges = dot32(jnp.where(cell == out_row, 1.0, 0.0), grid3)
        reach = 3 if level < 5 else length
        source = iota((128, 128), 0) >> down
        column = iota((128, 128), 1) - first_lane
        valid = (column >= 0) & (column < length)
        pairs = jnp.concatenate(
            [
                jnp.where(valid & (jnp.abs(source - column) == c), 1.0, 0.0)
                for c in range(reach)
            ],
            axis=1,
        )
        moved = dot32(charges, pairs)
        stacked = jnp.concatenate(
            [moved[:, c * 128 : (c + 1) * 128] for c in range(reach)], axis=0
        )
        out_bits = max(line_bits, 3)
        shape = (4 << out_bits, reach * count)
        across = iota(shape, 1) >> (count.bit_length() - 1)
        source = iota(shape, 1) & (count - 1)
        dz = (source >> line_bits) - (iota(shape, 0) >> out_bits) - ((slab >> down) - 1)
        dy = (source & (lines - 1)) - (iota(shape, 0) & (2**out_bits - 1))
        squared = (dz * dz + dy * dy + across * across).astype(jnp.float32)
        weight = 1.0 / jnp.sqrt(squared + 1.0)
        if level < 5:
            weight = (weight - 1.0 / jnp.sqrt(squared + 4.0)) / 2**level
            weight = jnp.where((jnp.abs(dz) <= 2) & (jnp.abs(dy) <= 2), weight, 0.0)
        else:
            weight = weight / F
        field3[first_row : first_row + (4 << out_bits), :] = dot32(weight, stacked)
        first_row = first_row + (4 << out_bits)
        first_lane = first_lane + length


def interpolate_x(along_x):
    lane = 0
    for level in range(1, 6):
        length = NX >> level
        rows = length if level < 5 else NX - lane
        weights = hat(iota((rows, NX), 1), iota((rows, NX), 0), 2**level, length)
        weights = jnp.where(iota((rows, NX), 0) < length, weights, 0.0)
        along_x[lane : lane + rows, :] = weights.astype(jnp.bfloat16)
        lane = lane + rows


def interpolate(slabs, pencils, fields, flats, along_x, lined_high, lined_low, base):
    slab = lax.axis_index("slab")
    pencil = lax.axis_index("pencil")
    upper = pencils * CY
    padded = [max(upper >> level, 8) for level in (3, 4, 5)]
    layers = [
        (1, 4 * slab - 2, 32, 16 * pencil - 8),
        (2, 2 * slab - 1, upper >> 2, 0),
    ]
    layers += [
        (level, (slab >> (level - 3)) - 1, lines, 0)
        for level, lines in zip((3, 4, 5), padded, strict=True)
    ]
    starts = [0, 0, 0, 4 * padded[0], 4 * (padded[0] + padded[1])]
    tops = [0, 0, 0, padded[0], padded[0] + padded[1]]
    field1, field2, field3 = fields
    flat1, flat2, flat3 = flats
    fields = [field1, field2, field3, field3, field3]
    flats = [flat1, flat2, flat3, flat3, flat3]

    for plane in range(12):
        fine_z = CZ * slab - 2 + plane
        for (level, plane0, lines, _), begin, top, field, flat in zip(
            layers, starts, tops, fields, flats, strict=True
        ):
            factor = 2**level
            count = (slabs * CZ) >> level
            numerator = jnp.clip(2 * fine_z + 1 - factor, 0, 2 * factor * (count - 1))
            lower = jnp.minimum(numerator >> (level + 1), count - 2)
            fraction = (numerator - (lower << (level + 1))).astype(jnp.float32) * (0.5 / factor)
            row = begin + (lower - plane0) * lines
            row = pl.multiple_of(row, 8)
            mixed = (1.0 - fraction) * field[pl.ds(row, lines), :]
            mixed += fraction * field[pl.ds(row + lines, lines), :]
            high, low = split_two(mixed)
            width = field.shape[1]
            there = slice(plane * width, (plane + 1) * width)
            flat[top : top + lines, there] = high.astype(jnp.float32)
            flat[flat.shape[0] // 2 + top : flat.shape[0] // 2 + top + lines, there] = low.astype(
                jnp.float32
            )

    def along_y(some):
        blocks = []
        for level, _, lines, line0 in some:
            shape = (48, lines)
            fine_y = CY * pencil - 8 + iota(shape, 0)
            blocks.append(hat(fine_y, line0 + iota(shape, 1), 2**level, upper >> level))
        return jnp.concatenate(blocks + blocks, axis=1).astype(jnp.bfloat16)

    for some, flat, first in ((layers[:1], flat1, 0), (layers[1:2], flat2, 256), (layers[2:], flat3, 384)):
        width = flat.shape[1] // 12
        lined = jnp.dot(
            along_y(some), flat[...].astype(jnp.bfloat16), preferred_element_type=jnp.float32
        )
        high, low = split_two(lined)
        for plane in range(12):
            there = slice(plane * width, (plane + 1) * width)
            rows = slice(48 * plane, 48 * plane + 48)
            lined_high[rows, first : first + width] = high[:, there]
            lined_low[rows, first : first + width] = low[:, there]

    fine = jnp.dot(lined_high[...], along_x[...], preferred_element_type=jnp.float32)
    fine += jnp.dot(lined_low[...], along_x[...], preferred_element_type=jnp.float32)
    fine = fine.reshape(12, 48, NX)
    base[0:8] += fine[0:8]
    base[8:12] = fine[8:12]


def halve_halo(total, near_first):
    out_row = iota((2 * CY, 5 * CY), 0)
    in_row = iota((2 * CY, 5 * CY), 1)
    near = ((in_row >> 6) << 4) + ((in_row & (CY - 1)) >> 1) + near_first
    far = in_row - 4 * CY + (CY - near_first)
    chosen = jnp.where(in_row < 4 * CY, near, far) == out_row
    left = jnp.where(chosen, 1.0, 0.0).astype(jnp.bfloat16)
    high, low = split_two(total)
    part = jnp.dot(left, high, preferred_element_type=jnp.float32)
    part += jnp.dot(left, low, preferred_element_type=jnp.float32)
    right = halve_columns(NX, NX // 2)
    high, low = split_two(part)
    whole = jnp.dot(high, right, preferred_element_type=jnp.float32)
    return whole + jnp.dot(low, right, preferred_element_type=jnp.float32)


def sort_atoms(own, planes, place_ref, sorted_ref, starts_ref, moved):
    atoms = own.shape[1]
    rows = atoms // 128
    for row in range(rows):
        planes[row : row + 1, :] = own[0:1, 128 * row : 128 * row + 128]
    plane = planes[...].astype(jnp.int32) - lax.axis_index("slab") * CZ
    bins = [jnp.where(plane == b, 1.0, 0.0) for b in range(CZ)]
    stacked = jnp.concatenate(bins, axis=0).astype(jnp.bfloat16)
    earlier = iota((128, 128), 0) < iota((128, 128), 1)
    earlier = jnp.where(earlier, 1.0, 0.0).astype(jnp.bfloat16)
    in_row = jnp.dot(stacked, earlier, preferred_element_type=jnp.float32)
    ones = jnp.ones((128, 128), jnp.bfloat16)
    of_row = jnp.dot(stacked, ones, preferred_element_type=jnp.float32).astype(jnp.bfloat16)
    size = (CZ * rows, CZ * rows)
    above = jnp.where(iota(size, 1) < iota(size, 0), 1.0, 0.0).astype(jnp.bfloat16)
    before = jnp.dot(above, of_row, preferred_element_type=jnp.float32)
    both = in_row + before
    place = sum(bins[b] * both[b * rows : (b + 1) * rows] for b in range(CZ))
    for b in range(CZ):
        starts_ref[b : b + 1, :] = before[b * rows : b * rows + 1, :]
    planes[...] = place
    for row in range(rows):
        place_ref[0:1, 128 * row : 128 * row + 128] = planes[row : row + 1, :]

    width = math.gcd(atoms, CHUNK)
    y0 = lax.axis_index("pencil") * CY
    moved[...] = jnp.zeros_like(moved)

    @pl.loop(0, atoms // width)
    def _(step):
        here = pl.ds(pl.multiple_of(step * width, width), width)
        line = own[1:2, here].astype(jnp.int32) - y0
        column = own[2:3, here].astype(jnp.int32)
        to = place_ref[0:1, here].astype(jnp.int32)
        at_row = iota16((rows, width), 0) == (to >> 7).astype(jnp.int16)
        none = jnp.zeros((), jnp.bfloat16)
        fields = [
            jnp.where(at_row, part.astype(jnp.float32).astype(jnp.bfloat16), none)
            for part in (line, column & 255, column >> 8)
        ]
        moved[...] += lax.dot_general(
            jnp.concatenate(fields, axis=0),
            one_hot((to & 127).astype(jnp.int16), 128),
            (((1,), (1,)), ((), ())),
            preferred_element_type=jnp.float32,
        )

    moved[rows : 2 * rows, :] += 256.0 * moved[2 * rows : 3 * rows, :]
    for row in range(rows):
        there = slice(128 * row, 128 * row + 128)
        sorted_ref[0:1, there] = moved[row : row + 1, :]
        sorted_ref[1:2, there] = moved[rows + row : rows + row + 1, :]


def pair_lines(wide0, paired, first, last):
    @pl.loop(first, last)
    def _(plane):
        values = wide0[plane]
        for b in (1, 2):
            paired[b - 1, plane] = pltpu.roll(values, b, 0) + pltpu.roll(values, 48 - b, 0)


def near_field(wide0, paired, base, first, last, before):
    @pl.loop(first, last)
    def _(plane):
        for block in range(6):
            rows = pl.ds(8 * block, 8)

            def near(b, k):
                if b:
                    return paired[b - 1, plane + 2 + k, rows, :]
                return wide0[plane + 2 + k, rows, :]

            table = {}
            for b in range(3):
                table[0, b] = near(b, 0)
                for a in (1, 2):
                    table[a, b] = near(b, a) + near(b, -a)
            groups = grouped(table)
            total = base[plane, rows, :] if before else None
            for c in range(3):
                part = sum(near_weight(c * c + k) * groups[k] for k in SQUARES)
                part = pair_x(part, c) if c else part
                total = part if total is None else total + part
            base[plane, rows, :] = total


def clear_outside(slabs, pencils, base):
    slab = lax.axis_index("slab")
    pencil = lax.axis_index("pencil")

    @pl.loop(0, 12)
    def _(plane):
        whole_plane = CZ * slab - 2 + plane
        inside_z = (whole_plane >= 0) & (whole_plane < slabs * CZ)
        row = CY * pencil - 8 + iota((48, NX), 0)
        valid = (row >= 0) & (row < pencils * CY) & inside_z
        base[plane] = jnp.where(valid, base[plane], 0.0)


def exchange_kernel(
    slabs,
    pencils,
    own,
    base,
    place_ref,
    sorted_ref,
    starts_ref,
    wide0,
    paired,
    wide1,
    wide2,
    wide3,
    planes,
    moved,
    below,
    above,
    total,
    total_below,
    total_above,
    field1,
    field2,
    field3,
    along_x,
    flat1,
    flat2,
    flat3,
    lined_high,
    lined_low,
    send,
    recv,
    send2,
    recv2,
    send3,
    recv3,
):
    slab = lax.axis_index("slab")
    pencil = lax.axis_index("pencil")
    atoms = own.shape[1]
    for ref in (wide0, wide1, wide2, total, total_below, total_above):
        ref[...] = jnp.zeros_like(ref)

    def along_pencil(step):
        return (slab, lax.rem(pencil + step, pencils))

    def along_slab(step):
        return (lax.rem(slab + step, slabs), pencil)

    barrier = pltpu.get_barrier_semaphore()

    @pl.loop(1, pencils)
    def _(step):
        pl.semaphore_signal(barrier, inc=1, device_id=along_pencil(step), device_id_type=MESH)

    @pl.loop(1, slabs)
    def _(step):
        pl.semaphore_signal(barrier, inc=1, device_id=along_slab(step), device_id_type=MESH)

    sort_atoms(own, planes, place_ref, sorted_ref, starts_ref, moved)
    pl.semaphore_wait(barrier, slabs + pencils - 2)

    def inside(dz, dy):
        z = slab + dz
        y = pencil + dy
        return (z >= 0) & (z < slabs) & (y >= 0) & (y < pencils)

    copies = []

    def add(source, target, dz, dy):
        copies.append((source, target, dz, dy))
        return len(copies) - 1

    parts = [(0, atoms // 2), (atoms // 2, atoms)]
    to_above = [add(own.at[:, a:b], below.at[:, a:b], 1, 0) for a, b in parts]
    to_below = [add(own.at[:, a:b], above.at[:, a:b], -1, 0) for a, b in parts]
    lines0 = {1: (36, 4), -1: (8, 40)}
    middle_y = [
        add(wide0.at[4:12, a : a + 4], wide0.at[4:12, b : b + 4], 0, dy)
        for dy, (a, b) in lines0.items()
    ]
    below_y = [
        add(wide0.at[0:4, a : a + 4], wide0.at[0:4, b : b + 4], 0, dy)
        for dy, (a, b) in lines0.items()
    ]
    above_y = [
        add(wide0.at[12:16, a : a + 4], wide0.at[12:16, b : b + 4], 0, dy)
        for dy, (a, b) in lines0.items()
    ]
    one_y, one_y_above = (
        [
            add(wide1.at[some, a : a + 4], wide1.at[some, b : b + 4], 0, dy)
            for dy, a, b in ((1, 20, 4), (-1, 8, 24))
        ]
        for some in (slice(0, 8), slice(8, 12))
    )
    two_z = [
        add(wide2.at[4:6], wide2.at[4 - 2 * dz : 6 - 2 * dz], dz, 0) for dz in (-2, -1, 1, 2)
    ]

    def copy_of(index, device):
        source, target, _, _ = copies[index]
        return pltpu.make_async_remote_copy(
            src_ref=source,
            dst_ref=target,
            send_sem=send.at[index],
            recv_sem=recv.at[index],
            device_id=device,
            device_id_type=MESH,
        )

    def start(indices, also=True):
        for index in indices:
            _, _, dz, dy = copies[index]

            @pl.when(inside(dz, dy) & also)
            def _(index=index, dz=dz, dy=dy):
                copy_of(index, (slab + dz, pencil + dy)).start()

    def arrived(indices, also=True):
        for index in indices:
            _, _, dz, dy = copies[index]

            @pl.when(inside(-dz, -dy) & also)
            def _(index=index, dz=dz, dy=dy):
                copy_of(index, (slab - dz, pencil - dy)).wait_recv()

    def sent(indices, also=True):
        for index in indices:
            _, _, dz, dy = copies[index]

            @pl.when(inside(dz, dy) & also)
            def _(index=index, dz=dz, dy=dy):
                copy_of(index, (slab + dz, pencil + dy)).wait_send()

    def pencil_copy(step):
        lines = pl.ds(pl.multiple_of(8 * pencil, 8), 8)
        return pltpu.make_async_remote_copy(
            src_ref=wide2.at[4:6, lines],
            dst_ref=wide2.at[4:6, lines],
            send_sem=send2.at[step],
            recv_sem=recv2.at[step],
            device_id=along_pencil(step),
            device_id_type=MESH,
        )

    def pencil_arrival(step):
        lines = pl.ds(pl.multiple_of(8 * lax.rem(pencil + pencils - step, pencils), 8), 8)
        return pltpu.make_async_remote_copy(
            src_ref=wide2.at[4:6, lines],
            dst_ref=wide2.at[4:6, lines],
            send_sem=send2.at[step],
            recv_sem=recv2.at[step],
            device_id=along_pencil(step),
            device_id_type=MESH,
        )

    def top_copy(step, slot):
        return pltpu.make_async_remote_copy(
            src_ref=wide3.at[slot],
            dst_ref=wide3.at[slot],
            send_sem=send3.at[step],
            recv_sem=recv3.at[step],
            device_id=along_slab(step),
            device_id_type=MESH,
        )

    for part in zip(to_above, to_below, strict=True):
        start(part)
    deposit(own, 0, atoms, total, CZ * slab, CZ)
    grid = total[...]
    wide0[4:12, 8:40, :] = grid.reshape(CZ, CY, NX)
    start(middle_y)
    one = halve(grid, ROWS // 4, 5, NX // 2)
    wide1[4:8, 8:24, :] = one.reshape(CZ // 2, CY // 2, NX // 2)
    two = halve(one, ROWS // 16, 4, NX // 4)
    wide2[4:6, pl.ds(pl.multiple_of(8 * pencil, 8), 8), :] = two.reshape(
        CZ // 4, CY // 4, NX // 4
    )
    for step in range(1, pencils):
        pencil_copy(step).start()

    has_below = slab > 0
    has_above = slab < slabs - 1

    def from_below(part):
        begin, end = parts[part]
        arrived([to_above[part]])

        @pl.when(has_below)
        def _():
            deposit(below, begin, end, total_below, CZ * slab - 4, 4, CZ * slab - 8)

    def from_above(part):
        begin, end = parts[part]
        arrived([to_below[part]])

        @pl.when(has_above)
        def _():
            deposit(above, begin, end, total_above, CZ * slab + CZ, 4, CZ * slab + CZ + 4)

    from_below(0)
    from_above(0)
    for step in range(1, pencils):
        pencil_arrival(step).wait_recv()
    start(two_z)
    lines2 = 8 * pencils
    three = halve(
        wide2[4:6].reshape(2 * lines2, NX // 4), lines2 // 2, lines2.bit_length() - 1, NX // 4
    )
    wide3[pl.ds(slab, 1)] = three[None]

    @pl.loop(1, slabs)
    def _(step):
        top_copy(step, slab).start()

    from_below(1)

    @pl.when(has_below)
    def _():
        halo = total_below[...]
        wide0[0:4, 8:40, :] = halo[0 : 4 * CY].reshape(4, CY, NX)
        wide1[0:4, 8:24, :] = halve_halo(halo, CY).reshape(4, CY // 2, NX // 2)

    start(below_y, has_below)
    start(one_y)
    from_above(1)

    @pl.when(has_above)
    def _():
        halo = total_above[...]
        wide0[12:16, 8:40, :] = halo[0 : 4 * CY].reshape(4, CY, NX)
        wide1[8:12, 8:24, :] = halve_halo(halo, 0).reshape(4, CY // 2, NX // 2)

    start(above_y, has_above)
    start(one_y_above, has_above)
    interpolate_x(along_x)
    arrived(middle_y)
    arrived(below_y, has_below)
    pair_lines(wide0, paired, 0, 12)
    near_field(wide0, paired, base, 0, 8, before=False)
    arrived(two_z)
    field_of(wide2, field2, 3, 2)

    @pl.loop(1, slabs)
    def _(step):
        copy = top_copy(step, lax.rem(slab + slabs - step, slabs))
        copy.wait_send()
        copy.wait_recv()

    upper_fields(slabs, pencils, wide3, field3)
    arrived(one_y)
    arrived(one_y_above, has_above)
    field_of(wide1, field1, 2, 1)
    interpolate(
        slabs,
        pencils,
        (field1, field2, field3),
        (flat1, flat2, flat3),
        along_x,
        lined_high,
        lined_low,
        base,
    )
    for step in range(1, pencils):
        pencil_copy(step).wait_send()
    sent([*to_above, *to_below, *middle_y, *two_z, *one_y])
    sent(one_y_above, has_above)
    arrived(above_y, has_above)
    pair_lines(wide0, paired, 12, 16)
    near_field(wide0, paired, base, 8, 12, before=True)
    clear_outside(slabs, pencils, base)
    sent(below_y, has_below)
    sent(above_y, has_above)


def exchange_call(slabs, pencils, own):
    atoms = own.shape[1]
    shapes = (
        (12, 48, NX),
        (1, atoms),
        (2, atoms),
        (CZ, 128),
    )
    field3_rows = sum(4 * max((pencils * CY) >> level, 8) for level in (3, 4, 5))
    return pl.pallas_call(
        functools.partial(exchange_kernel, slabs, pencils),
        out_shape=[jax.ShapeDtypeStruct(shape, jnp.float32) for shape in shapes],
        in_specs=[VMEM],
        out_specs=[VMEM] * 4,
        scratch_shapes=[
            pltpu.VMEM((16, 48, NX), jnp.float32),
            pltpu.VMEM((2, 16, 48, NX), jnp.float32),
            pltpu.VMEM((12, 32, NX // 2), jnp.float32),
            pltpu.VMEM((10, 8 * pencils, NX // 4), jnp.float32),
            pltpu.VMEM((slabs, 4 * pencils, 128), jnp.float32),
            pltpu.VMEM((atoms // 128, 128), jnp.float32),
            pltpu.VMEM((3 * atoms // 128, 128), jnp.float32),
            pltpu.VMEM((4, atoms), jnp.float32),
            pltpu.VMEM((4, atoms), jnp.float32),
            pltpu.VMEM((ROWS, NX), jnp.float32),
            pltpu.VMEM((5 * CY, NX), jnp.float32),
            pltpu.VMEM((5 * CY, NX), jnp.float32),
            pltpu.VMEM((8 * 32, NX // 2), jnp.float32),
            pltpu.VMEM((4 * 8 * pencils, NX // 4), jnp.float32),
            pltpu.VMEM((field3_rows, 128), jnp.float32),
            pltpu.VMEM((NX, NX), jnp.bfloat16),
            pltpu.VMEM((2 * 32, 12 * 256), jnp.float32),
            pltpu.VMEM((2 * 8 * pencils, 12 * 128), jnp.float32),
            pltpu.VMEM((2 * field3_rows // 4, 12 * 128), jnp.float32),
            pltpu.VMEM((12 * 48, NX), jnp.bfloat16),
            pltpu.VMEM((12 * 48, NX), jnp.bfloat16),
            pltpu.SemaphoreType.DMA((18,)),
            pltpu.SemaphoreType.DMA((18,)),
            pltpu.SemaphoreType.DMA((pencils,)),
            pltpu.SemaphoreType.DMA((pencils,)),
            pltpu.SemaphoreType.DMA((slabs,)),
            pltpu.SemaphoreType.DMA((slabs,)),
        ],
        cost_estimate=pl.CostEstimate(flops=10**10, bytes_accessed=2**23, transcendentals=0),
        compiler_params=pltpu.CompilerParams(
            collective_id=0, has_side_effects=True, vmem_limit_bytes=40 * 2**20
        ),
    )(own)


def field_kernel(
    own_ref,
    place_ref,
    sorted_ref,
    starts_ref,
    wide_pot,
    pot_ref,
    force_ref,
    slopes,
    bounds,
    found,
    by_row,
):
    def slope(after1, before1, after2, before2):
        return (8.0 * (after1 - before1) - (after2 - before2)) * (1.0 / 12.0)

    atoms = own_ref.shape[1]
    for plane in range(CZ):
        bounds[plane] = jnp.max(starts_ref[plane : plane + 1, :]).astype(jnp.int32)
    bounds[CZ] = jnp.int32(atoms)
    found[...] = jnp.zeros_like(found)
    size = math.gcd(atoms, 1024)

    @pl.loop(0, CZ)
    def _(plane):
        middle = wide_pot[plane + 2]
        own = middle[8:40]
        pot_ref[plane] = own
        at = [wide_pot[plane + 2 + k, 8:40, :] for k in (1, -1, 2, -2)]
        across = [pltpu.roll(middle, (-k) % 48, 0)[8:40] for k in (1, -1, 2, -2)]
        along = [shift_x(own, k) for k in (1, -1, 2, -2)]
        for direction, four in enumerate((at, across, along)):
            high, low = split_two(slope(*four))
            slopes[2 * direction * CY : (2 * direction + 1) * CY, :] = high
            slopes[(2 * direction + 1) * CY : (2 * direction + 2) * CY, :] = low
        first = bounds[plane]
        last = bounds[plane + 1]

        def block(step, carry):
            begin = pl.multiple_of(step * size, size)
            here = pl.ds(begin, size)
            table = one_hot(sorted_ref[1:2, here].astype(jnp.int32).astype(jnp.int16), NX)
            at_cell = jnp.dot(slopes[...], table, preferred_element_type=jnp.float32)
            index = begin + iota((1, size), 1)
            line = sorted_ref[0:1, here].astype(jnp.int32)
            line = jnp.where((index >= first) & (index < last), line, -1)
            at_row = iota((CY, size), 0) == line
            for direction in range(3):
                high = at_cell[2 * direction * CY : (2 * direction + 1) * CY]
                low = at_cell[(2 * direction + 1) * CY : (2 * direction + 2) * CY]
                found[direction : direction + 1, here] += jnp.sum(
                    jnp.where(at_row, high + low, 0.0), axis=0, keepdims=True
                )
            return carry

        lax.fori_loop(first // size, (last + size - 1) // size, block, 0)

    rows = atoms // 128
    for direction in range(3):
        for row in range(rows):
            there = slice(128 * row, 128 * row + 128)
            by_row[direction * rows + row : direction * rows + row + 1, :] = found[
                direction : direction + 1, there
            ]
    high, low = split_two(by_row[...])
    split = jnp.concatenate([high, low], axis=0)
    width = math.gcd(atoms, CHUNK)

    @pl.loop(0, atoms // width)
    def _(step):
        here = pl.ds(pl.multiple_of(step * width, width), width)
        to = place_ref[0:1, here].astype(jnp.int32)
        table = one_hot((to & 127).astype(jnp.int16), 128)
        values = jnp.dot(split, table, preferred_element_type=jnp.float32)
        at_row = iota((rows, width), 0) == to >> 7
        charges = own_ref[3:4, here]
        for direction in range(3):
            high = values[direction * rows : (direction + 1) * rows]
            low = values[(3 + direction) * rows : (4 + direction) * rows]
            chosen = jnp.sum(jnp.where(at_row, high + low, 0.0), axis=0, keepdims=True)
            force_ref[direction : direction + 1, here] = -charges * chosen


def field_call(base, own, order):
    atoms = own.shape[1]
    return pl.pallas_call(
        field_kernel,
        out_shape=[
            jax.ShapeDtypeStruct((CZ, CY, NX), jnp.float32),
            jax.ShapeDtypeStruct((3, atoms), jnp.float32),
        ],
        in_specs=[VMEM] * 5,
        out_specs=[VMEM] * 2,
        scratch_shapes=[
            pltpu.VMEM((6 * CY, NX), jnp.bfloat16),
            pltpu.SMEM((CZ + 1,), jnp.int32),
            pltpu.VMEM((3, atoms), jnp.float32),
            pltpu.VMEM((3 * atoms // 128, 128), jnp.float32),
        ],
        cost_estimate=pl.CostEstimate(flops=2 * 10**10, bytes_accessed=2**23, transcendentals=0),
        compiler_params=pltpu.CompilerParams(vmem_limit_bytes=40 * 2**20),
    )(own, *order, base)


def solution(mesh):
    slabs = mesh.shape["slab"]
    pencils = mesh.shape["pencil"]

    def body(atom_cell, charge):
        own = jnp.concatenate([atom_cell.astype(jnp.float32), charge[None]], axis=0)
        base, *order = exchange_call(slabs, pencils, own)
        potential, forces = field_call(base, own, order)
        return (potential, forces)

    return jax.shard_map(
        body,
        mesh=mesh,
        in_specs=(P(None, ("slab", "pencil")), P(("slab", "pencil"))),
        out_specs=(P("slab", "pencil", None), P(None, ("slab", "pencil"))),
        check_vma=False,
    )
```

```python
import functools
import math

import jax
import jax.numpy as jnp
from jax import lax
from jax.experimental import pallas as pl
from jax.experimental.pallas import tpu as pltpu
from jax.sharding import PartitionSpec as P

CZ = 8
CY = 32
NX = 512
F = 32
ROWS = CZ * CY
CHUNK = 2048
MESH = pl.DeviceIdType.MESH
VMEM = pl.BlockSpec(memory_space=pltpu.VMEM)
SQUARES = (0, 1, 2, 4, 5, 8)


def iota(shape, dim):
    return lax.broadcasted_iota(jnp.int32, shape, dim)


def iota16(shape, dim):
    return iota(shape, dim).astype(jnp.int16)


def one_hot(places, size):
    here = iota16((size, places.shape[1]), 0) == places
    return jnp.where(here, jnp.ones((), jnp.bfloat16), jnp.zeros((), jnp.bfloat16))


def near_weight(squared):
    return 1.0 / math.sqrt(squared + 0.25) - 1.0 / math.sqrt(squared + 4.0)


def level_weight(level, squared):
    return (1.0 / math.sqrt(squared + 1.0) - 1.0 / math.sqrt(squared + 4.0)) / 2**level


def split_two(values):
    high = values.astype(jnp.bfloat16)
    return high, (values - high.astype(jnp.float32)).astype(jnp.bfloat16)


def dot32(left, right):
    left_high, left_low = split_two(left)
    right_high, right_low = split_two(right)
    total = jnp.dot(left_high, right_high, preferred_element_type=jnp.float32)
    total += jnp.dot(left_high, right_low, preferred_element_type=jnp.float32)
    return total + jnp.dot(left_low, right_high, preferred_element_type=jnp.float32)


def halve_rows(rows_out, rows_in, line_bits):
    out_row = iota((rows_out, rows_in), 0)
    in_row = iota((rows_out, rows_in), 1)
    plane = in_row >> (line_bits + 1)
    line = (in_row & (2**line_bits - 1)) >> 1
    return jnp.where((plane << (line_bits - 1)) + line == out_row, 1.0, 0.0).astype(jnp.bfloat16)


def halve_columns(columns_in, columns_out):
    return jnp.where(
        iota((columns_in, columns_out), 0) >> 1 == iota((columns_in, columns_out), 1), 1.0, 0.0
    ).astype(jnp.bfloat16)


def halve(values, rows_out, line_bits, columns_out):
    rows, columns = values.shape
    left = halve_rows(rows_out, rows, line_bits)
    high, low = split_two(values)
    part = jnp.dot(left, high, preferred_element_type=jnp.float32)
    part += jnp.dot(left, low, preferred_element_type=jnp.float32)
    right = halve_columns(columns, columns_out)
    high, low = split_two(part)
    whole = jnp.dot(high, right, preferred_element_type=jnp.float32)
    return whole + jnp.dot(low, right, preferred_element_type=jnp.float32)


def deposit(atoms_ref, begin, end, total_ref, first_plane, planes, far_plane=None):
    near_rows = planes * CY
    rows = near_rows if far_plane is None else near_rows + CY
    width = math.gcd(end - begin, 2 * CHUNK)
    y0 = lax.axis_index("pencil") * CY

    @pl.loop(0, (end - begin) // width)
    def _(step):
        here = pl.ds(pl.multiple_of(begin + step * width, width), width)
        plane = atoms_ref[0:1, here].astype(jnp.int32) - first_plane
        line = atoms_ref[1:2, here].astype(jnp.int32) - y0
        columns = atoms_ref[2:3, here].astype(jnp.int32).astype(jnp.int16)
        high, low = split_two(atoms_ref[3:4, here])
        place = plane * CY + line
        if far_plane is not None:
            far = ((plane + first_plane - far_plane) >> 1) * (CY // 2) + (line >> 1)
            place = jnp.where((plane >= 0) & (plane < planes), place, near_rows + far)
        at_row = iota16((rows, width), 0) == place.astype(jnp.int16)
        none = jnp.zeros((), jnp.bfloat16)
        stacked = jnp.concatenate(
            [jnp.where(at_row, high, none), jnp.where(at_row, low, none)], axis=0
        )
        added = lax.dot_general(
            stacked,
            one_hot(columns, NX),
            (((1,), (1,)), ((), ())),
            preferred_element_type=jnp.float32,
        )
        total_ref[0:rows, :] += added[:rows] + added[rows:]


def shift_x(values, step):
    width = values.shape[-1]
    axis = values.ndim - 1
    column = iota(values.shape, axis)
    moved = pltpu.roll(values, (-step) % width, axis)
    return jnp.where((column + step >= 0) & (column + step < width), moved, 0.0)


def pair_x(values, step):
    return shift_x(values, step) + shift_x(values, -step)


def hat(fine, cell, factor, count):
    bits = factor.bit_length()
    numerator = jnp.clip(2 * fine + 1 - factor, 0, 2 * factor * (count - 1))
    lower = jnp.minimum(numerator >> bits, count - 2)
    fraction = (numerator - (lower << bits)).astype(jnp.float32) * (0.5 / factor)
    return jnp.where(
        cell == lower, 1.0 - fraction, jnp.where(cell == lower + 1, fraction, 0.0)
    )


def shift_y(values, step):
    lines = values.shape[0]
    line = iota(values.shape, 0) + step
    return jnp.where((line >= 0) & (line < lines), pltpu.roll(values, (-step) % lines, 0), 0.0)


def field_of(wide, field, shift, level):
    lines = wide.shape[1]

    @pl.loop(0, field.shape[0] // lines)
    def _(plane):
        table = {}
        for a in range(3):
            line = wide[plane + shift]
            if a:
                line = wide[plane + shift + a] + wide[plane + shift - a]
            table[a, 0] = line
            for b in (1, 2):
                table[a, b] = shift_y(line, b) + shift_y(line, -b)
        groups = grouped(table)
        total = None
        for c in range(3):
            part = sum(level_weight(level, c * c + k) * groups[k] for k in SQUARES)
            total = total + pair_x(part, c) if c else part
        field[pl.ds(pl.multiple_of(plane * lines, lines), lines), :] = total


def grouped(table):
    return {
        0: table[0, 0],
        1: table[0, 1] + table[1, 0],
        2: table[1, 1],
        4: table[0, 2] + table[2, 0],
        5: table[1, 2] + table[2, 1],
        8: table[2, 2],
    }


def upper_fields(slabs, pencils, wide3, field3):
    slab = lax.axis_index("slab")
    pencil_bits = pencils.bit_length() - 1
    rows3 = slabs * pencils * 4
    grid3 = wide3[...].reshape(rows3, 128)
    first_row = 0
    first_lane = 0
    for level in (3, 4, 5):
        down = level - 3
        line_bits = pencil_bits + 2 - down
        lines = 2**line_bits
        planes = slabs >> down
        count = planes * lines
        length = NX >> level
        if level == 3:
            charges = grid3
        else:
            shape = (count, rows3)
            out_row = iota(shape, 0)
            in_row = iota(shape, 1)
            in_plane = in_row >> (2 + pencil_bits)
            in_line = in_row & (4 * pencils - 1)
            cell = ((in_plane >> down) << line_bits) + (in_line >> down)
            charges = dot32(jnp.where(cell == out_row, 1.0, 0.0), grid3)
        reach = 3 if level < 5 else length
        source = iota((128, 128), 0) >> down
        column = iota((128, 128), 1) - first_lane
        valid = (column >= 0) & (column < length)
        pairs = jnp.concatenate(
            [
                jnp.where(valid & (jnp.abs(source - column) == c), 1.0, 0.0)
                for c in range(reach)
            ],
            axis=1,
        )
        moved = dot32(charges, pairs)
        stacked = jnp.concatenate(
            [moved[:, c * 128 : (c + 1) * 128] for c in range(reach)], axis=0
        )
        out_bits = max(line_bits, 3)
        shape = (4 << out_bits, reach * count)
        across = iota(shape, 1) >> (count.bit_length() - 1)
        source = iota(shape, 1) & (count - 1)
        dz = (source >> line_bits) - (iota(shape, 0) >> out_bits) - ((slab >> down) - 1)
        dy = (source & (lines - 1)) - (iota(shape, 0) & (2**out_bits - 1))
        squared = (dz * dz + dy * dy + across * across).astype(jnp.float32)
        weight = 1.0 / jnp.sqrt(squared + 1.0)
        if level < 5:
            weight = (weight - 1.0 / jnp.sqrt(squared + 4.0)) / 2**level
            weight = jnp.where((jnp.abs(dz) <= 2) & (jnp.abs(dy) <= 2), weight, 0.0)
        else:
            weight = weight / F
        field3[first_row : first_row + (4 << out_bits), :] = dot32(weight, stacked)
        first_row = first_row + (4 << out_bits)
        first_lane = first_lane + length


def interpolate_x(along_x):
    lane = 0
    for level in range(1, 6):
        length = NX >> level
        rows = length if level < 5 else NX - lane
        weights = hat(iota((rows, NX), 1), iota((rows, NX), 0), 2**level, length)
        weights = jnp.where(iota((rows, NX), 0) < length, weights, 0.0)
        along_x[lane : lane + rows, :] = weights.astype(jnp.bfloat16)
        lane = lane + rows


def interpolate(slabs, pencils, fields, flats, along_x, lined_high, lined_low, base):
    slab = lax.axis_index("slab")
    pencil = lax.axis_index("pencil")
    upper = pencils * CY
    padded = [max(upper >> level, 8) for level in (3, 4, 5)]
    layers = [
        (1, 4 * slab - 2, 32, 16 * pencil - 8),
        (2, 2 * slab - 1, upper >> 2, 0),
    ]
    layers += [
        (level, (slab >> (level - 3)) - 1, lines, 0)
        for level, lines in zip((3, 4, 5), padded, strict=True)
    ]
    starts = [0, 0, 0, 4 * padded[0], 4 * (padded[0] + padded[1])]
    tops = [0, 0, 0, padded[0], padded[0] + padded[1]]
    field1, field2, field3 = fields
    flat1, flat2, flat3 = flats
    fields = [field1, field2, field3, field3, field3]
    flats = [flat1, flat2, flat3, flat3, flat3]

    for plane in range(12):
        fine_z = CZ * slab - 2 + plane
        for (level, plane0, lines, _), begin, top, field, flat in zip(
            layers, starts, tops, fields, flats, strict=True
        ):
            factor = 2**level
            count = (slabs * CZ) >> level
            numerator = jnp.clip(2 * fine_z + 1 - factor, 0, 2 * factor * (count - 1))
            lower = jnp.minimum(numerator >> (level + 1), count - 2)
            fraction = (numerator - (lower << (level + 1))).astype(jnp.float32) * (0.5 / factor)
            row = begin + (lower - plane0) * lines
            row = pl.multiple_of(row, 8)
            mixed = (1.0 - fraction) * field[pl.ds(row, lines), :]
            mixed += fraction * field[pl.ds(row + lines, lines), :]
            high, low = split_two(mixed)
            width = field.shape[1]
            there = slice(plane * width, (plane + 1) * width)
            flat[top : top + lines, there] = high.astype(jnp.float32)
            flat[flat.shape[0] // 2 + top : flat.shape[0] // 2 + top + lines, there] = low.astype(
                jnp.float32
            )

    def along_y(some):
        blocks = []
        for level, _, lines, line0 in some:
            shape = (48, lines)
            fine_y = CY * pencil - 8 + iota(shape, 0)
            blocks.append(hat(fine_y, line0 + iota(shape, 1), 2**level, upper >> level))
        return jnp.concatenate(blocks + blocks, axis=1).astype(jnp.bfloat16)

    for some, flat, first in ((layers[:1], flat1, 0), (layers[1:2], flat2, 256), (layers[2:], flat3, 384)):
        width = flat.shape[1] // 12
        lined = jnp.dot(
            along_y(some), flat[...].astype(jnp.bfloat16), preferred_element_type=jnp.float32
        )
        high, low = split_two(lined)
        for plane in range(12):
            there = slice(plane * width, (plane + 1) * width)
            rows = slice(48 * plane, 48 * plane + 48)
            lined_high[rows, first : first + width] = high[:, there]
            lined_low[rows, first : first + width] = low[:, there]

    fine = jnp.dot(lined_high[...], along_x[...], preferred_element_type=jnp.float32)
    fine += jnp.dot(lined_low[...], along_x[...], preferred_element_type=jnp.float32)
    fine = fine.reshape(12, 48, NX)
    base[0:8] += fine[0:8]
    base[8:12] = fine[8:12]


def halve_halo(total, near_first):
    out_row = iota((2 * CY, 5 * CY), 0)
    in_row = iota((2 * CY, 5 * CY), 1)
    near = ((in_row >> 6) << 4) + ((in_row & (CY - 1)) >> 1) + near_first
    far = in_row - 4 * CY + (CY - near_first)
    chosen = jnp.where(in_row < 4 * CY, near, far) == out_row
    left = jnp.where(chosen, 1.0, 0.0).astype(jnp.bfloat16)
    high, low = split_two(total)
    part = jnp.dot(left, high, preferred_element_type=jnp.float32)
    part += jnp.dot(left, low, preferred_element_type=jnp.float32)
    right = halve_columns(NX, NX // 2)
    high, low = split_two(part)
    whole = jnp.dot(high, right, preferred_element_type=jnp.float32)
    return whole + jnp.dot(low, right, preferred_element_type=jnp.float32)


def sort_atoms(own, planes, place_ref, sorted_ref, starts_ref, moved):
    atoms = own.shape[1]
    rows = atoms // 128
    for row in range(rows):
        planes[row : row + 1, :] = own[0:1, 128 * row : 128 * row + 128]
    plane = planes[...].astype(jnp.int32) - lax.axis_index("slab") * CZ
    bins = [jnp.where(plane == b, 1.0, 0.0) for b in range(CZ)]
    stacked = jnp.concatenate(bins, axis=0).astype(jnp.bfloat16)
    earlier = iota((128, 128), 0) < iota((128, 128), 1)
    earlier = jnp.where(earlier, 1.0, 0.0).astype(jnp.bfloat16)
    in_row = jnp.dot(stacked, earlier, preferred_element_type=jnp.float32)
    ones = jnp.ones((128, 128), jnp.bfloat16)
    of_row = jnp.dot(stacked, ones, preferred_element_type=jnp.float32).astype(jnp.bfloat16)
    size = (CZ * rows, CZ * rows)
    above = jnp.where(iota(size, 1) < iota(size, 0), 1.0, 0.0).astype(jnp.bfloat16)
    before = jnp.dot(above, of_row, preferred_element_type=jnp.float32)
    both = in_row + before
    place = sum(bins[b] * both[b * rows : (b + 1) * rows] for b in range(CZ))
    for b in range(CZ):
        starts_ref[b : b + 1, :] = before[b * rows : b * rows + 1, :]
    planes[...] = place
    for row in range(rows):
        place_ref[0:1, 128 * row : 128 * row + 128] = planes[row : row + 1, :]

    width = math.gcd(atoms, CHUNK)
    y0 = lax.axis_index("pencil") * CY
    moved[...] = jnp.zeros_like(moved)

    @pl.loop(0, atoms // width)
    def _(step):
        here = pl.ds(pl.multiple_of(step * width, width), width)
        line = own[1:2, here].astype(jnp.int32) - y0
        column = own[2:3, here].astype(jnp.int32)
        to = place_ref[0:1, here].astype(jnp.int32)
        at_row = iota16((rows, width), 0) == (to >> 7).astype(jnp.int16)
        none = jnp.zeros((), jnp.bfloat16)
        fields = [
            jnp.where(at_row, part.astype(jnp.float32).astype(jnp.bfloat16), none)
            for part in (line, column & 255, column >> 8)
        ]
        moved[...] += lax.dot_general(
            jnp.concatenate(fields, axis=0),
            one_hot((to & 127).astype(jnp.int16), 128),
            (((1,), (1,)), ((), ())),
            preferred_element_type=jnp.float32,
        )

    moved[rows : 2 * rows, :] += 256.0 * moved[2 * rows : 3 * rows, :]
    for row in range(rows):
        there = slice(128 * row, 128 * row + 128)
        sorted_ref[0:1, there] = moved[row : row + 1, :]
        sorted_ref[1:2, there] = moved[rows + row : rows + row + 1, :]


def pair_lines(wide0, paired, first, last):
    @pl.loop(first, last)
    def _(plane):
        values = wide0[plane]
        for b in (1, 2):
            paired[b - 1, plane] = pltpu.roll(values, b, 0) + pltpu.roll(values, 48 - b, 0)


def near_field(wide0, paired, base, first, last, before):
    @pl.loop(first, last)
    def _(plane):
        for block in range(6):
            rows = pl.ds(8 * block, 8)

            def near(b, k):
                if b:
                    return paired[b - 1, plane + 2 + k, rows, :]
                return wide0[plane + 2 + k, rows, :]

            table = {}
            for b in range(3):
                table[0, b] = near(b, 0)
                for a in (1, 2):
                    table[a, b] = near(b, a) + near(b, -a)
            groups = grouped(table)
            total = base[plane, rows, :] if before else None
            for c in range(3):
                part = sum(near_weight(c * c + k) * groups[k] for k in SQUARES)
                part = pair_x(part, c) if c else part
                total = part if total is None else total + part
            base[plane, rows, :] = total


def clear_outside(slabs, pencils, base):
    slab = lax.axis_index("slab")
    pencil = lax.axis_index("pencil")

    flat = jnp.zeros((2, 48, NX), jnp.float32)
    edge = jnp.zeros((12, 8, NX), jnp.float32)

    @pl.when(slab == 0)
    def _():
        base[0:2] = flat

    @pl.when(slab == slabs - 1)
    def _():
        base[10:12] = flat

    @pl.when(pencil == 0)
    def _():
        base[:, 0:8, :] = edge

    @pl.when(pencil == pencils - 1)
    def _():
        base[:, 40:48, :] = edge


def exchange_kernel(
    slabs,
    pencils,
    own,
    base,
    place_ref,
    sorted_ref,
    starts_ref,
    wide0,
    paired,
    wide1,
    wide2,
    wide3,
    planes,
    moved,
    below,
    above,
    total,
    total_below,
    total_above,
    field1,
    field2,
    field3,
    along_x,
    flat1,
    flat2,
    flat3,
    lined_high,
    lined_low,
    send,
    recv,
    send2,
    recv2,
    send3,
    recv3,
):
    slab = lax.axis_index("slab")
    pencil = lax.axis_index("pencil")
    atoms = own.shape[1]
    for ref in (wide0, wide1, wide2, total, total_below, total_above):
        ref[...] = jnp.zeros_like(ref)

    def along_pencil(step):
        return (slab, lax.rem(pencil + step, pencils))

    def along_slab(step):
        return (lax.rem(slab + step, slabs), pencil)

    barrier = pltpu.get_barrier_semaphore()

    @pl.loop(1, pencils)
    def _(step):
        pl.semaphore_signal(barrier, inc=1, device_id=along_pencil(step), device_id_type=MESH)

    @pl.loop(1, slabs)
    def _(step):
        pl.semaphore_signal(barrier, inc=1, device_id=along_slab(step), device_id_type=MESH)

    sort_atoms(own, planes, place_ref, sorted_ref, starts_ref, moved)
    pl.semaphore_wait(barrier, slabs + pencils - 2)

    def inside(dz, dy):
        z = slab + dz
        y = pencil + dy
        return (z >= 0) & (z < slabs) & (y >= 0) & (y < pencils)

    copies = []

    def add(source, target, dz, dy):
        copies.append((source, target, dz, dy))
        return len(copies) - 1

    parts = [(0, atoms // 2), (atoms // 2, atoms)]
    to_above = [add(own.at[:, a:b], below.at[:, a:b], 1, 0) for a, b in parts]
    to_below = [add(own.at[:, a:b], above.at[:, a:b], -1, 0) for a, b in parts]
    lines0 = {1: (36, 4), -1: (8, 40)}
    middle_y = [
        add(wide0.at[4:12, a : a + 4], wide0.at[4:12, b : b + 4], 0, dy)
        for dy, (a, b) in lines0.items()
    ]
    below_y = [
        add(wide0.at[0:4, a : a + 4], wide0.at[0:4, b : b + 4], 0, dy)
        for dy, (a, b) in lines0.items()
    ]
    above_y = [
        add(wide0.at[12:16, a : a + 4], wide0.at[12:16, b : b + 4], 0, dy)
        for dy, (a, b) in lines0.items()
    ]
    one_y, one_y_above = (
        [
            add(wide1.at[some, a : a + 4], wide1.at[some, b : b + 4], 0, dy)
            for dy, a, b in ((1, 20, 4), (-1, 8, 24))
        ]
        for some in (slice(0, 8), slice(8, 12))
    )
    two_z = [
        add(wide2.at[4:6], wide2.at[4 - 2 * dz : 6 - 2 * dz], dz, 0) for dz in (-2, -1, 1, 2)
    ]

    def copy_of(index, device):
        source, target, _, _ = copies[index]
        return pltpu.make_async_remote_copy(
            src_ref=source,
            dst_ref=target,
            send_sem=send.at[index],
            recv_sem=recv.at[index],
            device_id=device,
            device_id_type=MESH,
        )

    def start(indices, also=True):
        for index in indices:
            _, _, dz, dy = copies[index]

            @pl.when(inside(dz, dy) & also)
            def _(index=index, dz=dz, dy=dy):
                copy_of(index, (slab + dz, pencil + dy)).start()

    def arrived(indices, also=True):
        for index in indices:
            _, _, dz, dy = copies[index]

            @pl.when(inside(-dz, -dy) & also)
            def _(index=index, dz=dz, dy=dy):
                copy_of(index, (slab - dz, pencil - dy)).wait_recv()

    def sent(indices, also=True):
        for index in indices:
            _, _, dz, dy = copies[index]

            @pl.when(inside(dz, dy) & also)
            def _(index=index, dz=dz, dy=dy):
                copy_of(index, (slab + dz, pencil + dy)).wait_send()

    def pencil_copy(step):
        lines = pl.ds(pl.multiple_of(8 * pencil, 8), 8)
        return pltpu.make_async_remote_copy(
            src_ref=wide2.at[4:6, lines],
            dst_ref=wide2.at[4:6, lines],
            send_sem=send2.at[step],
            recv_sem=recv2.at[step],
            device_id=along_pencil(step),
            device_id_type=MESH,
        )

    def pencil_arrival(step):
        lines = pl.ds(pl.multiple_of(8 * lax.rem(pencil + pencils - step, pencils), 8), 8)
        return pltpu.make_async_remote_copy(
            src_ref=wide2.at[4:6, lines],
            dst_ref=wide2.at[4:6, lines],
            send_sem=send2.at[step],
            recv_sem=recv2.at[step],
            device_id=along_pencil(step),
            device_id_type=MESH,
        )

    def top_copy(step, slot):
        return pltpu.make_async_remote_copy(
            src_ref=wide3.at[slot],
            dst_ref=wide3.at[slot],
            send_sem=send3.at[step],
            recv_sem=recv3.at[step],
            device_id=along_slab(step),
            device_id_type=MESH,
        )

    for part in zip(to_above, to_below, strict=True):
        start(part)
    deposit(own, 0, atoms, total, CZ * slab, CZ)
    grid = total[...]
    wide0[4:12, 8:40, :] = grid.reshape(CZ, CY, NX)
    start(middle_y)
    one = halve(grid, ROWS // 4, 5, NX // 2)
    wide1[4:8, 8:24, :] = one.reshape(CZ // 2, CY // 2, NX // 2)
    two = halve(one, ROWS // 16, 4, NX // 4)
    wide2[4:6, pl.ds(pl.multiple_of(8 * pencil, 8), 8), :] = two.reshape(
        CZ // 4, CY // 4, NX // 4
    )
    for step in range(1, pencils):
        pencil_copy(step).start()

    has_below = slab > 0
    has_above = slab < slabs - 1

    def from_below(part):
        begin, end = parts[part]
        arrived([to_above[part]])

        @pl.when(has_below)
        def _():
            deposit(below, begin, end, total_below, CZ * slab - 4, 4, CZ * slab - 8)

    def from_above(part):
        begin, end = parts[part]
        arrived([to_below[part]])

        @pl.when(has_above)
        def _():
            deposit(above, begin, end, total_above, CZ * slab + CZ, 4, CZ * slab + CZ + 4)

    from_below(0)
    from_above(0)
    for step in range(1, pencils):
        pencil_arrival(step).wait_recv()
    start(two_z)
    lines2 = 8 * pencils
    three = halve(
        wide2[4:6].reshape(2 * lines2, NX // 4), lines2 // 2, lines2.bit_length() - 1, NX // 4
    )
    wide3[pl.ds(slab, 1)] = three[None]

    @pl.loop(1, slabs)
    def _(step):
        top_copy(step, slab).start()

    from_below(1)

    @pl.when(has_below)
    def _():
        halo = total_below[...]
        wide0[0:4, 8:40, :] = halo[0 : 4 * CY].reshape(4, CY, NX)
        wide1[0:4, 8:24, :] = halve_halo(halo, CY).reshape(4, CY // 2, NX // 2)

    start(below_y, has_below)
    start(one_y)
    from_above(1)

    @pl.when(has_above)
    def _():
        halo = total_above[...]
        wide0[12:16, 8:40, :] = halo[0 : 4 * CY].reshape(4, CY, NX)
        wide1[8:12, 8:24, :] = halve_halo(halo, 0).reshape(4, CY // 2, NX // 2)

    start(above_y, has_above)
    start(one_y_above, has_above)
    interpolate_x(along_x)
    arrived(middle_y)
    arrived(below_y, has_below)
    pair_lines(wide0, paired, 0, 12)
    near_field(wide0, paired, base, 0, 8, before=False)
    arrived(two_z)
    field_of(wide2, field2, 3, 2)

    @pl.loop(1, slabs)
    def _(step):
        copy = top_copy(step, lax.rem(slab + slabs - step, slabs))
        copy.wait_send()
        copy.wait_recv()

    upper_fields(slabs, pencils, wide3, field3)
    arrived(one_y)
    arrived(one_y_above, has_above)
    field_of(wide1, field1, 2, 1)
    interpolate(
        slabs,
        pencils,
        (field1, field2, field3),
        (flat1, flat2, flat3),
        along_x,
        lined_high,
        lined_low,
        base,
    )
    for step in range(1, pencils):
        pencil_copy(step).wait_send()
    sent([*to_above, *to_below, *middle_y, *two_z, *one_y])
    sent(one_y_above, has_above)
    arrived(above_y, has_above)
    pair_lines(wide0, paired, 12, 16)
    near_field(wide0, paired, base, 8, 12, before=True)
    clear_outside(slabs, pencils, base)
    sent(below_y, has_below)
    sent(above_y, has_above)


def exchange_call(slabs, pencils, own):
    atoms = own.shape[1]
    shapes = (
        (12, 48, NX),
        (1, atoms),
        (2, atoms),
        (CZ, 128),
    )
    field3_rows = sum(4 * max((pencils * CY) >> level, 8) for level in (3, 4, 5))
    return pl.pallas_call(
        functools.partial(exchange_kernel, slabs, pencils),
        out_shape=[jax.ShapeDtypeStruct(shape, jnp.float32) for shape in shapes],
        in_specs=[VMEM],
        out_specs=[VMEM] * 4,
        scratch_shapes=[
            pltpu.VMEM((16, 48, NX), jnp.float32),
            pltpu.VMEM((2, 16, 48, NX), jnp.float32),
            pltpu.VMEM((12, 32, NX // 2), jnp.float32),
            pltpu.VMEM((10, 8 * pencils, NX // 4), jnp.float32),
            pltpu.VMEM((slabs, 4 * pencils, 128), jnp.float32),
            pltpu.VMEM((atoms // 128, 128), jnp.float32),
            pltpu.VMEM((3 * atoms // 128, 128), jnp.float32),
            pltpu.VMEM((4, atoms), jnp.float32),
            pltpu.VMEM((4, atoms), jnp.float32),
            pltpu.VMEM((ROWS, NX), jnp.float32),
            pltpu.VMEM((5 * CY, NX), jnp.float32),
            pltpu.VMEM((5 * CY, NX), jnp.float32),
            pltpu.VMEM((8 * 32, NX // 2), jnp.float32),
            pltpu.VMEM((4 * 8 * pencils, NX // 4), jnp.float32),
            pltpu.VMEM((field3_rows, 128), jnp.float32),
            pltpu.VMEM((NX, NX), jnp.bfloat16),
            pltpu.VMEM((2 * 32, 12 * 256), jnp.float32),
            pltpu.VMEM((2 * 8 * pencils, 12 * 128), jnp.float32),
            pltpu.VMEM((2 * field3_rows // 4, 12 * 128), jnp.float32),
            pltpu.VMEM((12 * 48, NX), jnp.bfloat16),
            pltpu.VMEM((12 * 48, NX), jnp.bfloat16),
            pltpu.SemaphoreType.DMA((18,)),
            pltpu.SemaphoreType.DMA((18,)),
            pltpu.SemaphoreType.DMA((pencils,)),
            pltpu.SemaphoreType.DMA((pencils,)),
            pltpu.SemaphoreType.DMA((slabs,)),
            pltpu.SemaphoreType.DMA((slabs,)),
        ],
        cost_estimate=pl.CostEstimate(flops=10**10, bytes_accessed=2**23, transcendentals=0),
        compiler_params=pltpu.CompilerParams(
            collective_id=0, has_side_effects=True, vmem_limit_bytes=40 * 2**20
        ),
    )(own)


def field_kernel(
    own_ref,
    place_ref,
    sorted_ref,
    starts_ref,
    wide_pot,
    pot_ref,
    force_ref,
    slopes,
    bounds,
    found,
    by_row,
):
    def slope(after1, before1, after2, before2):
        return (8.0 * (after1 - before1) - (after2 - before2)) * (1.0 / 12.0)

    atoms = own_ref.shape[1]
    for plane in range(CZ):
        bounds[plane] = jnp.max(starts_ref[plane : plane + 1, :]).astype(jnp.int32)
    bounds[CZ] = jnp.int32(atoms)
    found[...] = jnp.zeros_like(found)
    size = math.gcd(atoms, 1024)

    @pl.loop(0, CZ)
    def _(plane):
        middle = wide_pot[plane + 2]
        own = middle[8:40]
        pot_ref[plane] = own
        at = [wide_pot[plane + 2 + k, 8:40, :] for k in (1, -1, 2, -2)]
        across = [pltpu.roll(middle, (-k) % 48, 0)[8:40] for k in (1, -1, 2, -2)]
        along = [shift_x(own, k) for k in (1, -1, 2, -2)]
        for direction, four in enumerate((at, across, along)):
            high, low = split_two(slope(*four))
            slopes[2 * direction * CY : (2 * direction + 1) * CY, :] = high
            slopes[(2 * direction + 1) * CY : (2 * direction + 2) * CY, :] = low
        first = bounds[plane]
        last = bounds[plane + 1]

        def block(step, carry):
            begin = pl.multiple_of(step * size, size)
            here = pl.ds(begin, size)
            table = one_hot(sorted_ref[1:2, here].astype(jnp.int32).astype(jnp.int16), NX)
            at_cell = jnp.dot(slopes[...], table, preferred_element_type=jnp.float32)
            index = begin + iota((1, size), 1)
            line = sorted_ref[0:1, here].astype(jnp.int32)
            line = jnp.where((index >= first) & (index < last), line, -1)
            at_row = iota((CY, size), 0) == line
            for direction in range(3):
                high = at_cell[2 * direction * CY : (2 * direction + 1) * CY]
                low = at_cell[(2 * direction + 1) * CY : (2 * direction + 2) * CY]
                found[direction : direction + 1, here] += jnp.sum(
                    jnp.where(at_row, high + low, 0.0), axis=0, keepdims=True
                )
            return carry

        lax.fori_loop(first // size, (last + size - 1) // size, block, 0)

    rows = atoms // 128
    for direction in range(3):
        for row in range(rows):
            there = slice(128 * row, 128 * row + 128)
            by_row[direction * rows + row : direction * rows + row + 1, :] = found[
                direction : direction + 1, there
            ]
    high, low = split_two(by_row[...])
    split = jnp.concatenate([high, low], axis=0)
    width = math.gcd(atoms, CHUNK)

    @pl.loop(0, atoms // width)
    def _(step):
        here = pl.ds(pl.multiple_of(step * width, width), width)
        to = place_ref[0:1, here].astype(jnp.int32)
        table = one_hot((to & 127).astype(jnp.int16), 128)
        values = jnp.dot(split, table, preferred_element_type=jnp.float32)
        at_row = iota((rows, width), 0) == to >> 7
        charges = own_ref[3:4, here]
        for direction in range(3):
            high = values[direction * rows : (direction + 1) * rows]
            low = values[(3 + direction) * rows : (4 + direction) * rows]
            chosen = jnp.sum(jnp.where(at_row, high + low, 0.0), axis=0, keepdims=True)
            force_ref[direction : direction + 1, here] = -charges * chosen


def field_call(base, own, order):
    atoms = own.shape[1]
    return pl.pallas_call(
        field_kernel,
        out_shape=[
            jax.ShapeDtypeStruct((CZ, CY, NX), jnp.float32),
            jax.ShapeDtypeStruct((3, atoms), jnp.float32),
        ],
        in_specs=[VMEM] * 5,
        out_specs=[VMEM] * 2,
        scratch_shapes=[
            pltpu.VMEM((6 * CY, NX), jnp.bfloat16),
            pltpu.SMEM((CZ + 1,), jnp.int32),
            pltpu.VMEM((3, atoms), jnp.float32),
            pltpu.VMEM((3 * atoms // 128, 128), jnp.float32),
        ],
        cost_estimate=pl.CostEstimate(flops=2 * 10**10, bytes_accessed=2**23, transcendentals=0),
        compiler_params=pltpu.CompilerParams(vmem_limit_bytes=40 * 2**20),
    )(own, *order, base)


def solution(mesh):
    slabs = mesh.shape["slab"]
    pencils = mesh.shape["pencil"]

    def body(atom_cell, charge):
        own = jnp.concatenate([atom_cell.astype(jnp.float32), charge[None]], axis=0)
        base, *order = exchange_call(slabs, pencils, own)
        potential, forces = field_call(base, own, order)
        return (potential, forces)

    return jax.shard_map(
        body,
        mesh=mesh,
        in_specs=(P(None, ("slab", "pencil")), P(("slab", "pencil"))),
        out_specs=(P("slab", "pencil", None), P(None, ("slab", "pencil"))),
        check_vma=False,
    )
```

```python
import functools
import math

import jax
import jax.numpy as jnp
from jax import lax
from jax.experimental import pallas as pl
from jax.experimental.pallas import tpu as pltpu
from jax.sharding import PartitionSpec as P

CZ = 8
CY = 32
NX = 512
F = 32
ROWS = CZ * CY
CHUNK = 4096
MESH = pl.DeviceIdType.MESH
VMEM = pl.BlockSpec(memory_space=pltpu.VMEM)
SQUARES = (0, 1, 2, 4, 5, 8)


def iota(shape, dim):
    return lax.broadcasted_iota(jnp.int32, shape, dim)


def iota16(shape, dim):
    return iota(shape, dim).astype(jnp.int16)


def one_hot(places, size):
    here = iota16((size, places.shape[1]), 0) == places
    return jnp.where(here, jnp.ones((), jnp.bfloat16), jnp.zeros((), jnp.bfloat16))


def near_weight(squared):
    return 1.0 / math.sqrt(squared + 0.25) - 1.0 / math.sqrt(squared + 4.0)


def level_weight(level, squared):
    return (1.0 / math.sqrt(squared + 1.0) - 1.0 / math.sqrt(squared + 4.0)) / 2**level


def split_two(values):
    high = values.astype(jnp.bfloat16)
    return high, (values - high.astype(jnp.float32)).astype(jnp.bfloat16)


def dot32(left, right):
    left_high, left_low = split_two(left)
    right_high, right_low = split_two(right)
    total = jnp.dot(left_high, right_high, preferred_element_type=jnp.float32)
    total += jnp.dot(left_high, right_low, preferred_element_type=jnp.float32)
    return total + jnp.dot(left_low, right_high, preferred_element_type=jnp.float32)


def halve_rows(rows_out, rows_in, line_bits):
    out_row = iota((rows_out, rows_in), 0)
    in_row = iota((rows_out, rows_in), 1)
    plane = in_row >> (line_bits + 1)
    line = (in_row & (2**line_bits - 1)) >> 1
    return jnp.where((plane << (line_bits - 1)) + line == out_row, 1.0, 0.0).astype(jnp.bfloat16)


def halve_columns(columns_in, columns_out):
    return jnp.where(
        iota((columns_in, columns_out), 0) >> 1 == iota((columns_in, columns_out), 1), 1.0, 0.0
    ).astype(jnp.bfloat16)


def halve(values, rows_out, line_bits, columns_out):
    rows, columns = values.shape
    left = halve_rows(rows_out, rows, line_bits)
    high, low = split_two(values)
    part = jnp.dot(left, high, preferred_element_type=jnp.float32)
    part += jnp.dot(left, low, preferred_element_type=jnp.float32)
    right = halve_columns(columns, columns_out)
    high, low = split_two(part)
    whole = jnp.dot(high, right, preferred_element_type=jnp.float32)
    return whole + jnp.dot(low, right, preferred_element_type=jnp.float32)


def deposit(atoms_ref, begin, end, total_ref, first_plane, planes, far_plane=None):
    near_rows = planes * CY
    rows = near_rows if far_plane is None else near_rows + CY
    width = math.gcd(end - begin, CHUNK)
    fresh = begin == 0 and width == end
    y0 = lax.axis_index("pencil") * CY

    @pl.loop(0, (end - begin) // width)
    def _(step):
        here = pl.ds(pl.multiple_of(begin + step * width, width), width)
        plane = atoms_ref[0:1, here].astype(jnp.int32) - first_plane
        line = atoms_ref[1:2, here].astype(jnp.int32) - y0
        columns = atoms_ref[2:3, here].astype(jnp.int32).astype(jnp.int16)
        high, low = split_two(atoms_ref[3:4, here])
        place = plane * CY + line
        if far_plane is not None:
            far = ((plane + first_plane - far_plane) >> 1) * (CY // 2) + (line >> 1)
            place = jnp.where((plane >= 0) & (plane < planes), place, near_rows + far)
        at_row = iota16((rows, width), 0) == place.astype(jnp.int16)
        none = jnp.zeros((), jnp.bfloat16)
        stacked = jnp.concatenate(
            [jnp.where(at_row, high, none), jnp.where(at_row, low, none)], axis=0
        )
        added = lax.dot_general(
            stacked,
            one_hot(columns, NX),
            (((1,), (1,)), ((), ())),
            preferred_element_type=jnp.float32,
        )
        added = added[:rows] + added[rows:]
        if fresh:
            total_ref[0:rows, :] = added
        else:
            total_ref[0:rows, :] += added


def shift_x(values, step):
    width = values.shape[-1]
    axis = values.ndim - 1
    column = iota(values.shape, axis)
    moved = pltpu.roll(values, (-step) % width, axis)
    return jnp.where((column + step >= 0) & (column + step < width), moved, 0.0)


def pair_x(values, step):
    return shift_x(values, step) + shift_x(values, -step)


def hat(fine, cell, factor, count):
    bits = factor.bit_length()
    numerator = jnp.clip(2 * fine + 1 - factor, 0, 2 * factor * (count - 1))
    lower = jnp.minimum(numerator >> bits, count - 2)
    fraction = (numerator - (lower << bits)).astype(jnp.float32) * (0.5 / factor)
    return jnp.where(
        cell == lower, 1.0 - fraction, jnp.where(cell == lower + 1, fraction, 0.0)
    )


def shift_y(values, step):
    lines = values.shape[0]
    line = iota(values.shape, 0) + step
    return jnp.where((line >= 0) & (line < lines), pltpu.roll(values, (-step) % lines, 0), 0.0)


def field_of(wide, field, shift, level):
    lines = wide.shape[1]

    @pl.loop(0, field.shape[0] // lines)
    def _(plane):
        table = {}
        for a in range(3):
            line = wide[plane + shift]
            if a:
                line = wide[plane + shift + a] + wide[plane + shift - a]
            table[a, 0] = line
            for b in (1, 2):
                table[a, b] = shift_y(line, b) + shift_y(line, -b)
        groups = grouped(table)
        total = None
        for c in range(3):
            part = sum(level_weight(level, c * c + k) * groups[k] for k in SQUARES)
            total = total + pair_x(part, c) if c else part
        field[pl.ds(pl.multiple_of(plane * lines, lines), lines), :] = total


def grouped(table):
    return {
        0: table[0, 0],
        1: table[0, 1] + table[1, 0],
        2: table[1, 1],
        4: table[0, 2] + table[2, 0],
        5: table[1, 2] + table[2, 1],
        8: table[2, 2],
    }


def upper_fields(slabs, pencils, wide3, field3):
    slab = lax.axis_index("slab")
    pencil_bits = pencils.bit_length() - 1
    rows3 = slabs * pencils * 4
    grid3 = wide3[...].reshape(rows3, 128)
    first_row = 0
    first_lane = 0
    for level in (3, 4, 5):
        down = level - 3
        line_bits = pencil_bits + 2 - down
        lines = 2**line_bits
        planes = slabs >> down
        count = planes * lines
        length = NX >> level
        if level == 3:
            charges = grid3
        else:
            shape = (count, rows3)
            out_row = iota(shape, 0)
            in_row = iota(shape, 1)
            in_plane = in_row >> (2 + pencil_bits)
            in_line = in_row & (4 * pencils - 1)
            cell = ((in_plane >> down) << line_bits) + (in_line >> down)
            charges = dot32(jnp.where(cell == out_row, 1.0, 0.0), grid3)
        reach = 3 if level < 5 else length
        source = iota((128, 128), 0) >> down
        column = iota((128, 128), 1) - first_lane
        valid = (column >= 0) & (column < length)
        pairs = jnp.concatenate(
            [
                jnp.where(valid & (jnp.abs(source - column) == c), 1.0, 0.0)
                for c in range(reach)
            ],
            axis=1,
        )
        moved = dot32(charges, pairs)
        stacked = jnp.concatenate(
            [moved[:, c * 128 : (c + 1) * 128] for c in range(reach)], axis=0
        )
        out_bits = max(line_bits, 3)
        shape = (4 << out_bits, reach * count)
        across = iota(shape, 1) >> (count.bit_length() - 1)
        source = iota(shape, 1) & (count - 1)
        dz = (source >> line_bits) - (iota(shape, 0) >> out_bits) - ((slab >> down) - 1)
        dy = (source & (lines - 1)) - (iota(shape, 0) & (2**out_bits - 1))
        squared = (dz * dz + dy * dy + across * across).astype(jnp.float32)
        weight = 1.0 / jnp.sqrt(squared + 1.0)
        if level < 5:
            weight = (weight - 1.0 / jnp.sqrt(squared + 4.0)) / 2**level
            weight = jnp.where((jnp.abs(dz) <= 2) & (jnp.abs(dy) <= 2), weight, 0.0)
        else:
            weight = weight / F
        field3[first_row : first_row + (4 << out_bits), :] = dot32(weight, stacked)
        first_row = first_row + (4 << out_bits)
        first_lane = first_lane + length


def interpolate_x(along_x):
    lane = 0
    for level in range(1, 6):
        length = NX >> level
        rows = length if level < 5 else NX - lane
        weights = hat(iota((rows, NX), 1), iota((rows, NX), 0), 2**level, length)
        weights = jnp.where(iota((rows, NX), 0) < length, weights, 0.0)
        along_x[lane : lane + rows, :] = weights.astype(jnp.bfloat16)
        lane = lane + rows


def interpolate(slabs, pencils, fields, flats, along_x, lined_high, lined_low, base):
    slab = lax.axis_index("slab")
    pencil = lax.axis_index("pencil")
    upper = pencils * CY
    padded = [max(upper >> level, 8) for level in (3, 4, 5)]
    layers = [
        (1, 4 * slab - 2, 32, 16 * pencil - 8),
        (2, 2 * slab - 1, upper >> 2, 0),
    ]
    layers += [
        (level, (slab >> (level - 3)) - 1, lines, 0)
        for level, lines in zip((3, 4, 5), padded, strict=True)
    ]
    starts = [0, 0, 0, 4 * padded[0], 4 * (padded[0] + padded[1])]
    tops = [0, 0, 0, padded[0], padded[0] + padded[1]]
    field1, field2, field3 = fields
    flat1, flat2, flat3 = flats
    fields = [field1, field2, field3, field3, field3]
    flats = [flat1, flat2, flat3, flat3, flat3]

    for plane in range(12):
        fine_z = CZ * slab - 2 + plane
        for (level, plane0, lines, _), begin, top, field, flat in zip(
            layers, starts, tops, fields, flats, strict=True
        ):
            factor = 2**level
            count = (slabs * CZ) >> level
            numerator = jnp.clip(2 * fine_z + 1 - factor, 0, 2 * factor * (count - 1))
            lower = jnp.minimum(numerator >> (level + 1), count - 2)
            fraction = (numerator - (lower << (level + 1))).astype(jnp.float32) * (0.5 / factor)
            row = begin + (lower - plane0) * lines
            row = pl.multiple_of(row, 8)
            mixed = (1.0 - fraction) * field[pl.ds(row, lines), :]
            mixed += fraction * field[pl.ds(row + lines, lines), :]
            high, low = split_two(mixed)
            width = field.shape[1]
            there = slice(plane * width, (plane + 1) * width)
            flat[top : top + lines, there] = high.astype(jnp.float32)
            flat[flat.shape[0] // 2 + top : flat.shape[0] // 2 + top + lines, there] = low.astype(
                jnp.float32
            )

    def along_y(some):
        blocks = []
        for level, _, lines, line0 in some:
            shape = (48, lines)
            fine_y = CY * pencil - 8 + iota(shape, 0)
            blocks.append(hat(fine_y, line0 + iota(shape, 1), 2**level, upper >> level))
        return jnp.concatenate(blocks + blocks, axis=1).astype(jnp.bfloat16)

    for some, flat, first in ((layers[:1], flat1, 0), (layers[1:2], flat2, 256), (layers[2:], flat3, 384)):
        width = flat.shape[1] // 12
        lined = jnp.dot(
            along_y(some), flat[...].astype(jnp.bfloat16), preferred_element_type=jnp.float32
        )
        high, low = split_two(lined)
        for plane in range(12):
            there = slice(plane * width, (plane + 1) * width)
            rows = slice(48 * plane, 48 * plane + 48)
            lined_high[rows, first : first + width] = high[:, there]
            lined_low[rows, first : first + width] = low[:, there]

    fine = jnp.dot(lined_high[...], along_x[...], preferred_element_type=jnp.float32)
    fine += jnp.dot(lined_low[...], along_x[...], preferred_element_type=jnp.float32)
    fine = fine.reshape(12, 48, NX)
    base[0:8] += fine[0:8]
    base[8:12] = fine[8:12]


def halve_halo(total, near_first):
    out_row = iota((2 * CY, 5 * CY), 0)
    in_row = iota((2 * CY, 5 * CY), 1)
    near = ((in_row >> 6) << 4) + ((in_row & (CY - 1)) >> 1) + near_first
    far = in_row - 4 * CY + (CY - near_first)
    chosen = jnp.where(in_row < 4 * CY, near, far) == out_row
    left = jnp.where(chosen, 1.0, 0.0).astype(jnp.bfloat16)
    high, low = split_two(total)
    part = jnp.dot(left, high, preferred_element_type=jnp.float32)
    part += jnp.dot(left, low, preferred_element_type=jnp.float32)
    right = halve_columns(NX, NX // 2)
    high, low = split_two(part)
    whole = jnp.dot(high, right, preferred_element_type=jnp.float32)
    return whole + jnp.dot(low, right, preferred_element_type=jnp.float32)


def sort_atoms(own, planes, place_ref, sorted_ref, starts_ref, moved):
    atoms = own.shape[1]
    rows = atoms // 128
    for row in range(rows):
        planes[row : row + 1, :] = own[0:1, 128 * row : 128 * row + 128]
    plane = planes[...].astype(jnp.int32) - lax.axis_index("slab") * CZ
    bins = [jnp.where(plane == b, 1.0, 0.0) for b in range(CZ)]
    stacked = jnp.concatenate(bins, axis=0).astype(jnp.bfloat16)
    earlier = iota((128, 128), 0) < iota((128, 128), 1)
    earlier = jnp.where(earlier, 1.0, 0.0).astype(jnp.bfloat16)
    in_row = jnp.dot(stacked, earlier, preferred_element_type=jnp.float32)
    ones = jnp.ones((128, 128), jnp.bfloat16)
    of_row = jnp.dot(stacked, ones, preferred_element_type=jnp.float32).astype(jnp.bfloat16)
    size = (CZ * rows, CZ * rows)
    above = jnp.where(iota(size, 1) < iota(size, 0), 1.0, 0.0).astype(jnp.bfloat16)
    before = jnp.dot(above, of_row, preferred_element_type=jnp.float32)
    both = in_row + before
    place = sum(bins[b] * both[b * rows : (b + 1) * rows] for b in range(CZ))
    for b in range(CZ):
        starts_ref[b : b + 1, :] = before[b * rows : b * rows + 1, :]
    planes[...] = place
    for row in range(rows):
        place_ref[0:1, 128 * row : 128 * row + 128] = planes[row : row + 1, :]

    width = math.gcd(atoms, CHUNK)
    y0 = lax.axis_index("pencil") * CY
    moved[...] = jnp.zeros_like(moved)

    @pl.loop(0, atoms // width)
    def _(step):
        here = pl.ds(pl.multiple_of(step * width, width), width)
        line = own[1:2, here].astype(jnp.int32) - y0
        column = own[2:3, here].astype(jnp.int32)
        to = place_ref[0:1, here].astype(jnp.int32)
        at_row = iota16((rows, width), 0) == (to >> 7).astype(jnp.int16)
        none = jnp.zeros((), jnp.bfloat16)
        fields = [
            jnp.where(at_row, part.astype(jnp.float32).astype(jnp.bfloat16), none)
            for part in (line, column & 255, column >> 8)
        ]
        moved[...] += lax.dot_general(
            jnp.concatenate(fields, axis=0),
            one_hot((to & 127).astype(jnp.int16), 128),
            (((1,), (1,)), ((), ())),
            preferred_element_type=jnp.float32,
        )

    moved[rows : 2 * rows, :] += 256.0 * moved[2 * rows : 3 * rows, :]
    for row in range(rows):
        there = slice(128 * row, 128 * row + 128)
        sorted_ref[0:1, there] = moved[row : row + 1, :]
        sorted_ref[1:2, there] = moved[rows + row : rows + row + 1, :]


def pair_lines(wide0, paired, first, last):
    @pl.loop(first, last)
    def _(plane):
        values = wide0[plane]
        for b in (1, 2):
            paired[b - 1, plane] = pltpu.roll(values, b, 0) + pltpu.roll(values, 48 - b, 0)


def near_field(wide0, paired, base, first, last, before):
    @pl.loop(first, last)
    def _(plane):
        for block in range(6):
            rows = pl.ds(8 * block, 8)

            def near(b, k):
                if b:
                    return paired[b - 1, plane + 2 + k, rows, :]
                return wide0[plane + 2 + k, rows, :]

            table = {}
            for b in range(3):
                table[0, b] = near(b, 0)
                for a in (1, 2):
                    table[a, b] = near(b, a) + near(b, -a)
            groups = grouped(table)
            total = base[plane, rows, :] if before else None
            for c in range(3):
                part = sum(near_weight(c * c + k) * groups[k] for k in SQUARES)
                part = pair_x(part, c) if c else part
                total = part if total is None else total + part
            base[plane, rows, :] = total


def clear_outside(slabs, pencils, base):
    slab = lax.axis_index("slab")
    pencil = lax.axis_index("pencil")

    flat = jnp.zeros((2, 48, NX), jnp.float32)
    edge = jnp.zeros((12, 8, NX), jnp.float32)

    @pl.when(slab == 0)
    def _():
        base[0:2] = flat

    @pl.when(slab == slabs - 1)
    def _():
        base[10:12] = flat

    @pl.when(pencil == 0)
    def _():
        base[:, 0:8, :] = edge

    @pl.when(pencil == pencils - 1)
    def _():
        base[:, 40:48, :] = edge


def exchange_kernel(
    slabs,
    pencils,
    own,
    base,
    place_ref,
    sorted_ref,
    starts_ref,
    wide0,
    paired,
    wide1,
    wide2,
    wide3,
    planes,
    moved,
    below,
    above,
    total,
    total_below,
    total_above,
    field1,
    field2,
    field3,
    along_x,
    flat1,
    flat2,
    flat3,
    lined_high,
    lined_low,
    send,
    recv,
    send2,
    recv2,
    send3,
    recv3,
):
    slab = lax.axis_index("slab")
    pencil = lax.axis_index("pencil")
    atoms = own.shape[1]
    for ref in (wide0, wide1, wide2, total, total_below, total_above):
        ref[...] = jnp.zeros_like(ref)

    def along_pencil(step):
        return (slab, lax.rem(pencil + step, pencils))

    def along_slab(step):
        return (lax.rem(slab + step, slabs), pencil)

    barrier = pltpu.get_barrier_semaphore()

    @pl.loop(1, pencils)
    def _(step):
        pl.semaphore_signal(barrier, inc=1, device_id=along_pencil(step), device_id_type=MESH)

    @pl.loop(1, slabs)
    def _(step):
        pl.semaphore_signal(barrier, inc=1, device_id=along_slab(step), device_id_type=MESH)

    sort_atoms(own, planes, place_ref, sorted_ref, starts_ref, moved)
    pl.semaphore_wait(barrier, slabs + pencils - 2)

    def inside(dz, dy):
        z = slab + dz
        y = pencil + dy
        return (z >= 0) & (z < slabs) & (y >= 0) & (y < pencils)

    copies = []

    def add(source, target, dz, dy):
        copies.append((source, target, dz, dy))
        return len(copies) - 1

    parts = [(0, atoms // 2), (atoms // 2, atoms)]
    to_above = [add(own.at[:, a:b], below.at[:, a:b], 1, 0) for a, b in parts]
    to_below = [add(own.at[:, a:b], above.at[:, a:b], -1, 0) for a, b in parts]
    lines0 = {1: (36, 4), -1: (8, 40)}
    middle_y = [
        add(wide0.at[4:12, a : a + 4], wide0.at[4:12, b : b + 4], 0, dy)
        for dy, (a, b) in lines0.items()
    ]
    below_y = [
        add(wide0.at[0:4, a : a + 4], wide0.at[0:4, b : b + 4], 0, dy)
        for dy, (a, b) in lines0.items()
    ]
    above_y = [
        add(wide0.at[12:16, a : a + 4], wide0.at[12:16, b : b + 4], 0, dy)
        for dy, (a, b) in lines0.items()
    ]
    one_y, one_y_above = (
        [
            add(wide1.at[some, a : a + 4], wide1.at[some, b : b + 4], 0, dy)
            for dy, a, b in ((1, 20, 4), (-1, 8, 24))
        ]
        for some in (slice(0, 8), slice(8, 12))
    )
    two_z = [
        add(wide2.at[4:6], wide2.at[4 - 2 * dz : 6 - 2 * dz], dz, 0) for dz in (-2, -1, 1, 2)
    ]

    def copy_of(index, device):
        source, target, _, _ = copies[index]
        return pltpu.make_async_remote_copy(
            src_ref=source,
            dst_ref=target,
            send_sem=send.at[index],
            recv_sem=recv.at[index],
            device_id=device,
            device_id_type=MESH,
        )

    def start(indices, also=True):
        for index in indices:
            _, _, dz, dy = copies[index]

            @pl.when(inside(dz, dy) & also)
            def _(index=index, dz=dz, dy=dy):
                copy_of(index, (slab + dz, pencil + dy)).start()

    def arrived(indices, also=True):
        for index in indices:
            _, _, dz, dy = copies[index]

            @pl.when(inside(-dz, -dy) & also)
            def _(index=index, dz=dz, dy=dy):
                copy_of(index, (slab - dz, pencil - dy)).wait_recv()

    def sent(indices, also=True):
        for index in indices:
            _, _, dz, dy = copies[index]

            @pl.when(inside(dz, dy) & also)
            def _(index=index, dz=dz, dy=dy):
                copy_of(index, (slab + dz, pencil + dy)).wait_send()

    def pencil_copy(step):
        lines = pl.ds(pl.multiple_of(8 * pencil, 8), 8)
        return pltpu.make_async_remote_copy(
            src_ref=wide2.at[4:6, lines],
            dst_ref=wide2.at[4:6, lines],
            send_sem=send2.at[step],
            recv_sem=recv2.at[step],
            device_id=along_pencil(step),
            device_id_type=MESH,
        )

    def pencil_arrival(step):
        lines = pl.ds(pl.multiple_of(8 * lax.rem(pencil + pencils - step, pencils), 8), 8)
        return pltpu.make_async_remote_copy(
            src_ref=wide2.at[4:6, lines],
            dst_ref=wide2.at[4:6, lines],
            send_sem=send2.at[step],
            recv_sem=recv2.at[step],
            device_id=along_pencil(step),
            device_id_type=MESH,
        )

    def top_copy(step, slot):
        return pltpu.make_async_remote_copy(
            src_ref=wide3.at[slot],
            dst_ref=wide3.at[slot],
            send_sem=send3.at[step],
            recv_sem=recv3.at[step],
            device_id=along_slab(step),
            device_id_type=MESH,
        )

    for part in zip(to_above, to_below, strict=True):
        start(part)
    deposit(own, 0, atoms, total, CZ * slab, CZ)
    grid = total[...]
    wide0[4:12, 8:40, :] = grid.reshape(CZ, CY, NX)
    start(middle_y)
    one = halve(grid, ROWS // 4, 5, NX // 2)
    wide1[4:8, 8:24, :] = one.reshape(CZ // 2, CY // 2, NX // 2)
    two = halve(one, ROWS // 16, 4, NX // 4)
    wide2[4:6, pl.ds(pl.multiple_of(8 * pencil, 8), 8), :] = two.reshape(
        CZ // 4, CY // 4, NX // 4
    )
    for step in range(1, pencils):
        pencil_copy(step).start()

    has_below = slab > 0
    has_above = slab < slabs - 1

    def from_below(part):
        begin, end = parts[part]
        arrived([to_above[part]])

        @pl.when(has_below)
        def _():
            deposit(below, begin, end, total_below, CZ * slab - 4, 4, CZ * slab - 8)

    def from_above(part):
        begin, end = parts[part]
        arrived([to_below[part]])

        @pl.when(has_above)
        def _():
            deposit(above, begin, end, total_above, CZ * slab + CZ, 4, CZ * slab + CZ + 4)

    from_below(0)
    from_above(0)
    for step in range(1, pencils):
        pencil_arrival(step).wait_recv()
    start(two_z)
    lines2 = 8 * pencils
    three = halve(
        wide2[4:6].reshape(2 * lines2, NX // 4), lines2 // 2, lines2.bit_length() - 1, NX // 4
    )
    wide3[pl.ds(slab, 1)] = three[None]

    @pl.loop(1, slabs)
    def _(step):
        top_copy(step, slab).start()

    from_below(1)

    @pl.when(has_below)
    def _():
        halo = total_below[...]
        wide0[0:4, 8:40, :] = halo[0 : 4 * CY].reshape(4, CY, NX)
        wide1[0:4, 8:24, :] = halve_halo(halo, CY).reshape(4, CY // 2, NX // 2)

    start(below_y, has_below)
    start(one_y)
    from_above(1)

    @pl.when(has_above)
    def _():
        halo = total_above[...]
        wide0[12:16, 8:40, :] = halo[0 : 4 * CY].reshape(4, CY, NX)
        wide1[8:12, 8:24, :] = halve_halo(halo, 0).reshape(4, CY // 2, NX // 2)

    start(above_y, has_above)
    start(one_y_above, has_above)
    interpolate_x(along_x)
    arrived(middle_y)
    arrived(below_y, has_below)
    pair_lines(wide0, paired, 0, 12)
    near_field(wide0, paired, base, 0, 8, before=False)
    arrived(two_z)
    field_of(wide2, field2, 3, 2)

    @pl.loop(1, slabs)
    def _(step):
        copy = top_copy(step, lax.rem(slab + slabs - step, slabs))
        copy.wait_send()
        copy.wait_recv()

    upper_fields(slabs, pencils, wide3, field3)
    arrived(one_y)
    arrived(one_y_above, has_above)
    field_of(wide1, field1, 2, 1)
    interpolate(
        slabs,
        pencils,
        (field1, field2, field3),
        (flat1, flat2, flat3),
        along_x,
        lined_high,
        lined_low,
        base,
    )
    for step in range(1, pencils):
        pencil_copy(step).wait_send()
    sent([*to_above, *to_below, *middle_y, *two_z, *one_y])
    sent(one_y_above, has_above)
    arrived(above_y, has_above)
    pair_lines(wide0, paired, 12, 16)
    near_field(wide0, paired, base, 8, 12, before=True)
    clear_outside(slabs, pencils, base)
    sent(below_y, has_below)
    sent(above_y, has_above)


def exchange_call(slabs, pencils, own):
    atoms = own.shape[1]
    shapes = (
        (12, 48, NX),
        (1, atoms),
        (2, atoms),
        (CZ, 128),
    )
    field3_rows = sum(4 * max((pencils * CY) >> level, 8) for level in (3, 4, 5))
    return pl.pallas_call(
        functools.partial(exchange_kernel, slabs, pencils),
        out_shape=[jax.ShapeDtypeStruct(shape, jnp.float32) for shape in shapes],
        in_specs=[VMEM],
        out_specs=[VMEM] * 4,
        scratch_shapes=[
            pltpu.VMEM((16, 48, NX), jnp.float32),
            pltpu.VMEM((2, 16, 48, NX), jnp.float32),
            pltpu.VMEM((12, 32, NX // 2), jnp.float32),
            pltpu.VMEM((10, 8 * pencils, NX // 4), jnp.float32),
            pltpu.VMEM((slabs, 4 * pencils, 128), jnp.float32),
            pltpu.VMEM((atoms // 128, 128), jnp.float32),
            pltpu.VMEM((3 * atoms // 128, 128), jnp.float32),
            pltpu.VMEM((4, atoms), jnp.float32),
            pltpu.VMEM((4, atoms), jnp.float32),
            pltpu.VMEM((ROWS, NX), jnp.float32),
            pltpu.VMEM((5 * CY, NX), jnp.float32),
            pltpu.VMEM((5 * CY, NX), jnp.float32),
            pltpu.VMEM((8 * 32, NX // 2), jnp.float32),
            pltpu.VMEM((4 * 8 * pencils, NX // 4), jnp.float32),
            pltpu.VMEM((field3_rows, 128), jnp.float32),
            pltpu.VMEM((NX, NX), jnp.bfloat16),
            pltpu.VMEM((2 * 32, 12 * 256), jnp.float32),
            pltpu.VMEM((2 * 8 * pencils, 12 * 128), jnp.float32),
            pltpu.VMEM((2 * field3_rows // 4, 12 * 128), jnp.float32),
            pltpu.VMEM((12 * 48, NX), jnp.bfloat16),
            pltpu.VMEM((12 * 48, NX), jnp.bfloat16),
            pltpu.SemaphoreType.DMA((18,)),
            pltpu.SemaphoreType.DMA((18,)),
            pltpu.SemaphoreType.DMA((pencils,)),
            pltpu.SemaphoreType.DMA((pencils,)),
            pltpu.SemaphoreType.DMA((slabs,)),
            pltpu.SemaphoreType.DMA((slabs,)),
        ],
        cost_estimate=pl.CostEstimate(flops=10**10, bytes_accessed=2**23, transcendentals=0),
        compiler_params=pltpu.CompilerParams(
            collective_id=0, has_side_effects=True, vmem_limit_bytes=40 * 2**20
        ),
    )(own)


def field_kernel(
    own_ref,
    place_ref,
    sorted_ref,
    starts_ref,
    wide_pot,
    pot_ref,
    force_ref,
    slopes,
    bounds,
    found,
    by_row,
):
    def slope(after1, before1, after2, before2):
        return (8.0 * (after1 - before1) - (after2 - before2)) * (1.0 / 12.0)

    atoms = own_ref.shape[1]
    for plane in range(CZ):
        bounds[plane] = jnp.max(starts_ref[plane : plane + 1, :]).astype(jnp.int32)
    bounds[CZ] = jnp.int32(atoms)
    found[...] = jnp.zeros_like(found)
    size = math.gcd(atoms, 1024)

    @pl.loop(0, CZ)
    def _(plane):
        middle = wide_pot[plane + 2]
        own = middle[8:40]
        pot_ref[plane] = own
        at = [wide_pot[plane + 2 + k, 8:40, :] for k in (1, -1, 2, -2)]
        across = [pltpu.roll(middle, (-k) % 48, 0)[8:40] for k in (1, -1, 2, -2)]
        along = [shift_x(own, k) for k in (1, -1, 2, -2)]
        for direction, four in enumerate((at, across, along)):
            high, low = split_two(slope(*four))
            slopes[2 * direction * CY : (2 * direction + 1) * CY, :] = high
            slopes[(2 * direction + 1) * CY : (2 * direction + 2) * CY, :] = low
        first = bounds[plane]
        last = bounds[plane + 1]

        def block(step, carry):
            begin = pl.multiple_of(step * size, size)
            here = pl.ds(begin, size)
            table = one_hot(sorted_ref[1:2, here].astype(jnp.int32).astype(jnp.int16), NX)
            at_cell = jnp.dot(slopes[...], table, preferred_element_type=jnp.float32)
            index = begin + iota((1, size), 1)
            line = sorted_ref[0:1, here].astype(jnp.int32)
            line = jnp.where((index >= first) & (index < last), line, -1)
            at_row = iota((CY, size), 0) == line
            for direction in range(3):
                high = at_cell[2 * direction * CY : (2 * direction + 1) * CY]
                low = at_cell[(2 * direction + 1) * CY : (2 * direction + 2) * CY]
                found[direction : direction + 1, here] += jnp.sum(
                    jnp.where(at_row, high + low, 0.0), axis=0, keepdims=True
                )
            return carry

        lax.fori_loop(first // size, (last + size - 1) // size, block, 0)

    rows = atoms // 128
    for direction in range(3):
        for row in range(rows):
            there = slice(128 * row, 128 * row + 128)
            by_row[direction * rows + row : direction * rows + row + 1, :] = found[
                direction : direction + 1, there
            ]
    high, low = split_two(by_row[...])
    split = jnp.concatenate([high, low], axis=0)
    width = math.gcd(atoms, CHUNK)

    @pl.loop(0, atoms // width)
    def _(step):
        here = pl.ds(pl.multiple_of(step * width, width), width)
        to = place_ref[0:1, here].astype(jnp.int32)
        table = one_hot((to & 127).astype(jnp.int16), 128)
        values = jnp.dot(split, table, preferred_element_type=jnp.float32)
        at_row = iota((rows, width), 0) == to >> 7
        charges = own_ref[3:4, here]
        for direction in range(3):
            high = values[direction * rows : (direction + 1) * rows]
            low = values[(3 + direction) * rows : (4 + direction) * rows]
            chosen = jnp.sum(jnp.where(at_row, high + low, 0.0), axis=0, keepdims=True)
            force_ref[direction : direction + 1, here] = -charges * chosen


def field_call(base, own, order):
    atoms = own.shape[1]
    return pl.pallas_call(
        field_kernel,
        out_shape=[
            jax.ShapeDtypeStruct((CZ, CY, NX), jnp.float32),
            jax.ShapeDtypeStruct((3, atoms), jnp.float32),
        ],
        in_specs=[VMEM] * 5,
        out_specs=[VMEM] * 2,
        scratch_shapes=[
            pltpu.VMEM((6 * CY, NX), jnp.bfloat16),
            pltpu.SMEM((CZ + 1,), jnp.int32),
            pltpu.VMEM((3, atoms), jnp.float32),
            pltpu.VMEM((3 * atoms // 128, 128), jnp.float32),
        ],
        cost_estimate=pl.CostEstimate(flops=2 * 10**10, bytes_accessed=2**23, transcendentals=0),
        compiler_params=pltpu.CompilerParams(vmem_limit_bytes=40 * 2**20),
    )(own, *order, base)


def solution(mesh):
    slabs = mesh.shape["slab"]
    pencils = mesh.shape["pencil"]

    def body(atom_cell, charge):
        own = jnp.concatenate([atom_cell.astype(jnp.float32), charge[None]], axis=0)
        base, *order = exchange_call(slabs, pencils, own)
        potential, forces = field_call(base, own, order)
        return (potential, forces)

    return jax.shard_map(
        body,
        mesh=mesh,
        in_specs=(P(None, ("slab", "pencil")), P(("slab", "pencil"))),
        out_specs=(P("slab", "pencil", None), P(None, ("slab", "pencil"))),
        check_vma=False,
    )
```

```python
import functools
import math

import jax
import jax.numpy as jnp
from jax import lax
from jax.experimental import pallas as pl
from jax.experimental.pallas import tpu as pltpu
from jax.sharding import PartitionSpec as P

CZ = 8
CY = 32
NX = 512
F = 32
ROWS = CZ * CY
CHUNK = 4096
MESH = pl.DeviceIdType.MESH
VMEM = pl.BlockSpec(memory_space=pltpu.VMEM)
SQUARES = (0, 1, 2, 4, 5, 8)


def iota(shape, dim):
    return lax.broadcasted_iota(jnp.int32, shape, dim)


def iota16(shape, dim):
    return iota(shape, dim).astype(jnp.int16)


def one_hot(places, size):
    here = iota16((size, places.shape[1]), 0) == places
    return jnp.where(here, jnp.ones((), jnp.bfloat16), jnp.zeros((), jnp.bfloat16))


def near_weight(squared):
    return 1.0 / math.sqrt(squared + 0.25) - 1.0 / math.sqrt(squared + 4.0)


def level_weight(level, squared):
    return (1.0 / math.sqrt(squared + 1.0) - 1.0 / math.sqrt(squared + 4.0)) / 2**level


def split_two(values):
    high = values.astype(jnp.bfloat16)
    return high, (values - high.astype(jnp.float32)).astype(jnp.bfloat16)


def dot32(left, right):
    left_high, left_low = split_two(left)
    right_high, right_low = split_two(right)
    total = jnp.dot(left_high, right_high, preferred_element_type=jnp.float32)
    total += jnp.dot(left_high, right_low, preferred_element_type=jnp.float32)
    return total + jnp.dot(left_low, right_high, preferred_element_type=jnp.float32)


def halve_rows(rows_out, rows_in, line_bits):
    out_row = iota((rows_out, rows_in), 0)
    in_row = iota((rows_out, rows_in), 1)
    plane = in_row >> (line_bits + 1)
    line = (in_row & (2**line_bits - 1)) >> 1
    return jnp.where((plane << (line_bits - 1)) + line == out_row, 1.0, 0.0).astype(jnp.bfloat16)


def halve_columns(columns_in, columns_out):
    return jnp.where(
        iota((columns_in, columns_out), 0) >> 1 == iota((columns_in, columns_out), 1), 1.0, 0.0
    ).astype(jnp.bfloat16)


def halve(values, rows_out, line_bits, columns_out):
    rows, columns = values.shape
    left = halve_rows(rows_out, rows, line_bits)
    high, low = split_two(values)
    part = jnp.dot(left, high, preferred_element_type=jnp.float32)
    part += jnp.dot(left, low, preferred_element_type=jnp.float32)
    right = halve_columns(columns, columns_out)
    high, low = split_two(part)
    whole = jnp.dot(high, right, preferred_element_type=jnp.float32)
    return whole + jnp.dot(low, right, preferred_element_type=jnp.float32)


def deposit(atoms_ref, begin, end, total_ref, first_plane, planes, far_plane=None):
    near_rows = planes * CY
    rows = near_rows if far_plane is None else near_rows + CY
    width = math.gcd(end - begin, CHUNK)
    fresh = begin == 0 and width == end
    y0 = lax.axis_index("pencil") * CY

    @pl.loop(0, (end - begin) // width)
    def _(step):
        here = pl.ds(pl.multiple_of(begin + step * width, width), width)
        plane = atoms_ref[0:1, here].astype(jnp.int32) - first_plane
        line = atoms_ref[1:2, here].astype(jnp.int32) - y0
        columns = atoms_ref[2:3, here].astype(jnp.int32).astype(jnp.int16)
        high, low = split_two(atoms_ref[3:4, here])
        place = plane * CY + line
        if far_plane is not None:
            far = ((plane + first_plane - far_plane) >> 1) * (CY // 2) + (line >> 1)
            place = jnp.where((plane >= 0) & (plane < planes), place, near_rows + far)
        at_row = iota16((rows, width), 0) == place.astype(jnp.int16)
        none = jnp.zeros((), jnp.bfloat16)
        stacked = jnp.concatenate(
            [jnp.where(at_row, high, none), jnp.where(at_row, low, none)], axis=0
        )
        added = lax.dot_general(
            stacked,
            one_hot(columns, NX),
            (((1,), (1,)), ((), ())),
            preferred_element_type=jnp.float32,
        )
        added = added[:rows] + added[rows:]
        if fresh:
            total_ref[0:rows, :] = added
        else:
            total_ref[0:rows, :] += added


def shift_x(values, step):
    width = values.shape[-1]
    axis = values.ndim - 1
    column = iota(values.shape, axis)
    moved = pltpu.roll(values, (-step) % width, axis)
    return jnp.where((column + step >= 0) & (column + step < width), moved, 0.0)


def pair_x(values, step):
    return shift_x(values, step) + shift_x(values, -step)


def hat(fine, cell, factor, count):
    bits = factor.bit_length()
    numerator = jnp.clip(2 * fine + 1 - factor, 0, 2 * factor * (count - 1))
    lower = jnp.minimum(numerator >> bits, count - 2)
    fraction = (numerator - (lower << bits)).astype(jnp.float32) * (0.5 / factor)
    return jnp.where(
        cell == lower, 1.0 - fraction, jnp.where(cell == lower + 1, fraction, 0.0)
    )


def shift_y(values, step):
    lines = values.shape[0]
    line = iota(values.shape, 0) + step
    return jnp.where((line >= 0) & (line < lines), pltpu.roll(values, (-step) % lines, 0), 0.0)


def field_of(wide, field, shift, level):
    lines = wide.shape[1]

    @pl.loop(0, field.shape[0] // lines)
    def _(plane):
        table = {}
        for a in range(3):
            line = wide[plane + shift]
            if a:
                line = wide[plane + shift + a] + wide[plane + shift - a]
            table[a, 0] = line
            for b in (1, 2):
                table[a, b] = shift_y(line, b) + shift_y(line, -b)
        groups = grouped(table)
        total = None
        for c in range(3):
            part = sum(level_weight(level, c * c + k) * groups[k] for k in SQUARES)
            total = total + pair_x(part, c) if c else part
        field[pl.ds(pl.multiple_of(plane * lines, lines), lines), :] = total


def grouped(table):
    return {
        0: table[0, 0],
        1: table[0, 1] + table[1, 0],
        2: table[1, 1],
        4: table[0, 2] + table[2, 0],
        5: table[1, 2] + table[2, 1],
        8: table[2, 2],
    }


def upper_fields(slabs, pencils, wide3, field3):
    slab = lax.axis_index("slab")
    pencil_bits = pencils.bit_length() - 1
    rows3 = slabs * pencils * 4
    grid3 = wide3[...].reshape(rows3, 128)
    first_row = 0
    first_lane = 0
    for level in (3, 4, 5):
        down = level - 3
        line_bits = pencil_bits + 2 - down
        lines = 2**line_bits
        planes = slabs >> down
        count = planes * lines
        length = NX >> level
        if level == 3:
            charges = grid3
        else:
            shape = (count, rows3)
            out_row = iota(shape, 0)
            in_row = iota(shape, 1)
            in_plane = in_row >> (2 + pencil_bits)
            in_line = in_row & (4 * pencils - 1)
            cell = ((in_plane >> down) << line_bits) + (in_line >> down)
            charges = dot32(jnp.where(cell == out_row, 1.0, 0.0), grid3)
        reach = 3 if level < 5 else length
        source = iota((128, 128), 0) >> down
        column = iota((128, 128), 1) - first_lane
        valid = (column >= 0) & (column < length)
        pairs = jnp.concatenate(
            [
                jnp.where(valid & (jnp.abs(source - column) == c), 1.0, 0.0)
                for c in range(reach)
            ],
            axis=1,
        )
        moved = dot32(charges, pairs)
        stacked = jnp.concatenate(
            [moved[:, c * 128 : (c + 1) * 128] for c in range(reach)], axis=0
        )
        out_bits = max(line_bits, 3)
        shape = (4 << out_bits, reach * count)
        across = iota(shape, 1) >> (count.bit_length() - 1)
        source = iota(shape, 1) & (count - 1)
        dz = (source >> line_bits) - (iota(shape, 0) >> out_bits) - ((slab >> down) - 1)
        dy = (source & (lines - 1)) - (iota(shape, 0) & (2**out_bits - 1))
        squared = (dz * dz + dy * dy + across * across).astype(jnp.float32)
        weight = 1.0 / jnp.sqrt(squared + 1.0)
        if level < 5:
            weight = (weight - 1.0 / jnp.sqrt(squared + 4.0)) / 2**level
            weight = jnp.where((jnp.abs(dz) <= 2) & (jnp.abs(dy) <= 2), weight, 0.0)
        else:
            weight = weight / F
        field3[first_row : first_row + (4 << out_bits), :] = dot32(weight, stacked)
        first_row = first_row + (4 << out_bits)
        first_lane = first_lane + length


def interpolate_x(along_x):
    lane = 0
    for level in range(1, 6):
        length = NX >> level
        rows = length if level < 5 else NX - lane
        weights = hat(iota((rows, NX), 1), iota((rows, NX), 0), 2**level, length)
        weights = jnp.where(iota((rows, NX), 0) < length, weights, 0.0)
        along_x[lane : lane + rows, :] = weights.astype(jnp.bfloat16)
        lane = lane + rows


def interpolate(slabs, pencils, fields, flats, along_x, lined_high, lined_low, base):
    slab = lax.axis_index("slab")
    pencil = lax.axis_index("pencil")
    upper = pencils * CY
    padded = [max(upper >> level, 8) for level in (3, 4, 5)]
    layers = [
        (1, 4 * slab - 2, 32, 16 * pencil - 8),
        (2, 2 * slab - 1, upper >> 2, 0),
    ]
    layers += [
        (level, (slab >> (level - 3)) - 1, lines, 0)
        for level, lines in zip((3, 4, 5), padded, strict=True)
    ]
    starts = [0, 0, 0, 4 * padded[0], 4 * (padded[0] + padded[1])]
    tops = [0, 0, 0, padded[0], padded[0] + padded[1]]
    field1, field2, field3 = fields
    flat1, flat2, flat3 = flats
    fields = [field1, field2, field3, field3, field3]
    flats = [flat1, flat2, flat3, flat3, flat3]

    for plane in range(12):
        fine_z = CZ * slab - 2 + plane
        for (level, plane0, lines, _), begin, top, field, flat in zip(
            layers, starts, tops, fields, flats, strict=True
        ):
            factor = 2**level
            count = (slabs * CZ) >> level
            numerator = jnp.clip(2 * fine_z + 1 - factor, 0, 2 * factor * (count - 1))
            lower = jnp.minimum(numerator >> (level + 1), count - 2)
            fraction = (numerator - (lower << (level + 1))).astype(jnp.float32) * (0.5 / factor)
            row = begin + (lower - plane0) * lines
            row = pl.multiple_of(row, 8)
            mixed = (1.0 - fraction) * field[pl.ds(row, lines), :]
            mixed += fraction * field[pl.ds(row + lines, lines), :]
            high, low = split_two(mixed)
            width = field.shape[1]
            there = slice(plane * width, (plane + 1) * width)
            flat[top : top + lines, there] = high.astype(jnp.float32)
            flat[flat.shape[0] // 2 + top : flat.shape[0] // 2 + top + lines, there] = low.astype(
                jnp.float32
            )

    def along_y(some):
        blocks = []
        for level, _, lines, line0 in some:
            shape = (48, lines)
            fine_y = CY * pencil - 8 + iota(shape, 0)
            blocks.append(hat(fine_y, line0 + iota(shape, 1), 2**level, upper >> level))
        return jnp.concatenate(blocks + blocks, axis=1).astype(jnp.bfloat16)

    for some, flat, first in ((layers[:1], flat1, 0), (layers[1:2], flat2, 256), (layers[2:], flat3, 384)):
        width = flat.shape[1] // 12
        lined = jnp.dot(
            along_y(some), flat[...].astype(jnp.bfloat16), preferred_element_type=jnp.float32
        )
        high, low = split_two(lined)
        for plane in range(12):
            there = slice(plane * width, (plane + 1) * width)
            rows = slice(48 * plane, 48 * plane + 48)
            lined_high[rows, first : first + width] = high[:, there]
            lined_low[rows, first : first + width] = low[:, there]

    fine = jnp.dot(lined_high[...], along_x[...], preferred_element_type=jnp.float32)
    fine += jnp.dot(lined_low[...], along_x[...], preferred_element_type=jnp.float32)
    fine = fine.reshape(12, 48, NX)
    base[0:8] += fine[0:8]
    base[8:12] = fine[8:12]


def halve_halo(total, near_first):
    out_row = iota((2 * CY, 5 * CY), 0)
    in_row = iota((2 * CY, 5 * CY), 1)
    near = ((in_row >> 6) << 4) + ((in_row & (CY - 1)) >> 1) + near_first
    far = in_row - 4 * CY + (CY - near_first)
    chosen = jnp.where(in_row < 4 * CY, near, far) == out_row
    left = jnp.where(chosen, 1.0, 0.0).astype(jnp.bfloat16)
    high, low = split_two(total)
    part = jnp.dot(left, high, preferred_element_type=jnp.float32)
    part += jnp.dot(left, low, preferred_element_type=jnp.float32)
    right = halve_columns(NX, NX // 2)
    high, low = split_two(part)
    whole = jnp.dot(high, right, preferred_element_type=jnp.float32)
    return whole + jnp.dot(low, right, preferred_element_type=jnp.float32)


def sort_atoms(own, planes, place_ref, sorted_ref, starts_ref, moved):
    atoms = own.shape[1]
    rows = atoms // 128
    for row in range(rows):
        planes[row : row + 1, :] = own[0:1, 128 * row : 128 * row + 128]
    plane = planes[...].astype(jnp.int32) - lax.axis_index("slab") * CZ
    bins = [jnp.where(plane == b, 1.0, 0.0) for b in range(CZ)]
    stacked = jnp.concatenate(bins, axis=0).astype(jnp.bfloat16)
    earlier = iota((128, 128), 0) < iota((128, 128), 1)
    earlier = jnp.where(earlier, 1.0, 0.0).astype(jnp.bfloat16)
    in_row = jnp.dot(stacked, earlier, preferred_element_type=jnp.float32)
    ones = jnp.ones((128, 128), jnp.bfloat16)
    of_row = jnp.dot(stacked, ones, preferred_element_type=jnp.float32).astype(jnp.bfloat16)
    size = (CZ * rows, CZ * rows)
    above = jnp.where(iota(size, 1) < iota(size, 0), 1.0, 0.0).astype(jnp.bfloat16)
    before = jnp.dot(above, of_row, preferred_element_type=jnp.float32)
    both = in_row + before
    place = sum(bins[b] * both[b * rows : (b + 1) * rows] for b in range(CZ))
    for b in range(CZ):
        starts_ref[b : b + 1, :] = before[b * rows : b * rows + 1, :]
    planes[...] = place
    for row in range(rows):
        place_ref[0:1, 128 * row : 128 * row + 128] = planes[row : row + 1, :]

    width = math.gcd(atoms, CHUNK)
    y0 = lax.axis_index("pencil") * CY
    moved[...] = jnp.zeros_like(moved)

    @pl.loop(0, atoms // width)
    def _(step):
        here = pl.ds(pl.multiple_of(step * width, width), width)
        line = own[1:2, here].astype(jnp.int32) - y0
        column = own[2:3, here].astype(jnp.int32)
        to = place_ref[0:1, here].astype(jnp.int32)
        at_row = iota16((rows, width), 0) == (to >> 7).astype(jnp.int16)
        none = jnp.zeros((), jnp.bfloat16)
        fields = [
            jnp.where(at_row, part.astype(jnp.float32).astype(jnp.bfloat16), none)
            for part in (line, column & 255, column >> 8)
        ]
        moved[...] += lax.dot_general(
            jnp.concatenate(fields, axis=0),
            one_hot((to & 127).astype(jnp.int16), 128),
            (((1,), (1,)), ((), ())),
            preferred_element_type=jnp.float32,
        )

    moved[rows : 2 * rows, :] += 256.0 * moved[2 * rows : 3 * rows, :]
    for row in range(rows):
        there = slice(128 * row, 128 * row + 128)
        sorted_ref[0:1, there] = moved[row : row + 1, :]
        sorted_ref[1:2, there] = moved[rows + row : rows + row + 1, :]


def pair_lines(wide0, paired, first, last):
    @pl.loop(first, last)
    def _(plane):
        values = wide0[plane]
        for b in (1, 2):
            paired[b - 1, plane] = pltpu.roll(values, b, 0) + pltpu.roll(values, 48 - b, 0)


def near_field(wide0, paired, base, first, last, before):
    @pl.loop(first, last)
    def _(plane):
        def rows_of(block):
            rows = pl.ds(8 * block, 8)

            def near(b, k):
                if b:
                    return paired[b - 1, plane + 2 + k, rows, :]
                return wide0[plane + 2 + k, rows, :]

            table = {}
            for b in range(3):
                table[0, b] = near(b, 0)
                for a in (1, 2):
                    table[a, b] = near(b, a) + near(b, -a)
            groups = grouped(table)
            total = base[plane, rows, :] if before else None
            for c in range(3):
                part = sum(near_weight(c * c + k) * groups[k] for k in SQUARES)
                part = pair_x(part, c) if c else part
                total = part if total is None else total + part
            base[plane, rows, :] = total

        for block in range(1, 5):
            rows_of(block)

        @pl.when((plane >= 2) & (plane < 2 + CZ))
        def _():
            for block in (0, 5):
                rows_of(block)

        @pl.when((plane < 2) | (plane >= 2 + CZ))
        def _():
            for begin in (0, 40):
                base[plane, begin : begin + 8, :] = jnp.zeros((8, NX), jnp.float32)


def clear_outside(slabs, pencils, base):
    slab = lax.axis_index("slab")
    pencil = lax.axis_index("pencil")

    flat = jnp.zeros((2, 48, NX), jnp.float32)
    edge = jnp.zeros((12, 8, NX), jnp.float32)

    @pl.when(slab == 0)
    def _():
        base[0:2] = flat

    @pl.when(slab == slabs - 1)
    def _():
        base[10:12] = flat

    @pl.when(pencil == 0)
    def _():
        base[:, 0:8, :] = edge

    @pl.when(pencil == pencils - 1)
    def _():
        base[:, 40:48, :] = edge


def exchange_kernel(
    slabs,
    pencils,
    own,
    base,
    place_ref,
    sorted_ref,
    starts_ref,
    wide0,
    paired,
    wide1,
    wide2,
    wide3,
    planes,
    moved,
    below,
    above,
    total,
    total_below,
    total_above,
    field1,
    field2,
    field3,
    along_x,
    flat1,
    flat2,
    flat3,
    lined_high,
    lined_low,
    send,
    recv,
    send2,
    recv2,
    send3,
    recv3,
):
    slab = lax.axis_index("slab")
    pencil = lax.axis_index("pencil")
    atoms = own.shape[1]
    for ref in (wide0, wide1, wide2, total, total_below, total_above):
        ref[...] = jnp.zeros_like(ref)

    def along_pencil(step):
        return (slab, lax.rem(pencil + step, pencils))

    def along_slab(step):
        return (lax.rem(slab + step, slabs), pencil)

    barrier = pltpu.get_barrier_semaphore()

    @pl.loop(1, pencils)
    def _(step):
        pl.semaphore_signal(barrier, inc=1, device_id=along_pencil(step), device_id_type=MESH)

    @pl.loop(1, slabs)
    def _(step):
        pl.semaphore_signal(barrier, inc=1, device_id=along_slab(step), device_id_type=MESH)

    sort_atoms(own, planes, place_ref, sorted_ref, starts_ref, moved)
    pl.semaphore_wait(barrier, slabs + pencils - 2)

    def inside(dz, dy):
        z = slab + dz
        y = pencil + dy
        return (z >= 0) & (z < slabs) & (y >= 0) & (y < pencils)

    copies = []

    def add(source, target, dz, dy):
        copies.append((source, target, dz, dy))
        return len(copies) - 1

    parts = [(0, atoms // 2), (atoms // 2, atoms)]
    to_above = [add(own.at[:, a:b], below.at[:, a:b], 1, 0) for a, b in parts]
    to_below = [add(own.at[:, a:b], above.at[:, a:b], -1, 0) for a, b in parts]
    lines0 = {1: (36, 4), -1: (8, 40)}
    middle_y = [
        add(wide0.at[4:12, a : a + 4], wide0.at[4:12, b : b + 4], 0, dy)
        for dy, (a, b) in lines0.items()
    ]
    below_y = [
        add(wide0.at[0:4, a : a + 4], wide0.at[0:4, b : b + 4], 0, dy)
        for dy, (a, b) in lines0.items()
    ]
    above_y = [
        add(wide0.at[12:16, a : a + 4], wide0.at[12:16, b : b + 4], 0, dy)
        for dy, (a, b) in lines0.items()
    ]
    one_y, one_y_above = (
        [
            add(wide1.at[some, a : a + 4], wide1.at[some, b : b + 4], 0, dy)
            for dy, a, b in ((1, 20, 4), (-1, 8, 24))
        ]
        for some in (slice(0, 8), slice(8, 12))
    )
    two_z = [
        add(wide2.at[4:6], wide2.at[4 - 2 * dz : 6 - 2 * dz], dz, 0) for dz in (-2, -1, 1, 2)
    ]

    def copy_of(index, device):
        source, target, _, _ = copies[index]
        return pltpu.make_async_remote_copy(
            src_ref=source,
            dst_ref=target,
            send_sem=send.at[index],
            recv_sem=recv.at[index],
            device_id=device,
            device_id_type=MESH,
        )

    def start(indices, also=True):
        for index in indices:
            _, _, dz, dy = copies[index]

            @pl.when(inside(dz, dy) & also)
            def _(index=index, dz=dz, dy=dy):
                copy_of(index, (slab + dz, pencil + dy)).start()

    def arrived(indices, also=True):
        for index in indices:
            _, _, dz, dy = copies[index]

            @pl.when(inside(-dz, -dy) & also)
            def _(index=index, dz=dz, dy=dy):
                copy_of(index, (slab - dz, pencil - dy)).wait_recv()

    def sent(indices, also=True):
        for index in indices:
            _, _, dz, dy = copies[index]

            @pl.when(inside(dz, dy) & also)
            def _(index=index, dz=dz, dy=dy):
                copy_of(index, (slab + dz, pencil + dy)).wait_send()

    def pencil_copy(step):
        lines = pl.ds(pl.multiple_of(8 * pencil, 8), 8)
        return pltpu.make_async_remote_copy(
            src_ref=wide2.at[4:6, lines],
            dst_ref=wide2.at[4:6, lines],
            send_sem=send2.at[step],
            recv_sem=recv2.at[step],
            device_id=along_pencil(step),
            device_id_type=MESH,
        )

    def pencil_arrival(step):
        lines = pl.ds(pl.multiple_of(8 * lax.rem(pencil + pencils - step, pencils), 8), 8)
        return pltpu.make_async_remote_copy(
            src_ref=wide2.at[4:6, lines],
            dst_ref=wide2.at[4:6, lines],
            send_sem=send2.at[step],
            recv_sem=recv2.at[step],
            device_id=along_pencil(step),
            device_id_type=MESH,
        )

    def top_copy(step, slot):
        return pltpu.make_async_remote_copy(
            src_ref=wide3.at[slot],
            dst_ref=wide3.at[slot],
            send_sem=send3.at[step],
            recv_sem=recv3.at[step],
            device_id=along_slab(step),
            device_id_type=MESH,
        )

    for part in zip(to_above, to_below, strict=True):
        start(part)
    deposit(own, 0, atoms, total, CZ * slab, CZ)
    grid = total[...]
    wide0[4:12, 8:40, :] = grid.reshape(CZ, CY, NX)
    start(middle_y)
    one = halve(grid, ROWS // 4, 5, NX // 2)
    wide1[4:8, 8:24, :] = one.reshape(CZ // 2, CY // 2, NX // 2)
    two = halve(one, ROWS // 16, 4, NX // 4)
    wide2[4:6, pl.ds(pl.multiple_of(8 * pencil, 8), 8), :] = two.reshape(
        CZ // 4, CY // 4, NX // 4
    )
    for step in range(1, pencils):
        pencil_copy(step).start()

    has_below = slab > 0
    has_above = slab < slabs - 1

    def from_below(part):
        begin, end = parts[part]
        arrived([to_above[part]])

        @pl.when(has_below)
        def _():
            deposit(below, begin, end, total_below, CZ * slab - 4, 4, CZ * slab - 8)

    def from_above(part):
        begin, end = parts[part]
        arrived([to_below[part]])

        @pl.when(has_above)
        def _():
            deposit(above, begin, end, total_above, CZ * slab + CZ, 4, CZ * slab + CZ + 4)

    from_below(0)
    from_above(0)
    for step in range(1, pencils):
        pencil_arrival(step).wait_recv()
    start(two_z)
    lines2 = 8 * pencils
    three = halve(
        wide2[4:6].reshape(2 * lines2, NX // 4), lines2 // 2, lines2.bit_length() - 1, NX // 4
    )
    wide3[pl.ds(slab, 1)] = three[None]

    @pl.loop(1, slabs)
    def _(step):
        top_copy(step, slab).start()

    from_below(1)

    @pl.when(has_below)
    def _():
        halo = total_below[...]
        wide0[0:4, 8:40, :] = halo[0 : 4 * CY].reshape(4, CY, NX)
        wide1[0:4, 8:24, :] = halve_halo(halo, CY).reshape(4, CY // 2, NX // 2)

    start(below_y, has_below)
    start(one_y)
    from_above(1)

    @pl.when(has_above)
    def _():
        halo = total_above[...]
        wide0[12:16, 8:40, :] = halo[0 : 4 * CY].reshape(4, CY, NX)
        wide1[8:12, 8:24, :] = halve_halo(halo, 0).reshape(4, CY // 2, NX // 2)

    start(above_y, has_above)
    start(one_y_above, has_above)
    interpolate_x(along_x)
    arrived(middle_y)
    arrived(below_y, has_below)
    pair_lines(wide0, paired, 0, 12)
    near_field(wide0, paired, base, 0, 8, before=False)
    arrived(two_z)
    field_of(wide2, field2, 3, 2)

    @pl.loop(1, slabs)
    def _(step):
        copy = top_copy(step, lax.rem(slab + slabs - step, slabs))
        copy.wait_send()
        copy.wait_recv()

    upper_fields(slabs, pencils, wide3, field3)
    arrived(one_y)
    arrived(one_y_above, has_above)
    field_of(wide1, field1, 2, 1)
    interpolate(
        slabs,
        pencils,
        (field1, field2, field3),
        (flat1, flat2, flat3),
        along_x,
        lined_high,
        lined_low,
        base,
    )
    for step in range(1, pencils):
        pencil_copy(step).wait_send()
    sent([*to_above, *to_below, *middle_y, *two_z, *one_y])
    sent(one_y_above, has_above)
    arrived(above_y, has_above)
    pair_lines(wide0, paired, 12, 16)
    near_field(wide0, paired, base, 8, 12, before=True)
    clear_outside(slabs, pencils, base)
    sent(below_y, has_below)
    sent(above_y, has_above)


def exchange_call(slabs, pencils, own):
    atoms = own.shape[1]
    shapes = (
        (12, 48, NX),
        (1, atoms),
        (2, atoms),
        (CZ, 128),
    )
    field3_rows = sum(4 * max((pencils * CY) >> level, 8) for level in (3, 4, 5))
    return pl.pallas_call(
        functools.partial(exchange_kernel, slabs, pencils),
        out_shape=[jax.ShapeDtypeStruct(shape, jnp.float32) for shape in shapes],
        in_specs=[VMEM],
        out_specs=[VMEM] * 4,
        scratch_shapes=[
            pltpu.VMEM((16, 48, NX), jnp.float32),
            pltpu.VMEM((2, 16, 48, NX), jnp.float32),
            pltpu.VMEM((12, 32, NX // 2), jnp.float32),
            pltpu.VMEM((10, 8 * pencils, NX // 4), jnp.float32),
            pltpu.VMEM((slabs, 4 * pencils, 128), jnp.float32),
            pltpu.VMEM((atoms // 128, 128), jnp.float32),
            pltpu.VMEM((3 * atoms // 128, 128), jnp.float32),
            pltpu.VMEM((4, atoms), jnp.float32),
            pltpu.VMEM((4, atoms), jnp.float32),
            pltpu.VMEM((ROWS, NX), jnp.float32),
            pltpu.VMEM((5 * CY, NX), jnp.float32),
            pltpu.VMEM((5 * CY, NX), jnp.float32),
            pltpu.VMEM((8 * 32, NX // 2), jnp.float32),
            pltpu.VMEM((4 * 8 * pencils, NX // 4), jnp.float32),
            pltpu.VMEM((field3_rows, 128), jnp.float32),
            pltpu.VMEM((NX, NX), jnp.bfloat16),
            pltpu.VMEM((2 * 32, 12 * 256), jnp.float32),
            pltpu.VMEM((2 * 8 * pencils, 12 * 128), jnp.float32),
            pltpu.VMEM((2 * field3_rows // 4, 12 * 128), jnp.float32),
            pltpu.VMEM((12 * 48, NX), jnp.bfloat16),
            pltpu.VMEM((12 * 48, NX), jnp.bfloat16),
            pltpu.SemaphoreType.DMA((18,)),
            pltpu.SemaphoreType.DMA((18,)),
            pltpu.SemaphoreType.DMA((pencils,)),
            pltpu.SemaphoreType.DMA((pencils,)),
            pltpu.SemaphoreType.DMA((slabs,)),
            pltpu.SemaphoreType.DMA((slabs,)),
        ],
        cost_estimate=pl.CostEstimate(flops=10**10, bytes_accessed=2**23, transcendentals=0),
        compiler_params=pltpu.CompilerParams(
            collective_id=0, has_side_effects=True, vmem_limit_bytes=40 * 2**20
        ),
    )(own)


def field_kernel(
    own_ref,
    place_ref,
    sorted_ref,
    starts_ref,
    wide_pot,
    pot_ref,
    force_ref,
    slopes,
    bounds,
    found,
    by_row,
):
    def slope(after1, before1, after2, before2):
        return (8.0 * (after1 - before1) - (after2 - before2)) * (1.0 / 12.0)

    atoms = own_ref.shape[1]
    for plane in range(CZ):
        bounds[plane] = jnp.max(starts_ref[plane : plane + 1, :]).astype(jnp.int32)
    bounds[CZ] = jnp.int32(atoms)
    found[...] = jnp.zeros_like(found)
    size = math.gcd(atoms, 1024)

    @pl.loop(0, CZ)
    def _(plane):
        middle = wide_pot[plane + 2]
        own = middle[8:40]
        pot_ref[plane] = own
        at = [wide_pot[plane + 2 + k, 8:40, :] for k in (1, -1, 2, -2)]
        across = [pltpu.roll(middle, (-k) % 48, 0)[8:40] for k in (1, -1, 2, -2)]
        along = [shift_x(own, k) for k in (1, -1, 2, -2)]
        for direction, four in enumerate((at, across, along)):
            high, low = split_two(slope(*four))
            slopes[2 * direction * CY : (2 * direction + 1) * CY, :] = high
            slopes[(2 * direction + 1) * CY : (2 * direction + 2) * CY, :] = low
        first = bounds[plane]
        last = bounds[plane + 1]

        def block(step, carry):
            begin = pl.multiple_of(step * size, size)
            here = pl.ds(begin, size)
            table = one_hot(sorted_ref[1:2, here].astype(jnp.int32).astype(jnp.int16), NX)
            at_cell = jnp.dot(slopes[...], table, preferred_element_type=jnp.float32)
            index = begin + iota((1, size), 1)
            line = sorted_ref[0:1, here].astype(jnp.int32)
            line = jnp.where((index >= first) & (index < last), line, -1)
            at_row = iota((CY, size), 0) == line
            for direction in range(3):
                high = at_cell[2 * direction * CY : (2 * direction + 1) * CY]
                low = at_cell[(2 * direction + 1) * CY : (2 * direction + 2) * CY]
                found[direction : direction + 1, here] += jnp.sum(
                    jnp.where(at_row, high + low, 0.0), axis=0, keepdims=True
                )
            return carry

        lax.fori_loop(first // size, (last + size - 1) // size, block, 0)

    rows = atoms // 128
    for direction in range(3):
        for row in range(rows):
            there = slice(128 * row, 128 * row + 128)
            by_row[direction * rows + row : direction * rows + row + 1, :] = found[
                direction : direction + 1, there
            ]
    high, low = split_two(by_row[...])
    split = jnp.concatenate([high, low], axis=0)
    width = math.gcd(atoms, CHUNK)

    @pl.loop(0, atoms // width)
    def _(step):
        here = pl.ds(pl.multiple_of(step * width, width), width)
        to = place_ref[0:1, here].astype(jnp.int32)
        table = one_hot((to & 127).astype(jnp.int16), 128)
        values = jnp.dot(split, table, preferred_element_type=jnp.float32)
        at_row = iota((rows, width), 0) == to >> 7
        charges = own_ref[3:4, here]
        for direction in range(3):
            high = values[direction * rows : (direction + 1) * rows]
            low = values[(3 + direction) * rows : (4 + direction) * rows]
            chosen = jnp.sum(jnp.where(at_row, high + low, 0.0), axis=0, keepdims=True)
            force_ref[direction : direction + 1, here] = -charges * chosen


def field_call(base, own, order):
    atoms = own.shape[1]
    return pl.pallas_call(
        field_kernel,
        out_shape=[
            jax.ShapeDtypeStruct((CZ, CY, NX), jnp.float32),
            jax.ShapeDtypeStruct((3, atoms), jnp.float32),
        ],
        in_specs=[VMEM] * 5,
        out_specs=[VMEM] * 2,
        scratch_shapes=[
            pltpu.VMEM((6 * CY, NX), jnp.bfloat16),
            pltpu.SMEM((CZ + 1,), jnp.int32),
            pltpu.VMEM((3, atoms), jnp.float32),
            pltpu.VMEM((3 * atoms // 128, 128), jnp.float32),
        ],
        cost_estimate=pl.CostEstimate(flops=2 * 10**10, bytes_accessed=2**23, transcendentals=0),
        compiler_params=pltpu.CompilerParams(vmem_limit_bytes=40 * 2**20),
    )(own, *order, base)


def solution(mesh):
    slabs = mesh.shape["slab"]
    pencils = mesh.shape["pencil"]

    def body(atom_cell, charge):
        own = jnp.concatenate([atom_cell.astype(jnp.float32), charge[None]], axis=0)
        base, *order = exchange_call(slabs, pencils, own)
        potential, forces = field_call(base, own, order)
        return (potential, forces)

    return jax.shard_map(
        body,
        mesh=mesh,
        in_specs=(P(None, ("slab", "pencil")), P(("slab", "pencil"))),
        out_specs=(P("slab", "pencil", None), P(None, ("slab", "pencil"))),
        check_vma=False,
    )
```

```python
import functools
import math

import jax
import jax.numpy as jnp
from jax import lax
from jax.experimental import pallas as pl
from jax.experimental.pallas import tpu as pltpu
from jax.sharding import PartitionSpec as P

CZ = 8
CY = 32
NX = 512
F = 32
ROWS = CZ * CY
CHUNK = 4096
MESH = pl.DeviceIdType.MESH
VMEM = pl.BlockSpec(memory_space=pltpu.VMEM)
SQUARES = (0, 1, 2, 4, 5, 8)


def iota(shape, dim):
    return lax.broadcasted_iota(jnp.int32, shape, dim)


def iota16(shape, dim):
    return iota(shape, dim).astype(jnp.int16)


def one_hot(places, size):
    here = iota16((size, places.shape[1]), 0) == places
    return jnp.where(here, jnp.ones((), jnp.bfloat16), jnp.zeros((), jnp.bfloat16))


def near_weight(squared):
    return 1.0 / math.sqrt(squared + 0.25) - 1.0 / math.sqrt(squared + 4.0)


def level_weight(level, squared):
    return (1.0 / math.sqrt(squared + 1.0) - 1.0 / math.sqrt(squared + 4.0)) / 2**level


def split_two(values):
    high = values.astype(jnp.bfloat16)
    return high, (values - high.astype(jnp.float32)).astype(jnp.bfloat16)


def dot32(left, right):
    left_high, left_low = split_two(left)
    right_high, right_low = split_two(right)
    total = jnp.dot(left_high, right_high, preferred_element_type=jnp.float32)
    total += jnp.dot(left_high, right_low, preferred_element_type=jnp.float32)
    return total + jnp.dot(left_low, right_high, preferred_element_type=jnp.float32)


def halve_rows(rows_out, rows_in, line_bits):
    out_row = iota((rows_out, rows_in), 0)
    in_row = iota((rows_out, rows_in), 1)
    plane = in_row >> (line_bits + 1)
    line = (in_row & (2**line_bits - 1)) >> 1
    return jnp.where((plane << (line_bits - 1)) + line == out_row, 1.0, 0.0).astype(jnp.bfloat16)


def halve_columns(columns_in, columns_out):
    return jnp.where(
        iota((columns_in, columns_out), 0) >> 1 == iota((columns_in, columns_out), 1), 1.0, 0.0
    ).astype(jnp.bfloat16)


def halve(values, rows_out, line_bits, columns_out):
    rows, columns = values.shape
    left = halve_rows(rows_out, rows, line_bits)
    high, low = split_two(values)
    part = jnp.dot(left, high, preferred_element_type=jnp.float32)
    part += jnp.dot(left, low, preferred_element_type=jnp.float32)
    right = halve_columns(columns, columns_out)
    high, low = split_two(part)
    whole = jnp.dot(high, right, preferred_element_type=jnp.float32)
    return whole + jnp.dot(low, right, preferred_element_type=jnp.float32)


def deposit(atoms_ref, begin, end, total_ref, first_plane, planes, far_plane=None):
    near_rows = planes * CY
    rows = near_rows if far_plane is None else near_rows + CY
    width = math.gcd(end - begin, CHUNK)
    fresh = begin == 0 and width == end
    y0 = lax.axis_index("pencil") * CY

    @pl.loop(0, (end - begin) // width)
    def _(step):
        here = pl.ds(pl.multiple_of(begin + step * width, width), width)
        plane = atoms_ref[0:1, here].astype(jnp.int32) - first_plane
        line = atoms_ref[1:2, here].astype(jnp.int32) - y0
        columns = atoms_ref[2:3, here].astype(jnp.int32).astype(jnp.int16)
        high, low = split_two(atoms_ref[3:4, here])
        place = plane * CY + line
        if far_plane is not None:
            far = ((plane + first_plane - far_plane) >> 1) * (CY // 2) + (line >> 1)
            place = jnp.where((plane >= 0) & (plane < planes), place, near_rows + far)
        at_row = iota16((rows, width), 0) == place.astype(jnp.int16)
        none = jnp.zeros((), jnp.bfloat16)
        stacked = jnp.concatenate(
            [jnp.where(at_row, high, none), jnp.where(at_row, low, none)], axis=0
        )
        added = lax.dot_general(
            stacked,
            one_hot(columns, NX),
            (((1,), (1,)), ((), ())),
            preferred_element_type=jnp.float32,
        )
        added = added[:rows] + added[rows:]
        if fresh:
            total_ref[0:rows, :] = added
        else:
            total_ref[0:rows, :] += added


def shift_x(values, step):
    width = values.shape[-1]
    axis = values.ndim - 1
    column = iota(values.shape, axis)
    moved = pltpu.roll(values, (-step) % width, axis)
    return jnp.where((column + step >= 0) & (column + step < width), moved, 0.0)


def pair_x(values, step):
    return shift_x(values, step) + shift_x(values, -step)


def hat(fine, cell, factor, count):
    bits = factor.bit_length()
    numerator = jnp.clip(2 * fine + 1 - factor, 0, 2 * factor * (count - 1))
    lower = jnp.minimum(numerator >> bits, count - 2)
    fraction = (numerator - (lower << bits)).astype(jnp.float32) * (0.5 / factor)
    return jnp.where(
        cell == lower, 1.0 - fraction, jnp.where(cell == lower + 1, fraction, 0.0)
    )


def shift_y(values, step):
    lines = values.shape[0]
    line = iota(values.shape, 0) + step
    return jnp.where((line >= 0) & (line < lines), pltpu.roll(values, (-step) % lines, 0), 0.0)


def field_of(wide, field, shift, level):
    lines = wide.shape[1]

    @pl.loop(0, field.shape[0] // lines)
    def _(plane):
        table = {}
        for a in range(3):
            line = wide[plane + shift]
            if a:
                line = wide[plane + shift + a] + wide[plane + shift - a]
            table[a, 0] = line
            for b in (1, 2):
                table[a, b] = shift_y(line, b) + shift_y(line, -b)
        groups = grouped(table)
        total = None
        for c in range(3):
            part = sum(level_weight(level, c * c + k) * groups[k] for k in SQUARES)
            total = total + pair_x(part, c) if c else part
        field[pl.ds(pl.multiple_of(plane * lines, lines), lines), :] = total


def grouped(table):
    return {
        0: table[0, 0],
        1: table[0, 1] + table[1, 0],
        2: table[1, 1],
        4: table[0, 2] + table[2, 0],
        5: table[1, 2] + table[2, 1],
        8: table[2, 2],
    }


def upper_fields(slabs, pencils, wide3, field3):
    slab = lax.axis_index("slab")
    pencil_bits = pencils.bit_length() - 1
    rows3 = slabs * pencils * 4
    grid3 = wide3[...].reshape(rows3, 128)
    first_row = 0
    first_lane = 0
    for level in (3, 4, 5):
        down = level - 3
        line_bits = pencil_bits + 2 - down
        lines = 2**line_bits
        planes = slabs >> down
        count = planes * lines
        length = NX >> level
        if level == 3:
            charges = grid3
        else:
            shape = (count, rows3)
            out_row = iota(shape, 0)
            in_row = iota(shape, 1)
            in_plane = in_row >> (2 + pencil_bits)
            in_line = in_row & (4 * pencils - 1)
            cell = ((in_plane >> down) << line_bits) + (in_line >> down)
            charges = dot32(jnp.where(cell == out_row, 1.0, 0.0), grid3)
        reach = 3 if level < 5 else length
        source = iota((128, 128), 0) >> down
        column = iota((128, 128), 1) - first_lane
        valid = (column >= 0) & (column < length)
        pairs = jnp.concatenate(
            [
                jnp.where(valid & (jnp.abs(source - column) == c), 1.0, 0.0)
                for c in range(reach)
            ],
            axis=1,
        )
        moved = dot32(charges, pairs)
        stacked = jnp.concatenate(
            [moved[:, c * 128 : (c + 1) * 128] for c in range(reach)], axis=0
        )
        out_bits = max(line_bits, 3)
        shape = (4 << out_bits, reach * count)
        across = iota(shape, 1) >> (count.bit_length() - 1)
        source = iota(shape, 1) & (count - 1)
        dz = (source >> line_bits) - (iota(shape, 0) >> out_bits) - ((slab >> down) - 1)
        dy = (source & (lines - 1)) - (iota(shape, 0) & (2**out_bits - 1))
        squared = (dz * dz + dy * dy + across * across).astype(jnp.float32)
        weight = 1.0 / jnp.sqrt(squared + 1.0)
        if level < 5:
            weight = (weight - 1.0 / jnp.sqrt(squared + 4.0)) / 2**level
            weight = jnp.where((jnp.abs(dz) <= 2) & (jnp.abs(dy) <= 2), weight, 0.0)
        else:
            weight = weight / F
        field3[first_row : first_row + (4 << out_bits), :] = dot32(weight, stacked)
        first_row = first_row + (4 << out_bits)
        first_lane = first_lane + length


def interpolate_x(along_x):
    lane = 0
    for level in range(1, 6):
        length = NX >> level
        rows = length if level < 5 else NX - lane
        weights = hat(iota((rows, NX), 1), iota((rows, NX), 0), 2**level, length)
        weights = jnp.where(iota((rows, NX), 0) < length, weights, 0.0)
        along_x[lane : lane + rows, :] = weights.astype(jnp.bfloat16)
        lane = lane + rows


def interpolate(slabs, pencils, fields, flats, along_x, lined_high, lined_low, base):
    slab = lax.axis_index("slab")
    pencil = lax.axis_index("pencil")
    upper = pencils * CY
    padded = [max(upper >> level, 8) for level in (3, 4, 5)]
    layers = [
        (1, 4 * slab - 2, 32, 16 * pencil - 8),
        (2, 2 * slab - 1, upper >> 2, 0),
    ]
    layers += [
        (level, (slab >> (level - 3)) - 1, lines, 0)
        for level, lines in zip((3, 4, 5), padded, strict=True)
    ]
    starts = [0, 0, 0, 4 * padded[0], 4 * (padded[0] + padded[1])]
    tops = [0, 0, 0, padded[0], padded[0] + padded[1]]
    field1, field2, field3 = fields
    flat1, flat2, flat3 = flats
    fields = [field1, field2, field3, field3, field3]
    flats = [flat1, flat2, flat3, flat3, flat3]

    for plane in range(12):
        fine_z = CZ * slab - 2 + plane
        for (level, plane0, lines, _), begin, top, field, flat in zip(
            layers, starts, tops, fields, flats, strict=True
        ):
            factor = 2**level
            count = (slabs * CZ) >> level
            numerator = jnp.clip(2 * fine_z + 1 - factor, 0, 2 * factor * (count - 1))
            lower = jnp.minimum(numerator >> (level + 1), count - 2)
            fraction = (numerator - (lower << (level + 1))).astype(jnp.float32) * (0.5 / factor)
            row = begin + (lower - plane0) * lines
            row = pl.multiple_of(row, 8)
            mixed = (1.0 - fraction) * field[pl.ds(row, lines), :]
            mixed += fraction * field[pl.ds(row + lines, lines), :]
            high, low = split_two(mixed)
            width = field.shape[1]
            there = slice(plane * width, (plane + 1) * width)
            flat[top : top + lines, there] = high.astype(jnp.float32)
            flat[flat.shape[0] // 2 + top : flat.shape[0] // 2 + top + lines, there] = low.astype(
                jnp.float32
            )

    def along_y(some):
        blocks = []
        for level, _, lines, line0 in some:
            shape = (48, lines)
            fine_y = CY * pencil - 8 + iota(shape, 0)
            blocks.append(hat(fine_y, line0 + iota(shape, 1), 2**level, upper >> level))
        return jnp.concatenate(blocks + blocks, axis=1).astype(jnp.bfloat16)

    for some, flat, first in ((layers[:1], flat1, 0), (layers[1:2], flat2, 256), (layers[2:], flat3, 384)):
        width = flat.shape[1] // 12
        lined = jnp.dot(
            along_y(some), flat[...].astype(jnp.bfloat16), preferred_element_type=jnp.float32
        )
        high, low = split_two(lined)
        for plane in range(12):
            there = slice(plane * width, (plane + 1) * width)
            rows = slice(48 * plane, 48 * plane + 48)
            lined_high[rows, first : first + width] = high[:, there]
            lined_low[rows, first : first + width] = low[:, there]

    fine = jnp.dot(lined_high[...], along_x[...], preferred_element_type=jnp.float32)
    fine += jnp.dot(lined_low[...], along_x[...], preferred_element_type=jnp.float32)
    fine = fine.reshape(12, 48, NX)
    base[0:8] += fine[0:8]
    base[8:12] = fine[8:12]


def halve_halo(total, near_first):
    out_row = iota((2 * CY, 5 * CY), 0)
    in_row = iota((2 * CY, 5 * CY), 1)
    near = ((in_row >> 6) << 4) + ((in_row & (CY - 1)) >> 1) + near_first
    far = in_row - 4 * CY + (CY - near_first)
    chosen = jnp.where(in_row < 4 * CY, near, far) == out_row
    left = jnp.where(chosen, 1.0, 0.0).astype(jnp.bfloat16)
    high, low = split_two(total)
    part = jnp.dot(left, high, preferred_element_type=jnp.float32)
    part += jnp.dot(left, low, preferred_element_type=jnp.float32)
    right = halve_columns(NX, NX // 2)
    high, low = split_two(part)
    whole = jnp.dot(high, right, preferred_element_type=jnp.float32)
    return whole + jnp.dot(low, right, preferred_element_type=jnp.float32)


def sort_atoms(own, planes, place_ref, sorted_ref, starts_ref, moved):
    atoms = own.shape[1]
    rows = atoms // 128
    for row in range(rows):
        planes[row : row + 1, :] = own[0:1, 128 * row : 128 * row + 128]
    plane = planes[...].astype(jnp.int32) - lax.axis_index("slab") * CZ
    bins = [jnp.where(plane == b, 1.0, 0.0) for b in range(CZ)]
    stacked = jnp.concatenate(bins, axis=0).astype(jnp.bfloat16)
    earlier = iota((128, 128), 0) < iota((128, 128), 1)
    earlier = jnp.where(earlier, 1.0, 0.0).astype(jnp.bfloat16)
    both = jnp.concatenate([earlier, jnp.ones((128, 128), jnp.bfloat16)], axis=1)
    counts = jnp.dot(stacked, both, preferred_element_type=jnp.float32)
    in_row = counts[:, :128]
    of_row = counts[:, 128:].astype(jnp.bfloat16)
    size = (CZ * rows, CZ * rows)
    above = jnp.where(iota(size, 1) < iota(size, 0), 1.0, 0.0).astype(jnp.bfloat16)
    before = jnp.dot(above, of_row, preferred_element_type=jnp.float32)
    both = in_row + before
    place = sum(bins[b] * both[b * rows : (b + 1) * rows] for b in range(CZ))
    for b in range(CZ):
        starts_ref[b : b + 1, :] = before[b * rows : b * rows + 1, :]
    planes[...] = place
    for row in range(rows):
        place_ref[0:1, 128 * row : 128 * row + 128] = planes[row : row + 1, :]

    width = math.gcd(atoms, CHUNK)
    y0 = lax.axis_index("pencil") * CY
    moved[...] = jnp.zeros_like(moved)

    @pl.loop(0, atoms // width)
    def _(step):
        here = pl.ds(pl.multiple_of(step * width, width), width)
        line = own[1:2, here].astype(jnp.int32) - y0
        column = own[2:3, here].astype(jnp.int32)
        to = place_ref[0:1, here].astype(jnp.int32)
        at_row = iota16((rows, width), 0) == (to >> 7).astype(jnp.int16)
        none = jnp.zeros((), jnp.bfloat16)
        fields = [
            jnp.where(at_row, part.astype(jnp.float32).astype(jnp.bfloat16), none)
            for part in (line, column & 255, column >> 8)
        ]
        moved[...] += lax.dot_general(
            jnp.concatenate(fields, axis=0),
            one_hot((to & 127).astype(jnp.int16), 128),
            (((1,), (1,)), ((), ())),
            preferred_element_type=jnp.float32,
        )

    moved[rows : 2 * rows, :] += 256.0 * moved[2 * rows : 3 * rows, :]
    for row in range(rows):
        there = slice(128 * row, 128 * row + 128)
        sorted_ref[0:1, there] = moved[row : row + 1, :]
        sorted_ref[1:2, there] = moved[rows + row : rows + row + 1, :]


def pair_lines(wide0, paired, first, last):
    @pl.loop(first, last)
    def _(plane):
        values = wide0[plane]
        for b in (1, 2):
            paired[b - 1, plane] = pltpu.roll(values, b, 0) + pltpu.roll(values, 48 - b, 0)


def near_field(wide0, paired, base, first, last, before):
    @pl.loop(first, last)
    def _(plane):
        for block in range(6):
            rows = pl.ds(8 * block, 8)

            def near(b, k):
                if b:
                    return paired[b - 1, plane + 2 + k, rows, :]
                return wide0[plane + 2 + k, rows, :]

            table = {}
            for b in range(3):
                table[0, b] = near(b, 0)
                for a in (1, 2):
                    table[a, b] = near(b, a) + near(b, -a)
            groups = grouped(table)
            total = base[plane, rows, :] if before else None
            for c in range(3):
                part = sum(near_weight(c * c + k) * groups[k] for k in SQUARES)
                part = pair_x(part, c) if c else part
                total = part if total is None else total + part
            base[plane, rows, :] = total


def clear_outside(slabs, pencils, base):
    slab = lax.axis_index("slab")
    pencil = lax.axis_index("pencil")

    flat = jnp.zeros((2, 48, NX), jnp.float32)
    edge = jnp.zeros((12, 8, NX), jnp.float32)

    @pl.when(slab == 0)
    def _():
        base[0:2] = flat

    @pl.when(slab == slabs - 1)
    def _():
        base[10:12] = flat

    @pl.when(pencil == 0)
    def _():
        base[:, 0:8, :] = edge

    @pl.when(pencil == pencils - 1)
    def _():
        base[:, 40:48, :] = edge


def exchange_kernel(
    slabs,
    pencils,
    own,
    base,
    place_ref,
    sorted_ref,
    starts_ref,
    wide0,
    paired,
    wide1,
    wide2,
    wide3,
    planes,
    moved,
    below,
    above,
    total,
    total_below,
    total_above,
    field1,
    field2,
    field3,
    along_x,
    flat1,
    flat2,
    flat3,
    lined_high,
    lined_low,
    send,
    recv,
    send2,
    recv2,
    send3,
    recv3,
):
    slab = lax.axis_index("slab")
    pencil = lax.axis_index("pencil")
    atoms = own.shape[1]
    for ref in (wide0, wide1, wide2, total):
        ref[...] = jnp.zeros_like(ref)

    def along_pencil(step):
        return (slab, lax.rem(pencil + step, pencils))

    def along_slab(step):
        return (lax.rem(slab + step, slabs), pencil)

    barrier = pltpu.get_barrier_semaphore()

    @pl.loop(1, pencils)
    def _(step):
        pl.semaphore_signal(barrier, inc=1, device_id=along_pencil(step), device_id_type=MESH)

    @pl.loop(1, slabs)
    def _(step):
        pl.semaphore_signal(barrier, inc=1, device_id=along_slab(step), device_id_type=MESH)

    sort_atoms(own, planes, place_ref, sorted_ref, starts_ref, moved)
    pl.semaphore_wait(barrier, slabs + pencils - 2)

    def inside(dz, dy):
        z = slab + dz
        y = pencil + dy
        return (z >= 0) & (z < slabs) & (y >= 0) & (y < pencils)

    copies = []

    def add(source, target, dz, dy):
        copies.append((source, target, dz, dy))
        return len(copies) - 1

    parts = [(0, atoms // 2), (atoms // 2, atoms)]
    to_above = [add(own.at[:, a:b], below.at[:, a:b], 1, 0) for a, b in parts]
    to_below = [add(own.at[:, a:b], above.at[:, a:b], -1, 0) for a, b in parts]
    lines0 = {1: (36, 4), -1: (8, 40)}
    middle_y = [
        add(wide0.at[4:12, a : a + 4], wide0.at[4:12, b : b + 4], 0, dy)
        for dy, (a, b) in lines0.items()
    ]
    below_y = [
        add(wide0.at[0:4, a : a + 4], wide0.at[0:4, b : b + 4], 0, dy)
        for dy, (a, b) in lines0.items()
    ]
    above_y = [
        add(wide0.at[12:16, a : a + 4], wide0.at[12:16, b : b + 4], 0, dy)
        for dy, (a, b) in lines0.items()
    ]
    one_y, one_y_above = (
        [
            add(wide1.at[some, a : a + 4], wide1.at[some, b : b + 4], 0, dy)
            for dy, a, b in ((1, 20, 4), (-1, 8, 24))
        ]
        for some in (slice(0, 8), slice(8, 12))
    )
    two_z = [
        add(wide2.at[4:6], wide2.at[4 - 2 * dz : 6 - 2 * dz], dz, 0) for dz in (-2, -1, 1, 2)
    ]

    def copy_of(index, device):
        source, target, _, _ = copies[index]
        return pltpu.make_async_remote_copy(
            src_ref=source,
            dst_ref=target,
            send_sem=send.at[index],
            recv_sem=recv.at[index],
            device_id=device,
            device_id_type=MESH,
        )

    def start(indices, also=True):
        for index in indices:
            _, _, dz, dy = copies[index]

            @pl.when(inside(dz, dy) & also)
            def _(index=index, dz=dz, dy=dy):
                copy_of(index, (slab + dz, pencil + dy)).start()

    def arrived(indices, also=True):
        for index in indices:
            _, _, dz, dy = copies[index]

            @pl.when(inside(-dz, -dy) & also)
            def _(index=index, dz=dz, dy=dy):
                copy_of(index, (slab - dz, pencil - dy)).wait_recv()

    def sent(indices, also=True):
        for index in indices:
            _, _, dz, dy = copies[index]

            @pl.when(inside(dz, dy) & also)
            def _(index=index, dz=dz, dy=dy):
                copy_of(index, (slab + dz, pencil + dy)).wait_send()

    def pencil_copy(step):
        lines = pl.ds(pl.multiple_of(8 * pencil, 8), 8)
        return pltpu.make_async_remote_copy(
            src_ref=wide2.at[4:6, lines],
            dst_ref=wide2.at[4:6, lines],
            send_sem=send2.at[step],
            recv_sem=recv2.at[step],
            device_id=along_pencil(step),
            device_id_type=MESH,
        )

    def pencil_arrival(step):
        lines = pl.ds(pl.multiple_of(8 * lax.rem(pencil + pencils - step, pencils), 8), 8)
        return pltpu.make_async_remote_copy(
            src_ref=wide2.at[4:6, lines],
            dst_ref=wide2.at[4:6, lines],
            send_sem=send2.at[step],
            recv_sem=recv2.at[step],
            device_id=along_pencil(step),
            device_id_type=MESH,
        )

    def top_copy(step, slot):
        return pltpu.make_async_remote_copy(
            src_ref=wide3.at[slot],
            dst_ref=wide3.at[slot],
            send_sem=send3.at[step],
            recv_sem=recv3.at[step],
            device_id=along_slab(step),
            device_id_type=MESH,
        )

    for part in zip(to_above, to_below, strict=True):
        start(part)
    deposit(own, 0, atoms, total, CZ * slab, CZ)
    grid = total[...]
    wide0[4:12, 8:40, :] = grid.reshape(CZ, CY, NX)
    start(middle_y)
    one = halve(grid, ROWS // 4, 5, NX // 2)
    wide1[4:8, 8:24, :] = one.reshape(CZ // 2, CY // 2, NX // 2)
    two = halve(one, ROWS // 16, 4, NX // 4)
    wide2[4:6, pl.ds(pl.multiple_of(8 * pencil, 8), 8), :] = two.reshape(
        CZ // 4, CY // 4, NX // 4
    )
    for step in range(1, pencils):
        pencil_copy(step).start()

    has_below = slab > 0
    has_above = slab < slabs - 1

    def from_below(part):
        begin, end = parts[part]
        arrived([to_above[part]])

        @pl.when(has_below)
        def _():
            deposit(below, begin, end, total_below, CZ * slab - 4, 4, CZ * slab - 8)

    def from_above(part):
        begin, end = parts[part]
        arrived([to_below[part]])

        @pl.when(has_above)
        def _():
            deposit(above, begin, end, total_above, CZ * slab + CZ, 4, CZ * slab + CZ + 4)

    from_below(0)
    from_above(0)
    for step in range(1, pencils):
        pencil_arrival(step).wait_recv()
    start(two_z)
    lines2 = 8 * pencils
    three = halve(
        wide2[4:6].reshape(2 * lines2, NX // 4), lines2 // 2, lines2.bit_length() - 1, NX // 4
    )
    wide3[pl.ds(slab, 1)] = three[None]

    @pl.loop(1, slabs)
    def _(step):
        top_copy(step, slab).start()

    from_below(1)

    @pl.when(has_below)
    def _():
        halo = total_below[...]
        wide0[0:4, 8:40, :] = halo[0 : 4 * CY].reshape(4, CY, NX)
        wide1[0:4, 8:24, :] = halve_halo(halo, CY).reshape(4, CY // 2, NX // 2)

    start(below_y, has_below)
    start(one_y)
    from_above(1)

    @pl.when(has_above)
    def _():
        halo = total_above[...]
        wide0[12:16, 8:40, :] = halo[0 : 4 * CY].reshape(4, CY, NX)
        wide1[8:12, 8:24, :] = halve_halo(halo, 0).reshape(4, CY // 2, NX // 2)

    start(above_y, has_above)
    start(one_y_above, has_above)
    interpolate_x(along_x)
    arrived(middle_y)
    arrived(below_y, has_below)
    pair_lines(wide0, paired, 0, 12)
    near_field(wide0, paired, base, 0, 8, before=False)
    arrived(two_z)
    field_of(wide2, field2, 3, 2)

    @pl.loop(1, slabs)
    def _(step):
        copy = top_copy(step, lax.rem(slab + slabs - step, slabs))
        copy.wait_send()
        copy.wait_recv()

    upper_fields(slabs, pencils, wide3, field3)
    arrived(one_y)
    arrived(one_y_above, has_above)
    field_of(wide1, field1, 2, 1)
    interpolate(
        slabs,
        pencils,
        (field1, field2, field3),
        (flat1, flat2, flat3),
        along_x,
        lined_high,
        lined_low,
        base,
    )
    for step in range(1, pencils):
        pencil_copy(step).wait_send()
    sent([*to_above, *to_below, *middle_y, *two_z, *one_y])
    sent(one_y_above, has_above)
    arrived(above_y, has_above)
    pair_lines(wide0, paired, 12, 16)
    near_field(wide0, paired, base, 8, 12, before=True)
    clear_outside(slabs, pencils, base)
    sent(below_y, has_below)
    sent(above_y, has_above)


def exchange_call(slabs, pencils, own):
    atoms = own.shape[1]
    shapes = (
        (12, 48, NX),
        (1, atoms),
        (2, atoms),
        (CZ, 128),
    )
    field3_rows = sum(4 * max((pencils * CY) >> level, 8) for level in (3, 4, 5))
    return pl.pallas_call(
        functools.partial(exchange_kernel, slabs, pencils),
        out_shape=[jax.ShapeDtypeStruct(shape, jnp.float32) for shape in shapes],
        in_specs=[VMEM],
        out_specs=[VMEM] * 4,
        scratch_shapes=[
            pltpu.VMEM((16, 48, NX), jnp.float32),
            pltpu.VMEM((2, 16, 48, NX), jnp.float32),
            pltpu.VMEM((12, 32, NX // 2), jnp.float32),
            pltpu.VMEM((10, 8 * pencils, NX // 4), jnp.float32),
            pltpu.VMEM((slabs, 4 * pencils, 128), jnp.float32),
            pltpu.VMEM((atoms // 128, 128), jnp.float32),
            pltpu.VMEM((3 * atoms // 128, 128), jnp.float32),
            pltpu.VMEM((4, atoms), jnp.float32),
            pltpu.VMEM((4, atoms), jnp.float32),
            pltpu.VMEM((ROWS, NX), jnp.float32),
            pltpu.VMEM((5 * CY, NX), jnp.float32),
            pltpu.VMEM((5 * CY, NX), jnp.float32),
            pltpu.VMEM((8 * 32, NX // 2), jnp.float32),
            pltpu.VMEM((4 * 8 * pencils, NX // 4), jnp.float32),
            pltpu.VMEM((field3_rows, 128), jnp.float32),
            pltpu.VMEM((NX, NX), jnp.bfloat16),
            pltpu.VMEM((2 * 32, 12 * 256), jnp.float32),
            pltpu.VMEM((2 * 8 * pencils, 12 * 128), jnp.float32),
            pltpu.VMEM((2 * field3_rows // 4, 12 * 128), jnp.float32),
            pltpu.VMEM((12 * 48, NX), jnp.bfloat16),
            pltpu.VMEM((12 * 48, NX), jnp.bfloat16),
            pltpu.SemaphoreType.DMA((18,)),
            pltpu.SemaphoreType.DMA((18,)),
            pltpu.SemaphoreType.DMA((pencils,)),
            pltpu.SemaphoreType.DMA((pencils,)),
            pltpu.SemaphoreType.DMA((slabs,)),
            pltpu.SemaphoreType.DMA((slabs,)),
        ],
        cost_estimate=pl.CostEstimate(flops=10**10, bytes_accessed=2**23, transcendentals=0),
        compiler_params=pltpu.CompilerParams(
            collective_id=0, has_side_effects=True, vmem_limit_bytes=40 * 2**20
        ),
    )(own)


def field_kernel(
    own_ref,
    place_ref,
    sorted_ref,
    starts_ref,
    wide_pot,
    pot_ref,
    force_ref,
    slopes,
    bounds,
    found,
    by_row,
):
    def slope(after1, before1, after2, before2):
        return (8.0 * (after1 - before1) - (after2 - before2)) * (1.0 / 12.0)

    atoms = own_ref.shape[1]
    for plane in range(CZ):
        bounds[plane] = jnp.max(starts_ref[plane : plane + 1, :]).astype(jnp.int32)
    bounds[CZ] = jnp.int32(atoms)
    found[...] = jnp.zeros_like(found)
    size = math.gcd(atoms, 1024)

    @pl.loop(0, CZ)
    def _(plane):
        middle = wide_pot[plane + 2]
        own = middle[8:40]
        pot_ref[plane] = own
        at = [wide_pot[plane + 2 + k, 8:40, :] for k in (1, -1, 2, -2)]
        across = [pltpu.roll(middle, (-k) % 48, 0)[8:40] for k in (1, -1, 2, -2)]
        along = [shift_x(own, k) for k in (1, -1, 2, -2)]
        for direction, four in enumerate((at, across, along)):
            high, low = split_two(slope(*four))
            slopes[2 * direction * CY : (2 * direction + 1) * CY, :] = high
            slopes[(2 * direction + 1) * CY : (2 * direction + 2) * CY, :] = low
        first = bounds[plane]
        last = bounds[plane + 1]

        def block(step, carry):
            begin = pl.multiple_of(step * size, size)
            here = pl.ds(begin, size)
            table = one_hot(sorted_ref[1:2, here].astype(jnp.int32).astype(jnp.int16), NX)
            at_cell = jnp.dot(slopes[...], table, preferred_element_type=jnp.float32)
            index = begin + iota((1, size), 1)
            line = sorted_ref[0:1, here].astype(jnp.int32)
            line = jnp.where((index >= first) & (index < last), line, -1)
            at_row = iota((CY, size), 0) == line
            for direction in range(3):
                high = at_cell[2 * direction * CY : (2 * direction + 1) * CY]
                low = at_cell[(2 * direction + 1) * CY : (2 * direction + 2) * CY]
                found[direction : direction + 1, here] += jnp.sum(
                    jnp.where(at_row, high + low, 0.0), axis=0, keepdims=True
                )
            return carry

        lax.fori_loop(first // size, (last + size - 1) // size, block, 0)

    rows = atoms // 128
    for direction in range(3):
        for row in range(rows):
            there = slice(128 * row, 128 * row + 128)
            by_row[direction * rows + row : direction * rows + row + 1, :] = found[
                direction : direction + 1, there
            ]
    high, low = split_two(by_row[...])
    split = jnp.concatenate([high, low], axis=0)
    width = math.gcd(atoms, CHUNK)

    @pl.loop(0, atoms // width)
    def _(step):
        here = pl.ds(pl.multiple_of(step * width, width), width)
        to = place_ref[0:1, here].astype(jnp.int32)
        table = one_hot((to & 127).astype(jnp.int16), 128)
        values = jnp.dot(split, table, preferred_element_type=jnp.float32)
        at_row = iota((rows, width), 0) == to >> 7
        charges = own_ref[3:4, here]
        for direction in range(3):
            high = values[direction * rows : (direction + 1) * rows]
            low = values[(3 + direction) * rows : (4 + direction) * rows]
            chosen = jnp.sum(jnp.where(at_row, high + low, 0.0), axis=0, keepdims=True)
            force_ref[direction : direction + 1, here] = -charges * chosen


def field_call(base, own, order):
    atoms = own.shape[1]
    return pl.pallas_call(
        field_kernel,
        out_shape=[
            jax.ShapeDtypeStruct((CZ, CY, NX), jnp.float32),
            jax.ShapeDtypeStruct((3, atoms), jnp.float32),
        ],
        in_specs=[VMEM] * 5,
        out_specs=[VMEM] * 2,
        scratch_shapes=[
            pltpu.VMEM((6 * CY, NX), jnp.bfloat16),
            pltpu.SMEM((CZ + 1,), jnp.int32),
            pltpu.VMEM((3, atoms), jnp.float32),
            pltpu.VMEM((3 * atoms // 128, 128), jnp.float32),
        ],
        cost_estimate=pl.CostEstimate(flops=2 * 10**10, bytes_accessed=2**23, transcendentals=0),
        compiler_params=pltpu.CompilerParams(vmem_limit_bytes=40 * 2**20),
    )(own, *order, base)


def solution(mesh):
    slabs = mesh.shape["slab"]
    pencils = mesh.shape["pencil"]

    def body(atom_cell, charge):
        own = jnp.concatenate([atom_cell.astype(jnp.float32), charge[None]], axis=0)
        base, *order = exchange_call(slabs, pencils, own)
        potential, forces = field_call(base, own, order)
        return (potential, forces)

    return jax.shard_map(
        body,
        mesh=mesh,
        in_specs=(P(None, ("slab", "pencil")), P(("slab", "pencil"))),
        out_specs=(P("slab", "pencil", None), P(None, ("slab", "pencil"))),
        check_vma=False,
    )
```
